32 devices in a mesh: dp: 4 (over z), ctx: 4 (over y, core), tp: 2 (over x).
Axes of the slice: x: 2, y: 2, z: 4, core: 2. Of those that a mesh axis runs over, the one named last changes fastest.
Arguments:
- tokens_in: bfloat16 [12, 1024, 768], P('dp', 'ctx'), may hold values from -6 to 6
- block_ids: int32 [12, 1024], P('dp'), may hold values from 0 to 7, never falling along the last dimension, each value on 1 to 256 neighbouring positions
- rel_buckets: int32 [2047], replicated, may hold values from 0 to 31
- routes: int32 [12, 1024, 2], P('dp', 'ctx'), may hold values from 0 to 7, all different within a row; in each aligned block of 256 rows (0 to 255, 256 to 511, ..., all dimensions but the last counted through in order) at most 128 rows name the same one
- attn_gain: bfloat16 [1, 768], P(None, 'dp'), may hold values from 0.25 to 1.75
- w_qkv: bfloat16 [1, 3, 768, 768], P(None, None, 'dp', 'tp'), may hold values from -0.21875 to 0.21875
- w_attn_out: bfloat16 [1, 768, 768], P(None, 'tp', 'dp'), may hold values from -0.4375 to 0.4375
- bias_table: bfloat16 [1, 32, 12], P(None, 'dp', 'tp'), may hold values from -4 to 4
- moe_gain: bfloat16 [1, 768], P(None, 'dp'), may hold values from 0.25 to 1.75
- w_router: bfloat16 [1, 768, 8], P(None, 'dp'), may hold values from -0.15625 to 0.15625
- w_expert_in: bfloat16 [1, 8, 768, 3072], P(None, 'dp', 'ctx', 'tp'), may hold values from -0.21875 to 0.21875
- w_expert_out: bfloat16 [1, 8, 3072, 768], P(None, 'dp', 'tp', 'ctx'), may hold values from -0.21875 to 0.21875
- cotangent: bfloat16 [12, 1024, 768], P('dp', 'ctx'), may hold values from -6 to 6
Outputs:
- tokens_out: bfloat16 [12, 1024, 768], P('dp', 'ctx')
- grad_tokens: float32 [12, 1024, 768], P('dp', 'ctx')
- grad_attn_gain: float32 [1, 768], P(None, 'dp')
- grad_qkv: float32 [1, 3, 768, 768], P(None, None, 'dp', 'tp')
- grad_attn_out: float32 [1, 768, 768], P(None, 'tp', 'dp')
- grad_bias_table: float32 [1, 32, 12], P(None, 'dp', 'tp')
- grad_moe_gain: float32 [1, 768], P(None, 'dp')
- grad_router: float32 [1, 768, 8], P(None, 'dp')
- grad_expert_in: float32 [1, 8, 768, 3072], P(None, 'dp', 'ctx', 'tp')
- grad_expert_out: float32 [1, 8, 3072, 768], P(None, 'dp', 'tp', 'ctx')
The draws below stay inside these ranges and needn't reach their ends.
Inputs may be any that keep to these rules, and one draw needn't show every extreme that they name: `routes`: in each aligned block of 256 rows (one piece of one sequence), every row names 2 different experts, no expert is named by more than 128 rows, and in some or all blocks one expert is named by exactly 128 rows; every expert is named somewhere. `block_ids`: along each sequence the block numbers start at 0, never fall and rise by at most one; every block holds 1 to 256 tokens and one holds exactly 256.
All inputs are finite; a program needn't handle non-finite values.
Results may differ from the reference program's by a relative error of at most 0.015.
Values may be sent and summed in bfloat16 or wider, within the bound.
A program may use at most 256 MiB of HBM per device.

```python
import math
import jax
import jax.numpy as jnp
import numpy as np
from jax import lax

D = 768
H = 12
HD = 64
FF = 3072
TOP = 2
NB = 32
LEN = 1024
BLK = 256
LAYERS = 1
STRETCH = 256
SEQS = 12
EXPERTS = 8
CAP = 128
N_CTX = 4
N_TP = 2


def touch_ends(array, own_key, least, top_value):
    extent = array.shape
    place = [jax.random.randint(jax.random.fold_in(own_key, axis), (), 0, extent[axis]) for axis in range(len(extent))]
    array = array.at[tuple(place)].set(least)
    longest = extent.index(max(extent))
    place[longest] = (place[longest] + 1) % extent[longest]
    return array.at[tuple(place)].set(top_value)


def block_scale(rng, shape, split, smallest, top_value):
    def one(axis_at, blocks):
        steps = jax.random.uniform(jax.random.fold_in(jax.random.fold_in(rng, 6), axis_at), (blocks,), jnp.float32, smallest / len(split), top_value / len(split))
        return jnp.repeat(jnp.exp(steps), shape[axis_at] // blocks).reshape((-1,) + (1,) * (len(shape) - axis_at - 1))

    factor_of = one(*split[0])
    for cut in split[1:]:
        factor_of = factor_of * one(*cut)
    return factor_of


def length_profile(count, total, limit, skew):
    portions = [(1 << 20) // math.isqrt(rank ** skew) + 1 for rank in range(2, count + 1)]
    rest, holding = total - limit - (count - 1), [1] * (count - 1)
    while rest > 0:
        candidates = [i for i in range(count - 1) if holding[i] < limit]
        pool, remaining = sum([portions[i] for i in candidates]), rest
        for i in candidates:
            more = min(limit - holding[i], max(1, remaining * portions[i] // pool), rest)
            holding[i] = holding[i] + more
            rest = rest - more
    return np.array([limit] + holding)


def uneven_parts(stream_key, number_of, total, reach, slope):
    if number_of == 2:
        one = jax.random.randint(stream_key, (), max(1, total - reach), min(reach, total - 1) + 1)
        return jnp.stack([one, total - one])
    lengths = jnp.asarray(length_profile(number_of, total, reach, slope), jnp.int32)
    pairs = (number_of - 1) // 2
    giver, sink = lengths[1:1 + 2 * pairs:2], lengths[2:2 + 2 * pairs:2]
    slack = jnp.minimum(giver - 1, reach - sink)
    passed = jax.random.randint(jax.random.fold_in(stream_key, 1), (pairs,), 0, 1 << 20) % (slack + 1)
    lengths = lengths.at[1:1 + 2 * pairs:2].set(giver - passed).at[2:2 + 2 * pairs:2].set(sink + passed)
    return lengths[jax.random.permutation(jax.random.fold_in(stream_key, 2), number_of)]


def routed_block(key, own, number, rows, amount, top, bound, slope):
    order = jax.random.permutation(key, amount)
    crowded, ordinary = load_shares(amount, rows * top, bound, slope, True), load_shares(amount, rows * top, bound, slope, False)
    places = jnp.arange(amount)

    def named(sizes, turn):
        used = int((sizes > 0).sum())
        fixed = max(1, used // 4)
        shifted = fixed + (places - fixed + turn * (used - fixed)) % max(1, amount - fixed)
        return jnp.zeros((amount,), jnp.int32).at[order[jnp.where(places < fixed, places, shifted)]].set(jnp.asarray(sizes, jnp.int32))

    sizes = jnp.where(number % 4 == 0, named(crowded, number // 4), named(ordinary, number - number // 4 - 1))
    mixed = jax.random.permutation(jax.random.fold_in(own, 3), amount)
    giver, taker = mixed[0:amount // 2 * 2:2], mixed[1:amount // 2 * 2:2]
    room = jnp.minimum(sizes[giver] - 1, bound - sizes[taker]) // 2
    room = jnp.where((giver == order[0]) | (taker == order[0]) | (sizes[taker] == 0), 0, jnp.maximum(room, 0))
    shifted = jax.random.randint(jax.random.fold_in(own, 4), (amount // 2,), 0, 1 << 20) % (room + 1)
    sizes = sizes.at[giver].add(-shifted).at[taker].add(shifted)
    members = jnp.searchsorted(jnp.cumsum(sizes), jnp.arange(rows * top), side="right").astype(jnp.int32)
    grid = members.reshape(top, rows).T
    grid = grid[jax.random.permutation(jax.random.fold_in(own, 1), rows)]
    turn = jax.random.randint(jax.random.fold_in(own, 2), (rows, 1), 0, top)
    return jnp.take_along_axis(grid, (jnp.arange(top)[None, :] + turn) % top, axis=1)


def load_shares(count, total, bound, slope, full):
    portions = [(1 << 20) // math.isqrt(standing ** slope) + 1 for standing in range(1, count + 1)]
    largest = bound if full else min(bound, max(-(-total // count), total * portions[0] // sum(portions)))
    least = 1 if total - largest >= count - 1 else 0
    counts, spare = [largest] + [least] * (count - 1), total - largest - least * (count - 1)
    while spare > 0:
        free = [i for i in range(1, count) if counts[i] < largest] or [i for i in range(1, count) if counts[i] < bound]
        pool, budget = sum([portions[i] for i in free]), spare
        for i in free:
            more = min(bound - counts[i], max(1, budget * portions[i] // pool), spare)
            counts[i] = counts[i] + more
            spare = spare - more
    return np.array(counts)


def gaussian(stream_key, dims, deviation, most, cuts=(), kind=jnp.bfloat16):
    drawn = jax.random.normal(stream_key, dims, jnp.float32) * deviation
    if len(cuts) > 0:
        drawn = block_scale(stream_key, dims, cuts, -0.22, 0.18) * drawn
    return jnp.clip(drawn, min=-most, max=most).astype(kind)


def setup_inputs(seed: int = 0) -> dict:
    key_of = jax.random.split(jax.random.key(seed), 14)
    tokens_in = gaussian(key_of[0], (SEQS, LEN, D), 1.0, 6.0, ((0, 4), (1, 4)))
    block_ids = jax.vmap(lambda own: jnp.searchsorted(jnp.cumsum(uneven_parts(own, 2 * LEN // BLK, LEN, BLK, 1)), jnp.arange(LEN), side="right"))(jax.random.split(key_of[1], SEQS)).reshape((SEQS, LEN)).astype(jnp.int32)
    rel_buckets = touch_ends(jax.random.randint(key_of[2], (2 * LEN - 1,), 0, NB), jax.random.fold_in(key_of[2], 1), 0, NB - 1).astype(jnp.int32)
    routes_keys = jax.random.split(jax.random.fold_in(key_of[3], 1), SEQS * LEN // STRETCH)
    routes_turns = jax.random.permutation(jax.random.fold_in(key_of[3], 3), SEQS * LEN // STRETCH)
    routes = jax.vmap(lambda own, number: routed_block(jax.random.fold_in(key_of[3], 2), own, number, STRETCH, EXPERTS, TOP, CAP, 1))(routes_keys, routes_turns).reshape((SEQS, LEN, TOP))
    attn_gain = jnp.clip(1.0 + 0.15 * jax.random.normal(key_of[4], (LAYERS, D), jnp.float32), 0.25, 1.75).astype(jnp.bfloat16)
    w_qkv = gaussian(key_of[5], (LAYERS, 3, D, D), D ** -0.5, 0.21875, ((2, 4), (3, 2)))
    w_attn_out = gaussian(key_of[6], (LAYERS, D, D), (D // 4) ** -0.5, 0.4375, ((1, 2), (2, 4)))
    bias_table = gaussian(key_of[7], (LAYERS, NB, H), 1.0, 4.0, ((1, 4), (2, 2)))
    moe_gain = jnp.clip(1.0 + 0.15 * jax.random.normal(key_of[8], (LAYERS, D), jnp.float32), 0.25, 1.75).astype(jnp.bfloat16)
    w_router = gaussian(key_of[9], (LAYERS, D, EXPERTS), (2 * D) ** -0.5, 0.15625, ((1, 4),))
    w_expert_in = gaussian(key_of[10], (LAYERS, EXPERTS, D, FF), D ** -0.5, 0.21875, ((1, 4), (2, 4), (3, 2)))
    w_expert_out = gaussian(key_of[11], (LAYERS, EXPERTS, FF, D), (FF // 4) ** -0.5, 0.21875, ((1, 4), (2, 2), (3, 4)))
    cotangent = gaussian(key_of[12], (SEQS, LEN, D), 1.0, 6.0, ((0, 4), (1, 4)))
    return {"tokens_in": tokens_in, "block_ids": block_ids, "rel_buckets": rel_buckets, "routes": routes, "attn_gain": attn_gain, "w_qkv": w_qkv, "w_attn_out": w_attn_out, "bias_table": bias_table, "moe_gain": moe_gain, "w_router": w_router, "w_expert_in": w_expert_in, "w_expert_out": w_expert_out, "cotangent": cotangent}


@jax.custom_vjp
def low(v):
    return lax.optimization_barrier(v.astype(jnp.bfloat16)).astype(jnp.float32)

@jax.custom_vjp
def low_back(v):
    return v

def low_keep(v):
    return (low(v), None)

def low_pass(kept, grad):
    return (grad,)

def back_keep(v):
    return (v, None)

def back_low(kept, grad):
    return (low(grad),)
low.defvjp(low_keep, low_pass)
low_back.defvjp(back_keep, back_low)
EPSILON = 1e-06
FULL_PRECISION = lax.Precision.HIGHEST

def norm_rows(value_matrix, gain):
    factor = lax.rsqrt(lax.optimization_barrier(jnp.mean(value_matrix * value_matrix, axis=-1, keepdims=True)) + EPSILON)
    return value_matrix * factor * gain

def sequence_attention(queries, key_rows, value_rows, seq_ids, rel_bias):
    places = jnp.arange(LEN, dtype=jnp.int32)
    offsets = (places[:, None] - places[None, :] + (LEN - 1)).astype(jnp.int32)
    bias_full = rel_bias[:, offsets]
    raw_scores = jnp.einsum('qhd,khd->hqk', queries, key_rows, precision=FULL_PRECISION) * HD ** (-0.5)
    scores = low_back(raw_scores) + bias_full
    visible = seq_ids[None, :] <= seq_ids[:, None]
    probs = jax.nn.softmax(jnp.where(visible[None], scores, -1e+30), axis=-1)
    return jnp.einsum('hqk,khd->qhd', low(probs), value_rows, precision=FULL_PRECISION)

def expert_block(inputs, w_in, w_out):
    piece_len = FF // N_TP
    pieces_pre = [jnp.dot(low_back(inputs), w_in[:, index * piece_len:(index + 1) * piece_len], precision=FULL_PRECISION) for index in range(N_TP)]
    pre_act = low_back(jnp.concatenate(pieces_pre, axis=1))
    hidden = low(jax.nn.gelu(pre_act))
    pieces_out = [low(jnp.dot(hidden[:, index * piece_len:(index + 1) * piece_len], w_out[index * piece_len:(index + 1) * piece_len], precision=FULL_PRECISION)) for index in range(N_TP)]
    return low_back(lax.optimization_barrier(jnp.sum(jnp.stack(pieces_out), axis=0)))

def mixture(moe_in, route_rows, w_router, w_in, w_out):
    token_count = moe_in.shape[0]
    capacity = SEQS * N_CTX * CAP
    logits = jnp.dot(moe_in, w_router, precision=FULL_PRECISION)
    gates = jax.nn.softmax(jnp.take_along_axis(logits, route_rows, axis=1), axis=-1)
    flat_routes = route_rows.reshape(-1).astype(jnp.int32)
    hit_counts = (flat_routes[:, None] == jnp.arange(EXPERTS, dtype=jnp.int32)[None, :]).astype(jnp.int32)
    rank = (lax.optimization_barrier(jnp.sum(jnp.cumsum(hit_counts, axis=0).astype(jnp.int32) * hit_counts, axis=1)) - 1).astype(jnp.int32)
    slot = (flat_routes * capacity + rank).astype(jnp.int32)
    source_row = (jnp.arange(token_count * TOP, dtype=jnp.int32) // TOP).astype(jnp.int32)
    owner = jnp.zeros((EXPERTS * capacity,), jnp.int32).at[slot].set(source_row)
    inputs = moe_in[owner].reshape(EXPERTS, capacity, D)
    run_expert = jax.checkpoint(expert_block)
    outputs = lax.map(lambda packed: run_expert(packed[0], packed[1], packed[2]), (inputs, w_in, w_out))
    picked = outputs.reshape(EXPERTS * capacity, D)[slot].reshape(token_count, TOP, D)
    return lax.optimization_barrier(jnp.sum(gates[:, :, None] * picked, axis=1))

def layer_forward(value_matrix, weights, routes, block_ids, rel_buckets):
    gain_attn, query_key_value_weight, output_weight, table, gain_moe, wrouter, w_in, w_out = weights
    seq_count = value_matrix.shape[0]
    normalized_input = low(norm_rows(value_matrix, gain_attn))
    output_projection = low_back(low(jnp.einsum('xim,fmh->fxih', normalized_input, query_key_value_weight, precision=FULL_PRECISION)))
    shaped = output_projection.reshape(3, seq_count, LEN, H, HD)
    rel_bias = table[rel_buckets].T
    attend = jax.checkpoint(sequence_attention)
    attention_output = lax.map(lambda packed: attend(packed[0], packed[1], packed[2], packed[3], rel_bias), (shaped[0], shaped[1], shaped[2], block_ids))
    attention_output = low_back(low(attention_output.reshape(seq_count, LEN, D)))
    middle_activation = value_matrix + low_back(jnp.einsum('bio,ok->bik', attention_output, output_weight, precision=FULL_PRECISION))
    moe_in = low(norm_rows(middle_activation, gain_moe)).reshape(seq_count * LEN, D)
    mixed = mixture(moe_in, routes.reshape(seq_count * LEN, TOP), wrouter, w_in, w_out)
    return middle_activation + mixed.reshape(middle_activation.shape)

def reference(tokens_in, block_ids, rel_buckets, routes, attn_gain, w_qkv, w_attn_out, bias_table, moe_gain, w_router, w_expert_in, w_expert_out, cotangent):
    floats = (tokens_in.astype(jnp.float32), attn_gain.astype(jnp.float32), w_qkv.astype(jnp.float32), w_attn_out.astype(jnp.float32), bias_table.astype(jnp.float32), moe_gain.astype(jnp.float32), w_router.astype(jnp.float32), w_expert_in.astype(jnp.float32), w_expert_out.astype(jnp.float32))

    def forward(value_matrix, gain_attn, query_key_value_weight, output_weight, table, gain_moe, wrouter, w_in, w_out):
        for layer_index in range(LAYERS):
            weights = (gain_attn[layer_index], query_key_value_weight[layer_index], output_weight[layer_index], table[layer_index], gain_moe[layer_index], wrouter[layer_index], w_in[layer_index], w_out[layer_index])
            value_matrix = layer_forward(value_matrix, weights, routes, block_ids, rel_buckets)
        return value_matrix
    result, pullback = jax.vjp(forward, *floats)
    grads = pullback(cotangent.astype(jnp.float32))
    return (result.astype(jnp.bfloat16), grads[0], grads[1], grads[2], grads[3], grads[4], grads[5], grads[6], grads[7], grads[8])
```

```python
import functools

import jax
import jax.numpy as jnp
from jax import lax
from jax.experimental import pallas as pl
from jax.experimental.pallas import tpu as pltpu
from jax.sharding import PartitionSpec as P

HD = 64
NB = 32
EPSILON = 1e-06
FULL_PRECISION = lax.Precision.HIGHEST
MASKED = -1e30
BF16 = jnp.bfloat16
F32 = jnp.float32
VMEM_BYTES = 60 * 1024 * 1024
GELU_C = 0.7978845608028654
GELU_A = 0.044715


def params():
    return pltpu.CompilerParams(vmem_limit_bytes=VMEM_BYTES)


def cost(flops, nbytes, trans=0):
    return pl.CostEstimate(flops=int(flops), bytes_accessed=int(nbytes), transcendentals=int(trans))


def dot(a, b):
    return lax.dot_general(a, b, (((1,), (0,)), ((), ())), preferred_element_type=F32)


def dot_nt(a, b):
    return lax.dot_general(a, b, (((1,), (1,)), ((), ())), preferred_element_type=F32)


def dot_tn(a, b):
    return lax.dot_general(a, b, (((0,), (0,)), ((), ())), preferred_element_type=F32)


def bias_kernel(win_ref, out_ref):
    for block in range(4):
        row = win_ref[0, block : block + 1, :]
        wide = jnp.broadcast_to(row, (256, 512))
        rolled = pltpu.roll(wide, 257, 1, stride=1, stride_axis=0)
        out_ref[0, block * 256 : (block + 1) * 256, :] = rolled[:, :256].astype(BF16)


def expand_bias(windows):
    heads = windows.shape[0]
    return pl.pallas_call(
        bias_kernel,
        name="expand_bias",
        grid=(heads,),
        in_specs=[pl.BlockSpec((1, 4, 512), lambda h: (h, 0, 0))],
        out_specs=pl.BlockSpec((1, 1024, 256), lambda h: (h, 0, 0)),
        out_shape=jax.ShapeDtypeStruct((heads, 1024, 256), BF16),
        compiler_params=params(),
        cost_estimate=cost(heads * 2 * 1024 * 512, heads * 1024 * 256 * 2),
    )(windows)


def attend_kernel(q_ref, k_ref, v_ref, bias_ref, idq_ref, idk_ref, out_ref, lse_ref, mask_ref):
    @pl.when(pl.program_id(0) == 0)
    def _():
        mask_ref[...] = jnp.where(idk_ref[...] <= idq_ref[...], 0.0, MASKED)

    queries = q_ref[...]
    keys = k_ref[...]
    values_t = v_ref[...].T
    low_half = lax.broadcasted_iota(jnp.int32, queries.shape, 1) < HD
    zero = jnp.zeros_like(queries)
    parts = []
    for head in range(2):
        own = jnp.where(low_half, queries, zero) if head == 0 else jnp.where(low_half, zero, queries)
        scores = dot_nt(keys, own) + bias_ref[head].astype(F32) + mask_ref[...]
        top = jnp.max(scores, axis=0, keepdims=True)
        weights = jnp.exp(scores - top)
        total = jnp.sum(weights, axis=0, keepdims=True)
        part = dot(values_t[head * HD : (head + 1) * HD], weights.astype(BF16)) * (1.0 / total)
        parts.append(part)
        lse_ref[0, head : head + 1, :] = top + jnp.log(total)
    out_ref[...] = jnp.concatenate(parts, axis=0).T.astype(BF16)


def attend(queries, keys, values, bias, ids_query, ids_key):
    rows, width = queries.shape
    length = keys.shape[0]
    pairs = width // (2 * HD)
    return pl.pallas_call(
        attend_kernel,
        name="attend",
        grid=(pairs,),
        in_specs=[
            pl.BlockSpec((rows, 128), lambda p: (0, p)),
            pl.BlockSpec((length, 128), lambda p: (0, p)),
            pl.BlockSpec((length, 128), lambda p: (0, p)),
            pl.BlockSpec((2, length, rows), lambda p: (p, 0, 0)),
            pl.BlockSpec((1, rows), lambda p: (0, 0)),
            pl.BlockSpec((length, 1), lambda p: (0, 0)),
        ],
        out_specs=[
            pl.BlockSpec((rows, 128), lambda p: (0, p)),
            pl.BlockSpec((1, 2, rows), lambda p: (p, 0, 0)),
        ],
        out_shape=[
            jax.ShapeDtypeStruct((rows, width), BF16),
            jax.ShapeDtypeStruct((pairs, 2, rows), F32),
        ],
        scratch_shapes=[pltpu.VMEM((length, rows), F32)],
        compiler_params=params(),
        cost_estimate=cost(pairs * 2 * 4 * rows * length * 128, 6 * rows * length * 2, pairs * 2 * rows * length),
    )(queries, keys, values, bias, ids_query, ids_key)


def attend_back_kernel(
    q_ref, k_ref, v_ref, do_ref, bias_ref, lse_ref, idq_ref, idk_ref, dq_ref, dk_ref, dv_ref, rel_ref, mask_ref
):
    @pl.when(pl.program_id(0) == 0)
    def _():
        mask_ref[...] = jnp.where(idk_ref[...] <= idq_ref[...], 0.0, MASKED)

    queries = q_ref[...]
    keys = k_ref[...]
    values = v_ref[...]
    grad_out = do_ref[...]
    keys_t = keys.T
    low_half = lax.broadcasted_iota(jnp.int32, queries.shape, 1) < HD
    zero = jnp.zeros_like(queries)
    dk = None
    dv = None
    dq_parts = []
    for head in range(2):
        own = (lambda a: jnp.where(low_half, a, zero)) if head == 0 else (lambda a: jnp.where(low_half, zero, a))
        q_own = own(queries)
        do_own = own(grad_out)
        scores = dot_nt(keys, q_own) + bias_ref[head].astype(F32) + mask_ref[...]
        probs = jnp.exp(scores - lse_ref[0, head : head + 1, :])
        dprobs = dot_nt(values, do_own)
        delta = jnp.sum(probs * dprobs, axis=0, keepdims=True)
        dscores = probs * (dprobs - delta)
        low = dscores.astype(BF16)
        dv_head = dot(probs.astype(BF16), do_own)
        dk_head = dot(low, q_own)
        dv = dv_head if dv is None else dv + dv_head
        dk = dk_head if dk is None else dk + dk_head
        dq_parts.append(dot(keys_t[head * HD : (head + 1) * HD], low))
        for block in range(4):
            tile = dscores[block * 256 : (block + 1) * 256]
            wide = jnp.concatenate([tile, jnp.zeros_like(tile)], axis=1)
            total = None
            for group in range(32):
                moved = pltpu.roll(wide[group * 8 : group * 8 + 8], 248 - 8 * group, 1)
                total = moved if total is None else total + moved
            row = lax.broadcasted_iota(jnp.int32, total.shape, 0)
            amount = 7 - row
            for bit in (1, 2, 4):
                total = jnp.where((amount & bit) != 0, pltpu.roll(total, bit, 1), total)
            rel_ref[0, head, block : block + 1, :] = jnp.sum(total, axis=0, keepdims=True)
    dq_ref[...] = (jnp.concatenate(dq_parts, axis=0).T * (HD ** (-0.5))).astype(BF16)
    dk_ref[...] = dk.astype(BF16)
    dv_ref[...] = dv.astype(BF16)


def attend_back(queries, keys, values, grad_out, bias, lse, ids_query, ids_key):
    rows, width = queries.shape
    length = keys.shape[0]
    pairs = width // (2 * HD)
    return pl.pallas_call(
        attend_back_kernel,
        name="attend_back",
        grid=(pairs,),
        in_specs=[
            pl.BlockSpec((rows, 128), lambda p: (0, p)),
            pl.BlockSpec((length, 128), lambda p: (0, p)),
            pl.BlockSpec((length, 128), lambda p: (0, p)),
            pl.BlockSpec((rows, 128), lambda p: (0, p)),
            pl.BlockSpec((2, length, rows), lambda p: (p, 0, 0)),
            pl.BlockSpec((1, 2, rows), lambda p: (p, 0, 0)),
            pl.BlockSpec((1, rows), lambda p: (0, 0)),
            pl.BlockSpec((length, 1), lambda p: (0, 0)),
        ],
        out_specs=[
            pl.BlockSpec((rows, 128), lambda p: (0, p)),
            pl.BlockSpec((length, 128), lambda p: (0, p)),
            pl.BlockSpec((length, 128), lambda p: (0, p)),
            pl.BlockSpec((1, 2, 4, 512), lambda p: (p, 0, 0, 0)),
        ],
        out_shape=[
            jax.ShapeDtypeStruct((rows, width), BF16),
            jax.ShapeDtypeStruct((length, width), BF16),
            jax.ShapeDtypeStruct((length, width), BF16),
            jax.ShapeDtypeStruct((pairs, 2, 4, 512), F32),
        ],
        scratch_shapes=[pltpu.VMEM((length, rows), F32)],
        compiler_params=params(),
        cost_estimate=cost(pairs * 2 * 10 * rows * length * 128, 8 * rows * length * 2, pairs * 2 * rows * length),
    )(queries, keys, values, grad_out, bias, lse, ids_query, ids_key)


def one_hot(place, cap):
    groups, rows = place.shape
    slots = lax.broadcasted_iota(jnp.int32, (cap, rows), 0).astype(F32)
    return [slots == place[group : group + 1, :] for group in range(groups)]


def diagonal(cap):
    return lax.broadcasted_iota(jnp.int32, (cap, cap), 0) == lax.broadcasted_iota(jnp.int32, (cap, cap), 1)


def dispatch_kernel(groups, cap, place_ref, rows_ref, out_ref):
    rows = rows_ref[0]
    picks = one_hot(place_ref[0], cap)
    pick = jnp.concatenate([jnp.where(p, 1.0, 0.0).astype(BF16) for p in picks], axis=0)
    out_ref[:, 0] = dot(pick, rows).astype(BF16).reshape(groups, cap, rows.shape[1])


def dispatch(place, rows, cap):
    seqs, groups, stretch = place.shape
    width = rows.shape[2]
    return pl.pallas_call(
        functools.partial(dispatch_kernel, groups, cap),
        name="dispatch_rows",
        grid=(seqs,),
        in_specs=[
            pl.BlockSpec((1, groups, stretch), lambda s: (s, 0, 0)),
            pl.BlockSpec((1, stretch, width), lambda s: (s, 0, 0)),
        ],
        out_specs=pl.BlockSpec((groups, 1, cap, width), lambda s: (0, s, 0, 0)),
        out_shape=jax.ShapeDtypeStruct((groups, seqs, cap, width), BF16),
        compiler_params=params(),
        cost_estimate=cost(seqs * 2 * groups * cap * stretch * width, seqs * 2 * (stretch + groups * cap) * width),
    )(place, rows)


def norm_factor(value):
    return lax.rsqrt(jnp.mean(value * value, axis=-1, keepdims=True) + EPSILON)


def middle_kernel(
    groups, cap, own_ref, other_ref, x_ref, wout_ref, gain_ref, router_ref, hits_ref, place_ref,
    middle_ref, moe_ref, gates_ref, send_ref, slot_gate_ref,
):
    mid = x_ref[...].astype(F32) + (dot(own_ref[...], wout_ref[0]) + dot(other_ref[...], wout_ref[1]))
    middle_ref[...] = mid
    moe_in = (mid * norm_factor(mid) * gain_ref[...].astype(F32)).astype(BF16)
    moe_ref[...] = moe_in
    logits = dot_nt(router_ref[...], moe_in)
    hit = hits_ref[...] > 0.5
    top = jnp.max(jnp.where(hit, logits, MASKED), axis=0, keepdims=True)
    raw = jnp.where(hit, jnp.exp(jnp.where(hit, logits, top) - top), 0.0)
    gates = raw / jnp.sum(raw, axis=0, keepdims=True)
    gates_ref[...] = gates
    picks = one_hot(place_ref[...], cap)
    pick = jnp.concatenate([jnp.where(p, 1.0, 0.0).astype(BF16) for p in picks], axis=0)
    send_ref[...] = dot(pick, moe_in).astype(BF16).reshape(groups, cap, moe_in.shape[1])
    eye = diagonal(cap)
    for group in range(groups):
        column = jnp.sum(jnp.where(picks[group], gates[group : group + 1, :], 0.0), axis=1, keepdims=True)
        slot_gate_ref[group] = jnp.sum(jnp.where(eye, column, 0.0), axis=0, keepdims=True)


def middle_stage(own, other, x, wout, gain, router, hits, place, cap):
    rows, width = x.shape
    experts = router.shape[0]
    groups = place.shape[0]
    return pl.pallas_call(
        functools.partial(middle_kernel, groups, cap),
        name="middle_stage",
        out_shape=[
            jax.ShapeDtypeStruct((rows, width), F32),
            jax.ShapeDtypeStruct((rows, width), BF16),
            jax.ShapeDtypeStruct((experts, rows), F32),
            jax.ShapeDtypeStruct((groups, cap, width), BF16),
            jax.ShapeDtypeStruct((groups, 1, cap), F32),
        ],
        compiler_params=params(),
        cost_estimate=cost(2 * rows * width * width + 2 * groups * cap * rows * width, rows * width * 16),
    )(own, other, x, wout, gain, router, hits, place)


def expert_kernel(
    first, final, tiles, groups, cap, x_ref, g_ref, gate_ref, w_ref, *refs
):
    if first:
        acc_in = None
    else:
        acc_in, refs = refs[0], refs[1:]
    part_out, din_out, h_out, acc_out, xt_ref, dy_ref, dyt_ref, part_ref, din_ref = refs
    step = pl.program_id(0)
    rows = groups * cap
    width = x_ref.shape[-1]
    slices = w_ref.shape[0]
    piece = width // slices

    @pl.when(step == 0)
    def _():
        eye = diagonal(cap)
        xt_ref[...] = x_ref[...].reshape(rows, width).T
        for group in range(groups):
            gate = jnp.sum(jnp.where(eye, gate_ref[group], 0.0), axis=1, keepdims=True)
            dy_ref[group * cap : (group + 1) * cap] = (g_ref[group, 0].astype(F32) * gate).astype(BF16)
        dyt_ref[...] = dy_ref[...].T

    x = x_ref[...].reshape(rows, width)
    w_in = w_ref[:, 0, 0].reshape(width, -1)
    w_out_t = w_ref[:, 1, 0].reshape(width, -1)
    dy = dy_ref[...]
    pre = dot(x, w_in)
    square = pre * pre
    inner = jnp.tanh(GELU_C * pre * (1.0 + GELU_A * square))
    half = 0.5 * (1.0 + inner)
    hidden = (pre * half).astype(BF16)
    slope = half + (0.5 * GELU_C) * pre * (1.0 - inner * inner) * (1.0 + (3.0 * GELU_A) * square)
    dhid = dot(dy, w_out_t)
    dpre = (dhid * slope).astype(BF16)
    part = dot_nt(hidden, w_out_t)
    din = dot_nt(dpre, w_in)
    dw_in = dot(xt_ref[...], dpre)
    dw_out_t = dot(dyt_ref[...], hidden)

    @pl.when(step == 0)
    def _():
        part_ref[...] = part
        din_ref[...] = din

    @pl.when(step > 0)
    def _():
        part_ref[...] += part
        din_ref[...] += din

    me = lax.axis_index("ctx")
    for index in range(slices):
        place = index ^ me
        grad_in = dw_in[index * piece : (index + 1) * piece]
        grad_out = dw_out_t[index * piece : (index + 1) * piece]
        if not first:
            grad_in += acc_in[0, place, 0]
            grad_out += acc_in[0, place, 1]
        acc_out[0, place, 0] = grad_in.astype(acc_out.dtype)
        acc_out[0, place, 1] = grad_out.astype(acc_out.dtype)

    @pl.when(step == tiles - 1)
    def _():
        eye = diagonal(cap)
        for group in range(groups):
            gate = jnp.sum(jnp.where(eye, gate_ref[group], 0.0), axis=1, keepdims=True)
            gated = part_ref[group * cap : (group + 1) * cap] * gate
            part_out[group] = gated.astype(BF16)
            din_out[group] = din_ref[group * cap : (group + 1) * cap].astype(BF16)
            h = jnp.sum(gated * g_ref[group, 0].astype(F32), axis=1, keepdims=True)
            h_out[group] = jnp.sum(jnp.where(eye, h, 0.0), axis=0, keepdims=True)


def experts(x, cot_slots, seq_index, gate, weights, acc, final, tile=512):
    groups, cap, width = x.shape
    slices, _, halves, piece, half_len = weights.shape
    per_half = half_len // tile
    tiles = halves * per_half
    rows = groups * cap
    first = acc is None
    acc_spec = pl.BlockSpec((1, slices, 2, piece, tile), lambda f: (f // per_half, 0, 0, 0, f % per_half))
    in_specs = [
        pl.BlockSpec((groups, cap, width), lambda f: (0, 0, 0)),
        pl.BlockSpec((groups, 1, cap, width), lambda f: (0, seq_index, 0, 0)),
        pl.BlockSpec((groups, 1, cap), lambda f: (0, 0, 0)),
        pl.BlockSpec((slices, 2, 1, piece, tile), lambda f: (0, 0, f // per_half, 0, f % per_half)),
    ]
    args = [x, cot_slots, gate, weights]
    aliases = {}
    if not first:
        in_specs.append(acc_spec)
        args.append(acc)
        if not final:
            aliases = {4: 3}
    acc_shape = (halves, slices, 2, piece, half_len)
    return pl.pallas_call(
        functools.partial(expert_kernel, first, final, tiles, groups, cap),
        name="experts",
        grid=(tiles,),
        in_specs=in_specs,
        out_specs=[
            pl.BlockSpec((groups, cap, width), lambda f: (0, 0, 0)),
            pl.BlockSpec((groups, cap, width), lambda f: (0, 0, 0)),
            pl.BlockSpec((groups, 1, cap), lambda f: (0, 0, 0)),
            acc_spec,
        ],
        out_shape=[
            jax.ShapeDtypeStruct((groups, cap, width), BF16),
            jax.ShapeDtypeStruct((groups, cap, width), BF16),
            jax.ShapeDtypeStruct((groups, 1, cap), F32),
            jax.ShapeDtypeStruct(acc_shape, BF16 if final else F32),
        ],
        scratch_shapes=[
            pltpu.VMEM((width, rows), BF16),
            pltpu.VMEM((rows, width), BF16),
            pltpu.VMEM((width, rows), BF16),
            pltpu.VMEM((rows, width), F32),
            pltpu.VMEM((rows, width), F32),
        ],
        input_output_aliases=aliases,
        compiler_params=params(),
        cost_estimate=cost(12 * rows * width * halves * half_len, 2 * width * halves * half_len * 10, rows * halves * half_len),
    )(*args)


def combine_kernel(groups, cap, place_ref, din_ref, h_ref, din_out, h_out):
    picks = one_hot(place_ref[...], cap)
    pick = jnp.concatenate([jnp.where(p, 1.0, 0.0).astype(BF16) for p in picks], axis=0)
    rows = groups * cap
    din_out[...] = dot_tn(pick, din_ref[...].reshape(rows, din_ref.shape[-1])).astype(BF16)
    eye = diagonal(cap)
    for group in range(groups):
        column = jnp.sum(jnp.where(eye, h_ref[group], 0.0), axis=1, keepdims=True)
        h_out[group : group + 1, :] = jnp.sum(jnp.where(picks[group], column, 0.0), axis=0, keepdims=True)


def combine(place, din, h, cap):
    groups, stretch = place.shape
    width = din.shape[-1]
    return pl.pallas_call(
        functools.partial(combine_kernel, groups, cap),
        name="combine_back",
        out_shape=[
            jax.ShapeDtypeStruct((stretch, width), BF16),
            jax.ShapeDtypeStruct((groups, stretch), F32),
        ],
        compiler_params=params(),
        cost_estimate=cost(2 * groups * cap * stretch * width, 4 * stretch * width * 2),
    )(place, din, h)


def combine_out_kernel(groups, cap, place_ref, part_ref, out_ref):
    picks = one_hot(place_ref[...], cap)
    pick = jnp.concatenate([jnp.where(p, 1.0, 0.0).astype(BF16) for p in picks], axis=0)
    out_ref[...] = dot_tn(pick, part_ref[...].reshape(groups * cap, part_ref.shape[-1])).astype(BF16)


def combine_out(place, part, cap):
    groups, stretch = place.shape
    width = part.shape[-1]
    return pl.pallas_call(
        functools.partial(combine_out_kernel, groups, cap),
        name="combine_out",
        out_shape=jax.ShapeDtypeStruct((stretch, width), BF16),
        compiler_params=params(),
        cost_estimate=cost(2 * groups * cap * stretch * width, 4 * stretch * width * 2),
    )(place, part)


def middle_back_kernel(
    own_ref, other_ref, h_ref, gates_ref, router_ref, moe_ref, mid_ref, gain_ref, cot_ref, att_ref, wout_ref,
    gmid_ref, datt_ref, gain_grad_ref, router_grad_ref, wout_grad_ref,
):
    h = h_ref[...]
    dlogits = h - gates_ref[...] * jnp.sum(h, axis=0, keepdims=True)
    router = router_ref[...]
    dmoe = own_ref[...].astype(F32) + other_ref[...].astype(F32)
    dmoe = dmoe + lax.dot_general(
        dlogits, router.astype(F32), (((0,), (0,)), ((), ())), precision=FULL_PRECISION, preferred_element_type=F32
    )
    router_grad_ref[...] = lax.dot_general(
        dlogits, moe_ref[...].astype(F32), (((1,), (0,)), ((), ())), precision=FULL_PRECISION, preferred_element_type=F32
    )
    mid = mid_ref[...]
    gain = gain_ref[...].astype(F32)
    factor = norm_factor(mid)
    normed = mid * factor
    gain_grad_ref[...] = jnp.sum(dmoe * normed, axis=0, keepdims=True)
    scaled = dmoe * gain
    dmid = factor * (scaled - normed * jnp.mean(scaled * normed, axis=-1, keepdims=True))
    gmid = cot_ref[...].astype(F32) + dmid
    gmid_ref[...] = gmid
    dattn = gmid.astype(BF16)
    datt_ref[...] = dot_nt(dattn, wout_ref[...]).astype(BF16)
    wout_grad_ref[...] = dot_tn(att_ref[...], dattn)


def middle_back(own, other, h, gates, router, moe_in, mid, gain, cot, attended, wout):
    rows, width = mid.shape
    local = attended.shape[1]
    return pl.pallas_call(
        middle_back_kernel,
        name="middle_back",
        out_shape=[
            jax.ShapeDtypeStruct((rows, width), F32),
            jax.ShapeDtypeStruct((rows, local), BF16),
            jax.ShapeDtypeStruct((1, width), F32),
            jax.ShapeDtypeStruct(router.shape, F32),
            jax.ShapeDtypeStruct((local, width), F32),
        ],
        compiler_params=params(),
        cost_estimate=cost(6 * rows * width * local, 30 * rows * width),
    )(own, other, h, gates, router, moe_in, mid, gain, cot, attended, wout)


def flip(value, axis, bit):
    count = lax.axis_size(axis)
    return lax.ppermute(value, axis, [(i, i ^ bit) for i in range(count)])


def all_to_all_dp(value):
    return lax.all_to_all(value, "dp", split_axis=0, concat_axis=0, tiled=True)


def on_device(
    tokens_in, block_ids, rel_buckets, routes, attn_gain, w_qkv, w_attn_out, bias_table, moe_gain, w_router,
    w_expert_in, w_expert_out, cotangent,
):
    seqs, stretch, width = tokens_in.shape
    dp = lax.axis_size("dp")
    ctx_count = lax.axis_size("ctx")
    tp_count = lax.axis_size("tp")
    expert_count = w_router.shape[2]
    assert w_expert_in.shape[1] == tp_count == 2 and ctx_count == 4
    cap = max(2, 2 * stretch * routes.shape[2] // expert_count)
    ctx = lax.axis_index("ctx")
    tp = lax.axis_index("tp")
    local = w_qkv.shape[3]
    heads = local // HD

    wqkv = lax.all_gather(w_qkv[0], "dp", axis=1, tiled=True)
    wout_own = lax.all_gather(w_attn_out[0], "dp", axis=1, tiled=True)
    wout_other = flip(wout_own, "tp", 1)
    table = lax.all_gather(bias_table[0], "dp", axis=0, tiled=True)
    gains = lax.all_gather(jnp.concatenate([attn_gain, moe_gain], axis=0), "dp", axis=1, tiled=True)
    gain_attn, gain_moe = gains[0:1], gains[1:2]
    router = lax.all_gather(w_router[0], "dp", axis=0, tiled=True).T.reshape(dp, 2, width).transpose(1, 0, 2)
    router = jnp.where(tp == 0, router, router[::-1]).reshape(expert_count, width)

    across = flip(tokens_in, "ctx", 2)
    beside, beyond = flip(jnp.stack([tokens_in, across]), "ctx", 1)
    pieces = jnp.stack([tokens_in, beside, across, beyond], axis=1)

    w_in = w_expert_in[0]
    w_out_t = w_expert_out[0].transpose(0, 2, 1)
    both = jnp.stack([w_in, w_out_t], axis=1)
    keep = lax.dynamic_index_in_dim(both, tp, 0, keepdims=False)
    give = lax.dynamic_index_in_dim(both, 1 - tp, 0, keepdims=False)
    got = flip(give, "tp", 1)
    weights = lax.all_gather(jnp.stack([keep, got], axis=1), "ctx", axis=0, tiled=False)

    e_order = jnp.arange(expert_count, dtype=jnp.int32).reshape(dp, 2).T
    e_order = jnp.where(tp == 0, e_order, e_order[::-1]).reshape(1, expert_count, 1)
    hits = ((routes[:, None, :, 0] == e_order) | (routes[:, None, :, 1] == e_order)).astype(F32)
    before = (
        lax.broadcasted_iota(jnp.int32, (stretch, stretch), 0) < lax.broadcasted_iota(jnp.int32, (stretch, stretch), 1)
    ).astype(BF16)
    ranks = jnp.einsum("set,tu->seu", hits.astype(BF16), before, preferred_element_type=F32)
    places = jnp.where(hits > 0.5, ranks, -1.0)[:, :dp]

    cot_slots = all_to_all_dp(dispatch(places, cotangent, cap))

    one_hot_bucket = (rel_buckets[:, None] == jnp.arange(NB, dtype=jnp.int32)[None, :]).astype(F32)
    one_hot_bucket = jnp.pad(one_hot_bucket, ((0, 1), (0, 0)))
    starts = [(ctx - (ctx ^ b)) * stretch + 3 * stretch for b in range(4)]
    hot_windows = jnp.stack([lax.dynamic_slice_in_dim(one_hot_bucket, s, 2 * stretch, 0) for s in starts])
    windows = jnp.einsum("bmn,nh->hbm", hot_windows, table.astype(F32), precision=FULL_PRECISION)
    bias = expand_bias(windows)

    x32 = pieces.astype(F32)
    normed = (x32 * norm_factor(x32) * gain_attn.astype(F32)[None, None]).astype(BF16)
    own_normed = normed[:, 0].reshape(seqs * stretch, width)
    queries = jnp.dot(own_normed, wqkv[0], preferred_element_type=F32).astype(BF16) * jnp.asarray(HD ** (-0.5), BF16)
    queries = queries.reshape(seqs, stretch, local)
    flat = normed.reshape(seqs * 4 * stretch, width)
    keys = jnp.dot(flat, wqkv[1], preferred_element_type=F32).astype(BF16).reshape(seqs, 4 * stretch, local)
    values = jnp.dot(flat, wqkv[2], preferred_element_type=F32).astype(BF16).reshape(seqs, 4 * stretch, local)

    ids = block_ids.reshape(seqs, 4, stretch)
    ids_pieces = [lax.dynamic_index_in_dim(ids, ctx ^ b, 1, keepdims=False) for b in range(4)]
    ids_query = ids_pieces[0].reshape(seqs, 1, stretch)
    ids_key = jnp.stack(ids_pieces, axis=1).reshape(seqs, 4 * stretch, 1)

    wout_pair = jnp.stack([wout_own, wout_other])
    attended, lse, mids, moes, gates, partials = [], [], [], [], [], []
    returned_din, returned_h = [], []
    acc = None
    for s in range(seqs):
        att, stat = attend(queries[s], keys[s], values[s], bias, ids_query[s], ids_key[s])
        attended.append(att)
        lse.append(stat)
        mid, moe_in, gate, send, slot_gate = middle_stage(
            att, flip(att, "tp", 1), tokens_in[s], wout_pair, gain_moe, router, hits[s], places[s], cap
        )
        mids.append(mid)
        moes.append(moe_in)
        gates.append(gate)
        received = all_to_all_dp(send)
        received_gate = all_to_all_dp(slot_gate)
        part, din, h, acc = experts(received, cot_slots, s, received_gate, weights, acc, s == seqs - 1)
        returned_din.append(all_to_all_dp(din))
        returned_h.append(all_to_all_dp(h))
        partials.append(all_to_all_dp(part))

    beside_sum = acc[:, 0::2].astype(F32) + flip(acc[:, 1::2], "ctx", 1).astype(F32)
    mine = beside_sum[:, 0] + flip(beside_sum[:, 1].astype(BF16), "ctx", 2).astype(F32)
    other = flip(mine[1].astype(BF16), "tp", 1).astype(F32)
    ordered = jnp.where(tp == 0, jnp.stack([mine[0], other]), jnp.stack([other, mine[0]]))
    grad_expert_in = ordered[:, 0]
    grad_expert_out = ordered[:, 1].transpose(0, 2, 1)

    tokens_out, gmids = [], []
    projections = []
    rel_grad = 0.0
    gain_moe_grad = 0.0
    router_grad = 0.0
    wout_grad = 0.0
    for s in range(seqs):
        out_own = combine_out(places[s], partials[s], cap)
        out_other = flip(out_own, "tp", 1)
        tokens_out.append((mids[s] + (out_own.astype(F32) + out_other.astype(F32))).astype(BF16))
        din_own, h_own = combine(places[s], returned_din[s], returned_h[s], cap)
        din_other = flip(din_own, "tp", 1)
        h_all = jnp.concatenate([h_own, flip(h_own, "tp", 1)], axis=0)
        gmid, datt, d_gain, d_router, d_wout = middle_back(
            din_own, din_other, h_all, gates[s], router, moes[s], mids[s], gain_moe, cotangent[s], attended[s], wout_own
        )
        gmids.append(gmid)
        gain_moe_grad += d_gain
        router_grad += d_router
        wout_grad += d_wout
        dq, dk, dv, rel = attend_back(
            queries[s], keys[s], values[s], datt, bias, lse[s], ids_query[s], ids_key[s]
        )
        rel_grad += rel
        dkv = jnp.stack([dk, dv]).reshape(2, 4, stretch, local)
        near = dkv[:, 0::2].astype(F32) + flip(dkv[:, 1::2], "ctx", 1).astype(F32)
        full = near[:, 0] + flip(near[:, 1].astype(BF16), "ctx", 2).astype(F32)
        projections.append(jnp.concatenate([dq[None], full.astype(BF16)], axis=0))
    grad_proj = jnp.concatenate(projections, axis=1)
    grad_wqkv = jnp.einsum("rd,jre->jde", own_normed, grad_proj, preferred_element_type=F32)
    dnormed_own = jnp.einsum("jre,jde->rd", grad_proj, wqkv, preferred_element_type=F32).astype(BF16)
    dnormed = dnormed_own.astype(F32) + flip(dnormed_own, "tp", 1).astype(F32)
    own_x = tokens_in.reshape(seqs * stretch, width).astype(F32)
    factor = norm_factor(own_x)
    unit = own_x * factor
    grad_gain_attn = jnp.sum(dnormed * unit, axis=0)
    scaled = dnormed * gain_attn.astype(F32)
    dres = factor * (scaled - unit * jnp.mean(scaled * unit, axis=-1, keepdims=True))
    grad_tokens = jnp.concatenate(gmids, axis=0) + dres

    rel_flat = rel_grad.reshape(heads, 4, 2 * stretch)
    grad_table = jnp.einsum("bmn,hbm->nh", hot_windows, rel_flat, precision=FULL_PRECISION)
    router_grad = router_grad.reshape(2, dp, width)
    router_grad = jnp.where(tp == 0, router_grad, router_grad[::-1]).transpose(1, 0, 2).reshape(expert_count, width).T

    def reduced(value, dim):
        return lax.psum(lax.psum_scatter(value, "dp", scatter_dimension=dim, tiled=True), "ctx")

    g_attn = reduced(grad_gain_attn, 0)
    g_qkv = reduced(grad_wqkv, 1)
    g_wout = reduced(wout_grad, 1)
    g_table = reduced(grad_table, 0)
    g_moe = reduced(gain_moe_grad[0], 0)
    g_router = reduced(router_grad, 0)
    return (
        jnp.stack(tokens_out),
        grad_tokens.reshape(seqs, stretch, width),
        g_attn[None],
        g_qkv[None],
        g_wout[None],
        g_table[None],
        g_moe[None],
        g_router[None],
        grad_expert_in[None],
        grad_expert_out[None],
    )


def solution(mesh):
    return jax.shard_map(
        on_device,
        mesh=mesh,
        in_specs=(
            P("dp", "ctx", None),
            P("dp", None),
            P(),
            P("dp", "ctx", None),
            P(None, "dp"),
            P(None, None, "dp", "tp"),
            P(None, "tp", "dp"),
            P(None, "dp", "tp"),
            P(None, "dp"),
            P(None, "dp", None),
            P(None, "dp", "ctx", "tp"),
            P(None, "dp", "tp", "ctx"),
            P("dp", "ctx", None),
        ),
        out_specs=(
            P("dp", "ctx", None),
            P("dp", "ctx", None),
            P(None, "dp"),
            P(None, None, "dp", "tp"),
            P(None, "tp", "dp"),
            P(None, "dp", "tp"),
            P(None, "dp"),
            P(None, "dp", None),
            P(None, "dp", "ctx", "tp"),
            P(None, "dp", "tp", "ctx"),
        ),
        check_vma=False,
    )
```

```python
import functools

import jax
import jax.numpy as jnp
from jax import lax
from jax.experimental import pallas as pl
from jax.experimental.pallas import tpu as pltpu
from jax.sharding import PartitionSpec as P

HD = 64
NB = 32
EPSILON = 1e-06
FULL_PRECISION = lax.Precision.HIGHEST
MASKED = -1e30
BF16 = jnp.bfloat16
F32 = jnp.float32
VMEM_BYTES = 60 * 1024 * 1024
GELU_C = 0.7978845608028654
GELU_A = 0.044715


def params():
    return pltpu.CompilerParams(vmem_limit_bytes=VMEM_BYTES)


def cost(flops, nbytes, trans=0):
    return pl.CostEstimate(flops=int(flops), bytes_accessed=int(nbytes), transcendentals=int(trans))


def dot(a, b):
    return lax.dot_general(a, b, (((1,), (0,)), ((), ())), preferred_element_type=F32)


def dot_nt(a, b):
    return lax.dot_general(a, b, (((1,), (1,)), ((), ())), preferred_element_type=F32)


def dot_tn(a, b):
    return lax.dot_general(a, b, (((0,), (0,)), ((), ())), preferred_element_type=F32)


def bias_kernel(win_ref, out_ref):
    for block in range(4):
        row = win_ref[0, block : block + 1, :]
        wide = jnp.broadcast_to(row, (256, 512))
        rolled = pltpu.roll(wide, 257, 1, stride=1, stride_axis=0)
        out_ref[0, block * 256 : (block + 1) * 256, :] = rolled[:, :256].astype(BF16)


def expand_bias(windows):
    heads = windows.shape[0]
    return pl.pallas_call(
        bias_kernel,
        name="expand_bias",
        grid=(heads,),
        in_specs=[pl.BlockSpec((1, 4, 512), lambda h: (h, 0, 0))],
        out_specs=pl.BlockSpec((1, 1024, 256), lambda h: (h, 0, 0)),
        out_shape=jax.ShapeDtypeStruct((heads, 1024, 256), BF16),
        compiler_params=params(),
        cost_estimate=cost(heads * 2 * 1024 * 512, heads * 1024 * 256 * 2),
    )(windows)


def attend_kernel(q_ref, k_ref, v_ref, bias_ref, idq_ref, idk_ref, out_ref, lse_ref, mask_ref):
    @pl.when(pl.program_id(0) == 0)
    def _():
        mask_ref[...] = jnp.where(idk_ref[...] <= idq_ref[...], 0.0, MASKED)

    queries = q_ref[...]
    keys = k_ref[...]
    values_t = v_ref[...].T
    low_half = lax.broadcasted_iota(jnp.int32, queries.shape, 1) < HD
    zero = jnp.zeros_like(queries)
    parts = []
    for head in range(2):
        own = jnp.where(low_half, queries, zero) if head == 0 else jnp.where(low_half, zero, queries)
        scores = dot_nt(keys, own) + bias_ref[head].astype(F32) + mask_ref[...]
        top = jnp.max(scores, axis=0, keepdims=True)
        weights = jnp.exp(scores - top)
        total = jnp.sum(weights, axis=0, keepdims=True)
        part = dot(values_t[head * HD : (head + 1) * HD], weights.astype(BF16)) * (1.0 / total)
        parts.append(part)
        lse_ref[0, head : head + 1, :] = top + jnp.log(total)
    out_ref[...] = jnp.concatenate(parts, axis=0).T.astype(BF16)


def attend(queries, keys, values, bias, ids_query, ids_key):
    rows, width = queries.shape
    length = keys.shape[0]
    pairs = width // (2 * HD)
    return pl.pallas_call(
        attend_kernel,
        name="attend",
        grid=(pairs,),
        in_specs=[
            pl.BlockSpec((rows, 128), lambda p: (0, p)),
            pl.BlockSpec((length, 128), lambda p: (0, p)),
            pl.BlockSpec((length, 128), lambda p: (0, p)),
            pl.BlockSpec((2, length, rows), lambda p: (p, 0, 0)),
            pl.BlockSpec((1, rows), lambda p: (0, 0)),
            pl.BlockSpec((length, 1), lambda p: (0, 0)),
        ],
        out_specs=[
            pl.BlockSpec((rows, 128), lambda p: (0, p)),
            pl.BlockSpec((1, 2, rows), lambda p: (p, 0, 0)),
        ],
        out_shape=[
            jax.ShapeDtypeStruct((rows, width), BF16),
            jax.ShapeDtypeStruct((pairs, 2, rows), F32),
        ],
        scratch_shapes=[pltpu.VMEM((length, rows), F32)],
        compiler_params=params(),
        cost_estimate=cost(pairs * 2 * 4 * rows * length * 128, 6 * rows * length * 2, pairs * 2 * rows * length),
    )(queries, keys, values, bias, ids_query, ids_key)


def attend_back_kernel(
    q_ref, k_ref, v_ref, do_ref, bias_ref, lse_ref, idq_ref, idk_ref, dq_ref, dk_ref, dv_ref, rel_ref, mask_ref
):
    @pl.when(pl.program_id(0) == 0)
    def _():
        mask_ref[...] = jnp.where(idk_ref[...] <= idq_ref[...], 0.0, MASKED)

    queries = q_ref[...]
    keys = k_ref[...]
    values = v_ref[...]
    grad_out = do_ref[...]
    keys_t = keys.T
    low_half = lax.broadcasted_iota(jnp.int32, queries.shape, 1) < HD
    zero = jnp.zeros_like(queries)
    dk = None
    dv = None
    dq_parts = []
    for head in range(2):
        own = (lambda a: jnp.where(low_half, a, zero)) if head == 0 else (lambda a: jnp.where(low_half, zero, a))
        q_own = own(queries)
        do_own = own(grad_out)
        scores = dot_nt(keys, q_own) + bias_ref[head].astype(F32) + mask_ref[...]
        probs = jnp.exp(scores - lse_ref[0, head : head + 1, :])
        dprobs = dot_nt(values, do_own)
        delta = jnp.sum(probs * dprobs, axis=0, keepdims=True)
        dscores = probs * (dprobs - delta)
        low = dscores.astype(BF16)
        dv_head = dot(probs.astype(BF16), do_own)
        dk_head = dot(low, q_own)
        dv = dv_head if dv is None else dv + dv_head
        dk = dk_head if dk is None else dk + dk_head
        dq_parts.append(dot(keys_t[head * HD : (head + 1) * HD], low))
        for block in range(4):
            tile = dscores[block * 256 : (block + 1) * 256]
            wide = jnp.concatenate([tile, jnp.zeros_like(tile)], axis=1)
            total = None
            for group in range(32):
                moved = pltpu.roll(wide[group * 8 : group * 8 + 8], 248 - 8 * group, 1)
                total = moved if total is None else total + moved
            row = lax.broadcasted_iota(jnp.int32, total.shape, 0)
            amount = 7 - row
            for bit in (1, 2, 4):
                total = jnp.where((amount & bit) != 0, pltpu.roll(total, bit, 1), total)
            rel_ref[0, head, block : block + 1, :] = jnp.sum(total, axis=0, keepdims=True)
    dq_ref[...] = (jnp.concatenate(dq_parts, axis=0).T * (HD ** (-0.5))).astype(BF16)
    dk_ref[...] = dk.astype(BF16)
    dv_ref[...] = dv.astype(BF16)


def attend_back(queries, keys, values, grad_out, bias, lse, ids_query, ids_key):
    rows, width = queries.shape
    length = keys.shape[0]
    pairs = width // (2 * HD)
    return pl.pallas_call(
        attend_back_kernel,
        name="attend_back",
        grid=(pairs,),
        in_specs=[
            pl.BlockSpec((rows, 128), lambda p: (0, p)),
            pl.BlockSpec((length, 128), lambda p: (0, p)),
            pl.BlockSpec((length, 128), lambda p: (0, p)),
            pl.BlockSpec((rows, 128), lambda p: (0, p)),
            pl.BlockSpec((2, length, rows), lambda p: (p, 0, 0)),
            pl.BlockSpec((1, 2, rows), lambda p: (p, 0, 0)),
            pl.BlockSpec((1, rows), lambda p: (0, 0)),
            pl.BlockSpec((length, 1), lambda p: (0, 0)),
        ],
        out_specs=[
            pl.BlockSpec((rows, 128), lambda p: (0, p)),
            pl.BlockSpec((length, 128), lambda p: (0, p)),
            pl.BlockSpec((length, 128), lambda p: (0, p)),
            pl.BlockSpec((1, 2, 4, 512), lambda p: (p, 0, 0, 0)),
        ],
        out_shape=[
            jax.ShapeDtypeStruct((rows, width), BF16),
            jax.ShapeDtypeStruct((length, width), BF16),
            jax.ShapeDtypeStruct((length, width), BF16),
            jax.ShapeDtypeStruct((pairs, 2, 4, 512), F32),
        ],
        scratch_shapes=[pltpu.VMEM((length, rows), F32)],
        compiler_params=params(),
        cost_estimate=cost(pairs * 2 * 10 * rows * length * 128, 8 * rows * length * 2, pairs * 2 * rows * length),
    )(queries, keys, values, grad_out, bias, lse, ids_query, ids_key)


def one_hot(place, cap):
    groups, rows = place.shape
    slots = lax.broadcasted_iota(jnp.int32, (cap, rows), 0).astype(F32)
    return [slots == place[group : group + 1, :] for group in range(groups)]


def diagonal(cap):
    return lax.broadcasted_iota(jnp.int32, (cap, cap), 0) == lax.broadcasted_iota(jnp.int32, (cap, cap), 1)


def dispatch_kernel(groups, cap, place_ref, rows_ref, out_ref):
    rows = rows_ref[0]
    picks = one_hot(place_ref[0], cap)
    pick = jnp.concatenate([jnp.where(p, 1.0, 0.0).astype(BF16) for p in picks], axis=0)
    out_ref[:, 0] = dot(pick, rows).astype(BF16).reshape(groups, cap, rows.shape[1])


def dispatch(place, rows, cap):
    seqs, groups, stretch = place.shape
    width = rows.shape[2]
    return pl.pallas_call(
        functools.partial(dispatch_kernel, groups, cap),
        name="dispatch_rows",
        grid=(seqs,),
        in_specs=[
            pl.BlockSpec((1, groups, stretch), lambda s: (s, 0, 0)),
            pl.BlockSpec((1, stretch, width), lambda s: (s, 0, 0)),
        ],
        out_specs=pl.BlockSpec((groups, 1, cap, width), lambda s: (0, s, 0, 0)),
        out_shape=jax.ShapeDtypeStruct((groups, seqs, cap, width), BF16),
        compiler_params=params(),
        cost_estimate=cost(seqs * 2 * groups * cap * stretch * width, seqs * 2 * (stretch + groups * cap) * width),
    )(place, rows)


def norm_factor(value):
    return lax.rsqrt(jnp.mean(value * value, axis=-1, keepdims=True) + EPSILON)


def middle_kernel(
    groups, cap, own_ref, other_ref, x_ref, wout_ref, gain_ref, router_ref, hits_ref, place_ref,
    middle_ref, moe_ref, gates_ref, send_ref, slot_gate_ref,
):
    mid = x_ref[...].astype(F32) + (dot(own_ref[...], wout_ref[0]) + dot(other_ref[...], wout_ref[1]))
    middle_ref[...] = mid
    moe_in = (mid * norm_factor(mid) * gain_ref[...].astype(F32)).astype(BF16)
    moe_ref[...] = moe_in
    logits = dot_nt(router_ref[...], moe_in)
    hit = hits_ref[...] > 0.5
    top = jnp.max(jnp.where(hit, logits, MASKED), axis=0, keepdims=True)
    raw = jnp.where(hit, jnp.exp(jnp.where(hit, logits, top) - top), 0.0)
    gates = raw / jnp.sum(raw, axis=0, keepdims=True)
    gates_ref[...] = gates
    picks = one_hot(place_ref[...], cap)
    pick = jnp.concatenate([jnp.where(p, 1.0, 0.0).astype(BF16) for p in picks], axis=0)
    send_ref[...] = dot(pick, moe_in).astype(BF16).reshape(groups, cap, moe_in.shape[1])
    eye = diagonal(cap)
    for group in range(groups):
        column = jnp.sum(jnp.where(picks[group], gates[group : group + 1, :], 0.0), axis=1, keepdims=True)
        slot_gate_ref[group] = jnp.sum(jnp.where(eye, column, 0.0), axis=0, keepdims=True)


def middle_stage(own, other, x, wout, gain, router, hits, place, cap):
    rows, width = x.shape
    experts = router.shape[0]
    groups = place.shape[0]
    return pl.pallas_call(
        functools.partial(middle_kernel, groups, cap),
        name="middle_stage",
        out_shape=[
            jax.ShapeDtypeStruct((rows, width), F32),
            jax.ShapeDtypeStruct((rows, width), BF16),
            jax.ShapeDtypeStruct((experts, rows), F32),
            jax.ShapeDtypeStruct((groups, cap, width), BF16),
            jax.ShapeDtypeStruct((groups, 1, cap), F32),
        ],
        compiler_params=params(),
        cost_estimate=cost(2 * rows * width * width + 2 * groups * cap * rows * width, rows * width * 16),
    )(own, other, x, wout, gain, router, hits, place)


def expert_kernel(
    first, final, tiles, groups, cap, x_ref, g_ref, gate_ref, w_ref, *refs
):
    if first:
        acc_in = None
    else:
        acc_in, refs = refs[0], refs[1:]
    part_out, din_out, h_out, acc_out, xt_ref, dy_ref, dyt_ref, part_ref, din_ref = refs
    step = pl.program_id(0)
    rows = groups * cap
    width = x_ref.shape[-1]
    slices = w_ref.shape[0]
    piece = width // slices

    @pl.when(step == 0)
    def _():
        eye = diagonal(cap)
        xt_ref[...] = x_ref[...].reshape(rows, width).T
        for group in range(groups):
            gate = jnp.sum(jnp.where(eye, gate_ref[group], 0.0), axis=1, keepdims=True)
            dy_ref[group * cap : (group + 1) * cap] = (g_ref[group, 0].astype(F32) * gate).astype(BF16)
        dyt_ref[...] = dy_ref[...].T

    x = x_ref[...].reshape(rows, width)
    w_in = w_ref[:, 0, 0].reshape(width, -1)
    w_out_t = w_ref[:, 1, 0].reshape(width, -1)
    dy = dy_ref[...]
    pre = dot(x, w_in)
    square = pre * pre
    inner = jnp.tanh(GELU_C * pre * (1.0 + GELU_A * square))
    half = 0.5 * (1.0 + inner)
    hidden = (pre * half).astype(BF16)
    slope = half + (0.5 * GELU_C) * pre * (1.0 - inner * inner) * (1.0 + (3.0 * GELU_A) * square)
    dhid = dot(dy, w_out_t)
    dpre = (dhid * slope).astype(BF16)
    part = dot_nt(hidden, w_out_t)
    din = dot_nt(dpre, w_in)
    dw_in = dot(xt_ref[...], dpre)
    dw_out_t = dot(dyt_ref[...], hidden)

    @pl.when(step == 0)
    def _():
        part_ref[...] = part
        din_ref[...] = din

    @pl.when(step > 0)
    def _():
        part_ref[...] += part
        din_ref[...] += din

    me = lax.axis_index("ctx")
    for index in range(slices):
        place = index ^ me
        grad_in = dw_in[index * piece : (index + 1) * piece]
        grad_out = dw_out_t[index * piece : (index + 1) * piece]
        if not first:
            grad_in += acc_in[0, place, 0]
            grad_out += acc_in[0, place, 1]
        acc_out[0, place, 0] = grad_in.astype(acc_out.dtype)
        acc_out[0, place, 1] = grad_out.astype(acc_out.dtype)

    @pl.when(step == tiles - 1)
    def _():
        eye = diagonal(cap)
        for group in range(groups):
            gate = jnp.sum(jnp.where(eye, gate_ref[group], 0.0), axis=1, keepdims=True)
            gated = part_ref[group * cap : (group + 1) * cap] * gate
            part_out[group] = gated.astype(BF16)
            din_out[group] = din_ref[group * cap : (group + 1) * cap].astype(BF16)
            h = jnp.sum(gated * g_ref[group, 0].astype(F32), axis=1, keepdims=True)
            h_out[group] = jnp.sum(jnp.where(eye, h, 0.0), axis=0, keepdims=True)


def experts(x, cot_slots, seq_index, gate, weights, acc, final, tile=512):
    groups, cap, width = x.shape
    slices, _, halves, piece, half_len = weights.shape
    per_half = half_len // tile
    tiles = halves * per_half
    rows = groups * cap
    first = acc is None
    acc_spec = pl.BlockSpec((1, slices, 2, piece, tile), lambda f: (f // per_half, 0, 0, 0, f % per_half))
    in_specs = [
        pl.BlockSpec((groups, cap, width), lambda f: (0, 0, 0)),
        pl.BlockSpec((groups, 1, cap, width), lambda f: (0, seq_index, 0, 0)),
        pl.BlockSpec((groups, 1, cap), lambda f: (0, 0, 0)),
        pl.BlockSpec((slices, 2, 1, piece, tile), lambda f: (0, 0, f // per_half, 0, f % per_half)),
    ]
    args = [x, cot_slots, gate, weights]
    aliases = {}
    if not first:
        in_specs.append(acc_spec)
        args.append(acc)
        if not final:
            aliases = {4: 3}
    acc_shape = (halves, slices, 2, piece, half_len)
    return pl.pallas_call(
        functools.partial(expert_kernel, first, final, tiles, groups, cap),
        name="experts",
        grid=(tiles,),
        in_specs=in_specs,
        out_specs=[
            pl.BlockSpec((groups, cap, width), lambda f: (0, 0, 0)),
            pl.BlockSpec((groups, cap, width), lambda f: (0, 0, 0)),
            pl.BlockSpec((groups, 1, cap), lambda f: (0, 0, 0)),
            acc_spec,
        ],
        out_shape=[
            jax.ShapeDtypeStruct((groups, cap, width), BF16),
            jax.ShapeDtypeStruct((groups, cap, width), BF16),
            jax.ShapeDtypeStruct((groups, 1, cap), F32),
            jax.ShapeDtypeStruct(acc_shape, BF16 if final else F32),
        ],
        scratch_shapes=[
            pltpu.VMEM((width, rows), BF16),
            pltpu.VMEM((rows, width), BF16),
            pltpu.VMEM((width, rows), BF16),
            pltpu.VMEM((rows, width), F32),
            pltpu.VMEM((rows, width), F32),
        ],
        input_output_aliases=aliases,
        compiler_params=params(),
        cost_estimate=cost(12 * rows * width * halves * half_len, 2 * width * halves * half_len * 10, rows * halves * half_len),
    )(*args)


def combine_kernel(groups, cap, place_ref, din_ref, h_ref, din_out, h_out):
    picks = one_hot(place_ref[...], cap)
    pick = jnp.concatenate([jnp.where(p, 1.0, 0.0).astype(BF16) for p in picks], axis=0)
    rows = groups * cap
    din_out[...] = dot_tn(pick, din_ref[...].reshape(rows, din_ref.shape[-1])).astype(BF16)
    eye = diagonal(cap)
    for group in range(groups):
        column = jnp.sum(jnp.where(eye, h_ref[group], 0.0), axis=1, keepdims=True)
        h_out[group : group + 1, :] = jnp.sum(jnp.where(picks[group], column, 0.0), axis=0, keepdims=True)


def combine(place, din, h, cap):
    groups, stretch = place.shape
    width = din.shape[-1]
    return pl.pallas_call(
        functools.partial(combine_kernel, groups, cap),
        name="combine_back",
        out_shape=[
            jax.ShapeDtypeStruct((stretch, width), BF16),
            jax.ShapeDtypeStruct((groups, stretch), F32),
        ],
        compiler_params=params(),
        cost_estimate=cost(2 * groups * cap * stretch * width, 4 * stretch * width * 2),
    )(place, din, h)


def combine_out_kernel(groups, cap, place_ref, part_ref, out_ref):
    picks = one_hot(place_ref[...], cap)
    pick = jnp.concatenate([jnp.where(p, 1.0, 0.0).astype(BF16) for p in picks], axis=0)
    out_ref[...] = dot_tn(pick, part_ref[...].reshape(groups * cap, part_ref.shape[-1])).astype(BF16)


def combine_out(place, part, cap):
    groups, stretch = place.shape
    width = part.shape[-1]
    return pl.pallas_call(
        functools.partial(combine_out_kernel, groups, cap),
        name="combine_out",
        out_shape=jax.ShapeDtypeStruct((stretch, width), BF16),
        compiler_params=params(),
        cost_estimate=cost(2 * groups * cap * stretch * width, 4 * stretch * width * 2),
    )(place, part)


def middle_back_kernel(
    own_ref, other_ref, h_ref, gates_ref, router_ref, moe_ref, mid_ref, gain_ref, cot_ref, wout_ref,
    gmid_ref, datt_ref, gain_grad_ref, router_grad_ref, low_ref,
):
    h = h_ref[...]
    dlogits = h - gates_ref[...] * jnp.sum(h, axis=0, keepdims=True)
    router = router_ref[...]
    dmoe = own_ref[...].astype(F32) + other_ref[...].astype(F32)
    dmoe = dmoe + lax.dot_general(
        dlogits, router.astype(F32), (((0,), (0,)), ((), ())), precision=FULL_PRECISION, preferred_element_type=F32
    )
    router_grad_ref[...] = lax.dot_general(
        dlogits, moe_ref[...].astype(F32), (((1,), (0,)), ((), ())), precision=FULL_PRECISION, preferred_element_type=F32
    )
    mid = mid_ref[...]
    gain = gain_ref[...].astype(F32)
    factor = norm_factor(mid)
    normed = mid * factor
    gain_grad_ref[...] = jnp.sum(dmoe * normed, axis=0, keepdims=True)
    scaled = dmoe * gain
    dmid = factor * (scaled - normed * jnp.mean(scaled * normed, axis=-1, keepdims=True))
    gmid = cot_ref[...].astype(F32) + dmid
    gmid_ref[...] = gmid
    dattn = gmid.astype(BF16)
    datt_ref[...] = dot_nt(dattn, wout_ref[...]).astype(BF16)
    low_ref[...] = dattn


def middle_back(own, other, h, gates, router, moe_in, mid, gain, cot, wout):
    rows, width = mid.shape
    local = wout.shape[0]
    return pl.pallas_call(
        middle_back_kernel,
        name="middle_back",
        out_shape=[
            jax.ShapeDtypeStruct((rows, width), F32),
            jax.ShapeDtypeStruct((rows, local), BF16),
            jax.ShapeDtypeStruct((1, width), F32),
            jax.ShapeDtypeStruct(router.shape, F32),
            jax.ShapeDtypeStruct((rows, width), BF16),
        ],
        compiler_params=params(),
        cost_estimate=cost(2 * rows * width * local, 30 * rows * width),
    )(own, other, h, gates, router, moe_in, mid, gain, cot, wout)


MESH_ID = pl.DeviceIdType.MESH


def remote(src, dst, send_sem, recv_sem, **where):
    return pltpu.make_async_remote_copy(
        src_ref=src, dst_ref=dst, send_sem=send_sem, recv_sem=recv_sem, device_id=where, device_id_type=MESH_ID
    )


def greet(peers):
    barrier = pltpu.get_barrier_semaphore()
    for where in peers:
        pl.semaphore_signal(barrier, inc=1, device_id=where, device_id_type=MESH_ID)
    pl.semaphore_wait(barrier, len(peers))


def first_kernel(
    seqs, tok_ref, wqkv_ref, wout_ref, table_ref, ga_ref, gm_ref, router_ref,
    q_ref, k_ref, v_ref, normed_ref, wqkv_out, wout_out, table_out, gain_ref, gm_out, router_out,
    tok_all, n_all, ga_all, gm_all, router_all,
    z_send, z_recv, f_send, f_recv, t_send, t_recv, y_send, y_recv, l_sem,
):
    dp = lax.axis_index("dp")
    ctx = lax.axis_index("ctx")
    tp = lax.axis_index("tp")
    core = ctx % 2
    rows = wqkv_ref.shape[1]
    half = rows // 2
    orows = wout_ref.shape[0] // 2
    greet([{"dp": dp ^ b} for b in (1, 2, 3)] + [{"ctx": ctx ^ 1}, {"ctx": ctx ^ 2}])

    def w_rows(owner, side):
        return pl.ds(pl.multiple_of(owner * rows + side * half, 16), half)

    def o_rows(side):
        return pl.ds(pl.multiple_of(side * orows, 16), orows)

    def z_copies(b):
        to = {"dp": dp ^ b}
        return [
            remote(ga_ref, ga_all.at[dp], z_send.at[0, b - 1], z_recv.at[0, b - 1], **to),
            remote(gm_ref, gm_all.at[dp], z_send.at[1, b - 1], z_recv.at[1, b - 1], **to),
            remote(table_ref, table_out.at[dp], z_send.at[2, b - 1], z_recv.at[2, b - 1], **to),
            remote(router_ref, router_all.at[dp], z_send.at[3, b - 1], z_recv.at[3, b - 1], **to),
            remote(
                wqkv_ref.at[:, pl.ds(pl.multiple_of(core * half, 16), half)], wqkv_out.at[:, w_rows(dp, core)],
                z_send.at[4, b - 1], z_recv.at[4, b - 1], **to,
            ),
            remote(
                wout_ref.at[o_rows(core)], wout_out.at[dp, o_rows(core)],
                z_send.at[5, b - 1], z_recv.at[5, b - 1], **to,
            ),
        ]

    small = [z_copies(b) for b in (1, 2, 3)]
    for kind in range(6):
        for b in (3, 2, 1):
            small[b - 1][kind].start()
    beside = remote(tok_ref, tok_all.at[1], t_send.at[0], t_recv.at[0], ctx=ctx ^ 1)
    beside.start()
    across = [remote(tok_ref.at[s], tok_all.at[2, s], y_send.at[s], y_recv.at[s], ctx=ctx ^ 2) for s in range(seqs)]
    for copy in across:
        copy.start()
    own = [
        pltpu.make_async_copy(tok_ref, tok_all.at[0], l_sem.at[0]),
        pltpu.make_async_copy(ga_ref, ga_all.at[dp], l_sem.at[1]),
        pltpu.make_async_copy(gm_ref, gm_all.at[dp], l_sem.at[2]),
        pltpu.make_async_copy(table_ref, table_out.at[dp], l_sem.at[3]),
        pltpu.make_async_copy(router_ref, router_all.at[dp], l_sem.at[4]),
        pltpu.make_async_copy(wqkv_ref, wqkv_out.at[:, pl.ds(pl.multiple_of(dp * rows, 16), rows)], l_sem.at[5]),
        pltpu.make_async_copy(wout_ref, wout_out.at[dp], l_sem.at[6]),
    ]
    for copy in own:
        copy.start()
    for copy in own:
        copy.wait()

    for kind in range(4):
        for b in (3, 2, 1):
            small[b - 1][kind].wait_recv()
    count = ga_all.shape[0]
    piece = ga_all.shape[2]
    width = count * piece
    row = lax.broadcasted_iota(jnp.int32, (piece, width), 0)
    col = lax.broadcasted_iota(jnp.int32, (piece, width), 1)
    gain = 0.0
    gain_m = 0.0
    for d in range(count):
        spread = jnp.where(col == row + d * piece, 1.0, 0.0).astype(BF16)
        gain = gain + dot(ga_all[d], spread)
        gain_m = gain_m + dot(gm_all[d], spread)
    gain_ref[...] = gain
    gm_out[...] = gain_m.astype(BF16)
    experts_n = router_ref.shape[1]
    slot_row = lax.broadcasted_iota(jnp.int32, (experts_n, experts_n), 0)
    slot_col = lax.broadcasted_iota(jnp.int32, (experts_n, experts_n), 1)
    side = slot_row // count
    expert = (slot_row % count) * 2 + (side ^ tp)
    order = jnp.where(slot_col == expert, 1.0, 0.0).astype(BF16)
    router_out[...] = dot_nt(order, router_all[...].reshape(width, experts_n)).astype(BF16)

    def norm_piece(b):
        def body(s, carry):
            value = tok_all[b, s].astype(F32)
            out = (value * norm_factor(value) * gain_ref[...]).astype(BF16)
            n_all[b, s] = out
            return carry

        lax.fori_loop(0, seqs, body, 0)

    def project(b, s):
        x = n_all[b, s]
        k_ref[s, b] = dot(x, wqkv_out[1]).astype(BF16)
        v_ref[s, b] = dot(x, wqkv_out[2]).astype(BF16)

    norm_piece(0)
    normed_ref[...] = n_all[0]
    beside.wait_recv()
    norm_piece(1)

    forwards = []
    for b in (1, 2, 3):
        for kind, f in ((4, 0), (5, 1)):
            small[b - 1][kind].wait_recv()
            if f == 0:
                ref = wqkv_out.at[:, w_rows(dp ^ b, core)]
            else:
                ref = wout_out.at[dp ^ b, o_rows(core)]
            copy = remote(ref, ref, f_send.at[f, b - 1], f_recv.at[f, b - 1], ctx=ctx ^ 1)
            copy.start()
            forwards.append(copy)
    for copy in forwards:
        copy.wait_recv()

    def own_q(s, carry):
        q_ref[s] = (dot(n_all[0, s], wqkv_out[0]).astype(BF16) * (HD ** (-0.5))).astype(BF16)
        project(0, s)
        project(1, s)
        return carry

    lax.fori_loop(0, seqs, own_q, 0)
    later = []
    for s in range(seqs):
        across[s].wait_recv()
        copy = remote(tok_all.at[2, s], tok_all.at[3, s], t_send.at[1 + s], t_recv.at[1 + s], ctx=ctx ^ 1)
        copy.start()
        later.append(copy)
    norm_piece(2)
    for copy in later:
        copy.wait_recv()
    norm_piece(3)

    def others(s, carry):
        project(2, s)
        project(3, s)
        return carry

    lax.fori_loop(0, seqs, others, 0)
    for group in small:
        for copy in group:
            copy.wait_send()
    for copy in forwards + later + across + [beside]:
        copy.wait_send()


def first_stage(tokens, wqkv, wout, table, gain_attn, gain_moe, router):
    seqs, stretch, width = tokens.shape
    count, rows, local = wqkv.shape
    dp = width // rows
    experts_n = router.shape[1]
    any_spec = pl.BlockSpec(memory_space=pl.ANY)
    vmem = pl.BlockSpec(memory_space=pltpu.VMEM)
    dma = pltpu.SemaphoreType.DMA
    return pl.pallas_call(
        functools.partial(first_kernel, seqs),
        name="first_stage",
        in_specs=[any_spec] * 7,
        out_specs=[vmem] * 10,
        out_shape=[
            jax.ShapeDtypeStruct((seqs, stretch, local), BF16),
            jax.ShapeDtypeStruct((seqs, 4, stretch, local), BF16),
            jax.ShapeDtypeStruct((seqs, 4, stretch, local), BF16),
            jax.ShapeDtypeStruct((seqs, stretch, width), BF16),
            jax.ShapeDtypeStruct((3, width, local), BF16),
            jax.ShapeDtypeStruct((dp,) + wout.shape, BF16),
            jax.ShapeDtypeStruct((dp,) + table.shape, BF16),
            jax.ShapeDtypeStruct((1, width), F32),
            jax.ShapeDtypeStruct((1, width), BF16),
            jax.ShapeDtypeStruct((experts_n, width), BF16),
        ],
        scratch_shapes=[
            pltpu.VMEM((4, seqs, stretch, width), BF16),
            pltpu.VMEM((4, seqs, stretch, width), BF16),
            pltpu.VMEM((dp, 1, rows), BF16),
            pltpu.VMEM((dp, 1, rows), BF16),
            pltpu.VMEM((dp, rows, experts_n), BF16),
            dma((6, 3)), dma((6, 3)), dma((2, 3)), dma((2, 3)), dma((1 + seqs,)), dma((1 + seqs,)),
            dma((seqs,)), dma((seqs,)), dma((7,)),
        ],
        compiler_params=pltpu.CompilerParams(vmem_limit_bytes=VMEM_BYTES, collective_id=0, has_side_effects=True),
        cost_estimate=cost(40 * 10**9, 10**7),
    )(tokens, wqkv, wout, table, gain_attn, gain_moe, router)


def last_kernel(
    normed_ref, proj_ref, datt_ref, att_ref, small_ref,
    out_ref, router_out, gm_out, ga_out, table_out,
    grads, core_send, core_got, y_out, y_got, z_out, z_got, wide, s_own, s_core, s_y, s_x, s_z,
    c_sems, y_sems, z_sems, w_sems, s_sems,
):
    dp = lax.axis_index("dp")
    ctx = lax.axis_index("ctx")
    tp = lax.axis_index("tp")
    core = ctx % 2
    far = ctx // 2
    greet([{"dp": dp ^ b} for b in (1, 2, 3)] + [{"ctx": ctx ^ b} for b in (1, 2, 3)] + [{"tp": tp ^ 1}])
    count = z_got.shape[0] + 1
    width = normed_ref.shape[1]
    piece = width // count

    x_copy = remote(small_ref, s_x, s_sems.at[0, 0], s_sems.at[1, 0], tp=tp ^ 1)
    x_copy.start()
    normed_t = normed_ref[...].T
    for j in range(3):
        grads[j] = dot(normed_t, proj_ref[j])
    grads[3] = dot_tn(datt_ref[...], att_ref[...])
    give = 1 - core
    core_send[0] = grads[2 * give].astype(BF16)
    core_send[1] = grads[2 * give + 1].astype(BF16)
    c_copy = remote(core_send, core_got, c_sems.at[0], c_sems.at[1], ctx=ctx ^ 1)
    c_copy.start()
    x_copy.wait_recv()
    lines = lax.broadcasted_iota(jnp.int32, small_ref.shape, 0)
    s_own[...] = small_ref[...] + jnp.where(lines == 9, s_x[...], 0.0)
    sc_copy = remote(s_own, s_core, s_sems.at[0, 1], s_sems.at[1, 1], ctx=ctx ^ 1)
    sc_copy.start()
    c_copy.wait_recv()
    grads[2 * core] += core_got[0].astype(F32)
    grads[2 * core + 1] += core_got[1].astype(F32)
    y_out[...] = grads[2 * core + 1 - far].astype(BF16)
    order = (3, 2, 1, 0)
    y_copies = []
    for b in order:
        at = pl.ds(pl.multiple_of((dp ^ b) * piece, 16), piece)
        copy = remote(y_out.at[at], y_got.at[b], y_sems.at[0, b], y_sems.at[1, b], ctx=ctx ^ 2)
        copy.start()
        y_copies.append(copy)
    sc_copy.wait_recv()
    y_small = s_own[...] + s_core[...]
    s_y[0] = y_small
    sy_copy = remote(s_y.at[0], s_y.at[1], s_sems.at[0, 2], s_sems.at[1, 2], ctx=ctx ^ 2)
    sy_copy.start()
    mine = 2 * core + far
    z_copies = []
    total = None
    for copy, b in zip(y_copies, order):
        copy.wait_recv()
        at = pl.ds(pl.multiple_of((dp ^ b) * piece, 16), piece)
        value = grads[mine, at] + y_got[b].astype(F32)
        if b:
            z_out[b - 1] = value.astype(BF16)
            z_copy = remote(z_out.at[b - 1], z_got.at[b - 1], z_sems.at[0, b - 1], z_sems.at[1, b - 1], dp=dp ^ b)
            z_copy.start()
            z_copies.append((b, z_copy))
        else:
            total = value
    sy_copy.wait_recv()
    s_z[dp] = s_y[0] + s_y[1]
    sz_copies = []
    for b in (3, 2, 1):
        copy = remote(s_z.at[dp], s_z.at[dp], s_sems.at[0, 2 + b], s_sems.at[1, 2 + b], dp=dp ^ b)
        copy.start()
        sz_copies.append(copy)
    for b, copy in z_copies:
        copy.wait_recv()
        total = total + z_got[b - 1].astype(F32)
    wide[mine] = total.astype(BF16)
    w_copies = []
    for b in (3, 2, 1):
        copy = remote(wide.at[mine], wide.at[mine], w_sems.at[0, b - 1], w_sems.at[1, b - 1], ctx=ctx ^ b)
        copy.start()
        w_copies.append(copy)
    for copy in sz_copies:
        copy.wait_recv()
    small = s_z[0]
    for d in range(1, count):
        small = small + s_z[d]

    def exact(a, b, dims):
        return lax.dot_general(a, b, (dims, ((), ())), precision=FULL_PRECISION, preferred_element_type=F32)

    row = lax.broadcasted_iota(jnp.int32, (piece, width), 0)
    col = lax.broadcasted_iota(jnp.int32, (piece, width), 1)
    select = jnp.where(col == row + dp * piece, 1.0, 0.0)
    experts_n = router_out.shape[1]
    e_row = lax.broadcasted_iota(jnp.int32, (experts_n, experts_n), 0)
    e_col = lax.broadcasted_iota(jnp.int32, (experts_n, experts_n), 1)
    slot = ((e_row % 2) ^ tp) * count + e_row // 2
    arranged = exact(jnp.where(e_col == slot, 1.0, 0.0), small[:experts_n], ((1,), (0,)))
    router_out[...] = exact(select, arranged, ((1,), (1,)))
    gains = exact(small[8:16], select, ((1,), (1,)))
    gm_out[...] = gains[0:1]
    ga_out[...] = gains[1:2]
    t_rows, heads = table_out.shape
    t_row = lax.broadcasted_iota(jnp.int32, (t_rows, width), 0)
    t_col = lax.broadcasted_iota(jnp.int32, (t_rows, width), 1)
    table_out[...] = exact(jnp.where(t_col == t_row + dp * t_rows, 1.0, 0.0), small[16:24], ((1,), (1,)))[:, :heads]
    for copy in w_copies:
        copy.wait_recv()
    out_ref[...] = wide[...].astype(F32)
    for copy in [x_copy, c_copy, sc_copy, sy_copy] + y_copies + [c for _, c in z_copies] + sz_copies + w_copies:
        copy.wait_send()


def last_stage(normed, proj, datt, att, small, dp, table_rows, heads, experts_n):
    rows, width = normed.shape
    local = att.shape[1]
    piece = width // dp
    vmem = pl.BlockSpec(memory_space=pltpu.VMEM)
    dma = pltpu.SemaphoreType.DMA
    return pl.pallas_call(
        last_kernel,
        name="last_stage",
        in_specs=[vmem] * 5,
        out_specs=[vmem] * 5,
        out_shape=[
            jax.ShapeDtypeStruct((4, piece, local), F32),
            jax.ShapeDtypeStruct((piece, experts_n), F32),
            jax.ShapeDtypeStruct((1, piece), F32),
            jax.ShapeDtypeStruct((1, piece), F32),
            jax.ShapeDtypeStruct((table_rows, heads), F32),
        ],
        scratch_shapes=[
            pltpu.VMEM((4, width, local), F32),
            pltpu.VMEM((2, width, local), BF16),
            pltpu.VMEM((2, width, local), BF16),
            pltpu.VMEM((width, local), BF16),
            pltpu.VMEM((4, piece, local), BF16),
            pltpu.VMEM((3, piece, local), BF16),
            pltpu.VMEM((3, piece, local), BF16),
            pltpu.VMEM((4, piece, local), BF16),
            pltpu.VMEM(small.shape, F32),
            pltpu.VMEM(small.shape, F32),
            pltpu.VMEM((2,) + small.shape, F32),
            pltpu.VMEM(small.shape, F32),
            pltpu.VMEM((dp,) + small.shape, F32),
            dma((2,)), dma((2, 4)), dma((2, 3)), dma((2, 3)), dma((2, 6)),
        ],
        compiler_params=pltpu.CompilerParams(vmem_limit_bytes=VMEM_BYTES, collective_id=1, has_side_effects=True),
        cost_estimate=cost(8 * rows * width * local, 8 * rows * width),
    )(normed, proj, datt, att, small)


def moe_kernel(
    seqs, groups, cap, tile, *refs,
):
    sends, refs = refs[:seqs], refs[seqs:]
    slot_gates, refs = refs[:seqs], refs[seqs:]
    cots, refs = refs[:groups], refs[groups:]
    w_own, w_far, part_out, din_back, h_back, keep_out, give_out = refs[:7]
    (
        w_all, x_all, gate_all, g_all, xt_all, dyt_all, dy_ref, hid_all, dpre_all, part_acc, din_acc,
        part_all, din_all, h_all, tile_ref,
        x_sems, gate_sems, din_sems, h_sems, w_sems, own_sems, part_sems, out_sems,
    ) = refs[7:]
    dp = lax.axis_index("dp")
    ctx = lax.axis_index("ctx")
    greet([{"dp": dp ^ b} for b in range(1, groups)] + [{"ctx": ctx ^ 1}])
    width = x_all.shape[-1]
    rows = groups * cap
    slices = w_all.shape[2]
    piece = width // slices
    half_len = w_all.shape[4]
    per_half = half_len // tile
    tiles = w_all.shape[1] * per_half
    order = tuple(range(groups - 1, 0, -1))

    sent = []
    for s in range(seqs):
        for b in order:
            sent.append(
                remote(sends[s].at[dp ^ b], x_all.at[s, dp], x_sems.at[0, s, b - 1], x_sems.at[1, s, b - 1], dp=dp ^ b)
            )
            sent.append(
                remote(
                    slot_gates[s].at[dp ^ b], gate_all.at[s, dp],
                    gate_sems.at[0, s, b - 1], gate_sems.at[1, s, b - 1], dp=dp ^ b,
                )
            )
    w_copies = [
        remote(w_own, w_all.at[:, :, ctx], w_sems.at[0, 0], w_sems.at[1, 0], ctx=ctx ^ 1),
        remote(w_far, w_all.at[:, :, ctx ^ 2], w_sems.at[0, 1], w_sems.at[1, 1], ctx=ctx ^ 1),
    ]
    for copy in w_copies + sent:
        copy.start()
    local = [
        pltpu.make_async_copy(w_own, w_all.at[:, :, ctx], own_sems.at[0]),
        pltpu.make_async_copy(w_far, w_all.at[:, :, ctx ^ 2], own_sems.at[1]),
    ]
    for s in range(seqs):
        local.append(pltpu.make_async_copy(sends[s].at[dp], x_all.at[s, dp], own_sems.at[2 + 2 * s]))
        local.append(pltpu.make_async_copy(slot_gates[s].at[dp], gate_all.at[s, dp], own_sems.at[3 + 2 * s]))
    for b in range(groups):
        local.append(pltpu.make_async_copy(cots[b], g_all.at[dp ^ b], own_sems.at[2 + 2 * seqs + b]))
    for copy in local:
        copy.start()
    for copy in local:
        copy.wait()
    arrivals = [
        remote(w_all.at[:, :, ctx ^ 1], w_all.at[:, :, ctx ^ 1], w_sems.at[0, 0], w_sems.at[1, 0], ctx=ctx ^ 1),
        remote(w_all.at[:, :, ctx ^ 3], w_all.at[:, :, ctx ^ 3], w_sems.at[0, 1], w_sems.at[1, 1], ctx=ctx ^ 1),
    ]
    for copy in arrivals:
        copy.wait_recv()
    eye = diagonal(cap)

    def weights(io, f):
        lanes = pl.ds(pl.multiple_of((f % per_half) * tile, tile), tile)
        return w_all[io, f // per_half, :, :, lanes].reshape(width, tile)

    def gate_column(s, group):
        return jnp.sum(jnp.where(eye, gate_all[s, group], 0.0), axis=1, keepdims=True)

    def din_copy(s, b):
        return remote(
            din_all.at[s, dp ^ b], din_back.at[s, dp], din_sems.at[0, s, b - 1], din_sems.at[1, s, b - 1], dp=dp ^ b
        )

    def h_copy(s, b):
        return remote(h_all.at[s, dp ^ b], h_back.at[s, dp], h_sems.at[0, s, b - 1], h_sems.at[1, s, b - 1], dp=dp ^ b)

    def part_copy(s, b):
        return pltpu.make_async_copy(part_all.at[s, dp ^ b], part_out.at[b, s], part_sems.at[s, b])

    def own_copies(s):
        return [
            pltpu.make_async_copy(din_all.at[s, dp], din_back.at[s, dp], part_sems.at[s, groups]),
            pltpu.make_async_copy(h_all.at[s, dp], h_back.at[s, dp], part_sems.at[s, groups + 1]),
        ]

    def chunk(s, carry):
        for b in order:
            there = x_all.at[s, dp ^ b]
            remote(there, there, x_sems.at[0, s, b - 1], x_sems.at[1, s, b - 1], dp=dp ^ b).wait_recv()
            there = gate_all.at[s, dp ^ b]
            remote(there, there, gate_sems.at[0, s, b - 1], gate_sems.at[1, s, b - 1], dp=dp ^ b).wait_recv()
        x = x_all[s].reshape(rows, width)
        xt_all[s] = x.T
        for group in range(groups):
            dy_ref[group * cap : (group + 1) * cap] = (g_all[group, s].astype(F32) * gate_column(s, group)).astype(BF16)
        dyt_all[s] = dy_ref[...].T
        part_acc[...] = jnp.zeros_like(part_acc)
        din_acc[...] = jnp.zeros_like(din_acc)

        def step(f, carry):
            x = x_all[s].reshape(rows, width)
            w_in = weights(0, f)
            w_out_t = weights(1, f)
            pre = dot(x, w_in)
            dhid = dot(dy_ref[...], w_out_t)
            square = pre * pre
            inner = jnp.tanh(GELU_C * pre * (1.0 + GELU_A * square))
            half = 0.5 * (1.0 + inner)
            hidden = (pre * half).astype(BF16)
            slope = half + (0.5 * GELU_C) * pre * (1.0 - inner * inner) * (1.0 + (3.0 * GELU_A) * square)
            dpre = (dhid * slope).astype(BF16)
            hid_all[f, s] = hidden
            dpre_all[f, s] = dpre
            part_acc[...] += dot_nt(hidden, w_out_t)
            din_acc[...] += dot_nt(dpre, w_in)
            return carry

        lax.fori_loop(0, tiles, step, 0)
        for group in range(groups):
            at = slice(group * cap, (group + 1) * cap)
            din_all[s, group] = din_acc[at].astype(BF16)
            gated = part_acc[at] * gate_column(s, group)
            part_all[s, group] = gated.astype(BF16)
            h = jnp.sum(gated * g_all[group, s].astype(F32), axis=1, keepdims=True)
            h_all[s, group] = jnp.sum(jnp.where(eye, h, 0.0), axis=0, keepdims=True)
        for b in order:
            din_copy(s, b).start()
            h_copy(s, b).start()
        for copy in own_copies(s):
            copy.start()
        for b in range(groups):
            part_copy(s, b).start()
        return carry

    lax.fori_loop(0, seqs, chunk, 0)

    def out_copies(f, slot):
        lanes = pl.ds(pl.multiple_of((f % per_half) * tile, tile), tile)
        return [
            pltpu.make_async_copy(
                tile_ref.at[slot, 0], keep_out.at[f // per_half, :, :, :, lanes], out_sems.at[slot, 0]
            ),
            pltpu.make_async_copy(
                tile_ref.at[slot, 1], give_out.at[f // per_half, :, :, :, lanes], out_sems.at[slot, 1]
            ),
        ]

    def weight_grads(f, carry):
        slot = f % 2

        @pl.when(f >= 2)
        def _():
            for copy in out_copies(f - 2, slot):
                copy.wait()

        for io, (left, right) in enumerate(((xt_all, dpre_all), (dyt_all, hid_all))):
            total = dot(left[0], right[f, 0])
            for s in range(1, seqs):
                total = total + dot(left[s], right[f, s])
            for index in range(slices):
                place = index ^ ctx
                tile_ref[slot, place % 2, place // 2, io] = total[index * piece : (index + 1) * piece].astype(BF16)
        for copy in out_copies(f, slot):
            copy.start()
        return carry

    lax.fori_loop(0, tiles, weight_grads, 0)
    for f in (tiles - 2, tiles - 1):
        for copy in out_copies(f, f % 2):
            copy.wait()
    for s in range(seqs):
        for b in order:
            there = din_back.at[s, dp ^ b]
            remote(there, there, din_sems.at[0, s, b - 1], din_sems.at[1, s, b - 1], dp=dp ^ b).wait_recv()
            there = h_back.at[s, dp ^ b]
            remote(there, there, h_sems.at[0, s, b - 1], h_sems.at[1, s, b - 1], dp=dp ^ b).wait_recv()
            din_copy(s, b).wait_send()
            h_copy(s, b).wait_send()
        for copy in own_copies(s):
            copy.wait()
        for b in range(groups):
            part_copy(s, b).wait()
    for copy in w_copies + sent:
        copy.wait_send()


def moe_stage(sends, slot_gates, cots, w_own, w_far, tile=512):
    seqs = len(sends)
    groups, cap, width = sends[0].shape
    _, halves, piece, half_len = w_own.shape
    slices = width // piece
    tiles = halves * half_len // tile
    rows = groups * cap
    any_spec = pl.BlockSpec(memory_space=pl.ANY)
    vmem = pl.BlockSpec(memory_space=pltpu.VMEM)
    dma = pltpu.SemaphoreType.DMA
    return pl.pallas_call(
        functools.partial(moe_kernel, seqs, groups, cap, tile),
        name="moe_stage",
        in_specs=[any_spec] * (2 * seqs + groups + 2),
        out_specs=[any_spec, any_spec, vmem, any_spec, any_spec],
        out_shape=[
            jax.ShapeDtypeStruct((groups, seqs, cap, width), BF16),
            jax.ShapeDtypeStruct((seqs, groups, cap, width), BF16),
            jax.ShapeDtypeStruct((seqs, groups, 1, cap), F32),
            jax.ShapeDtypeStruct((halves, slices // 2, 2, piece, half_len), BF16),
            jax.ShapeDtypeStruct((halves, slices // 2, 2, piece, half_len), BF16),
        ],
        scratch_shapes=[
            pltpu.VMEM((2, halves, slices, piece, half_len), BF16),
            pltpu.VMEM((seqs, groups, cap, width), BF16),
            pltpu.VMEM((seqs, groups, 1, cap), F32),
            pltpu.VMEM((groups, seqs, cap, width), BF16),
            pltpu.VMEM((seqs, width, rows), BF16),
            pltpu.VMEM((seqs, width, rows), BF16),
            pltpu.VMEM((rows, width), BF16),
            pltpu.VMEM((tiles, seqs, rows, tile), BF16),
            pltpu.VMEM((tiles, seqs, rows, tile), BF16),
            pltpu.VMEM((rows, width), F32),
            pltpu.VMEM((rows, width), F32),
            pltpu.VMEM((seqs, groups, cap, width), BF16),
            pltpu.VMEM((seqs, groups, cap, width), BF16),
            pltpu.VMEM((seqs, groups, 1, cap), F32),
            pltpu.VMEM((2, 2, slices // 2, 2, piece, tile), BF16),
            dma((2, seqs, groups - 1)), dma((2, seqs, groups - 1)), dma((2, seqs, groups - 1)),
            dma((2, seqs, groups - 1)), dma((2, 2)), dma((2 + 2 * seqs + groups,)), dma((seqs, groups + 2)),
            dma((2, 2)),
        ],
        compiler_params=pltpu.CompilerParams(
            vmem_limit_bytes=63 * 1024 * 1024, collective_id=2, has_side_effects=True
        ),
        cost_estimate=cost(20 * seqs * rows * width * halves * half_len, 40 * width * halves * half_len),
    )(*sends, *slot_gates, *cots, w_own, w_far)


def flip(value, axis, bit):
    count = lax.axis_size(axis)
    return lax.ppermute(value, axis, [(i, i ^ bit) for i in range(count)])


def all_to_all_dp(value):
    return lax.all_to_all(value, "dp", split_axis=0, concat_axis=0, tiled=True)


def gathered(tokens, wqkv, wout, table, gain_attn, gain_moe, router):
    seqs, stretch, width = tokens.shape
    local = wqkv.shape[2]
    dp = lax.axis_size("dp")
    tp = lax.axis_index("tp")
    experts_n = router.shape[1]
    wqkv = lax.all_gather(wqkv, "dp", axis=1, tiled=True)
    wout = lax.all_gather(wout, "dp", axis=1, tiled=True)
    table = lax.all_gather(table, "dp", axis=0, tiled=True)
    gains = lax.all_gather(jnp.concatenate([gain_attn, gain_moe], axis=0), "dp", axis=1, tiled=True)
    gain_attn, gain_moe = gains[0:1].astype(F32), gains[1:2]
    router = lax.all_gather(router, "dp", axis=0, tiled=True).T.reshape(dp, 2, width).transpose(1, 0, 2)
    router = jnp.where(tp == 0, router, router[::-1]).reshape(experts_n, width)
    across = flip(tokens, "ctx", 2)
    beside, beyond = flip(jnp.stack([tokens, across]), "ctx", 1)
    x32 = jnp.stack([tokens, beside, across, beyond], axis=1).astype(F32)
    normed = (x32 * norm_factor(x32) * gain_attn[None, None]).astype(BF16)
    own = normed[:, 0].reshape(seqs * stretch, width)
    queries = jnp.dot(own, wqkv[0], preferred_element_type=F32).astype(BF16) * jnp.asarray(HD ** (-0.5), BF16)
    flat = normed.reshape(seqs * 4 * stretch, width)
    keys = jnp.dot(flat, wqkv[1], preferred_element_type=F32).astype(BF16).reshape(seqs, 4 * stretch, local)
    values = jnp.dot(flat, wqkv[2], preferred_element_type=F32).astype(BF16).reshape(seqs, 4 * stretch, local)
    return queries.reshape(seqs, stretch, local), keys, values, own, wqkv, wout, table, gain_attn, gain_moe, router


def on_device(
    tokens_in, block_ids, rel_buckets, routes, attn_gain, w_qkv, w_attn_out, bias_table, moe_gain, w_router,
    w_expert_in, w_expert_out, cotangent,
):
    seqs, stretch, width = tokens_in.shape
    dp = lax.axis_size("dp")
    ctx_count = lax.axis_size("ctx")
    tp_count = lax.axis_size("tp")
    expert_count = w_router.shape[2]
    assert w_expert_in.shape[1] == tp_count == 2 and ctx_count == 4
    cap = max(2, 2 * stretch * routes.shape[2] // expert_count)
    ctx = lax.axis_index("ctx")
    tp = lax.axis_index("tp")
    local = w_qkv.shape[3]
    heads = local // HD

    fits = dp == 4
    if fits:
        queries, keys, values, own_normed, wqkv, wout_parts, table, gain_attn, gain_moe, router = first_stage(
            tokens_in, w_qkv[0], w_attn_out[0], bias_table[0], attn_gain, moe_gain, w_router[0]
        )
        wout_own = wout_parts.transpose(1, 0, 2).reshape(local, width)
        table = table.reshape(NB, heads)
        keys = keys.reshape(seqs, 4 * stretch, local)
        values = values.reshape(seqs, 4 * stretch, local)
        own_normed = own_normed.reshape(seqs * stretch, width)
    else:
        queries, keys, values, own_normed, wqkv, wout_own, table, gain_attn, gain_moe, router = gathered(
            tokens_in, w_qkv[0], w_attn_out[0], bias_table[0], attn_gain, moe_gain, w_router[0]
        )
    wout_other = flip(wout_own, "tp", 1)

    w_in = w_expert_in[0]
    w_out_t = w_expert_out[0].transpose(0, 2, 1)
    both = jnp.stack([w_in, w_out_t], axis=1)
    keep = lax.dynamic_index_in_dim(both, tp, 0, keepdims=False)
    give = lax.dynamic_index_in_dim(both, 1 - tp, 0, keepdims=False)
    got = flip(give, "tp", 1)
    both = jnp.stack([keep, got], axis=1)
    if fits:
        far = flip(both, "ctx", 2)
    else:
        weights = lax.all_gather(both, "ctx", axis=0, tiled=False)

    e_order = jnp.arange(expert_count, dtype=jnp.int32).reshape(dp, 2).T
    e_order = jnp.where(tp == 0, e_order, e_order[::-1]).reshape(1, expert_count, 1)
    hits = ((routes[:, None, :, 0] == e_order) | (routes[:, None, :, 1] == e_order)).astype(F32)
    before = (
        lax.broadcasted_iota(jnp.int32, (stretch, stretch), 0) < lax.broadcasted_iota(jnp.int32, (stretch, stretch), 1)
    ).astype(BF16)
    ranks = jnp.einsum("set,tu->seu", hits.astype(BF16), before, preferred_element_type=F32)
    places = jnp.where(hits > 0.5, ranks, -1.0)[:, :dp]

    if fits:
        me = lax.axis_index("dp")
        near_places = jnp.stack([lax.dynamic_index_in_dim(places, me ^ b, 1, keepdims=False) for b in range(dp)], axis=1)
        cot_slots = dispatch(near_places, cotangent, cap)
        cot_slots = [cot_slots[0]] + [flip(cot_slots[b], "dp", b) for b in range(1, dp)]
    else:
        cot_slots = all_to_all_dp(dispatch(places, cotangent, cap))

    one_hot_bucket = (rel_buckets[:, None] == jnp.arange(NB, dtype=jnp.int32)[None, :]).astype(F32)
    one_hot_bucket = jnp.pad(one_hot_bucket, ((0, 1), (0, 0)))
    starts = [(ctx - (ctx ^ b)) * stretch + 3 * stretch for b in range(4)]
    hot_windows = jnp.stack([lax.dynamic_slice_in_dim(one_hot_bucket, s, 2 * stretch, 0) for s in starts])
    windows = jnp.einsum("bmn,nh->hbm", hot_windows, table.astype(F32), precision=FULL_PRECISION)
    bias = expand_bias(windows)

    ids = block_ids.reshape(seqs, 4, stretch)
    ids_pieces = [lax.dynamic_index_in_dim(ids, ctx ^ b, 1, keepdims=False) for b in range(4)]
    ids_query = ids_pieces[0].reshape(seqs, 1, stretch)
    ids_key = jnp.stack(ids_pieces, axis=1).reshape(seqs, 4 * stretch, 1)

    wout_pair = jnp.stack([wout_own, wout_other])
    attended, lse, mids, moes, gates, sends, slot_gates = [], [], [], [], [], [], []
    for s in range(seqs):
        att, stat = attend(queries[s], keys[s], values[s], bias, ids_query[s], ids_key[s])
        attended.append(att)
        lse.append(stat)
        mid, moe_in, gate, send, slot_gate = middle_stage(
            att, flip(att, "tp", 1), tokens_in[s], wout_pair, gain_moe, router, hits[s], places[s], cap
        )
        mids.append(mid)
        moes.append(moe_in)
        gates.append(gate)
        sends.append(send)
        slot_gates.append(slot_gate)
    if fits:
        parts, returned_din, returned_h, kept, given = moe_stage(sends, slot_gates, cot_slots, both, far)
        moved = [parts[0]] + [flip(parts[b], "dp", b) for b in range(1, dp)]
        partials = [jnp.stack([piece[s] for piece in moved]) for s in range(seqs)]
        out_places = near_places
    else:
        partials, returned_din, returned_h = [], [], []
        out_places = places
        acc = None
        for s in range(seqs):
            received = all_to_all_dp(sends[s])
            received_gate = all_to_all_dp(slot_gates[s])
            part, din, h, acc = experts(received, cot_slots, s, received_gate, weights, acc, s == seqs - 1)
            returned_din.append(all_to_all_dp(din))
            returned_h.append(all_to_all_dp(h))
            partials.append(all_to_all_dp(part))
        kept, given = acc[:, 0::2], acc[:, 1::2]

    beside_sum = kept.astype(F32) + flip(given, "ctx", 1).astype(F32)
    mine = beside_sum[:, 0] + flip(beside_sum[:, 1].astype(BF16), "ctx", 2).astype(F32)
    other = flip(mine[1].astype(BF16), "tp", 1).astype(F32)
    ordered = jnp.where(tp == 0, jnp.stack([mine[0], other]), jnp.stack([other, mine[0]]))
    grad_expert_in = ordered[:, 0]
    grad_expert_out = ordered[:, 1].transpose(0, 2, 1)

    tokens_out, gmids = [], []
    projections = []
    rel_grad = 0.0
    gain_moe_grad = 0.0
    router_grad = 0.0
    datts = []
    for s in range(seqs):
        out_own = combine_out(out_places[s], partials[s], cap)
        out_other = flip(out_own, "tp", 1)
        tokens_out.append((mids[s] + (out_own.astype(F32) + out_other.astype(F32))).astype(BF16))
        din_own, h_own = combine(places[s], returned_din[s], returned_h[s], cap)
        din_other = flip(din_own, "tp", 1)
        h_all = jnp.concatenate([h_own, flip(h_own, "tp", 1)], axis=0)
        gmid, datt, d_gain, d_router, dattn = middle_back(
            din_own, din_other, h_all, gates[s], router, moes[s], mids[s], gain_moe, cotangent[s], wout_own
        )
        datts.append(dattn)
        gmids.append(gmid)
        gain_moe_grad += d_gain
        router_grad += d_router
        dq, dk, dv, rel = attend_back(
            queries[s], keys[s], values[s], datt, bias, lse[s], ids_query[s], ids_key[s]
        )
        rel_grad += rel
        dkv = jnp.stack([dk, dv]).reshape(2, 4, stretch, local)
        near = dkv[:, 0::2].astype(F32) + flip(dkv[:, 1::2], "ctx", 1).astype(F32)
        full = near[:, 0] + flip(near[:, 1].astype(BF16), "ctx", 2).astype(F32)
        projections.append(jnp.concatenate([dq[None], full.astype(BF16)], axis=0))
    grad_proj = jnp.concatenate(projections, axis=1)
    dattn = jnp.concatenate(datts, axis=0)
    attended = jnp.concatenate(attended, axis=0)
    dnormed_part = jnp.einsum("jre,jde->rd", grad_proj, wqkv, preferred_element_type=F32)
    dnormed_own = dnormed_part.astype(BF16)
    dnormed = dnormed_own.astype(F32) + flip(dnormed_own, "tp", 1).astype(F32)
    own_x = tokens_in.reshape(seqs * stretch, width).astype(F32)
    factor = norm_factor(own_x)
    unit = own_x * factor
    scaled = dnormed * gain_attn
    dres = factor * (scaled - unit * jnp.mean(scaled * unit, axis=-1, keepdims=True))
    grad_tokens = jnp.concatenate(gmids, axis=0) + dres

    rel_flat = rel_grad.reshape(heads, 4, 2 * stretch)
    grad_table = jnp.einsum("bmn,hbm->nh", hot_windows, rel_flat, precision=FULL_PRECISION)
    if fits:
        gain_rows = jnp.concatenate([gain_moe_grad, jnp.sum(dnormed_part * unit, axis=0)[None]], axis=0)
        small = jnp.concatenate(
            [
                router_grad,
                jnp.pad(gain_rows, ((0, 6), (0, 0))),
                jnp.pad(grad_table.T, ((0, 8 - heads), (0, width - NB))),
            ],
            axis=0,
        )
        wide, g_router, g_moe, g_attn, g_table = last_stage(
            own_normed, grad_proj, dattn, attended, small, dp, NB // dp, heads, expert_count
        )
        g_qkv = wide[:3]
        g_wout = wide[3].T
    else:
        router_grad = router_grad.reshape(2, dp, width)
        router_grad = jnp.where(tp == 0, router_grad, router_grad[::-1])
        router_grad = router_grad.transpose(1, 0, 2).reshape(expert_count, width).T

        def reduced(value, dim):
            return lax.psum(lax.psum_scatter(value, "dp", scatter_dimension=dim, tiled=True), "ctx")

        g_attn = reduced(jnp.sum(dnormed * unit, axis=0)[None], 1)
        g_qkv = reduced(jnp.einsum("rd,jre->jde", own_normed, grad_proj, preferred_element_type=F32), 1)
        g_wout = reduced(jnp.einsum("re,rd->ed", attended, dattn, preferred_element_type=F32), 1)
        g_table = reduced(grad_table, 0)
        g_moe = reduced(gain_moe_grad, 1)
        g_router = reduced(router_grad, 0)
    return (
        jnp.stack(tokens_out),
        grad_tokens.reshape(seqs, stretch, width),
        g_attn,
        g_qkv[None],
        g_wout[None],
        g_table[None],
        g_moe,
        g_router[None],
        grad_expert_in[None],
        grad_expert_out[None],
    )


def solution(mesh):
    return jax.shard_map(
        on_device,
        mesh=mesh,
        in_specs=(
            P("dp", "ctx", None),
            P("dp", None),
            P(),
            P("dp", "ctx", None),
            P(None, "dp"),
            P(None, None, "dp", "tp"),
            P(None, "tp", "dp"),
            P(None, "dp", "tp"),
            P(None, "dp"),
            P(None, "dp", None),
            P(None, "dp", "ctx", "tp"),
            P(None, "dp", "tp", "ctx"),
            P("dp", "ctx", None),
        ),
        out_specs=(
            P("dp", "ctx", None),
            P("dp", "ctx", None),
            P(None, "dp"),
            P(None, None, "dp", "tp"),
            P(None, "tp", "dp"),
            P(None, "dp", "tp"),
            P(None, "dp"),
            P(None, "dp", None),
            P(None, "dp", "ctx", "tp"),
            P(None, "dp", "tp", "ctx"),
        ),
        check_vma=False,
    )
```

```python
import functools

import jax
import jax.numpy as jnp
from jax import lax
from jax.experimental import pallas as pl
from jax.experimental.pallas import tpu as pltpu
from jax.sharding import PartitionSpec as P

HD = 64
NB = 32
EPSILON = 1e-06
FULL_PRECISION = lax.Precision.HIGHEST
MASKED = -1e30
BF16 = jnp.bfloat16
F32 = jnp.float32
EARLY = 50
VMEM_BYTES = 60 * 1024 * 1024
GELU_C = 0.7978845608028654
GELU_A = 0.044715


def params():
    return pltpu.CompilerParams(vmem_limit_bytes=VMEM_BYTES)


def cost(flops, nbytes, trans=0, scale=1):
    return pl.CostEstimate(
        flops=int(flops) // scale, bytes_accessed=int(nbytes) // scale, transcendentals=int(trans) // scale
    )


def dot(a, b):
    return lax.dot_general(a, b, (((1,), (0,)), ((), ())), preferred_element_type=F32)


def dot_nt(a, b):
    return lax.dot_general(a, b, (((1,), (1,)), ((), ())), preferred_element_type=F32)


def dot_tn(a, b):
    return lax.dot_general(a, b, (((0,), (0,)), ((), ())), preferred_element_type=F32)


def bias_kernel(win_ref, out_ref):
    for block in range(4):
        row = win_ref[0, block : block + 1, :]
        wide = jnp.broadcast_to(row, (256, 512))
        rolled = pltpu.roll(wide, 257, 1, stride=1, stride_axis=0)
        out_ref[0, block * 256 : (block + 1) * 256, :] = rolled[:, :256].astype(BF16)


def expand_bias(windows):
    heads = windows.shape[0]
    return pl.pallas_call(
        bias_kernel,
        name="expand_bias",
        grid=(heads,),
        in_specs=[pl.BlockSpec((1, 4, 512), lambda h: (h, 0, 0))],
        out_specs=pl.BlockSpec((1, 1024, 256), lambda h: (h, 0, 0)),
        out_shape=jax.ShapeDtypeStruct((heads, 1024, 256), BF16),
        compiler_params=params(),
        cost_estimate=cost(heads * 2 * 1024 * 512, heads * 1024 * 256 * 2, scale=EARLY),
    )(windows)


def attend_kernel(q_ref, k_ref, v_ref, bias_ref, idq_ref, idk_ref, out_ref, lse_ref, mask_ref):
    @pl.when(pl.program_id(0) == 0)
    def _():
        mask_ref[...] = jnp.where(idk_ref[...] <= idq_ref[...], 0.0, MASKED)

    queries = q_ref[...]
    keys = k_ref[...]
    values_t = v_ref[...].T
    low_half = lax.broadcasted_iota(jnp.int32, queries.shape, 1) < HD
    zero = jnp.zeros_like(queries)
    parts = []
    for head in range(2):
        own = jnp.where(low_half, queries, zero) if head == 0 else jnp.where(low_half, zero, queries)
        scores = dot_nt(keys, own) + bias_ref[head].astype(F32) + mask_ref[...]
        top = jnp.max(scores, axis=0, keepdims=True)
        weights = jnp.exp(scores - top)
        total = jnp.sum(weights, axis=0, keepdims=True)
        part = dot(values_t[head * HD : (head + 1) * HD], weights.astype(BF16)) * (1.0 / total)
        parts.append(part)
        lse_ref[0, head : head + 1, :] = top + jnp.log(total)
    out_ref[...] = jnp.concatenate(parts, axis=0).T.astype(BF16)


def attend(queries, keys, values, bias, ids_query, ids_key):
    rows, width = queries.shape
    length = keys.shape[0]
    pairs = width // (2 * HD)
    return pl.pallas_call(
        attend_kernel,
        name="attend",
        grid=(pairs,),
        in_specs=[
            pl.BlockSpec((rows, 128), lambda p: (0, p)),
            pl.BlockSpec((length, 128), lambda p: (0, p)),
            pl.BlockSpec((length, 128), lambda p: (0, p)),
            pl.BlockSpec((2, length, rows), lambda p: (p, 0, 0)),
            pl.BlockSpec((1, rows), lambda p: (0, 0)),
            pl.BlockSpec((length, 1), lambda p: (0, 0)),
        ],
        out_specs=[
            pl.BlockSpec((rows, 128), lambda p: (0, p)),
            pl.BlockSpec((1, 2, rows), lambda p: (p, 0, 0)),
        ],
        out_shape=[
            jax.ShapeDtypeStruct((rows, width), BF16),
            jax.ShapeDtypeStruct((pairs, 2, rows), F32),
        ],
        scratch_shapes=[pltpu.VMEM((length, rows), F32)],
        compiler_params=params(),
        cost_estimate=cost(pairs * 2 * 4 * rows * length * 128, 6 * rows * length * 2, pairs * 2 * rows * length, scale=EARLY),
    )(queries, keys, values, bias, ids_query, ids_key)


def attend_back_kernel(
    q_ref, k_ref, v_ref, do_ref, bias_ref, lse_ref, idq_ref, idk_ref, dq_ref, dk_ref, dv_ref, rel_ref, mask_ref
):
    @pl.when(pl.program_id(0) == 0)
    def _():
        mask_ref[...] = jnp.where(idk_ref[...] <= idq_ref[...], 0.0, MASKED)

    queries = q_ref[...]
    keys = k_ref[...]
    values = v_ref[...]
    grad_out = do_ref[...]
    keys_t = keys.T
    low_half = lax.broadcasted_iota(jnp.int32, queries.shape, 1) < HD
    zero = jnp.zeros_like(queries)
    dk = None
    dv = None
    dq_parts = []
    for head in range(2):
        own = (lambda a: jnp.where(low_half, a, zero)) if head == 0 else (lambda a: jnp.where(low_half, zero, a))
        q_own = own(queries)
        do_own = own(grad_out)
        scores = dot_nt(keys, q_own) + bias_ref[head].astype(F32) + mask_ref[...]
        probs = jnp.exp(scores - lse_ref[0, head : head + 1, :])
        dprobs = dot_nt(values, do_own)
        delta = jnp.sum(probs * dprobs, axis=0, keepdims=True)
        dscores = probs * (dprobs - delta)
        low = dscores.astype(BF16)
        dv_head = dot(probs.astype(BF16), do_own)
        dk_head = dot(low, q_own)
        dv = dv_head if dv is None else dv + dv_head
        dk = dk_head if dk is None else dk + dk_head
        dq_parts.append(dot(keys_t[head * HD : (head + 1) * HD], low))
        for block in range(4):
            tile = dscores[block * 256 : (block + 1) * 256]
            wide = jnp.concatenate([tile, jnp.zeros_like(tile)], axis=1)
            total = None
            for group in range(32):
                moved = pltpu.roll(wide[group * 8 : group * 8 + 8], 248 - 8 * group, 1)
                total = moved if total is None else total + moved
            row = lax.broadcasted_iota(jnp.int32, total.shape, 0)
            amount = 7 - row
            for bit in (1, 2, 4):
                total = jnp.where((amount & bit) != 0, pltpu.roll(total, bit, 1), total)
            rel_ref[0, head, block : block + 1, :] = jnp.sum(total, axis=0, keepdims=True)
    dq_ref[...] = (jnp.concatenate(dq_parts, axis=0).T * (HD ** (-0.5))).astype(BF16)
    dk_ref[...] = dk.astype(BF16)
    dv_ref[...] = dv.astype(BF16)


def attend_back(queries, keys, values, grad_out, bias, lse, ids_query, ids_key):
    rows, width = queries.shape
    length = keys.shape[0]
    pairs = width // (2 * HD)
    return pl.pallas_call(
        attend_back_kernel,
        name="attend_back",
        grid=(pairs,),
        in_specs=[
            pl.BlockSpec((rows, 128), lambda p: (0, p)),
            pl.BlockSpec((length, 128), lambda p: (0, p)),
            pl.BlockSpec((length, 128), lambda p: (0, p)),
            pl.BlockSpec((rows, 128), lambda p: (0, p)),
            pl.BlockSpec((2, length, rows), lambda p: (p, 0, 0)),
            pl.BlockSpec((1, 2, rows), lambda p: (p, 0, 0)),
            pl.BlockSpec((1, rows), lambda p: (0, 0)),
            pl.BlockSpec((length, 1), lambda p: (0, 0)),
        ],
        out_specs=[
            pl.BlockSpec((rows, 128), lambda p: (0, p)),
            pl.BlockSpec((length, 128), lambda p: (0, p)),
            pl.BlockSpec((length, 128), lambda p: (0, p)),
            pl.BlockSpec((1, 2, 4, 512), lambda p: (p, 0, 0, 0)),
        ],
        out_shape=[
            jax.ShapeDtypeStruct((rows, width), BF16),
            jax.ShapeDtypeStruct((length, width), BF16),
            jax.ShapeDtypeStruct((length, width), BF16),
            jax.ShapeDtypeStruct((pairs, 2, 4, 512), F32),
        ],
        scratch_shapes=[pltpu.VMEM((length, rows), F32)],
        compiler_params=params(),
        cost_estimate=cost(pairs * 2 * 10 * rows * length * 128, 8 * rows * length * 2, pairs * 2 * rows * length),
    )(queries, keys, values, grad_out, bias, lse, ids_query, ids_key)


def one_hot(place, cap):
    groups, rows = place.shape
    slots = lax.broadcasted_iota(jnp.int32, (cap, rows), 0).astype(F32)
    return [slots == place[group : group + 1, :] for group in range(groups)]


def diagonal(cap):
    return lax.broadcasted_iota(jnp.int32, (cap, cap), 0) == lax.broadcasted_iota(jnp.int32, (cap, cap), 1)


def dispatch_kernel(groups, cap, place_ref, rows_ref, out_ref):
    rows = rows_ref[0]
    picks = one_hot(place_ref[0], cap)
    pick = jnp.concatenate([jnp.where(p, 1.0, 0.0).astype(BF16) for p in picks], axis=0)
    out_ref[:, 0] = dot(pick, rows).astype(BF16).reshape(groups, cap, rows.shape[1])


def dispatch(place, rows, cap):
    seqs, groups, stretch = place.shape
    width = rows.shape[2]
    return pl.pallas_call(
        functools.partial(dispatch_kernel, groups, cap),
        name="dispatch_rows",
        grid=(seqs,),
        in_specs=[
            pl.BlockSpec((1, groups, stretch), lambda s: (s, 0, 0)),
            pl.BlockSpec((1, stretch, width), lambda s: (s, 0, 0)),
        ],
        out_specs=pl.BlockSpec((groups, 1, cap, width), lambda s: (0, s, 0, 0)),
        out_shape=jax.ShapeDtypeStruct((groups, seqs, cap, width), BF16),
        compiler_params=params(),
        cost_estimate=cost(seqs * 2 * groups * cap * stretch * width, seqs * 2 * (stretch + groups * cap) * width),
    )(place, rows)


def norm_factor(value):
    return lax.rsqrt(jnp.mean(value * value, axis=-1, keepdims=True) + EPSILON)


def middle_kernel(
    groups, cap, own_ref, other_ref, x_ref, wout_ref, gain_ref, router_ref, hits_ref, place_ref,
    middle_ref, moe_ref, gates_ref, send_ref, slot_gate_ref,
):
    mid = x_ref[...].astype(F32) + (dot(own_ref[...], wout_ref[0]) + dot(other_ref[...], wout_ref[1]))
    middle_ref[...] = mid
    moe_in = (mid * norm_factor(mid) * gain_ref[...].astype(F32)).astype(BF16)
    moe_ref[...] = moe_in
    logits = dot_nt(router_ref[...], moe_in)
    hit = hits_ref[...] > 0.5
    top = jnp.max(jnp.where(hit, logits, MASKED), axis=0, keepdims=True)
    raw = jnp.where(hit, jnp.exp(jnp.where(hit, logits, top) - top), 0.0)
    gates = raw / jnp.sum(raw, axis=0, keepdims=True)
    gates_ref[...] = gates
    picks = one_hot(place_ref[...], cap)
    pick = jnp.concatenate([jnp.where(p, 1.0, 0.0).astype(BF16) for p in picks], axis=0)
    send_ref[...] = dot(pick, moe_in).astype(BF16).reshape(groups, cap, moe_in.shape[1])
    eye = diagonal(cap)
    for group in range(groups):
        column = jnp.sum(jnp.where(picks[group], gates[group : group + 1, :], 0.0), axis=1, keepdims=True)
        slot_gate_ref[group] = jnp.sum(jnp.where(eye, column, 0.0), axis=0, keepdims=True)


def middle_stage(own, other, x, wout, gain, router, hits, place, cap):
    rows, width = x.shape
    experts = router.shape[0]
    groups = place.shape[0]
    return pl.pallas_call(
        functools.partial(middle_kernel, groups, cap),
        name="middle_stage",
        out_shape=[
            jax.ShapeDtypeStruct((rows, width), F32),
            jax.ShapeDtypeStruct((rows, width), BF16),
            jax.ShapeDtypeStruct((experts, rows), F32),
            jax.ShapeDtypeStruct((groups, cap, width), BF16),
            jax.ShapeDtypeStruct((groups, 1, cap), F32),
        ],
        compiler_params=params(),
        cost_estimate=cost(2 * rows * width * width + 2 * groups * cap * rows * width, rows * width * 16, scale=EARLY),
    )(own, other, x, wout, gain, router, hits, place)


def expert_kernel(
    first, final, tiles, groups, cap, x_ref, g_ref, gate_ref, w_ref, *refs
):
    if first:
        acc_in = None
    else:
        acc_in, refs = refs[0], refs[1:]
    part_out, din_out, h_out, acc_out, xt_ref, dy_ref, dyt_ref, part_ref, din_ref = refs
    step = pl.program_id(0)
    rows = groups * cap
    width = x_ref.shape[-1]
    slices = w_ref.shape[0]
    piece = width // slices

    @pl.when(step == 0)
    def _():
        eye = diagonal(cap)
        xt_ref[...] = x_ref[...].reshape(rows, width).T
        for group in range(groups):
            gate = jnp.sum(jnp.where(eye, gate_ref[group], 0.0), axis=1, keepdims=True)
            dy_ref[group * cap : (group + 1) * cap] = (g_ref[group, 0].astype(F32) * gate).astype(BF16)
        dyt_ref[...] = dy_ref[...].T

    x = x_ref[...].reshape(rows, width)
    w_in = w_ref[:, 0, 0].reshape(width, -1)
    w_out_t = w_ref[:, 1, 0].reshape(width, -1)
    dy = dy_ref[...]
    pre = dot(x, w_in)
    square = pre * pre
    inner = jnp.tanh(GELU_C * pre * (1.0 + GELU_A * square))
    half = 0.5 * (1.0 + inner)
    hidden = (pre * half).astype(BF16)
    slope = half + (0.5 * GELU_C) * pre * (1.0 - inner * inner) * (1.0 + (3.0 * GELU_A) * square)
    dhid = dot(dy, w_out_t)
    dpre = (dhid * slope).astype(BF16)
    part = dot_nt(hidden, w_out_t)
    din = dot_nt(dpre, w_in)
    dw_in = dot(xt_ref[...], dpre)
    dw_out_t = dot(dyt_ref[...], hidden)

    @pl.when(step == 0)
    def _():
        part_ref[...] = part
        din_ref[...] = din

    @pl.when(step > 0)
    def _():
        part_ref[...] += part
        din_ref[...] += din

    me = lax.axis_index("ctx")
    for index in range(slices):
        place = index ^ me
        grad_in = dw_in[index * piece : (index + 1) * piece]
        grad_out = dw_out_t[index * piece : (index + 1) * piece]
        if not first:
            grad_in += acc_in[0, place, 0]
            grad_out += acc_in[0, place, 1]
        acc_out[0, place, 0] = grad_in.astype(acc_out.dtype)
        acc_out[0, place, 1] = grad_out.astype(acc_out.dtype)

    @pl.when(step == tiles - 1)
    def _():
        eye = diagonal(cap)
        for group in range(groups):
            gate = jnp.sum(jnp.where(eye, gate_ref[group], 0.0), axis=1, keepdims=True)
            gated = part_ref[group * cap : (group + 1) * cap] * gate
            part_out[group] = gated.astype(BF16)
            din_out[group] = din_ref[group * cap : (group + 1) * cap].astype(BF16)
            h = jnp.sum(gated * g_ref[group, 0].astype(F32), axis=1, keepdims=True)
            h_out[group] = jnp.sum(jnp.where(eye, h, 0.0), axis=0, keepdims=True)


def experts(x, cot_slots, seq_index, gate, weights, acc, final, tile=512):
    groups, cap, width = x.shape
    slices, _, halves, piece, half_len = weights.shape
    per_half = half_len // tile
    tiles = halves * per_half
    rows = groups * cap
    first = acc is None
    acc_spec = pl.BlockSpec((1, slices, 2, piece, tile), lambda f: (f // per_half, 0, 0, 0, f % per_half))
    in_specs = [
        pl.BlockSpec((groups, cap, width), lambda f: (0, 0, 0)),
        pl.BlockSpec((groups, 1, cap, width), lambda f: (0, seq_index, 0, 0)),
        pl.BlockSpec((groups, 1, cap), lambda f: (0, 0, 0)),
        pl.BlockSpec((slices, 2, 1, piece, tile), lambda f: (0, 0, f // per_half, 0, f % per_half)),
    ]
    args = [x, cot_slots, gate, weights]
    aliases = {}
    if not first:
        in_specs.append(acc_spec)
        args.append(acc)
        if not final:
            aliases = {4: 3}
    acc_shape = (halves, slices, 2, piece, half_len)
    return pl.pallas_call(
        functools.partial(expert_kernel, first, final, tiles, groups, cap),
        name="experts",
        grid=(tiles,),
        in_specs=in_specs,
        out_specs=[
            pl.BlockSpec((groups, cap, width), lambda f: (0, 0, 0)),
            pl.BlockSpec((groups, cap, width), lambda f: (0, 0, 0)),
            pl.BlockSpec((groups, 1, cap), lambda f: (0, 0, 0)),
            acc_spec,
        ],
        out_shape=[
            jax.ShapeDtypeStruct((groups, cap, width), BF16),
            jax.ShapeDtypeStruct((groups, cap, width), BF16),
            jax.ShapeDtypeStruct((groups, 1, cap), F32),
            jax.ShapeDtypeStruct(acc_shape, BF16 if final else F32),
        ],
        scratch_shapes=[
            pltpu.VMEM((width, rows), BF16),
            pltpu.VMEM((rows, width), BF16),
            pltpu.VMEM((width, rows), BF16),
            pltpu.VMEM((rows, width), F32),
            pltpu.VMEM((rows, width), F32),
        ],
        input_output_aliases=aliases,
        compiler_params=params(),
        cost_estimate=cost(12 * rows * width * halves * half_len, 2 * width * halves * half_len * 10, rows * halves * half_len),
    )(*args)


def combine_kernel(groups, cap, place_ref, din_ref, h_ref, din_out, h_out):
    picks = one_hot(place_ref[...], cap)
    pick = jnp.concatenate([jnp.where(p, 1.0, 0.0).astype(BF16) for p in picks], axis=0)
    rows = groups * cap
    din_out[...] = dot_tn(pick, din_ref[...].reshape(rows, din_ref.shape[-1])).astype(BF16)
    eye = diagonal(cap)
    for group in range(groups):
        column = jnp.sum(jnp.where(eye, h_ref[group], 0.0), axis=1, keepdims=True)
        h_out[group : group + 1, :] = jnp.sum(jnp.where(picks[group], column, 0.0), axis=0, keepdims=True)


def combine(place, din, h, cap):
    groups, stretch = place.shape
    width = din.shape[-1]
    return pl.pallas_call(
        functools.partial(combine_kernel, groups, cap),
        name="combine_back",
        out_shape=[
            jax.ShapeDtypeStruct((stretch, width), BF16),
            jax.ShapeDtypeStruct((groups, stretch), F32),
        ],
        compiler_params=params(),
        cost_estimate=cost(2 * groups * cap * stretch * width, 4 * stretch * width * 2),
    )(place, din, h)


def combine_out_kernel(groups, cap, place_ref, part_ref, out_ref):
    picks = one_hot(place_ref[...], cap)
    pick = jnp.concatenate([jnp.where(p, 1.0, 0.0).astype(BF16) for p in picks], axis=0)
    out_ref[...] = dot_tn(pick, part_ref[...].reshape(groups * cap, part_ref.shape[-1])).astype(BF16)


def combine_out(place, part, cap):
    groups, stretch = place.shape
    width = part.shape[-1]
    return pl.pallas_call(
        functools.partial(combine_out_kernel, groups, cap),
        name="combine_out",
        out_shape=jax.ShapeDtypeStruct((stretch, width), BF16),
        compiler_params=params(),
        cost_estimate=cost(2 * groups * cap * stretch * width, 4 * stretch * width * 2),
    )(place, part)


def middle_back_kernel(
    own_ref, other_ref, h_ref, gates_ref, router_ref, moe_ref, mid_ref, gain_ref, cot_ref, wout_ref,
    gmid_ref, datt_ref, gain_grad_ref, router_grad_ref, low_ref,
):
    h = h_ref[...]
    dlogits = h - gates_ref[...] * jnp.sum(h, axis=0, keepdims=True)
    router = router_ref[...]
    dmoe = own_ref[...].astype(F32) + other_ref[...].astype(F32)
    dmoe = dmoe + lax.dot_general(
        dlogits, router.astype(F32), (((0,), (0,)), ((), ())), precision=FULL_PRECISION, preferred_element_type=F32
    )
    router_grad_ref[...] = lax.dot_general(
        dlogits, moe_ref[...].astype(F32), (((1,), (0,)), ((), ())), precision=FULL_PRECISION, preferred_element_type=F32
    )
    mid = mid_ref[...]
    gain = gain_ref[...].astype(F32)
    factor = norm_factor(mid)
    normed = mid * factor
    gain_grad_ref[...] = jnp.sum(dmoe * normed, axis=0, keepdims=True)
    scaled = dmoe * gain
    dmid = factor * (scaled - normed * jnp.mean(scaled * normed, axis=-1, keepdims=True))
    gmid = cot_ref[...].astype(F32) + dmid
    gmid_ref[...] = gmid
    dattn = gmid.astype(BF16)
    datt_ref[...] = dot_nt(dattn, wout_ref[...]).astype(BF16)
    low_ref[...] = dattn


def middle_back(own, other, h, gates, router, moe_in, mid, gain, cot, wout):
    rows, width = mid.shape
    local = wout.shape[0]
    return pl.pallas_call(
        middle_back_kernel,
        name="middle_back",
        out_shape=[
            jax.ShapeDtypeStruct((rows, width), F32),
            jax.ShapeDtypeStruct((rows, local), BF16),
            jax.ShapeDtypeStruct((1, width), F32),
            jax.ShapeDtypeStruct(router.shape, F32),
            jax.ShapeDtypeStruct((rows, width), BF16),
        ],
        compiler_params=params(),
        cost_estimate=cost(2 * rows * width * local, 30 * rows * width),
    )(own, other, h, gates, router, moe_in, mid, gain, cot, wout)


MESH_ID = pl.DeviceIdType.MESH


def remote(src, dst, send_sem, recv_sem, **where):
    return pltpu.make_async_remote_copy(
        src_ref=src, dst_ref=dst, send_sem=send_sem, recv_sem=recv_sem, device_id=where, device_id_type=MESH_ID
    )


def greet(peers):
    barrier = pltpu.get_barrier_semaphore()
    for where in peers:
        pl.semaphore_signal(barrier, inc=1, device_id=where, device_id_type=MESH_ID)
    pl.semaphore_wait(barrier, len(peers))


def first_kernel(
    seqs, tok_ref, wqkv_ref, wout_ref, table_ref, ga_ref, gm_ref, router_ref, pair_ref,
    q_ref, k_ref, v_ref, normed_ref, wqkv_out, wout_out, table_out, gain_ref, gm_out, router_out, got_out, far_out,
    tok_all, n_all, ga_all, gm_all, router_all,
    z_send, z_recv, f_send, f_recv, t_send, t_recv, y_send, y_recv, l_sem, e_sems,
):
    dp = lax.axis_index("dp")
    ctx = lax.axis_index("ctx")
    tp = lax.axis_index("tp")
    core = ctx % 2
    rows = wqkv_ref.shape[1]
    half = rows // 2
    orows = wout_ref.shape[0] // 2
    greet([{"dp": dp ^ b} for b in (1, 2, 3)] + [{"ctx": ctx ^ 1}, {"ctx": ctx ^ 2}, {"tp": tp ^ 1}])

    def w_rows(owner, side):
        return pl.ds(pl.multiple_of(owner * rows + side * half, 16), half)

    def o_rows(side):
        return pl.ds(pl.multiple_of(side * orows, 16), orows)

    def z_copies(b):
        to = {"dp": dp ^ b}
        return [
            remote(ga_ref, ga_all.at[dp], z_send.at[0, b - 1], z_recv.at[0, b - 1], **to),
            remote(gm_ref, gm_all.at[dp], z_send.at[1, b - 1], z_recv.at[1, b - 1], **to),
            remote(table_ref, table_out.at[dp], z_send.at[2, b - 1], z_recv.at[2, b - 1], **to),
            remote(router_ref, router_all.at[dp], z_send.at[3, b - 1], z_recv.at[3, b - 1], **to),
            remote(
                wqkv_ref.at[:, pl.ds(pl.multiple_of(core * half, 16), half)], wqkv_out.at[:, w_rows(dp, core)],
                z_send.at[4, b - 1], z_recv.at[4, b - 1], **to,
            ),
            remote(
                wout_ref.at[o_rows(core)], wout_out.at[dp, o_rows(core)],
                z_send.at[5, b - 1], z_recv.at[5, b - 1], **to,
            ),
        ]

    small = [z_copies(b) for b in (1, 2, 3)]
    for kind in range(6):
        for b in (3, 2, 1):
            small[b - 1][kind].start()
    beside = remote(tok_ref, tok_all.at[1], t_send.at[0], t_recv.at[0], ctx=ctx ^ 1)
    beside.start()
    across = [remote(tok_ref.at[s], tok_all.at[2, s], y_send.at[s], y_recv.at[s], ctx=ctx ^ 2) for s in range(seqs)]
    expert_copies = [
        remote(pair_ref.at[1 - tp], got_out, e_sems.at[0, 0], e_sems.at[1, 0], tp=tp ^ 1),
        remote(pair_ref.at[tp], far_out, e_sems.at[0, 1], e_sems.at[1, 1], ctx=ctx ^ 2),
    ]
    for copy in across + expert_copies:
        copy.start()
    own = [
        pltpu.make_async_copy(tok_ref, tok_all.at[0], l_sem.at[0]),
        pltpu.make_async_copy(ga_ref, ga_all.at[dp], l_sem.at[1]),
        pltpu.make_async_copy(gm_ref, gm_all.at[dp], l_sem.at[2]),
        pltpu.make_async_copy(table_ref, table_out.at[dp], l_sem.at[3]),
        pltpu.make_async_copy(router_ref, router_all.at[dp], l_sem.at[4]),
        pltpu.make_async_copy(wqkv_ref, wqkv_out.at[:, pl.ds(pl.multiple_of(dp * rows, 16), rows)], l_sem.at[5]),
        pltpu.make_async_copy(wout_ref, wout_out.at[dp], l_sem.at[6]),
    ]
    for copy in own:
        copy.start()
    for copy in own:
        copy.wait()

    for kind in range(4):
        for b in (3, 2, 1):
            small[b - 1][kind].wait_recv()
    count = ga_all.shape[0]
    piece = ga_all.shape[2]
    width = count * piece
    row = lax.broadcasted_iota(jnp.int32, (piece, width), 0)
    col = lax.broadcasted_iota(jnp.int32, (piece, width), 1)
    gain = 0.0
    gain_m = 0.0
    for d in range(count):
        spread = jnp.where(col == row + d * piece, 1.0, 0.0).astype(BF16)
        gain = gain + dot(ga_all[d], spread)
        gain_m = gain_m + dot(gm_all[d], spread)
    gain_ref[...] = gain
    gm_out[...] = gain_m.astype(BF16)
    experts_n = router_ref.shape[1]
    slot_row = lax.broadcasted_iota(jnp.int32, (experts_n, experts_n), 0)
    slot_col = lax.broadcasted_iota(jnp.int32, (experts_n, experts_n), 1)
    side = slot_row // count
    expert = (slot_row % count) * 2 + (side ^ tp)
    order = jnp.where(slot_col == expert, 1.0, 0.0).astype(BF16)
    router_out[...] = dot_nt(order, router_all[...].reshape(width, experts_n)).astype(BF16)

    def norm_piece(b):
        def body(s, carry):
            value = tok_all[b, s].astype(F32)
            out = (value * norm_factor(value) * gain_ref[...]).astype(BF16)
            n_all[b, s] = out
            return carry

        lax.fori_loop(0, seqs, body, 0)

    def project(b, s):
        x = n_all[b, s]
        k_ref[s, b] = dot(x, wqkv_out[1]).astype(BF16)
        v_ref[s, b] = dot(x, wqkv_out[2]).astype(BF16)

    norm_piece(0)
    normed_ref[...] = n_all[0]
    beside.wait_recv()
    norm_piece(1)

    forwards = []
    for b in (1, 2, 3):
        for kind, f in ((4, 0), (5, 1)):
            small[b - 1][kind].wait_recv()
            if f == 0:
                ref = wqkv_out.at[:, w_rows(dp ^ b, core)]
            else:
                ref = wout_out.at[dp ^ b, o_rows(core)]
            copy = remote(ref, ref, f_send.at[f, b - 1], f_recv.at[f, b - 1], ctx=ctx ^ 1)
            copy.start()
            forwards.append(copy)
    for copy in forwards:
        copy.wait_recv()

    def own_q(s, carry):
        q_ref[s] = (dot(n_all[0, s], wqkv_out[0]).astype(BF16) * (HD ** (-0.5))).astype(BF16)
        project(0, s)
        project(1, s)
        return carry

    lax.fori_loop(0, seqs, own_q, 0)
    later = []
    for s in range(seqs):
        across[s].wait_recv()
        copy = remote(tok_all.at[2, s], tok_all.at[3, s], t_send.at[1 + s], t_recv.at[1 + s], ctx=ctx ^ 1)
        copy.start()
        later.append(copy)
    norm_piece(2)
    for copy in later:
        copy.wait_recv()
    norm_piece(3)

    def others(s, carry):
        project(2, s)
        project(3, s)
        return carry

    lax.fori_loop(0, seqs, others, 0)
    for copy in expert_copies:
        copy.wait()
    for group in small:
        for copy in group:
            copy.wait_send()
    for copy in forwards + later + across + [beside]:
        copy.wait_send()


def first_stage(tokens, wqkv, wout, table, gain_attn, gain_moe, router, expert_pair):
    seqs, stretch, width = tokens.shape
    count, rows, local = wqkv.shape
    dp = width // rows
    experts_n = router.shape[1]
    any_spec = pl.BlockSpec(memory_space=pl.ANY)
    vmem = pl.BlockSpec(memory_space=pltpu.VMEM)
    dma = pltpu.SemaphoreType.DMA
    return pl.pallas_call(
        functools.partial(first_kernel, seqs),
        name="first_stage",
        in_specs=[any_spec] * 8,
        out_specs=[vmem] * 10 + [any_spec] * 2,
        out_shape=[
            jax.ShapeDtypeStruct((seqs, stretch, local), BF16),
            jax.ShapeDtypeStruct((seqs, 4, stretch, local), BF16),
            jax.ShapeDtypeStruct((seqs, 4, stretch, local), BF16),
            jax.ShapeDtypeStruct((seqs, stretch, width), BF16),
            jax.ShapeDtypeStruct((3, width, local), BF16),
            jax.ShapeDtypeStruct((dp,) + wout.shape, BF16),
            jax.ShapeDtypeStruct((dp,) + table.shape, BF16),
            jax.ShapeDtypeStruct((1, width), F32),
            jax.ShapeDtypeStruct((1, width), BF16),
            jax.ShapeDtypeStruct((experts_n, width), BF16),
            jax.ShapeDtypeStruct(expert_pair.shape[1:], BF16),
            jax.ShapeDtypeStruct(expert_pair.shape[1:], BF16),
        ],
        scratch_shapes=[
            pltpu.VMEM((4, seqs, stretch, width), BF16),
            pltpu.VMEM((4, seqs, stretch, width), BF16),
            pltpu.VMEM((dp, 1, rows), BF16),
            pltpu.VMEM((dp, 1, rows), BF16),
            pltpu.VMEM((dp, rows, experts_n), BF16),
            dma((6, 3)), dma((6, 3)), dma((2, 3)), dma((2, 3)), dma((1 + seqs,)), dma((1 + seqs,)),
            dma((seqs,)), dma((seqs,)), dma((7,)), dma((2, 2)),
        ],
        compiler_params=pltpu.CompilerParams(vmem_limit_bytes=VMEM_BYTES, collective_id=0, has_side_effects=True),
        cost_estimate=cost(40 * 10**9, 10**7),
    )(tokens, wqkv, wout, table, gain_attn, gain_moe, router, expert_pair)


def back_kernel(seqs, groups, cap, *refs):
    mid_refs, moe_refs, gate_refs, lse_refs = (refs[i * seqs : (i + 1) * seqs] for i in range(4))
    refs = refs[4 * seqs :]
    din_ref, part_ref, q_ref, k_ref, v_ref, bias_ref, cot_ref, wout_ref = refs[:8]
    h_ref, place_ref, near_ref, idq_ref, idk_ref, router_ref, gain_ref = refs[8:15]
    out_ref, gmid_ref, low_ref, proj_ref, gain_grad_ref, router_grad_ref, rel_ref = refs[15:22]
    (
        mid_v, moe_v, gate_v, lse_v, din_v, part_v, q_v, k_v, v_v, bias_v, cot_v, wout_v,
        din_own, din_other, h_own, h_other, out_own, out_other, datt_v, mask_v, keep_v, give_v, core_v, y_v, far_v,
        load_sems, seq_sems, part_sems, x_sems, c_sems, y_sems,
    ) = refs[22:]
    dp = lax.axis_index("dp")
    ctx = lax.axis_index("ctx")
    tp = lax.axis_index("tp")
    greet([{"dp": dp ^ b} for b in range(1, groups)] + [{"ctx": ctx ^ 1}, {"ctx": ctx ^ 2}, {"tp": tp ^ 1}])
    rows = groups * cap
    stretch, width = mid_v.shape[1:]
    local = q_v.shape[2]
    pairs = local // (2 * HD)

    def part_copy(s, b):
        return remote(part_ref.at[b, s], part_v.at[b, s], part_sems.at[0, s, b], part_sems.at[1, s, b], dp=dp ^ b)

    for s in range(seqs):
        for b in range(groups - 1, 0, -1):
            part_copy(s, b).start()
    din_load = pltpu.make_async_copy(din_ref, din_v, load_sems.at[0])
    loads = [
        pltpu.make_async_copy(src, dst, load_sems.at[i + 1])
        for i, (src, dst) in enumerate(
            ((wout_ref, wout_v), (cot_ref, cot_v), (q_ref, q_v), (k_ref, k_v), (v_ref, v_v), (bias_ref, bias_v),
             (part_ref.at[0], part_v.at[0]))
        )
    ]
    for s in range(seqs):
        for i, (src, dst) in enumerate(((mid_refs, mid_v), (moe_refs, moe_v), (gate_refs, gate_v), (lse_refs, lse_v))):
            loads.append(pltpu.make_async_copy(src[s], dst.at[s], seq_sems.at[s, i]))
    din_load.start()
    for copy in loads:
        copy.start()
    gain_grad_ref[...] = jnp.zeros_like(gain_grad_ref)
    router_grad_ref[...] = jnp.zeros_like(router_grad_ref)
    rel_ref[...] = jnp.zeros_like(rel_ref)

    def din_copy(s):
        return remote(din_own.at[s], din_other.at[s], x_sems.at[0, 0, s], x_sems.at[1, 0, s], tp=tp ^ 1)

    def h_copy(s):
        return remote(h_own.at[s], h_other.at[s], x_sems.at[0, 1, s], x_sems.at[1, 1, s], tp=tp ^ 1)

    def out_copy(s):
        return remote(out_own.at[s], out_other.at[s], x_sems.at[0, 2, s], x_sems.at[1, 2, s], tp=tp ^ 1)

    def core_copy(s):
        return remote(give_v.at[s], core_v.at[s], c_sems.at[0, s], c_sems.at[1, s], ctx=ctx ^ 1)

    def y_copy(s):
        return remote(y_v.at[s], far_v.at[s], y_sems.at[0, s], y_sems.at[1, s], ctx=ctx ^ 2)

    def chosen(place):
        picks = one_hot(place, cap)
        return picks, jnp.concatenate([jnp.where(p, 1.0, 0.0).astype(BF16) for p in picks], axis=0)

    din_load.wait()

    def gather_back(s, carry):
        picks, pick = chosen(place_ref[s])
        din_own[s] = dot_tn(pick, din_v[s].reshape(rows, width)).astype(BF16)
        eye = diagonal(cap)
        for group in range(groups):
            column = jnp.sum(jnp.where(eye, h_ref[s, group], 0.0), axis=1, keepdims=True)
            h_own[s, group : group + 1, :] = jnp.sum(jnp.where(picks[group], column, 0.0), axis=0, keepdims=True)
        h_copy(s).start()
        din_copy(s).start()
        return carry

    lax.fori_loop(0, seqs, gather_back, 0)
    for copy in loads:
        copy.wait()

    def middle_back(s):
        h = jnp.concatenate([h_own[s], h_other[s]], axis=0)
        dlogits = h - gate_v[s] * jnp.sum(h, axis=0, keepdims=True)
        dmoe = din_own[s].astype(F32) + din_other[s].astype(F32)
        dmoe = dmoe + lax.dot_general(
            dlogits, router_ref[...].astype(F32), (((0,), (0,)), ((), ())),
            precision=FULL_PRECISION, preferred_element_type=F32,
        )
        router_grad_ref[...] += lax.dot_general(
            dlogits, moe_v[s].astype(F32), (((1,), (0,)), ((), ())),
            precision=FULL_PRECISION, preferred_element_type=F32,
        )
        mid = mid_v[s]
        factor = norm_factor(mid)
        normed = mid * factor
        gain_grad_ref[...] += jnp.sum(dmoe * normed, axis=0, keepdims=True)
        scaled = dmoe * gain_ref[...].astype(F32)
        dmid = factor * (scaled - normed * jnp.mean(scaled * normed, axis=-1, keepdims=True))
        gmid = cot_v[s].astype(F32) + dmid
        gmid_ref[s] = gmid
        dattn = gmid.astype(BF16)
        low_ref[s] = dattn
        datt_v[...] = dot_nt(dattn, wout_v[...]).astype(BF16)

    def core_sum(s):
        core_copy(s).wait_recv()
        for kind in range(2):
            keep_v[s, kind, 0] += core_v[s, kind, 0].astype(F32)
            y_v[s, kind] = (keep_v[s, kind, 1] + core_v[s, kind, 1].astype(F32)).astype(BF16)
        y_copy(s).start()

    def out_sum(s):
        for b in range(1, groups):
            part_copy(s, b).wait_recv()
        pick = chosen(near_ref[s])[1]
        out_own[s] = dot_tn(pick, part_v[:, s].reshape(rows, width)).astype(BF16)
        out_copy(s).start()

    def attention_back(s):
        mask_v[...] = jnp.where(idk_ref[s] <= idq_ref[s], 0.0, MASKED)

        def pair(p, carry):
            lanes = pl.ds(pl.multiple_of(p * 2 * HD, 2 * HD), 2 * HD)
            queries = q_v[s, :, lanes]
            keys = k_v[s, :, lanes]
            values = v_v[s, :, lanes]
            grad_out = datt_v[:, lanes]
            keys_t = keys.T
            low_half = lax.broadcasted_iota(jnp.int32, queries.shape, 1) < HD
            zero = jnp.zeros_like(queries)
            dk = None
            dv = None
            dq_parts = []
            for head in range(2):
                own = (lambda a: jnp.where(low_half, a, zero)) if head == 0 else (
                    lambda a: jnp.where(low_half, zero, a)
                )
                q_own = own(queries)
                do_own = own(grad_out)
                scores = dot_nt(keys, q_own) + bias_v[2 * p + head].astype(F32) + mask_v[...]
                probs = jnp.exp(scores - lse_v[s, p, head : head + 1, :])
                dprobs = dot_nt(values, do_own)
                delta = jnp.sum(probs * dprobs, axis=0, keepdims=True)
                dscores = probs * (dprobs - delta)
                low = dscores.astype(BF16)
                dv_head = dot(probs.astype(BF16), do_own)
                dk_head = dot(low, q_own)
                dv = dv_head if dv is None else dv + dv_head
                dk = dk_head if dk is None else dk + dk_head
                dq_parts.append(dot(keys_t[head * HD : (head + 1) * HD], low))
                for block in range(4):
                    tile = dscores[block * 256 : (block + 1) * 256]
                    wide = jnp.concatenate([tile, jnp.zeros_like(tile)], axis=1)
                    total = None
                    for group in range(32):
                        moved = pltpu.roll(wide[group * 8 : group * 8 + 8], 248 - 8 * group, 1)
                        total = moved if total is None else total + moved
                    row = lax.broadcasted_iota(jnp.int32, total.shape, 0)
                    amount = 7 - row
                    for bit in (1, 2, 4):
                        total = jnp.where((amount & bit) != 0, pltpu.roll(total, bit, 1), total)
                    rel_ref[p, head, block : block + 1, :] += jnp.sum(total, axis=0, keepdims=True)
            proj_ref[0, s, :, lanes] = (jnp.concatenate(dq_parts, axis=0).T * (HD ** (-0.5))).astype(BF16)
            for kind, value in enumerate((dk, dv)):
                for index in range(2):
                    at = 2 * index * stretch
                    keep_v[s, kind, index, :, lanes] = value[at : at + stretch]
                    give_v[s, kind, index, :, lanes] = value[at + stretch : at + 2 * stretch].astype(BF16)
            return carry

        lax.fori_loop(0, pairs, pair, 0)
        core_copy(s).start()

    def main(s, carry):
        h_copy(s).wait_recv()
        din_copy(s).wait_recv()
        middle_back(s)
        attention_back(s)

        @pl.when(s > 0)
        def _():
            core_sum(s - 1)
            out_sum(s - 1)

        return carry

    lax.fori_loop(0, seqs, main, 0)
    core_sum(seqs - 1)
    out_sum(seqs - 1)

    def finish_keys(s, carry):
        y_copy(s).wait_recv()
        for kind in range(2):
            proj_ref[1 + kind, s] = (keep_v[s, kind, 0] + far_v[s, kind].astype(F32)).astype(BF16)
        return carry

    def finish_out(s, carry):
        out_copy(s).wait_recv()
        out_ref[s] = (mid_v[s] + (out_own[s].astype(F32) + out_other[s].astype(F32))).astype(BF16)
        return carry

    lax.fori_loop(0, seqs, finish_keys, 0)
    lax.fori_loop(0, seqs, finish_out, 0)
    for s in range(seqs):
        for b in range(1, groups):
            part_copy(s, b).wait_send()
        for copy in (h_copy(s), din_copy(s), out_copy(s), core_copy(s), y_copy(s)):
            copy.wait_send()


def back_stage(mids, moes, gates, lse, din, parts, q, k, v, bias, cot, wout, h, places, near, ids_query, ids_key, router, gain):
    seqs = len(mids)
    groups, _, cap, width = parts.shape
    stretch = mids[0].shape[0]
    local = wout.shape[0]
    length = k.shape[1]
    pairs = local // (2 * HD)
    experts_n = router.shape[0]
    any_spec = pl.BlockSpec(memory_space=pl.ANY)
    vmem = pl.BlockSpec(memory_space=pltpu.VMEM)
    dma = pltpu.SemaphoreType.DMA
    return pl.pallas_call(
        functools.partial(back_kernel, seqs, groups, cap),
        name="back_stage",
        in_specs=[any_spec] * (4 * seqs + 8) + [vmem] * 7,
        out_specs=[vmem] * 7,
        out_shape=[
            jax.ShapeDtypeStruct((seqs, stretch, width), BF16),
            jax.ShapeDtypeStruct((seqs, stretch, width), F32),
            jax.ShapeDtypeStruct((seqs, stretch, width), BF16),
            jax.ShapeDtypeStruct((3, seqs, stretch, local), BF16),
            jax.ShapeDtypeStruct((1, width), F32),
            jax.ShapeDtypeStruct((experts_n, width), F32),
            jax.ShapeDtypeStruct((pairs, 2, 4, 2 * stretch), F32),
        ],
        scratch_shapes=[
            pltpu.VMEM((seqs, stretch, width), F32),
            pltpu.VMEM((seqs, stretch, width), BF16),
            pltpu.VMEM((seqs, experts_n, stretch), F32),
            pltpu.VMEM((seqs, pairs, 2, stretch), F32),
            pltpu.VMEM((seqs, groups, cap, width), BF16),
            pltpu.VMEM((groups, seqs, cap, width), BF16),
            pltpu.VMEM((seqs, stretch, local), BF16),
            pltpu.VMEM((seqs, length, local), BF16),
            pltpu.VMEM((seqs, length, local), BF16),
            pltpu.VMEM((2 * pairs, length, stretch), BF16),
            pltpu.VMEM((seqs, stretch, width), BF16),
            pltpu.VMEM((local, width), BF16),
            pltpu.VMEM((seqs, stretch, width), BF16),
            pltpu.VMEM((seqs, stretch, width), BF16),
            pltpu.VMEM((seqs, groups, stretch), F32),
            pltpu.VMEM((seqs, groups, stretch), F32),
            pltpu.VMEM((seqs, stretch, width), BF16),
            pltpu.VMEM((seqs, stretch, width), BF16),
            pltpu.VMEM((stretch, local), BF16),
            pltpu.VMEM((length, stretch), F32),
            pltpu.VMEM((seqs, 2, 2, stretch, local), F32),
            pltpu.VMEM((seqs, 2, 2, stretch, local), BF16),
            pltpu.VMEM((seqs, 2, 2, stretch, local), BF16),
            pltpu.VMEM((seqs, 2, stretch, local), BF16),
            pltpu.VMEM((seqs, 2, stretch, local), BF16),
            dma((8,)), dma((seqs, 4)), dma((2, seqs, groups)), dma((2, 3, seqs)), dma((2, seqs)), dma((2, seqs)),
        ],
        compiler_params=pltpu.CompilerParams(
            vmem_limit_bytes=63 * 1024 * 1024, collective_id=3, has_side_effects=True
        ),
        cost_estimate=cost(6 * 10**10, 10**7),
    )(*mids, *moes, *gates, *lse, din, parts, q, k, v, bias, cot, wout, h, places, near, ids_query, ids_key, router, gain)


def last_kernel(
    normed_ref, proj_ref, datt_ref, att_ref, small_ref, wqkv_ref, gmid_ref, x_ref, gain_ref,
    out_ref, router_out, gm_out, ga_out, table_out, gx_ref,
    dn_own, dn_other, ga_own, dn_sems, grads, core_send, core_got, y_out, y_got, z_out, z_got, wide, s_own, s_core, s_y, s_x, s_z,
    c_sems, y_sems, z_sems, w_sems, s_sems,
):
    dp = lax.axis_index("dp")
    ctx = lax.axis_index("ctx")
    tp = lax.axis_index("tp")
    core = ctx % 2
    far = ctx // 2
    greet([{"dp": dp ^ b} for b in (1, 2, 3)] + [{"ctx": ctx ^ b} for b in (1, 2, 3)] + [{"tp": tp ^ 1}])
    count = z_got.shape[0] + 1
    width = normed_ref.shape[1]
    piece = width // count

    seqs, stretch = x_ref.shape[:2]

    def unit_of(s):
        value = x_ref[s].astype(F32)
        factor = norm_factor(value)
        return factor, value * factor

    def rows_of(s):
        return pl.ds(pl.multiple_of(s * stretch, stretch), stretch)

    def input_grad(s, total):
        part = dot_nt(proj_ref[0, rows_of(s)], wqkv_ref[0])
        part = part + dot_nt(proj_ref[1, rows_of(s)], wqkv_ref[1])
        part = part + dot_nt(proj_ref[2, rows_of(s)], wqkv_ref[2])
        dn_own[s] = part.astype(BF16)
        return total + jnp.sum(part * unit_of(s)[1], axis=0, keepdims=True)

    own_gain = lax.fori_loop(0, seqs, input_grad, jnp.zeros((1, width), F32))
    lines = lax.broadcasted_iota(jnp.int32, small_ref.shape, 0)
    ga_own[...] = small_ref[...] + jnp.where(lines == 9, own_gain, 0.0)
    x_copy = remote(ga_own, s_x, s_sems.at[0, 0], s_sems.at[1, 0], tp=tp ^ 1)
    x_copy.start()
    dn_copies = [
        remote(dn_own.at[s], dn_other.at[s], dn_sems.at[0, s], dn_sems.at[1, s], tp=tp ^ 1) for s in range(seqs)
    ]
    for copy in dn_copies:
        copy.start()
    normed_t = normed_ref[...].T
    for j in range(3):
        grads[j] = dot(normed_t, proj_ref[j])
    grads[3] = dot_tn(datt_ref[...], att_ref[...])
    give = 1 - core
    core_send[0] = grads[2 * give].astype(BF16)
    core_send[1] = grads[2 * give + 1].astype(BF16)
    c_copy = remote(core_send, core_got, c_sems.at[0], c_sems.at[1], ctx=ctx ^ 1)
    c_copy.start()
    x_copy.wait_recv()
    s_own[...] = ga_own[...] + jnp.where(lines == 9, s_x[...], 0.0)
    sc_copy = remote(s_own, s_core, s_sems.at[0, 1], s_sems.at[1, 1], ctx=ctx ^ 1)
    sc_copy.start()
    c_copy.wait_recv()
    grads[2 * core] += core_got[0].astype(F32)
    grads[2 * core + 1] += core_got[1].astype(F32)
    y_out[...] = grads[2 * core + 1 - far].astype(BF16)
    order = (3, 2, 1, 0)
    y_copies = []
    for b in order:
        at = pl.ds(pl.multiple_of((dp ^ b) * piece, 16), piece)
        copy = remote(y_out.at[at], y_got.at[b], y_sems.at[0, b], y_sems.at[1, b], ctx=ctx ^ 2)
        copy.start()
        y_copies.append(copy)
    sc_copy.wait_recv()
    y_small = s_own[...] + s_core[...]
    s_y[0] = y_small
    sy_copy = remote(s_y.at[0], s_y.at[1], s_sems.at[0, 2], s_sems.at[1, 2], ctx=ctx ^ 2)
    sy_copy.start()
    mine = 2 * core + far
    z_copies = []
    total = None
    for copy, b in zip(y_copies, order):
        copy.wait_recv()
        at = pl.ds(pl.multiple_of((dp ^ b) * piece, 16), piece)
        value = grads[mine, at] + y_got[b].astype(F32)
        if b:
            z_out[b - 1] = value.astype(BF16)
            z_copy = remote(z_out.at[b - 1], z_got.at[b - 1], z_sems.at[0, b - 1], z_sems.at[1, b - 1], dp=dp ^ b)
            z_copy.start()
            z_copies.append((b, z_copy))
        else:
            total = value
    sy_copy.wait_recv()
    s_z[dp] = s_y[0] + s_y[1]
    sz_copies = []
    for b in (3, 2, 1):
        copy = remote(s_z.at[dp], s_z.at[dp], s_sems.at[0, 2 + b], s_sems.at[1, 2 + b], dp=dp ^ b)
        copy.start()
        sz_copies.append(copy)
    for b, copy in z_copies:
        copy.wait_recv()
        total = total + z_got[b - 1].astype(F32)
    wide[mine] = total.astype(BF16)
    w_copies = []
    for b in (3, 2, 1):
        copy = remote(wide.at[mine], wide.at[mine], w_sems.at[0, b - 1], w_sems.at[1, b - 1], ctx=ctx ^ b)
        copy.start()
        w_copies.append(copy)
    for copy in dn_copies:
        copy.wait_recv()

    def input_norm(s, carry):
        factor, unit = unit_of(s)
        scaled = (dn_own[s].astype(F32) + dn_other[s].astype(F32)) * gain_ref[...]
        dres = factor * (scaled - unit * jnp.mean(scaled * unit, axis=-1, keepdims=True))
        gx_ref[s] = gmid_ref[s] + dres
        return carry

    lax.fori_loop(0, seqs, input_norm, 0)
    for copy in sz_copies:
        copy.wait_recv()
    small = s_z[0]
    for d in range(1, count):
        small = small + s_z[d]

    def exact(a, b, dims):
        return lax.dot_general(a, b, (dims, ((), ())), precision=FULL_PRECISION, preferred_element_type=F32)

    row = lax.broadcasted_iota(jnp.int32, (piece, width), 0)
    col = lax.broadcasted_iota(jnp.int32, (piece, width), 1)
    select = jnp.where(col == row + dp * piece, 1.0, 0.0)
    experts_n = router_out.shape[1]
    e_row = lax.broadcasted_iota(jnp.int32, (experts_n, experts_n), 0)
    e_col = lax.broadcasted_iota(jnp.int32, (experts_n, experts_n), 1)
    slot = ((e_row % 2) ^ tp) * count + e_row // 2
    arranged = exact(jnp.where(e_col == slot, 1.0, 0.0), small[:experts_n], ((1,), (0,)))
    router_out[...] = exact(select, arranged, ((1,), (1,)))
    gains = exact(small[8:16], select, ((1,), (1,)))
    gm_out[...] = gains[0:1]
    ga_out[...] = gains[1:2]
    t_rows, heads = table_out.shape
    t_row = lax.broadcasted_iota(jnp.int32, (t_rows, width), 0)
    t_col = lax.broadcasted_iota(jnp.int32, (t_rows, width), 1)
    table_out[...] = exact(jnp.where(t_col == t_row + dp * t_rows, 1.0, 0.0), small[16:24], ((1,), (1,)))[:, :heads]
    for copy in w_copies:
        copy.wait_recv()
    out_ref[...] = wide[...].astype(F32)
    for copy in [x_copy, c_copy, sc_copy, sy_copy] + dn_copies + y_copies + [c for _, c in z_copies] + sz_copies + w_copies:
        copy.wait_send()


def last_stage(normed, proj, datt, att, small, wqkv, gmid, x, gain, dp, table_rows, heads, experts_n):
    rows, width = normed.shape
    local = att.shape[1]
    piece = width // dp
    vmem = pl.BlockSpec(memory_space=pltpu.VMEM)
    dma = pltpu.SemaphoreType.DMA
    return pl.pallas_call(
        last_kernel,
        name="last_stage",
        in_specs=[vmem] * 9,
        out_specs=[vmem] * 6,
        out_shape=[
            jax.ShapeDtypeStruct((4, piece, local), F32),
            jax.ShapeDtypeStruct((piece, experts_n), F32),
            jax.ShapeDtypeStruct((1, piece), F32),
            jax.ShapeDtypeStruct((1, piece), F32),
            jax.ShapeDtypeStruct((table_rows, heads), F32),
            jax.ShapeDtypeStruct(x.shape, F32),
        ],
        scratch_shapes=[
            pltpu.VMEM(x.shape, BF16),
            pltpu.VMEM(x.shape, BF16),
            pltpu.VMEM(small.shape, F32),
            dma((2, x.shape[0])),
            pltpu.VMEM((4, width, local), F32),
            pltpu.VMEM((2, width, local), BF16),
            pltpu.VMEM((2, width, local), BF16),
            pltpu.VMEM((width, local), BF16),
            pltpu.VMEM((4, piece, local), BF16),
            pltpu.VMEM((3, piece, local), BF16),
            pltpu.VMEM((3, piece, local), BF16),
            pltpu.VMEM((4, piece, local), BF16),
            pltpu.VMEM(small.shape, F32),
            pltpu.VMEM(small.shape, F32),
            pltpu.VMEM((2,) + small.shape, F32),
            pltpu.VMEM(small.shape, F32),
            pltpu.VMEM((dp,) + small.shape, F32),
            dma((2,)), dma((2, 4)), dma((2, 3)), dma((2, 3)), dma((2, 6)),
        ],
        compiler_params=pltpu.CompilerParams(vmem_limit_bytes=VMEM_BYTES, collective_id=1, has_side_effects=True),
        cost_estimate=cost(8 * rows * width * local, 8 * rows * width),
    )(normed, proj, datt, att, small, wqkv, gmid, x, gain)


def moe_kernel(
    seqs, groups, cap, tile, *refs,
):
    sends, refs = refs[:seqs], refs[seqs:]
    slot_gates, refs = refs[:seqs], refs[seqs:]
    cots, refs = refs[:groups], refs[groups:]
    w_own, w_far, part_out, din_back, h_back, keep_out, give_out = (refs[:2], refs[2:4]) + refs[4:9]
    (
        w_all, x_all, gate_all, g_all, xt_all, dyt_all, dy_ref, hid_all, dpre_all, part_acc, din_acc,
        part_all, din_all, h_all, tile_ref,
        x_sems, gate_sems, din_sems, h_sems, w_sems, own_sems, part_sems, out_sems, core_sems,
    ) = refs[9:]
    dp = lax.axis_index("dp")
    ctx = lax.axis_index("ctx")
    greet([{"dp": dp ^ b} for b in range(1, groups)] + [{"ctx": ctx ^ 1}])
    width = x_all.shape[-1]
    rows = groups * cap
    slices = w_all.shape[2]
    piece = width // slices
    half_len = w_all.shape[4]
    per_half = half_len // tile
    tiles = w_all.shape[1] * per_half
    order = tuple(range(groups - 1, 0, -1))

    sent = []
    for s in range(seqs):
        for b in order:
            sent.append(
                remote(sends[s].at[dp ^ b], x_all.at[s, dp], x_sems.at[0, s, b - 1], x_sems.at[1, s, b - 1], dp=dp ^ b)
            )
            sent.append(
                remote(
                    slot_gates[s].at[dp ^ b], gate_all.at[s, dp],
                    gate_sems.at[0, s, b - 1], gate_sems.at[1, s, b - 1], dp=dp ^ b,
                )
            )
    w_copies = []
    local = []
    arrivals = []
    for half in range(2):
        for index, (ref, place) in enumerate(((w_own[half], ctx), (w_far[half], ctx ^ 2))):
            sems = (w_sems.at[0, half, index], w_sems.at[1, half, index])
            w_copies.append(remote(ref, w_all.at[:, half, place], *sems, ctx=ctx ^ 1))
            there = w_all.at[:, half, place ^ 1]
            arrivals.append(remote(there, there, *sems, ctx=ctx ^ 1))
            local.append(pltpu.make_async_copy(ref, w_all.at[:, half, place], w_sems.at[2, half, index]))
    for copy in w_copies + sent:
        copy.start()
    for s in range(seqs):
        local.append(pltpu.make_async_copy(sends[s].at[dp], x_all.at[s, dp], own_sems.at[2 * s]))
        local.append(pltpu.make_async_copy(slot_gates[s].at[dp], gate_all.at[s, dp], own_sems.at[1 + 2 * s]))
    for b in range(groups):
        local.append(pltpu.make_async_copy(cots[b], g_all.at[dp ^ b], own_sems.at[2 * seqs + b]))
    for copy in local:
        copy.start()
    for copy in local:
        copy.wait()
    for copy in arrivals:
        copy.wait_recv()
    eye = diagonal(cap)

    def weights(io, f):
        lanes = pl.ds(pl.multiple_of((f % per_half) * tile, tile), tile)
        return w_all[io, f // per_half, :, :, lanes].reshape(width, tile)

    def gate_column(s, group):
        return jnp.sum(jnp.where(eye, gate_all[s, group], 0.0), axis=1, keepdims=True)

    def din_copy(s, b):
        return remote(
            din_all.at[s, dp ^ b], din_back.at[s, dp], din_sems.at[0, s, b - 1], din_sems.at[1, s, b - 1], dp=dp ^ b
        )

    def h_copy(s, b):
        return remote(h_all.at[s, dp ^ b], h_back.at[s, dp], h_sems.at[0, s, b - 1], h_sems.at[1, s, b - 1], dp=dp ^ b)

    def part_copy(s, b):
        return pltpu.make_async_copy(part_all.at[s, dp ^ b], part_out.at[b, s], part_sems.at[s, b])

    def own_copies(s):
        return [
            pltpu.make_async_copy(din_all.at[s, dp], din_back.at[s, dp], part_sems.at[s, groups]),
            pltpu.make_async_copy(h_all.at[s, dp], h_back.at[s, dp], part_sems.at[s, groups + 1]),
        ]

    def chunk(s, carry):
        for b in order:
            there = x_all.at[s, dp ^ b]
            remote(there, there, x_sems.at[0, s, b - 1], x_sems.at[1, s, b - 1], dp=dp ^ b).wait_recv()
            there = gate_all.at[s, dp ^ b]
            remote(there, there, gate_sems.at[0, s, b - 1], gate_sems.at[1, s, b - 1], dp=dp ^ b).wait_recv()
        x = x_all[s].reshape(rows, width)
        xt_all[s] = x.T
        for group in range(groups):
            dy_ref[group * cap : (group + 1) * cap] = (g_all[group, s].astype(F32) * gate_column(s, group)).astype(BF16)
        dyt_all[s] = dy_ref[...].T
        part_acc[...] = jnp.zeros_like(part_acc)
        din_acc[...] = jnp.zeros_like(din_acc)

        def step(f, carry):
            x = x_all[s].reshape(rows, width)
            w_in = weights(0, f)
            w_out_t = weights(1, f)
            pre = dot(x, w_in)
            dhid = dot(dy_ref[...], w_out_t)
            square = pre * pre
            inner = jnp.tanh(GELU_C * pre * (1.0 + GELU_A * square))
            half = 0.5 * (1.0 + inner)
            hidden = (pre * half).astype(BF16)
            slope = half + (0.5 * GELU_C) * pre * (1.0 - inner * inner) * (1.0 + (3.0 * GELU_A) * square)
            dpre = (dhid * slope).astype(BF16)
            hid_all[f, s] = hidden
            dpre_all[f, s] = dpre
            part_acc[...] += dot_nt(hidden, w_out_t)
            din_acc[...] += dot_nt(dpre, w_in)
            return carry

        lax.fori_loop(0, tiles, step, 0)
        for group in range(groups):
            at = slice(group * cap, (group + 1) * cap)
            din_all[s, group] = din_acc[at].astype(BF16)
            gated = part_acc[at] * gate_column(s, group)
            part_all[s, group] = gated.astype(BF16)
            h = jnp.sum(gated * g_all[group, s].astype(F32), axis=1, keepdims=True)
            h_all[s, group] = jnp.sum(jnp.where(eye, h, 0.0), axis=0, keepdims=True)
        for b in order:
            din_copy(s, b).start()
            h_copy(s, b).start()
        for copy in own_copies(s):
            copy.start()
        for b in range(groups):
            part_copy(s, b).start()
        return carry

    lax.fori_loop(0, seqs, chunk, 0)

    def tile_of(ref, f):
        lanes = pl.ds(pl.multiple_of((f % per_half) * tile, tile), tile)
        return ref.at[f // per_half, :, :, :, lanes]

    def keep_copy(f, slot):
        return pltpu.make_async_copy(tile_ref.at[slot, 0], tile_of(keep_out, f), out_sems.at[slot, 0])

    def give_copy(f, slot):
        return remote(
            tile_ref.at[slot, 1], tile_of(give_out, f), out_sems.at[slot, 1], core_sems.at[f], ctx=ctx ^ 1
        )

    def weight_grads(f, carry):
        slot = f % 2

        @pl.when(f >= 2)
        def _():
            keep_copy(f - 2, slot).wait()
            give_copy(f - 2, slot).wait_send()

        for io, (left, right) in enumerate(((xt_all, dpre_all), (dyt_all, hid_all))):
            total = dot(left[0], right[f, 0])
            for s in range(1, seqs):
                total = total + dot(left[s], right[f, s])
            for index in range(slices):
                place = index ^ ctx
                tile_ref[slot, place % 2, place // 2, io] = total[index * piece : (index + 1) * piece].astype(BF16)
        keep_copy(f, slot).start()
        give_copy(f, slot).start()
        return carry

    lax.fori_loop(0, tiles, weight_grads, 0)
    for f in (tiles - 2, tiles - 1):
        keep_copy(f, f % 2).wait()
        give_copy(f, f % 2).wait_send()
    for f in range(tiles):
        give_copy(f, f % 2).wait_recv()
    for s in range(seqs):
        for b in order:
            there = din_back.at[s, dp ^ b]
            remote(there, there, din_sems.at[0, s, b - 1], din_sems.at[1, s, b - 1], dp=dp ^ b).wait_recv()
            there = h_back.at[s, dp ^ b]
            remote(there, there, h_sems.at[0, s, b - 1], h_sems.at[1, s, b - 1], dp=dp ^ b).wait_recv()
            din_copy(s, b).wait_send()
            h_copy(s, b).wait_send()
        for copy in own_copies(s):
            copy.wait()
        for b in range(groups):
            part_copy(s, b).wait()
    for copy in w_copies + sent:
        copy.wait_send()


def moe_stage(sends, slot_gates, cots, keep, got, far_keep, far_got, tile=512):
    seqs = len(sends)
    groups, cap, width = sends[0].shape
    _, piece, half_len = keep.shape
    halves = 2
    slices = width // piece
    tiles = halves * half_len // tile
    rows = groups * cap
    any_spec = pl.BlockSpec(memory_space=pl.ANY)
    vmem = pl.BlockSpec(memory_space=pltpu.VMEM)
    dma = pltpu.SemaphoreType.DMA
    return pl.pallas_call(
        functools.partial(moe_kernel, seqs, groups, cap, tile),
        name="moe_stage",
        in_specs=[any_spec] * (2 * seqs + groups + 4),
        out_specs=[any_spec, any_spec, vmem, any_spec, any_spec],
        out_shape=[
            jax.ShapeDtypeStruct((groups, seqs, cap, width), BF16),
            jax.ShapeDtypeStruct((seqs, groups, cap, width), BF16),
            jax.ShapeDtypeStruct((seqs, groups, 1, cap), F32),
            jax.ShapeDtypeStruct((halves, slices // 2, 2, piece, half_len), BF16),
            jax.ShapeDtypeStruct((halves, slices // 2, 2, piece, half_len), BF16),
        ],
        scratch_shapes=[
            pltpu.VMEM((2, halves, slices, piece, half_len), BF16),
            pltpu.VMEM((seqs, groups, cap, width), BF16),
            pltpu.VMEM((seqs, groups, 1, cap), F32),
            pltpu.VMEM((groups, seqs, cap, width), BF16),
            pltpu.VMEM((seqs, width, rows), BF16),
            pltpu.VMEM((seqs, width, rows), BF16),
            pltpu.VMEM((rows, width), BF16),
            pltpu.VMEM((tiles, seqs, rows, tile), BF16),
            pltpu.VMEM((tiles, seqs, rows, tile), BF16),
            pltpu.VMEM((rows, width), F32),
            pltpu.VMEM((rows, width), F32),
            pltpu.VMEM((seqs, groups, cap, width), BF16),
            pltpu.VMEM((seqs, groups, cap, width), BF16),
            pltpu.VMEM((seqs, groups, 1, cap), F32),
            pltpu.VMEM((2, 2, slices // 2, 2, piece, tile), BF16),
            dma((2, seqs, groups - 1)), dma((2, seqs, groups - 1)), dma((2, seqs, groups - 1)),
            dma((2, seqs, groups - 1)), dma((3, 2, 2)), dma((2 * seqs + groups,)), dma((seqs, groups + 2)),
            dma((2, 2)), dma((tiles,)),
        ],
        compiler_params=pltpu.CompilerParams(
            vmem_limit_bytes=63 * 1024 * 1024, collective_id=2, has_side_effects=True
        ),
        cost_estimate=cost(20 * seqs * rows * width * halves * half_len, 40 * width * halves * half_len),
    )(*sends, *slot_gates, *cots, keep, got, far_keep, far_got)


def flip(value, axis, bit):
    count = lax.axis_size(axis)
    return lax.ppermute(value, axis, [(i, i ^ bit) for i in range(count)])


def all_to_all_dp(value):
    return lax.all_to_all(value, "dp", split_axis=0, concat_axis=0, tiled=True)


def gathered(tokens, wqkv, wout, table, gain_attn, gain_moe, router):
    seqs, stretch, width = tokens.shape
    local = wqkv.shape[2]
    dp = lax.axis_size("dp")
    tp = lax.axis_index("tp")
    experts_n = router.shape[1]
    wqkv = lax.all_gather(wqkv, "dp", axis=1, tiled=True)
    wout = lax.all_gather(wout, "dp", axis=1, tiled=True)
    table = lax.all_gather(table, "dp", axis=0, tiled=True)
    gains = lax.all_gather(jnp.concatenate([gain_attn, gain_moe], axis=0), "dp", axis=1, tiled=True)
    gain_attn, gain_moe = gains[0:1].astype(F32), gains[1:2]
    router = lax.all_gather(router, "dp", axis=0, tiled=True).T.reshape(dp, 2, width).transpose(1, 0, 2)
    router = jnp.where(tp == 0, router, router[::-1]).reshape(experts_n, width)
    across = flip(tokens, "ctx", 2)
    beside, beyond = flip(jnp.stack([tokens, across]), "ctx", 1)
    x32 = jnp.stack([tokens, beside, across, beyond], axis=1).astype(F32)
    normed = (x32 * norm_factor(x32) * gain_attn[None, None]).astype(BF16)
    own = normed[:, 0].reshape(seqs * stretch, width)
    queries = jnp.dot(own, wqkv[0], preferred_element_type=F32).astype(BF16) * jnp.asarray(HD ** (-0.5), BF16)
    flat = normed.reshape(seqs * 4 * stretch, width)
    keys = jnp.dot(flat, wqkv[1], preferred_element_type=F32).astype(BF16).reshape(seqs, 4 * stretch, local)
    values = jnp.dot(flat, wqkv[2], preferred_element_type=F32).astype(BF16).reshape(seqs, 4 * stretch, local)
    return queries.reshape(seqs, stretch, local), keys, values, own, wqkv, wout, table, gain_attn, gain_moe, router


def on_device(
    tokens_in, block_ids, rel_buckets, routes, attn_gain, w_qkv, w_attn_out, bias_table, moe_gain, w_router,
    w_expert_in, w_expert_out, cotangent,
):
    seqs, stretch, width = tokens_in.shape
    dp = lax.axis_size("dp")
    ctx_count = lax.axis_size("ctx")
    tp_count = lax.axis_size("tp")
    expert_count = w_router.shape[2]
    assert w_expert_in.shape[1] == tp_count == 2 and ctx_count == 4
    cap = max(2, 2 * stretch * routes.shape[2] // expert_count)
    ctx = lax.axis_index("ctx")
    tp = lax.axis_index("tp")
    local = w_qkv.shape[3]
    heads = local // HD

    fits = dp == 4
    e_order = jnp.arange(expert_count, dtype=jnp.int32).reshape(dp, 2).T
    e_order = jnp.where(tp == 0, e_order, e_order[::-1]).reshape(1, expert_count, 1)
    hits = ((routes[:, None, :, 0] == e_order) | (routes[:, None, :, 1] == e_order)).astype(F32)
    before = (
        lax.broadcasted_iota(jnp.int32, (stretch, stretch), 0) < lax.broadcasted_iota(jnp.int32, (stretch, stretch), 1)
    ).astype(BF16)
    ranks = jnp.einsum("set,tu->seu", hits.astype(BF16), before, preferred_element_type=F32)
    places = jnp.where(hits > 0.5, ranks, -1.0)[:, :dp]

    pair = jnp.stack([w_expert_in[0], w_expert_out[0].transpose(0, 2, 1)], axis=1)

    if fits:
        me = lax.axis_index("dp")
        near_places = jnp.stack([lax.dynamic_index_in_dim(places, me ^ b, 1, keepdims=False) for b in range(dp)], axis=1)
        cot_slots = dispatch(near_places, cotangent, cap)
        cot_slots, tokens_first, pair = lax.optimization_barrier((cot_slots, tokens_in, pair))
        cot_slots = [cot_slots[0]] + [flip(cot_slots[b], "dp", b) for b in range(1, dp)]
        (
            queries, keys, values, own_normed, wqkv, wout_parts, table, gain_attn, gain_moe, router, got, far_keep,
        ) = first_stage(
            tokens_first, w_qkv[0], w_attn_out[0], bias_table[0], attn_gain, moe_gain, w_router[0], pair
        )
        keep = lax.dynamic_index_in_dim(pair, tp, 0, keepdims=False)
        far_got = flip(got, "ctx", 2)
        wout_own = wout_parts.transpose(1, 0, 2).reshape(local, width)
        table = table.reshape(NB, heads)
        keys = keys.reshape(seqs, 4 * stretch, local)
        values = values.reshape(seqs, 4 * stretch, local)
        own_normed = own_normed.reshape(seqs * stretch, width)
    else:
        queries, keys, values, own_normed, wqkv, wout_own, table, gain_attn, gain_moe, router = gathered(
            tokens_in, w_qkv[0], w_attn_out[0], bias_table[0], attn_gain, moe_gain, w_router[0]
        )
        keep = lax.dynamic_index_in_dim(pair, tp, 0, keepdims=False)
        got = flip(lax.dynamic_index_in_dim(pair, 1 - tp, 0, keepdims=False), "tp", 1)
        weights = lax.all_gather(jnp.stack([keep, got], axis=1), "ctx", axis=0, tiled=False)
        cot_slots = all_to_all_dp(dispatch(places, cotangent, cap))
    wout_other = flip(wout_own, "tp", 1)

    one_hot_bucket = (rel_buckets[:, None] == jnp.arange(NB, dtype=jnp.int32)[None, :]).astype(F32)
    one_hot_bucket = jnp.pad(one_hot_bucket, ((0, 1), (0, 0)))
    starts = [(ctx - (ctx ^ b)) * stretch + 3 * stretch for b in range(4)]
    hot_windows = jnp.stack([lax.dynamic_slice_in_dim(one_hot_bucket, s, 2 * stretch, 0) for s in starts])
    windows = jnp.einsum("bmn,nh->hbm", hot_windows, table.astype(F32), precision=FULL_PRECISION)
    bias = expand_bias(windows)

    ids = block_ids.reshape(seqs, 4, stretch)
    ids_pieces = [lax.dynamic_index_in_dim(ids, ctx ^ b, 1, keepdims=False) for b in range(4)]
    ids_query = ids_pieces[0].reshape(seqs, 1, stretch)
    ids_key = jnp.stack(ids_pieces, axis=1).reshape(seqs, 4 * stretch, 1)

    wout_pair = jnp.stack([wout_own, wout_other])
    attended, lse, mids, moes, gates, sends, slot_gates = [], [], [], [], [], [], []
    for s in range(seqs):
        att, stat = attend(queries[s], keys[s], values[s], bias, ids_query[s], ids_key[s])
        attended.append(att)
        lse.append(stat)
        mid, moe_in, gate, send, slot_gate = middle_stage(
            att, flip(att, "tp", 1), tokens_in[s], wout_pair, gain_moe, router, hits[s], places[s], cap
        )
        mids.append(mid)
        moes.append(moe_in)
        gates.append(gate)
        sends.append(send)
        slot_gates.append(slot_gate)
    if fits:
        parts, returned_din, returned_h, kept, given = moe_stage(sends, slot_gates, cot_slots, keep, got, far_keep, far_got)
    else:
        partials, returned_din, returned_h = [], [], []
        acc = None
        for s in range(seqs):
            received = all_to_all_dp(sends[s])
            received_gate = all_to_all_dp(slot_gates[s])
            part, din, h, acc = experts(received, cot_slots, s, received_gate, weights, acc, s == seqs - 1)
            returned_din.append(all_to_all_dp(din))
            returned_h.append(all_to_all_dp(h))
            partials.append(all_to_all_dp(part))
        kept, given = acc[:, 0::2], flip(acc[:, 1::2], "ctx", 1)

    beside_sum = kept.astype(F32) + given.astype(F32)
    far_sum = flip(beside_sum[:, 1].astype(BF16), "ctx", 2)

    hits_of = (heads, 4, 2 * stretch)
    if fits:
        tokens_out, gmid, dattn, grad_proj, gain_moe_grad, router_grad, rel_grad = back_stage(
            mids, moes, gates, lse, returned_din, parts, queries, keys, values, bias, cotangent, wout_own,
            returned_h, places, near_places, ids_query, ids_key, router, gain_moe,
        )
        far_sum, grad_proj = lax.optimization_barrier((far_sum, grad_proj))
        mine = beside_sum[:, 0] + far_sum.astype(F32)
        other = flip(mine[1].astype(BF16), "tp", 1)
        grad_proj = grad_proj.reshape(3, seqs * stretch, local)
        dattn = dattn.reshape(seqs * stretch, width)
        grad_table = jnp.einsum("bmn,hbm->nh", hot_windows, rel_grad.reshape(hits_of), precision=FULL_PRECISION)
        small = jnp.concatenate(
            [
                router_grad,
                jnp.pad(gain_moe_grad, ((0, 7), (0, 0))),
                jnp.pad(grad_table.T, ((0, 8 - heads), (0, width - NB))),
            ],
            axis=0,
        )
        wide, g_router, g_moe, g_attn, g_table, grad_tokens = last_stage(
            own_normed, grad_proj, dattn, jnp.concatenate(attended, axis=0), small, wqkv, gmid, tokens_in, gain_attn,
            dp, NB // dp, heads, expert_count,
        )
        other, wide = lax.optimization_barrier((other, wide))
        g_qkv = wide[:3]
        g_wout = wide[3].T
    else:
        mine = beside_sum[:, 0] + far_sum.astype(F32)
        other = flip(mine[1].astype(BF16), "tp", 1)
        tokens_out, gmids = [], []
        projections = []
        rel_grad = 0.0
        gain_moe_grad = 0.0
        router_grad = 0.0
        datts = []
        for s in range(seqs):
            out_own = combine_out(places[s], partials[s], cap)
            out_other = flip(out_own, "tp", 1)
            tokens_out.append((mids[s] + (out_own.astype(F32) + out_other.astype(F32))).astype(BF16))
            din_own, h_own = combine(places[s], returned_din[s], returned_h[s], cap)
            din_other = flip(din_own, "tp", 1)
            h_all = jnp.concatenate([h_own, flip(h_own, "tp", 1)], axis=0)
            gmid, datt, d_gain, d_router, dattn = middle_back(
                din_own, din_other, h_all, gates[s], router, moes[s], mids[s], gain_moe, cotangent[s], wout_own
            )
            datts.append(dattn)
            gmids.append(gmid)
            gain_moe_grad += d_gain
            router_grad += d_router
            dq, dk, dv, rel = attend_back(
                queries[s], keys[s], values[s], datt, bias, lse[s], ids_query[s], ids_key[s]
            )
            rel_grad += rel
            dkv = jnp.stack([dk, dv]).reshape(2, 4, stretch, local)
            near = dkv[:, 0::2].astype(F32) + flip(dkv[:, 1::2], "ctx", 1).astype(F32)
            full = near[:, 0] + flip(near[:, 1].astype(BF16), "ctx", 2).astype(F32)
            projections.append(jnp.concatenate([dq[None], full.astype(BF16)], axis=0))
        grad_proj = jnp.concatenate(projections, axis=1)
        dattn = jnp.concatenate(datts, axis=0)
        attended = jnp.concatenate(attended, axis=0)
        dnormed_part = jnp.einsum("jre,jde->rd", grad_proj, wqkv, preferred_element_type=F32)
        dnormed_own = dnormed_part.astype(BF16)
        dnormed = dnormed_own.astype(F32) + flip(dnormed_own, "tp", 1).astype(F32)
        own_x = tokens_in.reshape(seqs * stretch, width).astype(F32)
        factor = norm_factor(own_x)
        unit = own_x * factor
        scaled = dnormed * gain_attn
        dres = factor * (scaled - unit * jnp.mean(scaled * unit, axis=-1, keepdims=True))
        grad_tokens = jnp.concatenate(gmids, axis=0) + dres
        grad_table = jnp.einsum("bmn,hbm->nh", hot_windows, rel_grad.reshape(hits_of), precision=FULL_PRECISION)
        router_grad = router_grad.reshape(2, dp, width)
        router_grad = jnp.where(tp == 0, router_grad, router_grad[::-1])
        router_grad = router_grad.transpose(1, 0, 2).reshape(expert_count, width).T

        def reduced(value, dim):
            return lax.psum(lax.psum_scatter(value, "dp", scatter_dimension=dim, tiled=True), "ctx")

        g_attn = reduced(jnp.sum(dnormed * unit, axis=0)[None], 1)
        g_qkv = reduced(jnp.einsum("rd,jre->jde", own_normed, grad_proj, preferred_element_type=F32), 1)
        g_wout = reduced(jnp.einsum("re,rd->ed", attended, dattn, preferred_element_type=F32), 1)
        g_table = reduced(grad_table, 0)
        g_moe = reduced(gain_moe_grad, 1)
        g_router = reduced(router_grad, 0)
        tokens_out = jnp.stack(tokens_out)
    other = other.astype(F32)
    ordered = jnp.where(tp == 0, jnp.stack([mine[0], other]), jnp.stack([other, mine[0]]))
    grad_expert_in = ordered[:, 0]
    grad_expert_out = ordered[:, 1].transpose(0, 2, 1)
    return (
        tokens_out,
        grad_tokens.reshape(seqs, stretch, width),
        g_attn,
        g_qkv[None],
        g_wout[None],
        g_table[None],
        g_moe,
        g_router[None],
        grad_expert_in[None],
        grad_expert_out[None],
    )


def solution(mesh):
    return jax.shard_map(
        on_device,
        mesh=mesh,
        in_specs=(
            P("dp", "ctx", None),
            P("dp", None),
            P(),
            P("dp", "ctx", None),
            P(None, "dp"),
            P(None, None, "dp", "tp"),
            P(None, "tp", "dp"),
            P(None, "dp", "tp"),
            P(None, "dp"),
            P(None, "dp", None),
            P(None, "dp", "ctx", "tp"),
            P(None, "dp", "tp", "ctx"),
            P("dp", "ctx", None),
        ),
        out_specs=(
            P("dp", "ctx", None),
            P("dp", "ctx", None),
            P(None, "dp"),
            P(None, None, "dp", "tp"),
            P(None, "tp", "dp"),
            P(None, "dp", "tp"),
            P(None, "dp"),
            P(None, "dp", None),
            P(None, "dp", "ctx", "tp"),
            P(None, "dp", "tp", "ctx"),
        ),
        check_vma=False,
    )
```

```python
import functools

import jax
import jax.numpy as jnp
from jax import lax
from jax.experimental import pallas as pl
from jax.experimental.pallas import tpu as pltpu
from jax.sharding import PartitionSpec as P

HD = 64
NB = 32
EPSILON = 1e-06
FULL_PRECISION = lax.Precision.HIGHEST
MASKED = -1e30
BF16 = jnp.bfloat16
F32 = jnp.float32
EARLY = 50
VMEM_BYTES = 60 * 1024 * 1024
GELU_C = 0.7978845608028654
GELU_A = 0.044715


def params():
    return pltpu.CompilerParams(vmem_limit_bytes=VMEM_BYTES)


def cost(flops, nbytes, trans=0, scale=1):
    return pl.CostEstimate(
        flops=int(flops) // scale, bytes_accessed=int(nbytes) // scale, transcendentals=int(trans) // scale
    )


def dot(a, b):
    return lax.dot_general(a, b, (((1,), (0,)), ((), ())), preferred_element_type=F32)


def dot_nt(a, b):
    return lax.dot_general(a, b, (((1,), (1,)), ((), ())), preferred_element_type=F32)


def dot_tn(a, b):
    return lax.dot_general(a, b, (((0,), (0,)), ((), ())), preferred_element_type=F32)


def bias_kernel(win_ref, out_ref):
    for block in range(4):
        row = win_ref[0, block : block + 1, :]
        wide = jnp.broadcast_to(row, (256, 512))
        rolled = pltpu.roll(wide, 257, 1, stride=1, stride_axis=0)
        out_ref[0, block * 256 : (block + 1) * 256, :] = rolled[:, :256].astype(BF16)


def expand_bias(windows):
    heads = windows.shape[0]
    return pl.pallas_call(
        bias_kernel,
        name="expand_bias",
        grid=(heads,),
        in_specs=[pl.BlockSpec((1, 4, 512), lambda h: (h, 0, 0))],
        out_specs=pl.BlockSpec((1, 1024, 256), lambda h: (h, 0, 0)),
        out_shape=jax.ShapeDtypeStruct((heads, 1024, 256), BF16),
        compiler_params=params(),
        cost_estimate=cost(heads * 2 * 1024 * 512, heads * 1024 * 256 * 2, scale=EARLY),
    )(windows)


def attend_kernel(q_ref, k_ref, v_ref, bias_ref, idq_ref, idk_ref, out_ref, lse_ref, mask_ref):
    @pl.when(pl.program_id(0) == 0)
    def _():
        mask_ref[...] = jnp.where(idk_ref[...] <= idq_ref[...], 0.0, MASKED)

    queries = q_ref[...]
    keys = k_ref[...]
    values_t = v_ref[...].T
    low_half = lax.broadcasted_iota(jnp.int32, queries.shape, 1) < HD
    zero = jnp.zeros_like(queries)
    parts = []
    for head in range(2):
        own = jnp.where(low_half, queries, zero) if head == 0 else jnp.where(low_half, zero, queries)
        scores = dot_nt(keys, own) + bias_ref[head].astype(F32) + mask_ref[...]
        top = jnp.max(scores, axis=0, keepdims=True)
        weights = jnp.exp(scores - top)
        total = jnp.sum(weights, axis=0, keepdims=True)
        part = dot(values_t[head * HD : (head + 1) * HD], weights.astype(BF16)) * (1.0 / total)
        parts.append(part)
        lse_ref[0, head : head + 1, :] = top + jnp.log(total)
    out_ref[...] = jnp.concatenate(parts, axis=0).T.astype(BF16)


def attend(queries, keys, values, bias, ids_query, ids_key):
    rows, width = queries.shape
    length = keys.shape[0]
    pairs = width // (2 * HD)
    return pl.pallas_call(
        attend_kernel,
        name="attend",
        grid=(pairs,),
        in_specs=[
            pl.BlockSpec((rows, 128), lambda p: (0, p)),
            pl.BlockSpec((length, 128), lambda p: (0, p)),
            pl.BlockSpec((length, 128), lambda p: (0, p)),
            pl.BlockSpec((2, length, rows), lambda p: (p, 0, 0)),
            pl.BlockSpec((1, rows), lambda p: (0, 0)),
            pl.BlockSpec((length, 1), lambda p: (0, 0)),
        ],
        out_specs=[
            pl.BlockSpec((rows, 128), lambda p: (0, p)),
            pl.BlockSpec((1, 2, rows), lambda p: (p, 0, 0)),
        ],
        out_shape=[
            jax.ShapeDtypeStruct((rows, width), BF16),
            jax.ShapeDtypeStruct((pairs, 2, rows), F32),
        ],
        scratch_shapes=[pltpu.VMEM((length, rows), F32)],
        compiler_params=params(),
        cost_estimate=cost(pairs * 2 * 4 * rows * length * 128, 6 * rows * length * 2, pairs * 2 * rows * length, scale=EARLY),
    )(queries, keys, values, bias, ids_query, ids_key)


def attend_back_kernel(
    q_ref, k_ref, v_ref, do_ref, bias_ref, lse_ref, idq_ref, idk_ref, dq_ref, dk_ref, dv_ref, rel_ref, mask_ref
):
    @pl.when(pl.program_id(0) == 0)
    def _():
        mask_ref[...] = jnp.where(idk_ref[...] <= idq_ref[...], 0.0, MASKED)

    queries = q_ref[...]
    keys = k_ref[...]
    values = v_ref[...]
    grad_out = do_ref[...]
    keys_t = keys.T
    low_half = lax.broadcasted_iota(jnp.int32, queries.shape, 1) < HD
    zero = jnp.zeros_like(queries)
    dk = None
    dv = None
    dq_parts = []
    for head in range(2):
        own = (lambda a: jnp.where(low_half, a, zero)) if head == 0 else (lambda a: jnp.where(low_half, zero, a))
        q_own = own(queries)
        do_own = own(grad_out)
        scores = dot_nt(keys, q_own) + bias_ref[head].astype(F32) + mask_ref[...]
        probs = jnp.exp(scores - lse_ref[0, head : head + 1, :])
        dprobs = dot_nt(values, do_own)
        delta = jnp.sum(probs * dprobs, axis=0, keepdims=True)
        dscores = probs * (dprobs - delta)
        low = dscores.astype(BF16)
        dv_head = dot(probs.astype(BF16), do_own)
        dk_head = dot(low, q_own)
        dv = dv_head if dv is None else dv + dv_head
        dk = dk_head if dk is None else dk + dk_head
        dq_parts.append(dot(keys_t[head * HD : (head + 1) * HD], low))
        for block in range(4):
            tile = dscores[block * 256 : (block + 1) * 256]
            wide = jnp.concatenate([tile, jnp.zeros_like(tile)], axis=1)
            total = None
            for group in range(32):
                moved = pltpu.roll(wide[group * 8 : group * 8 + 8], 248 - 8 * group, 1)
                total = moved if total is None else total + moved
            row = lax.broadcasted_iota(jnp.int32, total.shape, 0)
            amount = 7 - row
            for bit in (1, 2, 4):
                total = jnp.where((amount & bit) != 0, pltpu.roll(total, bit, 1), total)
            rel_ref[0, head, block : block + 1, :] = jnp.sum(total, axis=0, keepdims=True)
    dq_ref[...] = (jnp.concatenate(dq_parts, axis=0).T * (HD ** (-0.5))).astype(BF16)
    dk_ref[...] = dk.astype(BF16)
    dv_ref[...] = dv.astype(BF16)


def attend_back(queries, keys, values, grad_out, bias, lse, ids_query, ids_key):
    rows, width = queries.shape
    length = keys.shape[0]
    pairs = width // (2 * HD)
    return pl.pallas_call(
        attend_back_kernel,
        name="attend_back",
        grid=(pairs,),
        in_specs=[
            pl.BlockSpec((rows, 128), lambda p: (0, p)),
            pl.BlockSpec((length, 128), lambda p: (0, p)),
            pl.BlockSpec((length, 128), lambda p: (0, p)),
            pl.BlockSpec((rows, 128), lambda p: (0, p)),
            pl.BlockSpec((2, length, rows), lambda p: (p, 0, 0)),
            pl.BlockSpec((1, 2, rows), lambda p: (p, 0, 0)),
            pl.BlockSpec((1, rows), lambda p: (0, 0)),
            pl.BlockSpec((length, 1), lambda p: (0, 0)),
        ],
        out_specs=[
            pl.BlockSpec((rows, 128), lambda p: (0, p)),
            pl.BlockSpec((length, 128), lambda p: (0, p)),
            pl.BlockSpec((length, 128), lambda p: (0, p)),
            pl.BlockSpec((1, 2, 4, 512), lambda p: (p, 0, 0, 0)),
        ],
        out_shape=[
            jax.ShapeDtypeStruct((rows, width), BF16),
            jax.ShapeDtypeStruct((length, width), BF16),
            jax.ShapeDtypeStruct((length, width), BF16),
            jax.ShapeDtypeStruct((pairs, 2, 4, 512), F32),
        ],
        scratch_shapes=[pltpu.VMEM((length, rows), F32)],
        compiler_params=params(),
        cost_estimate=cost(pairs * 2 * 10 * rows * length * 128, 8 * rows * length * 2, pairs * 2 * rows * length),
    )(queries, keys, values, grad_out, bias, lse, ids_query, ids_key)


def one_hot(place, cap):
    groups, rows = place.shape
    slots = lax.broadcasted_iota(jnp.int32, (cap, rows), 0).astype(F32)
    return [slots == place[group : group + 1, :] for group in range(groups)]


def diagonal(cap):
    return lax.broadcasted_iota(jnp.int32, (cap, cap), 0) == lax.broadcasted_iota(jnp.int32, (cap, cap), 1)


def dispatch_kernel(groups, cap, place_ref, rows_ref, out_ref):
    rows = rows_ref[0]
    picks = one_hot(place_ref[0], cap)
    pick = jnp.concatenate([jnp.where(p, 1.0, 0.0).astype(BF16) for p in picks], axis=0)
    out_ref[:, 0] = dot(pick, rows).astype(BF16).reshape(groups, cap, rows.shape[1])


def dispatch(place, rows, cap):
    seqs, groups, stretch = place.shape
    width = rows.shape[2]
    return pl.pallas_call(
        functools.partial(dispatch_kernel, groups, cap),
        name="dispatch_rows",
        grid=(seqs,),
        in_specs=[
            pl.BlockSpec((1, groups, stretch), lambda s: (s, 0, 0)),
            pl.BlockSpec((1, stretch, width), lambda s: (s, 0, 0)),
        ],
        out_specs=pl.BlockSpec((groups, 1, cap, width), lambda s: (0, s, 0, 0)),
        out_shape=jax.ShapeDtypeStruct((groups, seqs, cap, width), BF16),
        compiler_params=params(),
        cost_estimate=cost(seqs * 2 * groups * cap * stretch * width, seqs * 2 * (stretch + groups * cap) * width),
    )(place, rows)


def norm_factor(value):
    return lax.rsqrt(jnp.mean(value * value, axis=-1, keepdims=True) + EPSILON)


def middle_kernel(
    groups, cap, own_ref, other_ref, x_ref, wout_ref, gain_ref, router_ref, hits_ref, place_ref,
    middle_ref, moe_ref, gates_ref, send_ref, slot_gate_ref,
):
    mid = x_ref[...].astype(F32) + (dot(own_ref[...], wout_ref[0]) + dot(other_ref[...], wout_ref[1]))
    middle_ref[...] = mid
    moe_in = (mid * norm_factor(mid) * gain_ref[...].astype(F32)).astype(BF16)
    moe_ref[...] = moe_in
    logits = dot_nt(router_ref[...], moe_in)
    hit = hits_ref[...] > 0.5
    top = jnp.max(jnp.where(hit, logits, MASKED), axis=0, keepdims=True)
    raw = jnp.where(hit, jnp.exp(jnp.where(hit, logits, top) - top), 0.0)
    gates = raw / jnp.sum(raw, axis=0, keepdims=True)
    gates_ref[...] = gates
    picks = one_hot(place_ref[...], cap)
    pick = jnp.concatenate([jnp.where(p, 1.0, 0.0).astype(BF16) for p in picks], axis=0)
    send_ref[...] = dot(pick, moe_in).astype(BF16).reshape(groups, cap, moe_in.shape[1])
    eye = diagonal(cap)
    for group in range(groups):
        column = jnp.sum(jnp.where(picks[group], gates[group : group + 1, :], 0.0), axis=1, keepdims=True)
        slot_gate_ref[group] = jnp.sum(jnp.where(eye, column, 0.0), axis=0, keepdims=True)


def middle_stage(own, other, x, wout, gain, router, hits, place, cap):
    rows, width = x.shape
    experts = router.shape[0]
    groups = place.shape[0]
    return pl.pallas_call(
        functools.partial(middle_kernel, groups, cap),
        name="middle_stage",
        out_shape=[
            jax.ShapeDtypeStruct((rows, width), F32),
            jax.ShapeDtypeStruct((rows, width), BF16),
            jax.ShapeDtypeStruct((experts, rows), F32),
            jax.ShapeDtypeStruct((groups, cap, width), BF16),
            jax.ShapeDtypeStruct((groups, 1, cap), F32),
        ],
        compiler_params=params(),
        cost_estimate=cost(2 * rows * width * width + 2 * groups * cap * rows * width, rows * width * 16, scale=EARLY),
    )(own, other, x, wout, gain, router, hits, place)


def expert_kernel(
    first, final, tiles, groups, cap, x_ref, g_ref, gate_ref, w_ref, *refs
):
    if first:
        acc_in = None
    else:
        acc_in, refs = refs[0], refs[1:]
    part_out, din_out, h_out, acc_out, xt_ref, dy_ref, dyt_ref, part_ref, din_ref = refs
    step = pl.program_id(0)
    rows = groups * cap
    width = x_ref.shape[-1]
    slices = w_ref.shape[0]
    piece = width // slices

    @pl.when(step == 0)
    def _():
        eye = diagonal(cap)
        xt_ref[...] = x_ref[...].reshape(rows, width).T
        for group in range(groups):
            gate = jnp.sum(jnp.where(eye, gate_ref[group], 0.0), axis=1, keepdims=True)
            dy_ref[group * cap : (group + 1) * cap] = (g_ref[group, 0].astype(F32) * gate).astype(BF16)
        dyt_ref[...] = dy_ref[...].T

    x = x_ref[...].reshape(rows, width)
    w_in = w_ref[:, 0, 0].reshape(width, -1)
    w_out_t = w_ref[:, 1, 0].reshape(width, -1)
    dy = dy_ref[...]
    pre = dot(x, w_in)
    square = pre * pre
    inner = jnp.tanh(GELU_C * pre * (1.0 + GELU_A * square))
    half = 0.5 * (1.0 + inner)
    hidden = (pre * half).astype(BF16)
    slope = half + (0.5 * GELU_C) * pre * (1.0 - inner * inner) * (1.0 + (3.0 * GELU_A) * square)
    dhid = dot(dy, w_out_t)
    dpre = (dhid * slope).astype(BF16)
    part = dot_nt(hidden, w_out_t)
    din = dot_nt(dpre, w_in)
    dw_in = dot(xt_ref[...], dpre)
    dw_out_t = dot(dyt_ref[...], hidden)

    @pl.when(step == 0)
    def _():
        part_ref[...] = part
        din_ref[...] = din

    @pl.when(step > 0)
    def _():
        part_ref[...] += part
        din_ref[...] += din

    me = lax.axis_index("ctx")
    for index in range(slices):
        place = index ^ me
        grad_in = dw_in[index * piece : (index + 1) * piece]
        grad_out = dw_out_t[index * piece : (index + 1) * piece]
        if not first:
            grad_in += acc_in[0, place, 0]
            grad_out += acc_in[0, place, 1]
        acc_out[0, place, 0] = grad_in.astype(acc_out.dtype)
        acc_out[0, place, 1] = grad_out.astype(acc_out.dtype)

    @pl.when(step == tiles - 1)
    def _():
        eye = diagonal(cap)
        for group in range(groups):
            gate = jnp.sum(jnp.where(eye, gate_ref[group], 0.0), axis=1, keepdims=True)
            gated = part_ref[group * cap : (group + 1) * cap] * gate
            part_out[group] = gated.astype(BF16)
            din_out[group] = din_ref[group * cap : (group + 1) * cap].astype(BF16)
            h = jnp.sum(gated * g_ref[group, 0].astype(F32), axis=1, keepdims=True)
            h_out[group] = jnp.sum(jnp.where(eye, h, 0.0), axis=0, keepdims=True)


def experts(x, cot_slots, seq_index, gate, weights, acc, final, tile=512):
    groups, cap, width = x.shape
    slices, _, halves, piece, half_len = weights.shape
    per_half = half_len // tile
    tiles = halves * per_half
    rows = groups * cap
    first = acc is None
    acc_spec = pl.BlockSpec((1, slices, 2, piece, tile), lambda f: (f // per_half, 0, 0, 0, f % per_half))
    in_specs = [
        pl.BlockSpec((groups, cap, width), lambda f: (0, 0, 0)),
        pl.BlockSpec((groups, 1, cap, width), lambda f: (0, seq_index, 0, 0)),
        pl.BlockSpec((groups, 1, cap), lambda f: (0, 0, 0)),
        pl.BlockSpec((slices, 2, 1, piece, tile), lambda f: (0, 0, f // per_half, 0, f % per_half)),
    ]
    args = [x, cot_slots, gate, weights]
    aliases = {}
    if not first:
        in_specs.append(acc_spec)
        args.append(acc)
        if not final:
            aliases = {4: 3}
    acc_shape = (halves, slices, 2, piece, half_len)
    return pl.pallas_call(
        functools.partial(expert_kernel, first, final, tiles, groups, cap),
        name="experts",
        grid=(tiles,),
        in_specs=in_specs,
        out_specs=[
            pl.BlockSpec((groups, cap, width), lambda f: (0, 0, 0)),
            pl.BlockSpec((groups, cap, width), lambda f: (0, 0, 0)),
            pl.BlockSpec((groups, 1, cap), lambda f: (0, 0, 0)),
            acc_spec,
        ],
        out_shape=[
            jax.ShapeDtypeStruct((groups, cap, width), BF16),
            jax.ShapeDtypeStruct((groups, cap, width), BF16),
            jax.ShapeDtypeStruct((groups, 1, cap), F32),
            jax.ShapeDtypeStruct(acc_shape, BF16 if final else F32),
        ],
        scratch_shapes=[
            pltpu.VMEM((width, rows), BF16),
            pltpu.VMEM((rows, width), BF16),
            pltpu.VMEM((width, rows), BF16),
            pltpu.VMEM((rows, width), F32),
            pltpu.VMEM((rows, width), F32),
        ],
        input_output_aliases=aliases,
        compiler_params=params(),
        cost_estimate=cost(12 * rows * width * halves * half_len, 2 * width * halves * half_len * 10, rows * halves * half_len),
    )(*args)


def combine_kernel(groups, cap, place_ref, din_ref, h_ref, din_out, h_out):
    picks = one_hot(place_ref[...], cap)
    pick = jnp.concatenate([jnp.where(p, 1.0, 0.0).astype(BF16) for p in picks], axis=0)
    rows = groups * cap
    din_out[...] = dot_tn(pick, din_ref[...].reshape(rows, din_ref.shape[-1])).astype(BF16)
    eye = diagonal(cap)
    for group in range(groups):
        column = jnp.sum(jnp.where(eye, h_ref[group], 0.0), axis=1, keepdims=True)
        h_out[group : group + 1, :] = jnp.sum(jnp.where(picks[group], column, 0.0), axis=0, keepdims=True)


def combine(place, din, h, cap):
    groups, stretch = place.shape
    width = din.shape[-1]
    return pl.pallas_call(
        functools.partial(combine_kernel, groups, cap),
        name="combine_back",
        out_shape=[
            jax.ShapeDtypeStruct((stretch, width), BF16),
            jax.ShapeDtypeStruct((groups, stretch), F32),
        ],
        compiler_params=params(),
        cost_estimate=cost(2 * groups * cap * stretch * width, 4 * stretch * width * 2),
    )(place, din, h)


def combine_out_kernel(groups, cap, place_ref, part_ref, out_ref):
    picks = one_hot(place_ref[...], cap)
    pick = jnp.concatenate([jnp.where(p, 1.0, 0.0).astype(BF16) for p in picks], axis=0)
    out_ref[...] = dot_tn(pick, part_ref[...].reshape(groups * cap, part_ref.shape[-1])).astype(BF16)


def combine_out(place, part, cap):
    groups, stretch = place.shape
    width = part.shape[-1]
    return pl.pallas_call(
        functools.partial(combine_out_kernel, groups, cap),
        name="combine_out",
        out_shape=jax.ShapeDtypeStruct((stretch, width), BF16),
        compiler_params=params(),
        cost_estimate=cost(2 * groups * cap * stretch * width, 4 * stretch * width * 2),
    )(place, part)


def middle_back_kernel(
    own_ref, other_ref, h_ref, gates_ref, router_ref, moe_ref, mid_ref, gain_ref, cot_ref, wout_ref,
    gmid_ref, datt_ref, gain_grad_ref, router_grad_ref, low_ref,
):
    h = h_ref[...]
    dlogits = h - gates_ref[...] * jnp.sum(h, axis=0, keepdims=True)
    router = router_ref[...]
    dmoe = own_ref[...].astype(F32) + other_ref[...].astype(F32)
    dmoe = dmoe + lax.dot_general(
        dlogits, router.astype(F32), (((0,), (0,)), ((), ())), precision=FULL_PRECISION, preferred_element_type=F32
    )
    router_grad_ref[...] = lax.dot_general(
        dlogits, moe_ref[...].astype(F32), (((1,), (0,)), ((), ())), precision=FULL_PRECISION, preferred_element_type=F32
    )
    mid = mid_ref[...]
    gain = gain_ref[...].astype(F32)
    factor = norm_factor(mid)
    normed = mid * factor
    gain_grad_ref[...] = jnp.sum(dmoe * normed, axis=0, keepdims=True)
    scaled = dmoe * gain
    dmid = factor * (scaled - normed * jnp.mean(scaled * normed, axis=-1, keepdims=True))
    gmid = cot_ref[...].astype(F32) + dmid
    gmid_ref[...] = gmid
    dattn = gmid.astype(BF16)
    datt_ref[...] = dot_nt(dattn, wout_ref[...]).astype(BF16)
    low_ref[...] = dattn


def middle_back(own, other, h, gates, router, moe_in, mid, gain, cot, wout):
    rows, width = mid.shape
    local = wout.shape[0]
    return pl.pallas_call(
        middle_back_kernel,
        name="middle_back",
        out_shape=[
            jax.ShapeDtypeStruct((rows, width), F32),
            jax.ShapeDtypeStruct((rows, local), BF16),
            jax.ShapeDtypeStruct((1, width), F32),
            jax.ShapeDtypeStruct(router.shape, F32),
            jax.ShapeDtypeStruct((rows, width), BF16),
        ],
        compiler_params=params(),
        cost_estimate=cost(2 * rows * width * local, 30 * rows * width),
    )(own, other, h, gates, router, moe_in, mid, gain, cot, wout)


MESH_ID = pl.DeviceIdType.MESH


def remote(src, dst, send_sem, recv_sem, **where):
    return pltpu.make_async_remote_copy(
        src_ref=src, dst_ref=dst, send_sem=send_sem, recv_sem=recv_sem, device_id=where, device_id_type=MESH_ID
    )


def greet(peers):
    barrier = pltpu.get_barrier_semaphore()
    for where in peers:
        pl.semaphore_signal(barrier, inc=1, device_id=where, device_id_type=MESH_ID)
    pl.semaphore_wait(barrier, len(peers))


def first_kernel(
    seqs, cap, tok_ref, wqkv_ref, wout_ref, table_ref, ga_ref, gm_ref, router_ref, pair_ref, near_ref, cot_ref,
    q_ref, k_ref, v_ref, normed_ref, wqkv_out, wout_out, table_out, gain_ref, gm_out, router_out, got_out, far_out,
    slots_ref, cot_out,
    tok_all, n_all, ga_all, gm_all, router_all,
    z_send, z_recv, f_send, f_recv, t_send, t_recv, y_send, y_recv, l_sem, e_sems, c_sems,
):
    dp = lax.axis_index("dp")
    ctx = lax.axis_index("ctx")
    tp = lax.axis_index("tp")
    core = ctx % 2
    rows = wqkv_ref.shape[1]
    half = rows // 2
    orows = wout_ref.shape[0] // 2
    greet([{"dp": dp ^ b} for b in (1, 2, 3)] + [{"ctx": ctx ^ 1}, {"ctx": ctx ^ 2}, {"tp": tp ^ 1}])

    def w_rows(owner, side):
        return pl.ds(pl.multiple_of(owner * rows + side * half, 16), half)

    def o_rows(side):
        return pl.ds(pl.multiple_of(side * orows, 16), orows)

    def z_copies(b):
        to = {"dp": dp ^ b}
        return [
            remote(ga_ref, ga_all.at[dp], z_send.at[0, b - 1], z_recv.at[0, b - 1], **to),
            remote(gm_ref, gm_all.at[dp], z_send.at[1, b - 1], z_recv.at[1, b - 1], **to),
            remote(table_ref, table_out.at[dp], z_send.at[2, b - 1], z_recv.at[2, b - 1], **to),
            remote(router_ref, router_all.at[dp], z_send.at[3, b - 1], z_recv.at[3, b - 1], **to),
            remote(
                wqkv_ref.at[:, pl.ds(pl.multiple_of(core * half, 16), half)], wqkv_out.at[:, w_rows(dp, core)],
                z_send.at[4, b - 1], z_recv.at[4, b - 1], **to,
            ),
            remote(
                wout_ref.at[o_rows(core)], wout_out.at[dp, o_rows(core)],
                z_send.at[5, b - 1], z_recv.at[5, b - 1], **to,
            ),
        ]

    small = [z_copies(b) for b in (1, 2, 3)]
    for kind in range(6):
        for b in (3, 2, 1):
            small[b - 1][kind].start()
    beside = remote(tok_ref, tok_all.at[1], t_send.at[0], t_recv.at[0], ctx=ctx ^ 1)
    beside.start()
    across = [remote(tok_ref.at[s], tok_all.at[2, s], y_send.at[s], y_recv.at[s], ctx=ctx ^ 2) for s in range(seqs)]
    expert_copies = [
        remote(pair_ref.at[1 - tp], got_out, e_sems.at[0, 0], e_sems.at[1, 0], tp=tp ^ 1),
        remote(pair_ref.at[tp], far_out, e_sems.at[0, 1], e_sems.at[1, 1], ctx=ctx ^ 2),
    ]
    for copy in across + expert_copies:
        copy.start()
    own = [
        pltpu.make_async_copy(tok_ref, tok_all.at[0], l_sem.at[0]),
        pltpu.make_async_copy(ga_ref, ga_all.at[dp], l_sem.at[1]),
        pltpu.make_async_copy(gm_ref, gm_all.at[dp], l_sem.at[2]),
        pltpu.make_async_copy(table_ref, table_out.at[dp], l_sem.at[3]),
        pltpu.make_async_copy(router_ref, router_all.at[dp], l_sem.at[4]),
        pltpu.make_async_copy(wqkv_ref, wqkv_out.at[:, pl.ds(pl.multiple_of(dp * rows, 16), rows)], l_sem.at[5]),
        pltpu.make_async_copy(wout_ref, wout_out.at[dp], l_sem.at[6]),
    ]
    for copy in own:
        copy.start()

    groups = slots_ref.shape[0]

    def cot_copy(s, b):
        return remote(
            slots_ref.at[b, s], cot_out.at[b - 1, s], c_sems.at[0, s, b - 1], c_sems.at[1, s, b - 1], dp=dp ^ b
        )

    def dispatch_cot(s, carry):
        picks = one_hot(near_ref[s], cap)
        pick = jnp.concatenate([jnp.where(p, 1.0, 0.0).astype(BF16) for p in picks], axis=0)
        slots_ref[:, s] = dot(pick, cot_ref[s]).astype(BF16).reshape(groups, cap, cot_ref.shape[2])

        @pl.when(s < seqs - 1)
        def _():
            for b in (3, 2, 1):
                cot_copy(s, b).start()

        return carry

    lax.fori_loop(0, seqs, dispatch_cot, 0)
    for copy in own:
        copy.wait()

    for kind in range(4):
        for b in (3, 2, 1):
            small[b - 1][kind].wait_recv()
    count = ga_all.shape[0]
    piece = ga_all.shape[2]
    width = count * piece
    row = lax.broadcasted_iota(jnp.int32, (piece, width), 0)
    col = lax.broadcasted_iota(jnp.int32, (piece, width), 1)
    gain = 0.0
    gain_m = 0.0
    for d in range(count):
        spread = jnp.where(col == row + d * piece, 1.0, 0.0).astype(BF16)
        gain = gain + dot(ga_all[d], spread)
        gain_m = gain_m + dot(gm_all[d], spread)
    gain_ref[...] = gain
    gm_out[...] = gain_m.astype(BF16)
    experts_n = router_ref.shape[1]
    slot_row = lax.broadcasted_iota(jnp.int32, (experts_n, experts_n), 0)
    slot_col = lax.broadcasted_iota(jnp.int32, (experts_n, experts_n), 1)
    side = slot_row // count
    expert = (slot_row % count) * 2 + (side ^ tp)
    order = jnp.where(slot_col == expert, 1.0, 0.0).astype(BF16)
    router_out[...] = dot_nt(order, router_all[...].reshape(width, experts_n)).astype(BF16)

    def norm_piece(b):
        def body(s, carry):
            value = tok_all[b, s].astype(F32)
            out = (value * norm_factor(value) * gain_ref[...]).astype(BF16)
            n_all[b, s] = out
            return carry

        lax.fori_loop(0, seqs, body, 0)

    def project(b, s):
        x = n_all[b, s]
        k_ref[s, b] = dot(x, wqkv_out[1]).astype(BF16)
        v_ref[s, b] = dot(x, wqkv_out[2]).astype(BF16)

    norm_piece(0)
    normed_ref[...] = n_all[0]
    beside.wait_recv()
    norm_piece(1)

    forwards = []
    for b in (1, 2, 3):
        for kind, f in ((4, 0), (5, 1)):
            small[b - 1][kind].wait_recv()
            if f == 0:
                ref = wqkv_out.at[:, w_rows(dp ^ b, core)]
            else:
                ref = wout_out.at[dp ^ b, o_rows(core)]
            copy = remote(ref, ref, f_send.at[f, b - 1], f_recv.at[f, b - 1], ctx=ctx ^ 1)
            copy.start()
            forwards.append(copy)
    for copy in forwards:
        copy.wait_recv()

    def own_q(s, carry):
        q_ref[s] = (dot(n_all[0, s], wqkv_out[0]).astype(BF16) * (HD ** (-0.5))).astype(BF16)
        project(0, s)
        project(1, s)
        return carry

    lax.fori_loop(0, seqs, own_q, 0)
    later = []
    for s in range(seqs):
        across[s].wait_recv()
        copy = remote(tok_all.at[2, s], tok_all.at[3, s], t_send.at[1 + s], t_recv.at[1 + s], ctx=ctx ^ 1)
        copy.start()
        later.append(copy)
    norm_piece(2)
    for copy in later:
        copy.wait_recv()
    norm_piece(3)

    def others(s, carry):
        project(2, s)
        project(3, s)
        return carry

    lax.fori_loop(0, seqs, others, 0)
    for copy in expert_copies:
        copy.wait()
    for s in range(seqs - 1):
        for b in (3, 2, 1):
            cot_copy(s, b).wait()
    for group in small:
        for copy in group:
            copy.wait_send()
    for copy in forwards + later + across + [beside]:
        copy.wait_send()


def first_stage(tokens, wqkv, wout, table, gain_attn, gain_moe, router, expert_pair, near, cot, cap):
    seqs, stretch, width = tokens.shape
    count, rows, local = wqkv.shape
    dp = width // rows
    experts_n = router.shape[1]
    any_spec = pl.BlockSpec(memory_space=pl.ANY)
    vmem = pl.BlockSpec(memory_space=pltpu.VMEM)
    dma = pltpu.SemaphoreType.DMA
    return pl.pallas_call(
        functools.partial(first_kernel, seqs, cap),
        name="first_stage",
        in_specs=[any_spec] * 8 + [vmem] * 2,
        out_specs=[vmem] * 10 + [any_spec] * 2 + [vmem, any_spec],
        out_shape=[
            jax.ShapeDtypeStruct((seqs, stretch, local), BF16),
            jax.ShapeDtypeStruct((seqs, 4, stretch, local), BF16),
            jax.ShapeDtypeStruct((seqs, 4, stretch, local), BF16),
            jax.ShapeDtypeStruct((seqs, stretch, width), BF16),
            jax.ShapeDtypeStruct((3, width, local), BF16),
            jax.ShapeDtypeStruct((dp,) + wout.shape, BF16),
            jax.ShapeDtypeStruct((dp,) + table.shape, BF16),
            jax.ShapeDtypeStruct((1, width), F32),
            jax.ShapeDtypeStruct((1, width), BF16),
            jax.ShapeDtypeStruct((experts_n, width), BF16),
            jax.ShapeDtypeStruct(expert_pair.shape[1:], BF16),
            jax.ShapeDtypeStruct(expert_pair.shape[1:], BF16),
            jax.ShapeDtypeStruct((dp, seqs, cap, width), BF16),
            jax.ShapeDtypeStruct((dp - 1, seqs - 1, cap, width), BF16),
        ],
        scratch_shapes=[
            pltpu.VMEM((4, seqs, stretch, width), BF16),
            pltpu.VMEM((4, seqs, stretch, width), BF16),
            pltpu.VMEM((dp, 1, rows), BF16),
            pltpu.VMEM((dp, 1, rows), BF16),
            pltpu.VMEM((dp, rows, experts_n), BF16),
            dma((6, 3)), dma((6, 3)), dma((2, 3)), dma((2, 3)), dma((1 + seqs,)), dma((1 + seqs,)),
            dma((seqs,)), dma((seqs,)), dma((7,)), dma((2, 2)), dma((2, seqs - 1, 3)),
        ],
        compiler_params=pltpu.CompilerParams(vmem_limit_bytes=VMEM_BYTES, collective_id=0, has_side_effects=True),
        cost_estimate=cost(40 * 10**9, 10**7),
    )(tokens, wqkv, wout, table, gain_attn, gain_moe, router, expert_pair, near, cot)


def back_kernel(seqs, groups, cap, *refs):
    seq_refs, refs = refs[:4], refs[4:]
    din_ref, part_ref, q_ref, k_ref, v_ref, bias_ref, cot_ref, wout_ref = refs[:8]
    h_ref, place_ref, near_ref, idq_ref, idk_ref, router_ref, gain_ref = refs[8:15]
    out_ref, gmid_ref, low_ref, proj_ref, gain_grad_ref, router_grad_ref, rel_ref = refs[15:22]
    (
        mid_v, moe_v, gate_v, lse_v, din_v, part_v, q_v, k_v, v_v, bias_v, cot_v, wout_v,
        din_own, din_other, h_own, h_other, out_own, out_other, datt_v, mask_v, keep_v, give_v, core_v, y_v, far_v,
        load_sems, seq_sems, part_sems, x_sems, c_sems, y_sems,
    ) = refs[22:]
    dp = lax.axis_index("dp")
    ctx = lax.axis_index("ctx")
    tp = lax.axis_index("tp")
    greet([{"dp": dp ^ b} for b in range(1, groups)] + [{"ctx": ctx ^ 1}, {"ctx": ctx ^ 2}, {"tp": tp ^ 1}])
    rows = groups * cap
    stretch, width = mid_v.shape[1:]
    local = q_v.shape[2]
    pairs = local // (2 * HD)

    def part_copy(s, b):
        return remote(part_ref.at[b, s], part_v.at[b, s], part_sems.at[0, s, b], part_sems.at[1, s, b], dp=dp ^ b)

    for s in range(seqs):
        for b in range(groups - 1, 0, -1):
            part_copy(s, b).start()
    din_load = pltpu.make_async_copy(din_ref, din_v, load_sems.at[0])
    loads = [
        pltpu.make_async_copy(src, dst, load_sems.at[i + 1])
        for i, (src, dst) in enumerate(
            ((wout_ref, wout_v), (cot_ref, cot_v), (q_ref, q_v), (k_ref, k_v), (v_ref, v_v), (bias_ref, bias_v),
             (part_ref.at[0], part_v.at[0]))
        )
    ]
    for i, (src, dst) in enumerate(zip(seq_refs, (mid_v, moe_v, gate_v, lse_v))):
        loads.append(pltpu.make_async_copy(src, dst, seq_sems.at[i]))
    din_load.start()
    for copy in loads:
        copy.start()
    gain_grad_ref[...] = jnp.zeros_like(gain_grad_ref)
    router_grad_ref[...] = jnp.zeros_like(router_grad_ref)
    rel_ref[...] = jnp.zeros_like(rel_ref)

    def din_copy(s):
        return remote(din_own.at[s], din_other.at[s], x_sems.at[0, 0, s], x_sems.at[1, 0, s], tp=tp ^ 1)

    def h_copy(s):
        return remote(h_own.at[s], h_other.at[s], x_sems.at[0, 1, s], x_sems.at[1, 1, s], tp=tp ^ 1)

    def out_copy(s):
        return remote(out_own.at[s], out_other.at[s], x_sems.at[0, 2, s], x_sems.at[1, 2, s], tp=tp ^ 1)

    def core_copy(s):
        return remote(give_v.at[s], core_v.at[s], c_sems.at[0, s], c_sems.at[1, s], ctx=ctx ^ 1)

    def y_copy(s):
        return remote(y_v.at[s], far_v.at[s], y_sems.at[0, s], y_sems.at[1, s], ctx=ctx ^ 2)

    def chosen(place):
        picks = one_hot(place, cap)
        return picks, jnp.concatenate([jnp.where(p, 1.0, 0.0).astype(BF16) for p in picks], axis=0)

    din_load.wait()

    def gather_back(s, carry):
        picks, pick = chosen(place_ref[s])
        din_own[s] = dot_tn(pick, din_v[s].reshape(rows, width)).astype(BF16)
        eye = diagonal(cap)
        for group in range(groups):
            column = jnp.sum(jnp.where(eye, h_ref[s, group], 0.0), axis=1, keepdims=True)
            h_own[s, group : group + 1, :] = jnp.sum(jnp.where(picks[group], column, 0.0), axis=0, keepdims=True)
        h_copy(s).start()
        din_copy(s).start()
        return carry

    lax.fori_loop(0, seqs, gather_back, 0)
    for copy in loads:
        copy.wait()

    def middle_back(s):
        h = jnp.concatenate([h_own[s], h_other[s]], axis=0)
        dlogits = h - gate_v[s] * jnp.sum(h, axis=0, keepdims=True)
        dmoe = din_own[s].astype(F32) + din_other[s].astype(F32)
        dmoe = dmoe + lax.dot_general(
            dlogits, router_ref[...].astype(F32), (((0,), (0,)), ((), ())),
            precision=FULL_PRECISION, preferred_element_type=F32,
        )
        router_grad_ref[...] += lax.dot_general(
            dlogits, moe_v[s].astype(F32), (((1,), (0,)), ((), ())),
            precision=FULL_PRECISION, preferred_element_type=F32,
        )
        mid = mid_v[s]
        factor = norm_factor(mid)
        normed = mid * factor
        gain_grad_ref[...] += jnp.sum(dmoe * normed, axis=0, keepdims=True)
        scaled = dmoe * gain_ref[...].astype(F32)
        dmid = factor * (scaled - normed * jnp.mean(scaled * normed, axis=-1, keepdims=True))
        gmid = cot_v[s].astype(F32) + dmid
        gmid_ref[s] = gmid
        dattn = gmid.astype(BF16)
        low_ref[s] = dattn
        datt_v[...] = dot_nt(dattn, wout_v[...]).astype(BF16)

    def core_sum(s):
        core_copy(s).wait_recv()
        for kind in range(2):
            keep_v[s, kind, 0] += core_v[s, kind, 0].astype(F32)
            y_v[s, kind] = (keep_v[s, kind, 1] + core_v[s, kind, 1].astype(F32)).astype(BF16)
        y_copy(s).start()

    def out_sum(s):
        for b in range(1, groups):
            part_copy(s, b).wait_recv()
        pick = chosen(near_ref[s])[1]
        out_own[s] = dot_tn(pick, part_v[:, s].reshape(rows, width)).astype(BF16)
        out_copy(s).start()

    def attention_back(s):
        mask_v[...] = jnp.where(idk_ref[s] <= idq_ref[s], 0.0, MASKED)

        def pair(p, carry):
            lanes = pl.ds(pl.multiple_of(p * 2 * HD, 2 * HD), 2 * HD)
            queries = q_v[s, :, lanes]
            keys = k_v[s, :, lanes]
            values = v_v[s, :, lanes]
            grad_out = datt_v[:, lanes]
            keys_t = keys.T
            low_half = lax.broadcasted_iota(jnp.int32, queries.shape, 1) < HD
            zero = jnp.zeros_like(queries)
            dk = None
            dv = None
            dq_parts = []
            for head in range(2):
                own = (lambda a: jnp.where(low_half, a, zero)) if head == 0 else (
                    lambda a: jnp.where(low_half, zero, a)
                )
                q_own = own(queries)
                do_own = own(grad_out)
                scores = dot_nt(keys, q_own) + bias_v[2 * p + head].astype(F32) + mask_v[...]
                probs = jnp.exp(scores - lse_v[s, p, head : head + 1, :])
                dprobs = dot_nt(values, do_own)
                delta = jnp.sum(probs * dprobs, axis=0, keepdims=True)
                dscores = probs * (dprobs - delta)
                low = dscores.astype(BF16)
                dv_head = dot(probs.astype(BF16), do_own)
                dk_head = dot(low, q_own)
                dv = dv_head if dv is None else dv + dv_head
                dk = dk_head if dk is None else dk + dk_head
                dq_parts.append(dot(keys_t[head * HD : (head + 1) * HD], low))
                for block in range(4):
                    tile = dscores[block * 256 : (block + 1) * 256]
                    wide = jnp.concatenate([tile, jnp.zeros_like(tile)], axis=1)
                    total = None
                    for group in range(32):
                        moved = pltpu.roll(wide[group * 8 : group * 8 + 8], 248 - 8 * group, 1)
                        total = moved if total is None else total + moved
                    row = lax.broadcasted_iota(jnp.int32, total.shape, 0)
                    amount = 7 - row
                    for bit in (1, 2, 4):
                        total = jnp.where((amount & bit) != 0, pltpu.roll(total, bit, 1), total)
                    rel_ref[p, head, block : block + 1, :] += jnp.sum(total, axis=0, keepdims=True)
            proj_ref[0, s, :, lanes] = (jnp.concatenate(dq_parts, axis=0).T * (HD ** (-0.5))).astype(BF16)
            for kind, value in enumerate((dk, dv)):
                for index in range(2):
                    at = 2 * index * stretch
                    keep_v[s, kind, index, :, lanes] = value[at : at + stretch]
                    give_v[s, kind, index, :, lanes] = value[at + stretch : at + 2 * stretch].astype(BF16)
            return carry

        lax.fori_loop(0, pairs, pair, 0)
        core_copy(s).start()

    def main(s, carry):
        h_copy(s).wait_recv()
        din_copy(s).wait_recv()
        middle_back(s)
        attention_back(s)

        @pl.when(s > 0)
        def _():
            core_sum(s - 1)
            out_sum(s - 1)

        return carry

    lax.fori_loop(0, seqs, main, 0)
    core_sum(seqs - 1)
    out_sum(seqs - 1)

    def finish_keys(s, carry):
        y_copy(s).wait_recv()
        for kind in range(2):
            proj_ref[1 + kind, s] = (keep_v[s, kind, 0] + far_v[s, kind].astype(F32)).astype(BF16)
        return carry

    def finish_out(s, carry):
        out_copy(s).wait_recv()
        out_ref[s] = (mid_v[s] + (out_own[s].astype(F32) + out_other[s].astype(F32))).astype(BF16)
        return carry

    lax.fori_loop(0, seqs, finish_keys, 0)
    lax.fori_loop(0, seqs, finish_out, 0)
    for s in range(seqs):
        for b in range(1, groups):
            part_copy(s, b).wait_send()
        for copy in (h_copy(s), din_copy(s), out_copy(s), core_copy(s), y_copy(s)):
            copy.wait_send()


def back_stage(mids, moes, gates, lse, din, parts, q, k, v, bias, cot, wout, h, places, near, ids_query, ids_key, router, gain):
    groups, _, cap, width = parts.shape
    seqs, stretch = mids.shape[:2]
    local = wout.shape[0]
    length = k.shape[1]
    pairs = local // (2 * HD)
    experts_n = router.shape[0]
    any_spec = pl.BlockSpec(memory_space=pl.ANY)
    vmem = pl.BlockSpec(memory_space=pltpu.VMEM)
    dma = pltpu.SemaphoreType.DMA
    return pl.pallas_call(
        functools.partial(back_kernel, seqs, groups, cap),
        name="back_stage",
        in_specs=[any_spec] * 12 + [vmem] * 7,
        out_specs=[vmem] * 7,
        out_shape=[
            jax.ShapeDtypeStruct((seqs, stretch, width), BF16),
            jax.ShapeDtypeStruct((seqs, stretch, width), F32),
            jax.ShapeDtypeStruct((seqs, stretch, width), BF16),
            jax.ShapeDtypeStruct((3, seqs, stretch, local), BF16),
            jax.ShapeDtypeStruct((1, width), F32),
            jax.ShapeDtypeStruct((experts_n, width), F32),
            jax.ShapeDtypeStruct((pairs, 2, 4, 2 * stretch), F32),
        ],
        scratch_shapes=[
            pltpu.VMEM((seqs, stretch, width), F32),
            pltpu.VMEM((seqs, stretch, width), BF16),
            pltpu.VMEM((seqs, experts_n, stretch), F32),
            pltpu.VMEM((seqs, pairs, 2, stretch), F32),
            pltpu.VMEM((seqs, groups, cap, width), BF16),
            pltpu.VMEM((groups, seqs, cap, width), BF16),
            pltpu.VMEM((seqs, stretch, local), BF16),
            pltpu.VMEM((seqs, length, local), BF16),
            pltpu.VMEM((seqs, length, local), BF16),
            pltpu.VMEM((2 * pairs, length, stretch), BF16),
            pltpu.VMEM((seqs, stretch, width), BF16),
            pltpu.VMEM((local, width), BF16),
            pltpu.VMEM((seqs, stretch, width), BF16),
            pltpu.VMEM((seqs, stretch, width), BF16),
            pltpu.VMEM((seqs, groups, stretch), F32),
            pltpu.VMEM((seqs, groups, stretch), F32),
            pltpu.VMEM((seqs, stretch, width), BF16),
            pltpu.VMEM((seqs, stretch, width), BF16),
            pltpu.VMEM((stretch, local), BF16),
            pltpu.VMEM((length, stretch), F32),
            pltpu.VMEM((seqs, 2, 2, stretch, local), F32),
            pltpu.VMEM((seqs, 2, 2, stretch, local), BF16),
            pltpu.VMEM((seqs, 2, 2, stretch, local), BF16),
            pltpu.VMEM((seqs, 2, stretch, local), BF16),
            pltpu.VMEM((seqs, 2, stretch, local), BF16),
            dma((8,)), dma((4,)), dma((2, seqs, groups)), dma((2, 3, seqs)), dma((2, seqs)), dma((2, seqs)),
        ],
        compiler_params=pltpu.CompilerParams(
            vmem_limit_bytes=63 * 1024 * 1024, collective_id=3, has_side_effects=True
        ),
        cost_estimate=cost(6 * 10**10, 10**7),
    )(mids, moes, gates, lse, din, parts, q, k, v, bias, cot, wout, h, places, near, ids_query, ids_key, router, gain)


def last_kernel(
    normed_ref, proj_ref, datt_ref, att_ref, small_ref, wqkv_ref, gmid_ref, x_ref, gain_ref,
    out_ref, router_out, gm_out, ga_out, table_out, gx_ref,
    dn_own, dn_other, ga_own, dn_sems, grads, core_send, core_got, y_out, y_got, z_out, z_got, wide, s_own, s_core, s_y, s_x, s_z,
    c_sems, y_sems, z_sems, w_sems, s_sems,
):
    dp = lax.axis_index("dp")
    ctx = lax.axis_index("ctx")
    tp = lax.axis_index("tp")
    core = ctx % 2
    far = ctx // 2
    greet([{"dp": dp ^ b} for b in (1, 2, 3)] + [{"ctx": ctx ^ b} for b in (1, 2, 3)] + [{"tp": tp ^ 1}])
    count = z_got.shape[0] + 1
    width = normed_ref.shape[1]
    piece = width // count

    seqs, stretch = x_ref.shape[:2]

    def unit_of(s):
        value = x_ref[s].astype(F32)
        factor = norm_factor(value)
        return factor, value * factor

    def rows_of(s):
        return pl.ds(pl.multiple_of(s * stretch, stretch), stretch)

    def input_grad(s, total):
        part = dot_nt(proj_ref[0, rows_of(s)], wqkv_ref[0])
        part = part + dot_nt(proj_ref[1, rows_of(s)], wqkv_ref[1])
        part = part + dot_nt(proj_ref[2, rows_of(s)], wqkv_ref[2])
        dn_own[s] = part.astype(BF16)
        return total + jnp.sum(part * unit_of(s)[1], axis=0, keepdims=True)

    own_gain = lax.fori_loop(0, seqs, input_grad, jnp.zeros((1, width), F32))
    lines = lax.broadcasted_iota(jnp.int32, small_ref.shape, 0)
    ga_own[...] = small_ref[...] + jnp.where(lines == 9, own_gain, 0.0)
    x_copy = remote(ga_own, s_x, s_sems.at[0, 0], s_sems.at[1, 0], tp=tp ^ 1)
    x_copy.start()
    dn_copies = [
        remote(dn_own.at[s], dn_other.at[s], dn_sems.at[0, s], dn_sems.at[1, s], tp=tp ^ 1) for s in range(seqs)
    ]
    for copy in dn_copies:
        copy.start()
    normed_t = normed_ref[...].T
    for j in range(3):
        grads[j] = dot(normed_t, proj_ref[j])
    grads[3] = dot_tn(datt_ref[...], att_ref[...])
    give = 1 - core
    core_send[0] = grads[2 * give].astype(BF16)
    core_send[1] = grads[2 * give + 1].astype(BF16)
    c_copy = remote(core_send, core_got, c_sems.at[0], c_sems.at[1], ctx=ctx ^ 1)
    c_copy.start()
    x_copy.wait_recv()
    s_own[...] = ga_own[...] + jnp.where(lines == 9, s_x[...], 0.0)
    sc_copy = remote(s_own, s_core, s_sems.at[0, 1], s_sems.at[1, 1], ctx=ctx ^ 1)
    sc_copy.start()
    c_copy.wait_recv()
    grads[2 * core] += core_got[0].astype(F32)
    grads[2 * core + 1] += core_got[1].astype(F32)
    y_out[...] = grads[2 * core + 1 - far].astype(BF16)
    order = (3, 2, 1, 0)
    y_copies = []
    for b in order:
        at = pl.ds(pl.multiple_of((dp ^ b) * piece, 16), piece)
        copy = remote(y_out.at[at], y_got.at[b], y_sems.at[0, b], y_sems.at[1, b], ctx=ctx ^ 2)
        copy.start()
        y_copies.append(copy)
    sc_copy.wait_recv()
    y_small = s_own[...] + s_core[...]
    s_y[0] = y_small
    sy_copy = remote(s_y.at[0], s_y.at[1], s_sems.at[0, 2], s_sems.at[1, 2], ctx=ctx ^ 2)
    sy_copy.start()
    mine = 2 * core + far
    z_copies = []
    total = None
    for copy, b in zip(y_copies, order):
        copy.wait_recv()
        at = pl.ds(pl.multiple_of((dp ^ b) * piece, 16), piece)
        value = grads[mine, at] + y_got[b].astype(F32)
        if b:
            z_out[b - 1] = value.astype(BF16)
            z_copy = remote(z_out.at[b - 1], z_got.at[b - 1], z_sems.at[0, b - 1], z_sems.at[1, b - 1], dp=dp ^ b)
            z_copy.start()
            z_copies.append((b, z_copy))
        else:
            total = value
    sy_copy.wait_recv()
    s_z[dp] = s_y[0] + s_y[1]
    sz_copies = []
    for b in (3, 2, 1):
        copy = remote(s_z.at[dp], s_z.at[dp], s_sems.at[0, 2 + b], s_sems.at[1, 2 + b], dp=dp ^ b)
        copy.start()
        sz_copies.append(copy)
    for b, copy in z_copies:
        copy.wait_recv()
        total = total + z_got[b - 1].astype(F32)
    wide[mine] = total.astype(BF16)
    w_copies = []
    for b in (3, 2, 1):
        copy = remote(wide.at[mine], wide.at[mine], w_sems.at[0, b - 1], w_sems.at[1, b - 1], ctx=ctx ^ b)
        copy.start()
        w_copies.append(copy)
    for copy in dn_copies:
        copy.wait_recv()

    def input_norm(s, carry):
        factor, unit = unit_of(s)
        scaled = (dn_own[s].astype(F32) + dn_other[s].astype(F32)) * gain_ref[...]
        dres = factor * (scaled - unit * jnp.mean(scaled * unit, axis=-1, keepdims=True))
        gx_ref[s] = gmid_ref[s] + dres
        return carry

    lax.fori_loop(0, seqs, input_norm, 0)
    for copy in sz_copies:
        copy.wait_recv()
    small = s_z[0]
    for d in range(1, count):
        small = small + s_z[d]

    def exact(a, b, dims):
        return lax.dot_general(a, b, (dims, ((), ())), precision=FULL_PRECISION, preferred_element_type=F32)

    row = lax.broadcasted_iota(jnp.int32, (piece, width), 0)
    col = lax.broadcasted_iota(jnp.int32, (piece, width), 1)
    select = jnp.where(col == row + dp * piece, 1.0, 0.0)
    experts_n = router_out.shape[1]
    e_row = lax.broadcasted_iota(jnp.int32, (experts_n, experts_n), 0)
    e_col = lax.broadcasted_iota(jnp.int32, (experts_n, experts_n), 1)
    slot = ((e_row % 2) ^ tp) * count + e_row // 2
    arranged = exact(jnp.where(e_col == slot, 1.0, 0.0), small[:experts_n], ((1,), (0,)))
    router_out[...] = exact(select, arranged, ((1,), (1,)))
    gains = exact(small[8:16], select, ((1,), (1,)))
    gm_out[...] = gains[0:1]
    ga_out[...] = gains[1:2]
    t_rows, heads = table_out.shape
    t_row = lax.broadcasted_iota(jnp.int32, (t_rows, width), 0)
    t_col = lax.broadcasted_iota(jnp.int32, (t_rows, width), 1)
    table_out[...] = exact(jnp.where(t_col == t_row + dp * t_rows, 1.0, 0.0), small[16:24], ((1,), (1,)))[:, :heads]
    for copy in w_copies:
        copy.wait_recv()
    out_ref[...] = wide[...].astype(F32)
    for copy in [x_copy, c_copy, sc_copy, sy_copy] + dn_copies + y_copies + [c for _, c in z_copies] + sz_copies + w_copies:
        copy.wait_send()


def last_stage(normed, proj, datt, att, small, wqkv, gmid, x, gain, dp, table_rows, heads, experts_n):
    rows, width = normed.shape
    local = att.shape[1]
    piece = width // dp
    vmem = pl.BlockSpec(memory_space=pltpu.VMEM)
    dma = pltpu.SemaphoreType.DMA
    return pl.pallas_call(
        last_kernel,
        name="last_stage",
        in_specs=[vmem] * 9,
        out_specs=[vmem] * 6,
        out_shape=[
            jax.ShapeDtypeStruct((4, piece, local), F32),
            jax.ShapeDtypeStruct((piece, experts_n), F32),
            jax.ShapeDtypeStruct((1, piece), F32),
            jax.ShapeDtypeStruct((1, piece), F32),
            jax.ShapeDtypeStruct((table_rows, heads), F32),
            jax.ShapeDtypeStruct(x.shape, F32),
        ],
        scratch_shapes=[
            pltpu.VMEM(x.shape, BF16),
            pltpu.VMEM(x.shape, BF16),
            pltpu.VMEM(small.shape, F32),
            dma((2, x.shape[0])),
            pltpu.VMEM((4, width, local), F32),
            pltpu.VMEM((2, width, local), BF16),
            pltpu.VMEM((2, width, local), BF16),
            pltpu.VMEM((width, local), BF16),
            pltpu.VMEM((4, piece, local), BF16),
            pltpu.VMEM((3, piece, local), BF16),
            pltpu.VMEM((3, piece, local), BF16),
            pltpu.VMEM((4, piece, local), BF16),
            pltpu.VMEM(small.shape, F32),
            pltpu.VMEM(small.shape, F32),
            pltpu.VMEM((2,) + small.shape, F32),
            pltpu.VMEM(small.shape, F32),
            pltpu.VMEM((dp,) + small.shape, F32),
            dma((2,)), dma((2, 4)), dma((2, 3)), dma((2, 3)), dma((2, 6)),
        ],
        compiler_params=pltpu.CompilerParams(vmem_limit_bytes=VMEM_BYTES, collective_id=1, has_side_effects=True),
        cost_estimate=cost(8 * rows * width * local, 8 * rows * width),
    )(normed, proj, datt, att, small, wqkv, gmid, x, gain)


def front_kernel(
    seqs, groups, cap,
    got_ref, cot_ref, q_ref, k_ref, v_ref, win_ref, idq_ref, idk_ref, x_ref, wout_ref, gain_ref, router_ref,
    hits_ref, place_ref,
    far_out, cot_out, row_out, gate_out, bias_ref, att_ref, lse_ref, mid_ref, moe_ref, gates_ref, send_ref, slot_ref,
    wout_other, att_other, mask_ref, w_sems, x_sems, z_sems, r_sems, g_sems, own_sems,
):
    dp = lax.axis_index("dp")
    ctx = lax.axis_index("ctx")
    tp = lax.axis_index("tp")
    greet([{"dp": dp ^ b} for b in range(1, groups)] + [{"ctx": ctx ^ 2}, {"tp": tp ^ 1}])
    width = x_ref.shape[2]
    local = q_ref.shape[2]
    pairs = local // (2 * HD)
    far_copy = remote(got_ref, far_out, w_sems.at[0, 0], w_sems.at[1, 0], ctx=ctx ^ 2)
    wout_copy = remote(wout_ref, wout_other, w_sems.at[0, 1], w_sems.at[1, 1], tp=tp ^ 1)
    order = tuple(range(groups - 1, 0, -1))
    cot_copies = [
        remote(cot_ref.at[b, seqs - 1], cot_out.at[b - 1], z_sems.at[0, b - 1], z_sems.at[1, b - 1], dp=dp ^ b)
        for b in order
    ]
    for copy in [far_copy, wout_copy] + cot_copies:
        copy.start()

    def expand(head, carry):
        for block in range(4):
            row = win_ref[head, block : block + 1, :]
            wide = jnp.broadcast_to(row, (256, 512))
            rolled = pltpu.roll(wide, 257, 1, stride=1, stride_axis=0)
            bias_ref[head, block * 256 : (block + 1) * 256, :] = rolled[:, :256].astype(BF16)
        return carry

    lax.fori_loop(0, 2 * pairs, expand, 0)

    def att_copy(s):
        return remote(att_ref.at[s], att_other.at[s], x_sems.at[0, s], x_sems.at[1, s], tp=tp ^ 1)

    def row_copy(b):
        return remote(send_ref.at[0, dp ^ b], row_out.at[dp], r_sems.at[0, b - 1], r_sems.at[1, b - 1], dp=dp ^ b)

    def gate_copy(b):
        return remote(slot_ref.at[0, dp ^ b], gate_out.at[dp], g_sems.at[0, b - 1], g_sems.at[1, b - 1], dp=dp ^ b)

    def own_row():
        return pltpu.make_async_copy(send_ref.at[0, dp], row_out.at[dp], own_sems.at[0])

    def own_gate():
        return pltpu.make_async_copy(slot_ref.at[0, dp], gate_out.at[dp], own_sems.at[1])

    def attention(s):
        mask_ref[...] = jnp.where(idk_ref[s] <= idq_ref[s], 0.0, MASKED)

        def pair(p, carry):
            lanes = pl.ds(pl.multiple_of(p * 2 * HD, 2 * HD), 2 * HD)
            queries = q_ref[s, :, lanes]
            keys = k_ref[s, :, lanes]
            values_t = v_ref[s, :, lanes].T
            low_half = lax.broadcasted_iota(jnp.int32, queries.shape, 1) < HD
            zero = jnp.zeros_like(queries)
            parts = []
            for head in range(2):
                own = jnp.where(low_half, queries, zero) if head == 0 else jnp.where(low_half, zero, queries)
                scores = dot_nt(keys, own) + bias_ref[2 * p + head].astype(F32) + mask_ref[...]
                top = jnp.max(scores, axis=0, keepdims=True)
                weights = jnp.exp(scores - top)
                total = jnp.sum(weights, axis=0, keepdims=True)
                part = dot(values_t[head * HD : (head + 1) * HD], weights.astype(BF16)) * (1.0 / total)
                parts.append(part)
                lse_ref[s, p, head : head + 1, :] = top + jnp.log(total)
            att_ref[s, :, lanes] = jnp.concatenate(parts, axis=0).T.astype(BF16)
            return carry

        lax.fori_loop(0, pairs, pair, 0)
        att_copy(s).start()

    def middle(s):
        att_copy(s).wait_recv()
        mid = x_ref[s].astype(F32) + (dot(att_ref[s], wout_ref[...]) + dot(att_other[s], wout_other[...]))
        mid_ref[s] = mid
        moe_in = (mid * norm_factor(mid) * gain_ref[...].astype(F32)).astype(BF16)
        moe_ref[s] = moe_in
        logits = dot_nt(router_ref[...], moe_in)
        hit = hits_ref[s] > 0.5
        top = jnp.max(jnp.where(hit, logits, MASKED), axis=0, keepdims=True)
        raw = jnp.where(hit, jnp.exp(jnp.where(hit, logits, top) - top), 0.0)
        gates = raw / jnp.sum(raw, axis=0, keepdims=True)
        gates_ref[s] = gates
        picks = one_hot(place_ref[s], cap)
        pick = jnp.concatenate([jnp.where(p, 1.0, 0.0).astype(BF16) for p in picks], axis=0)
        send_ref[s] = dot(pick, moe_in).astype(BF16).reshape(groups, cap, width)
        eye = diagonal(cap)
        for group in range(groups):
            column = jnp.sum(jnp.where(picks[group], gates[group : group + 1, :], 0.0), axis=1, keepdims=True)
            slot_ref[s, group] = jnp.sum(jnp.where(eye, column, 0.0), axis=0, keepdims=True)

    def main(s, carry):
        attention(s)

        @pl.when(s == 1)
        def _():
            wout_copy.wait_recv()

        @pl.when(s > 0)
        def _():
            middle(s - 1)

        @pl.when(s == 1)
        def _():
            for b in order:
                gate_copy(b).start()
                row_copy(b).start()
            own_row().start()
            own_gate().start()

        return carry

    lax.fori_loop(0, seqs, main, 0)
    middle(seqs - 1)
    for b in order:
        gate_copy(b).wait()
        row_copy(b).wait()
    own_row().wait()
    own_gate().wait()
    for copy in [far_copy] + cot_copies:
        copy.wait()
    wout_copy.wait_send()
    for s in range(seqs):
        att_copy(s).wait_send()


def front_stage(got, cot, q, k, v, windows, ids_query, ids_key, x, wout, gain, router, hits, places, cap):
    seqs, stretch, width = x.shape
    groups = places.shape[1]
    local = q.shape[2]
    length = k.shape[1]
    pairs = local // (2 * HD)
    experts_n = router.shape[0]
    any_spec = pl.BlockSpec(memory_space=pl.ANY)
    vmem = pl.BlockSpec(memory_space=pltpu.VMEM)
    dma = pltpu.SemaphoreType.DMA
    return pl.pallas_call(
        functools.partial(front_kernel, seqs, groups, cap),
        name="front_stage",
        in_specs=[any_spec] * 2 + [vmem] * 12,
        out_specs=[any_spec] * 3 + [vmem] * 9,
        out_shape=[
            jax.ShapeDtypeStruct(got.shape, BF16),
            jax.ShapeDtypeStruct((groups - 1, cap, width), BF16),
            jax.ShapeDtypeStruct((groups, cap, width), BF16),
            jax.ShapeDtypeStruct((groups, 1, cap), F32),
            jax.ShapeDtypeStruct((2 * pairs, length, stretch), BF16),
            jax.ShapeDtypeStruct((seqs, stretch, local), BF16),
            jax.ShapeDtypeStruct((seqs, pairs, 2, stretch), F32),
            jax.ShapeDtypeStruct((seqs, stretch, width), F32),
            jax.ShapeDtypeStruct((seqs, stretch, width), BF16),
            jax.ShapeDtypeStruct((seqs, experts_n, stretch), F32),
            jax.ShapeDtypeStruct((seqs, groups, cap, width), BF16),
            jax.ShapeDtypeStruct((seqs, groups, 1, cap), F32),
        ],
        scratch_shapes=[
            pltpu.VMEM((local, width), BF16),
            pltpu.VMEM((seqs, stretch, local), BF16),
            pltpu.VMEM((length, stretch), F32),
            dma((2, 2)), dma((2, seqs)), dma((2, groups - 1)), dma((2, groups - 1)), dma((2, groups - 1)), dma((2,)),
        ],
        compiler_params=pltpu.CompilerParams(vmem_limit_bytes=VMEM_BYTES, collective_id=4, has_side_effects=True),
        cost_estimate=cost(4 * 10**10, 10**7),
    )(got, cot, q, k, v, windows, ids_query, ids_key, x, wout, gain, router, hits, places)


def moe_kernel(
    seqs, groups, cap, tile, *refs,
):
    send_ref, slot_ref, row_ref, gate_ref, slots_ref, cot_ref, last_ref = refs[:7]
    refs = refs[7:]
    w_own, w_far, part_out, din_back, h_back, keep_out, give_out = (refs[:2], refs[2:4]) + refs[4:9]
    (
        w_all, x_all, gate_all, g_all, xt_all, dyt_all, dy_ref, hid_all, dpre_all, part_acc, din_acc,
        part_all, din_all, h_all, tile_ref,
        x_sems, gate_sems, din_sems, h_sems, w_sems, own_sems, cot_sems, part_sems, out_sems, core_sems,
    ) = refs[9:]
    dp = lax.axis_index("dp")
    ctx = lax.axis_index("ctx")
    greet([{"dp": dp ^ b} for b in range(1, groups)] + [{"ctx": ctx ^ 1}])
    width = x_all.shape[-1]
    rows = groups * cap
    slices = w_all.shape[2]
    piece = width // slices
    half_len = w_all.shape[4]
    per_half = half_len // tile
    tiles = w_all.shape[1] * per_half
    order = tuple(range(groups - 1, 0, -1))

    sent = []
    for s in range(1, seqs):
        for b in order:
            sent.append(
                remote(send_ref.at[s, dp ^ b], x_all.at[s, dp], x_sems.at[0, s, b - 1], x_sems.at[1, s, b - 1], dp=dp ^ b)
            )
            sent.append(
                remote(
                    slot_ref.at[s, dp ^ b], gate_all.at[s, dp],
                    gate_sems.at[0, s, b - 1], gate_sems.at[1, s, b - 1], dp=dp ^ b,
                )
            )
    w_copies = []
    local = []
    arrivals = []
    for half in range(2):
        for index, (ref, place) in enumerate(((w_own[half], ctx), (w_far[half], ctx ^ 2))):
            sems = (w_sems.at[0, half, index], w_sems.at[1, half, index])
            w_copies.append(remote(ref, w_all.at[:, half, place], *sems, ctx=ctx ^ 1))
            there = w_all.at[:, half, place ^ 1]
            arrivals.append(remote(there, there, *sems, ctx=ctx ^ 1))
            local.append(pltpu.make_async_copy(ref, w_all.at[:, half, place], w_sems.at[2, half, index]))
    for copy in w_copies + sent:
        copy.start()
    local.append(pltpu.make_async_copy(row_ref, x_all.at[0], own_sems.at[0]))
    local.append(pltpu.make_async_copy(gate_ref, gate_all.at[0], own_sems.at[1]))
    for s in range(1, seqs):
        local.append(pltpu.make_async_copy(send_ref.at[s, dp], x_all.at[s, dp], own_sems.at[2 * s]))
        local.append(pltpu.make_async_copy(slot_ref.at[s, dp], gate_all.at[s, dp], own_sems.at[1 + 2 * s]))
    local.append(pltpu.make_async_copy(slots_ref.at[0], g_all.at[dp], cot_sems.at[0, 0]))
    for b in range(1, groups):
        local.append(
            pltpu.make_async_copy(cot_ref.at[b - 1], g_all.at[dp ^ b, pl.ds(0, seqs - 1)], cot_sems.at[0, b])
        )
        local.append(pltpu.make_async_copy(last_ref.at[b - 1], g_all.at[dp ^ b, seqs - 1], cot_sems.at[1, b]))
    for copy in local:
        copy.start()
    for copy in local:
        copy.wait()
    for copy in arrivals:
        copy.wait_recv()
    eye = diagonal(cap)

    def weights(io, f):
        lanes = pl.ds(pl.multiple_of((f % per_half) * tile, tile), tile)
        return w_all[io, f // per_half, :, :, lanes].reshape(width, tile)

    def gate_column(s, group):
        return jnp.sum(jnp.where(eye, gate_all[s, group], 0.0), axis=1, keepdims=True)

    def din_copy(s, b):
        return remote(
            din_all.at[s, dp ^ b], din_back.at[s, dp], din_sems.at[0, s, b - 1], din_sems.at[1, s, b - 1], dp=dp ^ b
        )

    def h_copy(s, b):
        return remote(h_all.at[s, dp ^ b], h_back.at[s, dp], h_sems.at[0, s, b - 1], h_sems.at[1, s, b - 1], dp=dp ^ b)

    def part_copy(s, b):
        return pltpu.make_async_copy(part_all.at[s, dp ^ b], part_out.at[b, s], part_sems.at[s, b])

    def own_copies(s):
        return [
            pltpu.make_async_copy(din_all.at[s, dp], din_back.at[s, dp], part_sems.at[s, groups]),
            pltpu.make_async_copy(h_all.at[s, dp], h_back.at[s, dp], part_sems.at[s, groups + 1]),
        ]

    def chunk(s, carry):
        @pl.when(s > 0)
        def _():
            for b in order:
                there = x_all.at[s, dp ^ b]
                remote(there, there, x_sems.at[0, s, b - 1], x_sems.at[1, s, b - 1], dp=dp ^ b).wait_recv()
                there = gate_all.at[s, dp ^ b]
                remote(there, there, gate_sems.at[0, s, b - 1], gate_sems.at[1, s, b - 1], dp=dp ^ b).wait_recv()

        x = x_all[s].reshape(rows, width)
        xt_all[s] = x.T
        for group in range(groups):
            dy_ref[group * cap : (group + 1) * cap] = (g_all[group, s].astype(F32) * gate_column(s, group)).astype(BF16)
        dyt_all[s] = dy_ref[...].T
        part_acc[...] = jnp.zeros_like(part_acc)
        din_acc[...] = jnp.zeros_like(din_acc)

        def step(f, carry):
            x = x_all[s].reshape(rows, width)
            w_in = weights(0, f)
            w_out_t = weights(1, f)
            pre = dot(x, w_in)
            dhid = dot(dy_ref[...], w_out_t)
            square = pre * pre
            inner = jnp.tanh(GELU_C * pre * (1.0 + GELU_A * square))
            half = 0.5 * (1.0 + inner)
            hidden = (pre * half).astype(BF16)
            slope = half + (0.5 * GELU_C) * pre * (1.0 - inner * inner) * (1.0 + (3.0 * GELU_A) * square)
            dpre = (dhid * slope).astype(BF16)
            hid_all[f, s] = hidden
            dpre_all[f, s] = dpre
            part_acc[...] += dot_nt(hidden, w_out_t)
            din_acc[...] += dot_nt(dpre, w_in)
            return carry

        lax.fori_loop(0, tiles, step, 0)
        for group in range(groups):
            at = slice(group * cap, (group + 1) * cap)
            din_all[s, group] = din_acc[at].astype(BF16)
            gated = part_acc[at] * gate_column(s, group)
            part_all[s, group] = gated.astype(BF16)
            h = jnp.sum(gated * g_all[group, s].astype(F32), axis=1, keepdims=True)
            h_all[s, group] = jnp.sum(jnp.where(eye, h, 0.0), axis=0, keepdims=True)
        for b in order:
            din_copy(s, b).start()
            h_copy(s, b).start()
        for copy in own_copies(s):
            copy.start()
        for b in range(groups):
            part_copy(s, b).start()
        return carry

    lax.fori_loop(0, seqs, chunk, 0)

    def tile_of(ref, f):
        lanes = pl.ds(pl.multiple_of((f % per_half) * tile, tile), tile)
        return ref.at[f // per_half, :, :, :, lanes]

    def keep_copy(f, slot):
        return pltpu.make_async_copy(tile_ref.at[slot, 0], tile_of(keep_out, f), out_sems.at[slot, 0])

    def give_copy(f, slot):
        return remote(
            tile_ref.at[slot, 1], tile_of(give_out, f), out_sems.at[slot, 1], core_sems.at[f], ctx=ctx ^ 1
        )

    def weight_grads(f, carry):
        slot = f % 2

        @pl.when(f >= 2)
        def _():
            keep_copy(f - 2, slot).wait()
            give_copy(f - 2, slot).wait_send()

        for io, (left, right) in enumerate(((xt_all, dpre_all), (dyt_all, hid_all))):
            total = dot(left[0], right[f, 0])
            for s in range(1, seqs):
                total = total + dot(left[s], right[f, s])
            for index in range(slices):
                place = index ^ ctx
                tile_ref[slot, place % 2, place // 2, io] = total[index * piece : (index + 1) * piece].astype(BF16)
        keep_copy(f, slot).start()
        give_copy(f, slot).start()
        return carry

    lax.fori_loop(0, tiles, weight_grads, 0)
    for f in (tiles - 2, tiles - 1):
        keep_copy(f, f % 2).wait()
        give_copy(f, f % 2).wait_send()
    for f in range(tiles):
        give_copy(f, f % 2).wait_recv()
    for s in range(seqs):
        for b in order:
            there = din_back.at[s, dp ^ b]
            remote(there, there, din_sems.at[0, s, b - 1], din_sems.at[1, s, b - 1], dp=dp ^ b).wait_recv()
            there = h_back.at[s, dp ^ b]
            remote(there, there, h_sems.at[0, s, b - 1], h_sems.at[1, s, b - 1], dp=dp ^ b).wait_recv()
            din_copy(s, b).wait_send()
            h_copy(s, b).wait_send()
        for copy in own_copies(s):
            copy.wait()
        for b in range(groups):
            part_copy(s, b).wait()
    for copy in w_copies + sent:
        copy.wait_send()


def moe_stage(send, slot_gate, row, row_gate, slots, cot, last, keep, got, far_keep, far_got, tile=512):
    seqs, groups, cap, width = send.shape
    _, piece, half_len = keep.shape
    halves = 2
    slices = width // piece
    tiles = halves * half_len // tile
    rows = groups * cap
    any_spec = pl.BlockSpec(memory_space=pl.ANY)
    vmem = pl.BlockSpec(memory_space=pltpu.VMEM)
    dma = pltpu.SemaphoreType.DMA
    return pl.pallas_call(
        functools.partial(moe_kernel, seqs, groups, cap, tile),
        name="moe_stage",
        in_specs=[any_spec] * 11,
        out_specs=[any_spec, any_spec, vmem, any_spec, any_spec],
        out_shape=[
            jax.ShapeDtypeStruct((groups, seqs, cap, width), BF16),
            jax.ShapeDtypeStruct((seqs, groups, cap, width), BF16),
            jax.ShapeDtypeStruct((seqs, groups, 1, cap), F32),
            jax.ShapeDtypeStruct((halves, slices // 2, 2, piece, half_len), BF16),
            jax.ShapeDtypeStruct((halves, slices // 2, 2, piece, half_len), BF16),
        ],
        scratch_shapes=[
            pltpu.VMEM((2, halves, slices, piece, half_len), BF16),
            pltpu.VMEM((seqs, groups, cap, width), BF16),
            pltpu.VMEM((seqs, groups, 1, cap), F32),
            pltpu.VMEM((groups, seqs, cap, width), BF16),
            pltpu.VMEM((seqs, width, rows), BF16),
            pltpu.VMEM((seqs, width, rows), BF16),
            pltpu.VMEM((rows, width), BF16),
            pltpu.VMEM((tiles, seqs, rows, tile), BF16),
            pltpu.VMEM((tiles, seqs, rows, tile), BF16),
            pltpu.VMEM((rows, width), F32),
            pltpu.VMEM((rows, width), F32),
            pltpu.VMEM((seqs, groups, cap, width), BF16),
            pltpu.VMEM((seqs, groups, cap, width), BF16),
            pltpu.VMEM((seqs, groups, 1, cap), F32),
            pltpu.VMEM((2, 2, slices // 2, 2, piece, tile), BF16),
            dma((2, seqs, groups - 1)), dma((2, seqs, groups - 1)), dma((2, seqs, groups - 1)),
            dma((2, seqs, groups - 1)), dma((3, 2, 2)), dma((2 * seqs,)), dma((2, groups)), dma((seqs, groups + 2)),
            dma((2, 2)), dma((tiles,)),
        ],
        compiler_params=pltpu.CompilerParams(
            vmem_limit_bytes=63 * 1024 * 1024, collective_id=2, has_side_effects=True
        ),
        cost_estimate=cost(20 * seqs * rows * width * halves * half_len, 40 * width * halves * half_len),
    )(send, slot_gate, row, row_gate, slots, cot, last, keep, got, far_keep, far_got)


def flip(value, axis, bit):
    count = lax.axis_size(axis)
    return lax.ppermute(value, axis, [(i, i ^ bit) for i in range(count)])


def all_to_all_dp(value):
    return lax.all_to_all(value, "dp", split_axis=0, concat_axis=0, tiled=True)


def gathered(tokens, wqkv, wout, table, gain_attn, gain_moe, router):
    seqs, stretch, width = tokens.shape
    local = wqkv.shape[2]
    dp = lax.axis_size("dp")
    tp = lax.axis_index("tp")
    experts_n = router.shape[1]
    wqkv = lax.all_gather(wqkv, "dp", axis=1, tiled=True)
    wout = lax.all_gather(wout, "dp", axis=1, tiled=True)
    table = lax.all_gather(table, "dp", axis=0, tiled=True)
    gains = lax.all_gather(jnp.concatenate([gain_attn, gain_moe], axis=0), "dp", axis=1, tiled=True)
    gain_attn, gain_moe = gains[0:1].astype(F32), gains[1:2]
    router = lax.all_gather(router, "dp", axis=0, tiled=True).T.reshape(dp, 2, width).transpose(1, 0, 2)
    router = jnp.where(tp == 0, router, router[::-1]).reshape(experts_n, width)
    across = flip(tokens, "ctx", 2)
    beside, beyond = flip(jnp.stack([tokens, across]), "ctx", 1)
    x32 = jnp.stack([tokens, beside, across, beyond], axis=1).astype(F32)
    normed = (x32 * norm_factor(x32) * gain_attn[None, None]).astype(BF16)
    own = normed[:, 0].reshape(seqs * stretch, width)
    queries = jnp.dot(own, wqkv[0], preferred_element_type=F32).astype(BF16) * jnp.asarray(HD ** (-0.5), BF16)
    flat = normed.reshape(seqs * 4 * stretch, width)
    keys = jnp.dot(flat, wqkv[1], preferred_element_type=F32).astype(BF16).reshape(seqs, 4 * stretch, local)
    values = jnp.dot(flat, wqkv[2], preferred_element_type=F32).astype(BF16).reshape(seqs, 4 * stretch, local)
    return queries.reshape(seqs, stretch, local), keys, values, own, wqkv, wout, table, gain_attn, gain_moe, router


def on_device(
    tokens_in, block_ids, rel_buckets, routes, attn_gain, w_qkv, w_attn_out, bias_table, moe_gain, w_router,
    w_expert_in, w_expert_out, cotangent,
):
    seqs, stretch, width = tokens_in.shape
    dp = lax.axis_size("dp")
    ctx_count = lax.axis_size("ctx")
    tp_count = lax.axis_size("tp")
    expert_count = w_router.shape[2]
    assert w_expert_in.shape[1] == tp_count == 2 and ctx_count == 4
    cap = max(2, 2 * stretch * routes.shape[2] // expert_count)
    ctx = lax.axis_index("ctx")
    tp = lax.axis_index("tp")
    local = w_qkv.shape[3]
    heads = local // HD

    fits = dp == 4
    e_order = jnp.arange(expert_count, dtype=jnp.int32).reshape(dp, 2).T
    e_order = jnp.where(tp == 0, e_order, e_order[::-1]).reshape(1, expert_count, 1)
    hits = ((routes[:, None, :, 0] == e_order) | (routes[:, None, :, 1] == e_order)).astype(F32)
    before = (
        lax.broadcasted_iota(jnp.int32, (stretch, stretch), 0) < lax.broadcasted_iota(jnp.int32, (stretch, stretch), 1)
    ).astype(BF16)
    ranks = jnp.einsum("set,tu->seu", hits.astype(BF16), before, preferred_element_type=F32)
    places = jnp.where(hits > 0.5, ranks, -1.0)[:, :dp]

    pair = jnp.stack([w_expert_in[0], w_expert_out[0].transpose(0, 2, 1)], axis=1)

    if fits:
        me = lax.axis_index("dp")
        near_places = jnp.stack([lax.dynamic_index_in_dim(places, me ^ b, 1, keepdims=False) for b in range(dp)], axis=1)
        (
            queries, keys, values, own_normed, wqkv, wout_parts, table, gain_attn, gain_moe, router, got, far_keep,
            cot_slots, cot_in,
        ) = first_stage(
            tokens_in, w_qkv[0], w_attn_out[0], bias_table[0], attn_gain, moe_gain, w_router[0], pair,
            near_places, cotangent, cap,
        )
        keep = lax.dynamic_index_in_dim(pair, tp, 0, keepdims=False)
        wout_own = wout_parts.transpose(1, 0, 2).reshape(local, width)
        table = table.reshape(NB, heads)
        keys = keys.reshape(seqs, 4 * stretch, local)
        values = values.reshape(seqs, 4 * stretch, local)
        own_normed = own_normed.reshape(seqs * stretch, width)
    else:
        queries, keys, values, own_normed, wqkv, wout_own, table, gain_attn, gain_moe, router = gathered(
            tokens_in, w_qkv[0], w_attn_out[0], bias_table[0], attn_gain, moe_gain, w_router[0]
        )
        keep = lax.dynamic_index_in_dim(pair, tp, 0, keepdims=False)
        got = flip(lax.dynamic_index_in_dim(pair, 1 - tp, 0, keepdims=False), "tp", 1)
        weights = lax.all_gather(jnp.stack([keep, got], axis=1), "ctx", axis=0, tiled=False)
        cot_slots = all_to_all_dp(dispatch(places, cotangent, cap))

    one_hot_bucket = (rel_buckets[:, None] == jnp.arange(NB, dtype=jnp.int32)[None, :]).astype(F32)
    one_hot_bucket = jnp.pad(one_hot_bucket, ((0, 1), (0, 0)))
    starts = [(ctx - (ctx ^ b)) * stretch + 3 * stretch for b in range(4)]
    hot_windows = jnp.stack([lax.dynamic_slice_in_dim(one_hot_bucket, s, 2 * stretch, 0) for s in starts])
    windows = jnp.einsum("bmn,nh->hbm", hot_windows, table.astype(F32), precision=FULL_PRECISION)

    ids = block_ids.reshape(seqs, 4, stretch)
    ids_pieces = [lax.dynamic_index_in_dim(ids, ctx ^ b, 1, keepdims=False) for b in range(4)]
    ids_query = ids_pieces[0].reshape(seqs, 1, stretch)
    ids_key = jnp.stack(ids_pieces, axis=1).reshape(seqs, 4 * stretch, 1)

    if fits:
        (
            far_got, cot_last, row, row_gate, bias, attended, lse, mids, moes, gates, send, slot_gate,
        ) = front_stage(
            got, cot_slots, queries, keys, values, windows, ids_query, ids_key, tokens_in, wout_own, gain_moe, router,
            hits, places, cap,
        )
        parts, returned_din, returned_h, kept, given = moe_stage(
            send, slot_gate, row, row_gate, cot_slots, cot_in, cot_last, keep, got, far_keep, far_got
        )
    else:
        bias = expand_bias(windows)
        wout_pair = jnp.stack([wout_own, flip(wout_own, "tp", 1)])
        attended, lse, mids, moes, gates, sends, slot_gates = [], [], [], [], [], [], []
        for s in range(seqs):
            att, stat = attend(queries[s], keys[s], values[s], bias, ids_query[s], ids_key[s])
            attended.append(att)
            lse.append(stat)
            mid, moe_in, gate, send, slot_gate = middle_stage(
                att, flip(att, "tp", 1), tokens_in[s], wout_pair, gain_moe, router, hits[s], places[s], cap
            )
            mids.append(mid)
            moes.append(moe_in)
            gates.append(gate)
            sends.append(send)
            slot_gates.append(slot_gate)
        attended = jnp.stack(attended)
        partials, returned_din, returned_h = [], [], []
        acc = None
        for s in range(seqs):
            received = all_to_all_dp(sends[s])
            received_gate = all_to_all_dp(slot_gates[s])
            part, din, h, acc = experts(received, cot_slots, s, received_gate, weights, acc, s == seqs - 1)
            returned_din.append(all_to_all_dp(din))
            returned_h.append(all_to_all_dp(h))
            partials.append(all_to_all_dp(part))
        kept, given = acc[:, 0::2], flip(acc[:, 1::2], "ctx", 1)

    beside_sum = kept.astype(F32) + given.astype(F32)
    far_sum = flip(beside_sum[:, 1].astype(BF16), "ctx", 2)

    hits_of = (heads, 4, 2 * stretch)
    if fits:
        tokens_out, gmid, dattn, grad_proj, gain_moe_grad, router_grad, rel_grad = back_stage(
            mids, moes, gates, lse, returned_din, parts, queries, keys, values, bias, cotangent, wout_own,
            returned_h, places, near_places, ids_query, ids_key, router, gain_moe,
        )
        far_sum, grad_proj = lax.optimization_barrier((far_sum, grad_proj))
        mine = beside_sum[:, 0] + far_sum.astype(F32)
        other = flip(mine[1].astype(BF16), "tp", 1)
        grad_proj = grad_proj.reshape(3, seqs * stretch, local)
        dattn = dattn.reshape(seqs * stretch, width)
        grad_table = jnp.einsum("bmn,hbm->nh", hot_windows, rel_grad.reshape(hits_of), precision=FULL_PRECISION)
        small = jnp.concatenate(
            [
                router_grad,
                jnp.pad(gain_moe_grad, ((0, 7), (0, 0))),
                jnp.pad(grad_table.T, ((0, 8 - heads), (0, width - NB))),
            ],
            axis=0,
        )
        wide, g_router, g_moe, g_attn, g_table, grad_tokens = last_stage(
            own_normed, grad_proj, dattn, attended.reshape(seqs * stretch, local), small, wqkv, gmid, tokens_in, gain_attn,
            dp, NB // dp, heads, expert_count,
        )
        other, wide = lax.optimization_barrier((other, wide))
        g_qkv = wide[:3]
        g_wout = wide[3].T
    else:
        mine = beside_sum[:, 0] + far_sum.astype(F32)
        other = flip(mine[1].astype(BF16), "tp", 1)
        tokens_out, gmids = [], []
        projections = []
        rel_grad = 0.0
        gain_moe_grad = 0.0
        router_grad = 0.0
        datts = []
        for s in range(seqs):
            out_own = combine_out(places[s], partials[s], cap)
            out_other = flip(out_own, "tp", 1)
            tokens_out.append((mids[s] + (out_own.astype(F32) + out_other.astype(F32))).astype(BF16))
            din_own, h_own = combine(places[s], returned_din[s], returned_h[s], cap)
            din_other = flip(din_own, "tp", 1)
            h_all = jnp.concatenate([h_own, flip(h_own, "tp", 1)], axis=0)
            gmid, datt, d_gain, d_router, dattn = middle_back(
                din_own, din_other, h_all, gates[s], router, moes[s], mids[s], gain_moe, cotangent[s], wout_own
            )
            datts.append(dattn)
            gmids.append(gmid)
            gain_moe_grad += d_gain
            router_grad += d_router
            dq, dk, dv, rel = attend_back(
                queries[s], keys[s], values[s], datt, bias, lse[s], ids_query[s], ids_key[s]
            )
            rel_grad += rel
            dkv = jnp.stack([dk, dv]).reshape(2, 4, stretch, local)
            near = dkv[:, 0::2].astype(F32) + flip(dkv[:, 1::2], "ctx", 1).astype(F32)
            full = near[:, 0] + flip(near[:, 1].astype(BF16), "ctx", 2).astype(F32)
            projections.append(jnp.concatenate([dq[None], full.astype(BF16)], axis=0))
        grad_proj = jnp.concatenate(projections, axis=1)
        dattn = jnp.concatenate(datts, axis=0)
        attended = attended.reshape(seqs * stretch, local)
        dnormed_part = jnp.einsum("jre,jde->rd", grad_proj, wqkv, preferred_element_type=F32)
        dnormed_own = dnormed_part.astype(BF16)
        dnormed = dnormed_own.astype(F32) + flip(dnormed_own, "tp", 1).astype(F32)
        own_x = tokens_in.reshape(seqs * stretch, width).astype(F32)
        factor = norm_factor(own_x)
        unit = own_x * factor
        scaled = dnormed * gain_attn
        dres = factor * (scaled - unit * jnp.mean(scaled * unit, axis=-1, keepdims=True))
        grad_tokens = jnp.concatenate(gmids, axis=0) + dres
        grad_table = jnp.einsum("bmn,hbm->nh", hot_windows, rel_grad.reshape(hits_of), precision=FULL_PRECISION)
        router_grad = router_grad.reshape(2, dp, width)
        router_grad = jnp.where(tp == 0, router_grad, router_grad[::-1])
        router_grad = router_grad.transpose(1, 0, 2).reshape(expert_count, width).T

        def reduced(value, dim):
            return lax.psum(lax.psum_scatter(value, "dp", scatter_dimension=dim, tiled=True), "ctx")

        g_attn = reduced(jnp.sum(dnormed * unit, axis=0)[None], 1)
        g_qkv = reduced(jnp.einsum("rd,jre->jde", own_normed, grad_proj, preferred_element_type=F32), 1)
        g_wout = reduced(jnp.einsum("re,rd->ed", attended, dattn, preferred_element_type=F32), 1)
        g_table = reduced(grad_table, 0)
        g_moe = reduced(gain_moe_grad, 1)
        g_router = reduced(router_grad, 0)
        tokens_out = jnp.stack(tokens_out)
    other = other.astype(F32)
    ordered = jnp.where(tp == 0, jnp.stack([mine[0], other]), jnp.stack([other, mine[0]]))
    grad_expert_in = ordered[:, 0]
    grad_expert_out = ordered[:, 1].transpose(0, 2, 1)
    return (
        tokens_out,
        grad_tokens.reshape(seqs, stretch, width),
        g_attn,
        g_qkv[None],
        g_wout[None],
        g_table[None],
        g_moe,
        g_router[None],
        grad_expert_in[None],
        grad_expert_out[None],
    )


def solution(mesh):
    return jax.shard_map(
        on_device,
        mesh=mesh,
        in_specs=(
            P("dp", "ctx", None),
            P("dp", None),
            P(),
            P("dp", "ctx", None),
            P(None, "dp"),
            P(None, None, "dp", "tp"),
            P(None, "tp", "dp"),
            P(None, "dp", "tp"),
            P(None, "dp"),
            P(None, "dp", None),
            P(None, "dp", "ctx", "tp"),
            P(None, "dp", "tp", "ctx"),
            P("dp", "ctx", None),
        ),
        out_specs=(
            P("dp", "ctx", None),
            P("dp", "ctx", None),
            P(None, "dp"),
            P(None, None, "dp", "tp"),
            P(None, "tp", "dp"),
            P(None, "dp", "tp"),
            P(None, "dp"),
            P(None, "dp", None),
            P(None, "dp", "ctx", "tp"),
            P(None, "dp", "tp", "ctx"),
        ),
        check_vma=False,
    )
```

```python
import functools

import jax
import jax.numpy as jnp
from jax import lax
from jax.experimental import pallas as pl
from jax.experimental.pallas import tpu as pltpu
from jax.sharding import PartitionSpec as P

HD = 64
NB = 32
EPSILON = 1e-06
FULL_PRECISION = lax.Precision.HIGHEST
MASKED = -1e30
BF16 = jnp.bfloat16
F32 = jnp.float32
EARLY = 50
FIRST = 1
VMEM_BYTES = 60 * 1024 * 1024
GELU_C = 0.7978845608028654
GELU_A = 0.044715


def params():
    return pltpu.CompilerParams(vmem_limit_bytes=VMEM_BYTES)


def cost(flops, nbytes, trans=0, scale=1):
    return pl.CostEstimate(
        flops=int(flops) // scale, bytes_accessed=int(nbytes) // scale, transcendentals=int(trans) // scale
    )


def dot(a, b):
    return lax.dot_general(a, b, (((1,), (0,)), ((), ())), preferred_element_type=F32)


def dot_nt(a, b):
    return lax.dot_general(a, b, (((1,), (1,)), ((), ())), preferred_element_type=F32)


def dot_tn(a, b):
    return lax.dot_general(a, b, (((0,), (0,)), ((), ())), preferred_element_type=F32)


def bias_kernel(win_ref, out_ref):
    for block in range(4):
        row = win_ref[0, block : block + 1, :]
        wide = jnp.broadcast_to(row, (256, 512))
        rolled = pltpu.roll(wide, 257, 1, stride=1, stride_axis=0)
        out_ref[0, block * 256 : (block + 1) * 256, :] = rolled[:, :256].astype(BF16)


def expand_bias(windows):
    heads = windows.shape[0]
    return pl.pallas_call(
        bias_kernel,
        name="expand_bias",
        grid=(heads,),
        in_specs=[pl.BlockSpec((1, 4, 512), lambda h: (h, 0, 0))],
        out_specs=pl.BlockSpec((1, 1024, 256), lambda h: (h, 0, 0)),
        out_shape=jax.ShapeDtypeStruct((heads, 1024, 256), BF16),
        compiler_params=params(),
        cost_estimate=cost(heads * 2 * 1024 * 512, heads * 1024 * 256 * 2, scale=EARLY),
    )(windows)


def attend_kernel(q_ref, k_ref, v_ref, bias_ref, idq_ref, idk_ref, out_ref, lse_ref, mask_ref):
    @pl.when(pl.program_id(0) == 0)
    def _():
        mask_ref[...] = jnp.where(idk_ref[...] <= idq_ref[...], 0.0, MASKED)

    queries = q_ref[...]
    keys = k_ref[...]
    values_t = v_ref[...].T
    low_half = lax.broadcasted_iota(jnp.int32, queries.shape, 1) < HD
    zero = jnp.zeros_like(queries)
    parts = []
    for head in range(2):
        own = jnp.where(low_half, queries, zero) if head == 0 else jnp.where(low_half, zero, queries)
        scores = dot_nt(keys, own) + bias_ref[head].astype(F32) + mask_ref[...]
        top = jnp.max(scores, axis=0, keepdims=True)
        weights = jnp.exp(scores - top)
        total = jnp.sum(weights, axis=0, keepdims=True)
        part = dot(values_t[head * HD : (head + 1) * HD], weights.astype(BF16)) * (1.0 / total)
        parts.append(part)
        lse_ref[0, head : head + 1, :] = top + jnp.log(total)
    out_ref[...] = jnp.concatenate(parts, axis=0).T.astype(BF16)


def attend(queries, keys, values, bias, ids_query, ids_key):
    rows, width = queries.shape
    length = keys.shape[0]
    pairs = width // (2 * HD)
    return pl.pallas_call(
        attend_kernel,
        name="attend",
        grid=(pairs,),
        in_specs=[
            pl.BlockSpec((rows, 128), lambda p: (0, p)),
            pl.BlockSpec((length, 128), lambda p: (0, p)),
            pl.BlockSpec((length, 128), lambda p: (0, p)),
            pl.BlockSpec((2, length, rows), lambda p: (p, 0, 0)),
            pl.BlockSpec((1, rows), lambda p: (0, 0)),
            pl.BlockSpec((length, 1), lambda p: (0, 0)),
        ],
        out_specs=[
            pl.BlockSpec((rows, 128), lambda p: (0, p)),
            pl.BlockSpec((1, 2, rows), lambda p: (p, 0, 0)),
        ],
        out_shape=[
            jax.ShapeDtypeStruct((rows, width), BF16),
            jax.ShapeDtypeStruct((pairs, 2, rows), F32),
        ],
        scratch_shapes=[pltpu.VMEM((length, rows), F32)],
        compiler_params=params(),
        cost_estimate=cost(pairs * 2 * 4 * rows * length * 128, 6 * rows * length * 2, pairs * 2 * rows * length, scale=EARLY),
    )(queries, keys, values, bias, ids_query, ids_key)


def attend_back_kernel(
    q_ref, k_ref, v_ref, do_ref, bias_ref, lse_ref, idq_ref, idk_ref, dq_ref, dk_ref, dv_ref, rel_ref, mask_ref
):
    @pl.when(pl.program_id(0) == 0)
    def _():
        mask_ref[...] = jnp.where(idk_ref[...] <= idq_ref[...], 0.0, MASKED)

    queries = q_ref[...]
    keys = k_ref[...]
    values = v_ref[...]
    grad_out = do_ref[...]
    keys_t = keys.T
    low_half = lax.broadcasted_iota(jnp.int32, queries.shape, 1) < HD
    zero = jnp.zeros_like(queries)
    dk = None
    dv = None
    dq_parts = []
    for head in range(2):
        own = (lambda a: jnp.where(low_half, a, zero)) if head == 0 else (lambda a: jnp.where(low_half, zero, a))
        q_own = own(queries)
        do_own = own(grad_out)
        scores = dot_nt(keys, q_own) + bias_ref[head].astype(F32) + mask_ref[...]
        probs = jnp.exp(scores - lse_ref[0, head : head + 1, :])
        dprobs = dot_nt(values, do_own)
        delta = jnp.sum(probs * dprobs, axis=0, keepdims=True)
        dscores = probs * (dprobs - delta)
        low = dscores.astype(BF16)
        dv_head = dot(probs.astype(BF16), do_own)
        dk_head = dot(low, q_own)
        dv = dv_head if dv is None else dv + dv_head
        dk = dk_head if dk is None else dk + dk_head
        dq_parts.append(dot(keys_t[head * HD : (head + 1) * HD], low))
        for block in range(4):
            tile = dscores[block * 256 : (block + 1) * 256]
            wide = jnp.concatenate([tile, jnp.zeros_like(tile)], axis=1)
            total = None
            for group in range(32):
                moved = pltpu.roll(wide[group * 8 : group * 8 + 8], 248 - 8 * group, 1)
                total = moved if total is None else total + moved
            row = lax.broadcasted_iota(jnp.int32, total.shape, 0)
            amount = 7 - row
            for bit in (1, 2, 4):
                total = jnp.where((amount & bit) != 0, pltpu.roll(total, bit, 1), total)
            rel_ref[0, head, block : block + 1, :] = jnp.sum(total, axis=0, keepdims=True)
    dq_ref[...] = (jnp.concatenate(dq_parts, axis=0).T * (HD ** (-0.5))).astype(BF16)
    dk_ref[...] = dk.astype(BF16)
    dv_ref[...] = dv.astype(BF16)


def attend_back(queries, keys, values, grad_out, bias, lse, ids_query, ids_key):
    rows, width = queries.shape
    length = keys.shape[0]
    pairs = width // (2 * HD)
    return pl.pallas_call(
        attend_back_kernel,
        name="attend_back",
        grid=(pairs,),
        in_specs=[
            pl.BlockSpec((rows, 128), lambda p: (0, p)),
            pl.BlockSpec((length, 128), lambda p: (0, p)),
            pl.BlockSpec((length, 128), lambda p: (0, p)),
            pl.BlockSpec((rows, 128), lambda p: (0, p)),
            pl.BlockSpec((2, length, rows), lambda p: (p, 0, 0)),
            pl.BlockSpec((1, 2, rows), lambda p: (p, 0, 0)),
            pl.BlockSpec((1, rows), lambda p: (0, 0)),
            pl.BlockSpec((length, 1), lambda p: (0, 0)),
        ],
        out_specs=[
            pl.BlockSpec((rows, 128), lambda p: (0, p)),
            pl.BlockSpec((length, 128), lambda p: (0, p)),
            pl.BlockSpec((length, 128), lambda p: (0, p)),
            pl.BlockSpec((1, 2, 4, 512), lambda p: (p, 0, 0, 0)),
        ],
        out_shape=[
            jax.ShapeDtypeStruct((rows, width), BF16),
            jax.ShapeDtypeStruct((length, width), BF16),
            jax.ShapeDtypeStruct((length, width), BF16),
            jax.ShapeDtypeStruct((pairs, 2, 4, 512), F32),
        ],
        scratch_shapes=[pltpu.VMEM((length, rows), F32)],
        compiler_params=params(),
        cost_estimate=cost(pairs * 2 * 10 * rows * length * 128, 8 * rows * length * 2, pairs * 2 * rows * length),
    )(queries, keys, values, grad_out, bias, lse, ids_query, ids_key)


def one_hot(place, cap):
    groups, rows = place.shape
    slots = lax.broadcasted_iota(jnp.int32, (cap, rows), 0).astype(F32)
    return [slots == place[group : group + 1, :] for group in range(groups)]


def diagonal(cap):
    return lax.broadcasted_iota(jnp.int32, (cap, cap), 0) == lax.broadcasted_iota(jnp.int32, (cap, cap), 1)


def dispatch_kernel(groups, cap, place_ref, rows_ref, out_ref):
    rows = rows_ref[0]
    picks = one_hot(place_ref[0], cap)
    pick = jnp.concatenate([jnp.where(p, 1.0, 0.0).astype(BF16) for p in picks], axis=0)
    out_ref[:, 0] = dot(pick, rows).astype(BF16).reshape(groups, cap, rows.shape[1])


def dispatch(place, rows, cap):
    seqs, groups, stretch = place.shape
    width = rows.shape[2]
    return pl.pallas_call(
        functools.partial(dispatch_kernel, groups, cap),
        name="dispatch_rows",
        grid=(seqs,),
        in_specs=[
            pl.BlockSpec((1, groups, stretch), lambda s: (s, 0, 0)),
            pl.BlockSpec((1, stretch, width), lambda s: (s, 0, 0)),
        ],
        out_specs=pl.BlockSpec((groups, 1, cap, width), lambda s: (0, s, 0, 0)),
        out_shape=jax.ShapeDtypeStruct((groups, seqs, cap, width), BF16),
        compiler_params=params(),
        cost_estimate=cost(seqs * 2 * groups * cap * stretch * width, seqs * 2 * (stretch + groups * cap) * width),
    )(place, rows)


def norm_factor(value):
    return lax.rsqrt(jnp.mean(value * value, axis=-1, keepdims=True) + EPSILON)


def middle_kernel(
    groups, cap, own_ref, other_ref, x_ref, wout_ref, gain_ref, router_ref, hits_ref, place_ref,
    middle_ref, moe_ref, gates_ref, send_ref, slot_gate_ref,
):
    mid = x_ref[...].astype(F32) + (dot(own_ref[...], wout_ref[0]) + dot(other_ref[...], wout_ref[1]))
    middle_ref[...] = mid
    moe_in = (mid * norm_factor(mid) * gain_ref[...].astype(F32)).astype(BF16)
    moe_ref[...] = moe_in
    logits = dot_nt(router_ref[...], moe_in)
    hit = hits_ref[...] > 0.5
    top = jnp.max(jnp.where(hit, logits, MASKED), axis=0, keepdims=True)
    raw = jnp.where(hit, jnp.exp(jnp.where(hit, logits, top) - top), 0.0)
    gates = raw / jnp.sum(raw, axis=0, keepdims=True)
    gates_ref[...] = gates
    picks = one_hot(place_ref[...], cap)
    pick = jnp.concatenate([jnp.where(p, 1.0, 0.0).astype(BF16) for p in picks], axis=0)
    send_ref[...] = dot(pick, moe_in).astype(BF16).reshape(groups, cap, moe_in.shape[1])
    eye = diagonal(cap)
    for group in range(groups):
        column = jnp.sum(jnp.where(picks[group], gates[group : group + 1, :], 0.0), axis=1, keepdims=True)
        slot_gate_ref[group] = jnp.sum(jnp.where(eye, column, 0.0), axis=0, keepdims=True)


def middle_stage(own, other, x, wout, gain, router, hits, place, cap):
    rows, width = x.shape
    experts = router.shape[0]
    groups = place.shape[0]
    return pl.pallas_call(
        functools.partial(middle_kernel, groups, cap),
        name="middle_stage",
        out_shape=[
            jax.ShapeDtypeStruct((rows, width), F32),
            jax.ShapeDtypeStruct((rows, width), BF16),
            jax.ShapeDtypeStruct((experts, rows), F32),
            jax.ShapeDtypeStruct((groups, cap, width), BF16),
            jax.ShapeDtypeStruct((groups, 1, cap), F32),
        ],
        compiler_params=params(),
        cost_estimate=cost(2 * rows * width * width + 2 * groups * cap * rows * width, rows * width * 16, scale=EARLY),
    )(own, other, x, wout, gain, router, hits, place)


def expert_kernel(
    first, final, tiles, groups, cap, x_ref, g_ref, gate_ref, w_ref, *refs
):
    if first:
        acc_in = None
    else:
        acc_in, refs = refs[0], refs[1:]
    part_out, din_out, h_out, acc_out, xt_ref, dy_ref, dyt_ref, part_ref, din_ref = refs
    step = pl.program_id(0)
    rows = groups * cap
    width = x_ref.shape[-1]
    slices = w_ref.shape[0]
    piece = width // slices

    @pl.when(step == 0)
    def _():
        eye = diagonal(cap)
        xt_ref[...] = x_ref[...].reshape(rows, width).T
        for group in range(groups):
            gate = jnp.sum(jnp.where(eye, gate_ref[group], 0.0), axis=1, keepdims=True)
            dy_ref[group * cap : (group + 1) * cap] = (g_ref[group, 0].astype(F32) * gate).astype(BF16)
        dyt_ref[...] = dy_ref[...].T

    x = x_ref[...].reshape(rows, width)
    w_in = w_ref[:, 0, 0].reshape(width, -1)
    w_out_t = w_ref[:, 1, 0].reshape(width, -1)
    dy = dy_ref[...]
    pre = dot(x, w_in)
    square = pre * pre
    inner = jnp.tanh(GELU_C * pre * (1.0 + GELU_A * square))
    half = 0.5 * (1.0 + inner)
    hidden = (pre * half).astype(BF16)
    slope = half + (0.5 * GELU_C) * pre * (1.0 - inner * inner) * (1.0 + (3.0 * GELU_A) * square)
    dhid = dot(dy, w_out_t)
    dpre = (dhid * slope).astype(BF16)
    part = dot_nt(hidden, w_out_t)
    din = dot_nt(dpre, w_in)
    dw_in = dot(xt_ref[...], dpre)
    dw_out_t = dot(dyt_ref[...], hidden)

    @pl.when(step == 0)
    def _():
        part_ref[...] = part
        din_ref[...] = din

    @pl.when(step > 0)
    def _():
        part_ref[...] += part
        din_ref[...] += din

    me = lax.axis_index("ctx")
    for index in range(slices):
        place = index ^ me
        grad_in = dw_in[index * piece : (index + 1) * piece]
        grad_out = dw_out_t[index * piece : (index + 1) * piece]
        if not first:
            grad_in += acc_in[0, place, 0]
            grad_out += acc_in[0, place, 1]
        acc_out[0, place, 0] = grad_in.astype(acc_out.dtype)
        acc_out[0, place, 1] = grad_out.astype(acc_out.dtype)

    @pl.when(step == tiles - 1)
    def _():
        eye = diagonal(cap)
        for group in range(groups):
            gate = jnp.sum(jnp.where(eye, gate_ref[group], 0.0), axis=1, keepdims=True)
            gated = part_ref[group * cap : (group + 1) * cap] * gate
            part_out[group] = gated.astype(BF16)
            din_out[group] = din_ref[group * cap : (group + 1) * cap].astype(BF16)
            h = jnp.sum(gated * g_ref[group, 0].astype(F32), axis=1, keepdims=True)
            h_out[group] = jnp.sum(jnp.where(eye, h, 0.0), axis=0, keepdims=True)


def experts(x, cot_slots, seq_index, gate, weights, acc, final, tile=512):
    groups, cap, width = x.shape
    slices, _, halves, piece, half_len = weights.shape
    per_half = half_len // tile
    tiles = halves * per_half
    rows = groups * cap
    first = acc is None
    acc_spec = pl.BlockSpec((1, slices, 2, piece, tile), lambda f: (f // per_half, 0, 0, 0, f % per_half))
    in_specs = [
        pl.BlockSpec((groups, cap, width), lambda f: (0, 0, 0)),
        pl.BlockSpec((groups, 1, cap, width), lambda f: (0, seq_index, 0, 0)),
        pl.BlockSpec((groups, 1, cap), lambda f: (0, 0, 0)),
        pl.BlockSpec((slices, 2, 1, piece, tile), lambda f: (0, 0, f // per_half, 0, f % per_half)),
    ]
    args = [x, cot_slots, gate, weights]
    aliases = {}
    if not first:
        in_specs.append(acc_spec)
        args.append(acc)
        if not final:
            aliases = {4: 3}
    acc_shape = (halves, slices, 2, piece, half_len)
    return pl.pallas_call(
        functools.partial(expert_kernel, first, final, tiles, groups, cap),
        name="experts",
        grid=(tiles,),
        in_specs=in_specs,
        out_specs=[
            pl.BlockSpec((groups, cap, width), lambda f: (0, 0, 0)),
            pl.BlockSpec((groups, cap, width), lambda f: (0, 0, 0)),
            pl.BlockSpec((groups, 1, cap), lambda f: (0, 0, 0)),
            acc_spec,
        ],
        out_shape=[
            jax.ShapeDtypeStruct((groups, cap, width), BF16),
            jax.ShapeDtypeStruct((groups, cap, width), BF16),
            jax.ShapeDtypeStruct((groups, 1, cap), F32),
            jax.ShapeDtypeStruct(acc_shape, BF16 if final else F32),
        ],
        scratch_shapes=[
            pltpu.VMEM((width, rows), BF16),
            pltpu.VMEM((rows, width), BF16),
            pltpu.VMEM((width, rows), BF16),
            pltpu.VMEM((rows, width), F32),
            pltpu.VMEM((rows, width), F32),
        ],
        input_output_aliases=aliases,
        compiler_params=params(),
        cost_estimate=cost(12 * rows * width * halves * half_len, 2 * width * halves * half_len * 10, rows * halves * half_len),
    )(*args)


def combine_kernel(groups, cap, place_ref, din_ref, h_ref, din_out, h_out):
    picks = one_hot(place_ref[...], cap)
    pick = jnp.concatenate([jnp.where(p, 1.0, 0.0).astype(BF16) for p in picks], axis=0)
    rows = groups * cap
    din_out[...] = dot_tn(pick, din_ref[...].reshape(rows, din_ref.shape[-1])).astype(BF16)
    eye = diagonal(cap)
    for group in range(groups):
        column = jnp.sum(jnp.where(eye, h_ref[group], 0.0), axis=1, keepdims=True)
        h_out[group : group + 1, :] = jnp.sum(jnp.where(picks[group], column, 0.0), axis=0, keepdims=True)


def combine(place, din, h, cap):
    groups, stretch = place.shape
    width = din.shape[-1]
    return pl.pallas_call(
        functools.partial(combine_kernel, groups, cap),
        name="combine_back",
        out_shape=[
            jax.ShapeDtypeStruct((stretch, width), BF16),
            jax.ShapeDtypeStruct((groups, stretch), F32),
        ],
        compiler_params=params(),
        cost_estimate=cost(2 * groups * cap * stretch * width, 4 * stretch * width * 2),
    )(place, din, h)


def combine_out_kernel(groups, cap, place_ref, part_ref, out_ref):
    picks = one_hot(place_ref[...], cap)
    pick = jnp.concatenate([jnp.where(p, 1.0, 0.0).astype(BF16) for p in picks], axis=0)
    out_ref[...] = dot_tn(pick, part_ref[...].reshape(groups * cap, part_ref.shape[-1])).astype(BF16)


def combine_out(place, part, cap):
    groups, stretch = place.shape
    width = part.shape[-1]
    return pl.pallas_call(
        functools.partial(combine_out_kernel, groups, cap),
        name="combine_out",
        out_shape=jax.ShapeDtypeStruct((stretch, width), BF16),
        compiler_params=params(),
        cost_estimate=cost(2 * groups * cap * stretch * width, 4 * stretch * width * 2),
    )(place, part)


def middle_back_kernel(
    own_ref, other_ref, h_ref, gates_ref, router_ref, moe_ref, mid_ref, gain_ref, cot_ref, wout_ref,
    gmid_ref, datt_ref, gain_grad_ref, router_grad_ref, low_ref,
):
    h = h_ref[...]
    dlogits = h - gates_ref[...] * jnp.sum(h, axis=0, keepdims=True)
    router = router_ref[...]
    dmoe = own_ref[...].astype(F32) + other_ref[...].astype(F32)
    dmoe = dmoe + lax.dot_general(
        dlogits, router.astype(F32), (((0,), (0,)), ((), ())), precision=FULL_PRECISION, preferred_element_type=F32
    )
    router_grad_ref[...] = lax.dot_general(
        dlogits, moe_ref[...].astype(F32), (((1,), (0,)), ((), ())), precision=FULL_PRECISION, preferred_element_type=F32
    )
    mid = mid_ref[...]
    gain = gain_ref[...].astype(F32)
    factor = norm_factor(mid)
    normed = mid * factor
    gain_grad_ref[...] = jnp.sum(dmoe * normed, axis=0, keepdims=True)
    scaled = dmoe * gain
    dmid = factor * (scaled - normed * jnp.mean(scaled * normed, axis=-1, keepdims=True))
    gmid = cot_ref[...].astype(F32) + dmid
    gmid_ref[...] = gmid
    dattn = gmid.astype(BF16)
    datt_ref[...] = dot_nt(dattn, wout_ref[...]).astype(BF16)
    low_ref[...] = dattn


def middle_back(own, other, h, gates, router, moe_in, mid, gain, cot, wout):
    rows, width = mid.shape
    local = wout.shape[0]
    return pl.pallas_call(
        middle_back_kernel,
        name="middle_back",
        out_shape=[
            jax.ShapeDtypeStruct((rows, width), F32),
            jax.ShapeDtypeStruct((rows, local), BF16),
            jax.ShapeDtypeStruct((1, width), F32),
            jax.ShapeDtypeStruct(router.shape, F32),
            jax.ShapeDtypeStruct((rows, width), BF16),
        ],
        compiler_params=params(),
        cost_estimate=cost(2 * rows * width * local, 30 * rows * width),
    )(own, other, h, gates, router, moe_in, mid, gain, cot, wout)


MESH_ID = pl.DeviceIdType.MESH


def remote(src, dst, send_sem, recv_sem, **where):
    return pltpu.make_async_remote_copy(
        src_ref=src, dst_ref=dst, send_sem=send_sem, recv_sem=recv_sem, device_id=where, device_id_type=MESH_ID
    )


def greet(peers):
    barrier = pltpu.get_barrier_semaphore()
    for where in peers:
        pl.semaphore_signal(barrier, inc=1, device_id=where, device_id_type=MESH_ID)
    pl.semaphore_wait(barrier, len(peers))


def first_kernel(
    seqs, cap, tok_ref, wqkv_ref, wout_ref, table_ref, ga_ref, gm_ref, router_ref, pair_ref, near_ref, cot_ref,
    q_ref, k_ref, v_ref, normed_ref, wqkv_out, wout_out, table_out, gain_ref, gm_out, router_out, got_out,
    slots_ref, cot_out,
    tok_all, n_all, ga_all, gm_all, router_all,
    z_send, z_recv, f_send, f_recv, t_send, t_recv, y_send, y_recv, l_sem, e_sems, c_sems, wout_all,
):
    dp = lax.axis_index("dp")
    ctx = lax.axis_index("ctx")
    tp = lax.axis_index("tp")
    core = ctx % 2
    rows = wqkv_ref.shape[1]
    half = rows // 2
    orows = wout_ref.shape[0] // 2
    greet([{"dp": dp ^ b} for b in (1, 2, 3)] + [{"ctx": ctx ^ 1}, {"ctx": ctx ^ 2}, {"tp": tp ^ 1}])

    def w_rows(owner, side):
        return pl.ds(pl.multiple_of(owner * rows + side * half, 16), half)

    def o_rows(side):
        return pl.ds(pl.multiple_of(side * orows, 16), orows)

    def z_copies(b):
        to = {"dp": dp ^ b}
        return [
            remote(ga_ref, ga_all.at[dp], z_send.at[0, b - 1], z_recv.at[0, b - 1], **to),
            remote(gm_ref, gm_all.at[dp], z_send.at[1, b - 1], z_recv.at[1, b - 1], **to),
            remote(table_ref, table_out.at[dp], z_send.at[2, b - 1], z_recv.at[2, b - 1], **to),
            remote(router_ref, router_all.at[dp], z_send.at[3, b - 1], z_recv.at[3, b - 1], **to),
            remote(
                wqkv_ref.at[:, pl.ds(pl.multiple_of(core * half, 16), half)], wqkv_out.at[:, w_rows(dp, core)],
                z_send.at[4, b - 1], z_recv.at[4, b - 1], **to,
            ),
            remote(
                wout_ref.at[o_rows(core)], wout_all.at[dp, o_rows(core)],
                z_send.at[5, b - 1], z_recv.at[5, b - 1], **to,
            ),
        ]

    small = [z_copies(b) for b in (1, 2, 3)]
    for kind in range(6):
        for b in (3, 2, 1):
            small[b - 1][kind].start()
    beside = remote(tok_ref, tok_all.at[1], t_send.at[0], t_recv.at[0], ctx=ctx ^ 1)
    beside.start()
    across = [remote(tok_ref.at[s], tok_all.at[2, s], y_send.at[s], y_recv.at[s], ctx=ctx ^ 2) for s in range(seqs)]
    expert_copies = [
        remote(pair_ref.at[1 - tp], got_out, e_sems.at[0], e_sems.at[1], tp=tp ^ 1),
    ]
    for copy in across + expert_copies:
        copy.start()
    own = [
        pltpu.make_async_copy(tok_ref, tok_all.at[0], l_sem.at[0]),
        pltpu.make_async_copy(ga_ref, ga_all.at[dp], l_sem.at[1]),
        pltpu.make_async_copy(gm_ref, gm_all.at[dp], l_sem.at[2]),
        pltpu.make_async_copy(table_ref, table_out.at[dp], l_sem.at[3]),
        pltpu.make_async_copy(router_ref, router_all.at[dp], l_sem.at[4]),
        pltpu.make_async_copy(wqkv_ref, wqkv_out.at[:, pl.ds(pl.multiple_of(dp * rows, 16), rows)], l_sem.at[5]),
        pltpu.make_async_copy(wout_ref, wout_all.at[dp], l_sem.at[6]),
    ]
    for copy in own:
        copy.start()

    groups = slots_ref.shape[0]

    def cot_copy(s, b):
        return remote(
            slots_ref.at[b, s], cot_out.at[b - 1, s], c_sems.at[0, s, b - 1], c_sems.at[1, s, b - 1], dp=dp ^ b
        )

    def dispatch_cot(s, carry):
        picks = one_hot(near_ref[s], cap)
        pick = jnp.concatenate([jnp.where(p, 1.0, 0.0).astype(BF16) for p in picks], axis=0)
        slots_ref[:, s] = dot(pick, cot_ref[s]).astype(BF16).reshape(groups, cap, cot_ref.shape[2])

        @pl.when(s < FIRST)
        def _():
            for b in (3, 2, 1):
                cot_copy(s, b).start()

        return carry

    lax.fori_loop(0, seqs, dispatch_cot, 0)
    for copy in own:
        copy.wait()

    for kind in range(4):
        for b in (3, 2, 1):
            small[b - 1][kind].wait_recv()
    count = ga_all.shape[0]
    piece = ga_all.shape[2]
    width = count * piece
    row = lax.broadcasted_iota(jnp.int32, (piece, width), 0)
    col = lax.broadcasted_iota(jnp.int32, (piece, width), 1)
    gain = 0.0
    gain_m = 0.0
    for d in range(count):
        spread = jnp.where(col == row + d * piece, 1.0, 0.0).astype(BF16)
        gain = gain + dot(ga_all[d], spread)
        gain_m = gain_m + dot(gm_all[d], spread)
    gain_ref[...] = gain
    gm_out[...] = gain_m.astype(BF16)
    experts_n = router_ref.shape[1]
    slot_row = lax.broadcasted_iota(jnp.int32, (experts_n, experts_n), 0)
    slot_col = lax.broadcasted_iota(jnp.int32, (experts_n, experts_n), 1)
    side = slot_row // count
    expert = (slot_row % count) * 2 + (side ^ tp)
    order = jnp.where(slot_col == expert, 1.0, 0.0).astype(BF16)
    router_out[...] = dot_nt(order, router_all[...].reshape(width, experts_n)).astype(BF16)

    def norm_piece(b):
        def body(s, carry):
            value = tok_all[b, s].astype(F32)
            out = (value * norm_factor(value) * gain_ref[...]).astype(BF16)
            n_all[b, s] = out
            return carry

        lax.fori_loop(0, seqs, body, 0)

    def project(b, s):
        x = n_all[b, s]
        k_ref[s, b] = dot(x, wqkv_out[1]).astype(BF16)
        v_ref[s, b] = dot(x, wqkv_out[2]).astype(BF16)

    norm_piece(0)
    normed_ref[...] = n_all[0]
    beside.wait_recv()
    norm_piece(1)

    forwards = []
    for b in (1, 2, 3):
        for kind, f in ((4, 0), (5, 1)):
            small[b - 1][kind].wait_recv()
            if f == 0:
                ref = wqkv_out.at[:, w_rows(dp ^ b, core)]
            else:
                ref = wout_all.at[dp ^ b, o_rows(core)]
            copy = remote(ref, ref, f_send.at[f, b - 1], f_recv.at[f, b - 1], ctx=ctx ^ 1)
            copy.start()
            forwards.append(copy)
    for copy in forwards:
        copy.wait_recv()
    wout_out[...] = jnp.concatenate([wout_all[d] for d in range(wout_all.shape[0])], axis=1)

    def own_q(s, carry):
        q_ref[s] = (dot(n_all[0, s], wqkv_out[0]).astype(BF16) * (HD ** (-0.5))).astype(BF16)
        project(0, s)
        project(1, s)
        return carry

    lax.fori_loop(0, seqs, own_q, 0)
    later = []
    for s in range(seqs):
        across[s].wait_recv()
        copy = remote(tok_all.at[2, s], tok_all.at[3, s], t_send.at[1 + s], t_recv.at[1 + s], ctx=ctx ^ 1)
        copy.start()
        later.append(copy)
    norm_piece(2)
    for copy in later:
        copy.wait_recv()
    norm_piece(3)

    def others(s, carry):
        project(2, s)
        project(3, s)
        return carry

    lax.fori_loop(0, seqs, others, 0)
    for copy in expert_copies:
        copy.wait()
    for s in range(FIRST):
        for b in (3, 2, 1):
            cot_copy(s, b).wait()
    for group in small:
        for copy in group:
            copy.wait_send()
    for copy in forwards + later + across + [beside]:
        copy.wait_send()


def first_stage(tokens, wqkv, wout, table, gain_attn, gain_moe, router, expert_pair, near, cot, cap):
    seqs, stretch, width = tokens.shape
    count, rows, local = wqkv.shape
    dp = width // rows
    experts_n = router.shape[1]
    any_spec = pl.BlockSpec(memory_space=pl.ANY)
    vmem = pl.BlockSpec(memory_space=pltpu.VMEM)
    dma = pltpu.SemaphoreType.DMA
    return pl.pallas_call(
        functools.partial(first_kernel, seqs, cap),
        name="first_stage",
        in_specs=[any_spec] * 8 + [vmem] * 2,
        out_specs=[vmem] * 10 + [any_spec, vmem, any_spec],
        out_shape=[
            jax.ShapeDtypeStruct((seqs, stretch, local), BF16),
            jax.ShapeDtypeStruct((seqs, 4, stretch, local), BF16),
            jax.ShapeDtypeStruct((seqs, 4, stretch, local), BF16),
            jax.ShapeDtypeStruct((seqs, stretch, width), BF16),
            jax.ShapeDtypeStruct((3, width, local), BF16),
            jax.ShapeDtypeStruct((wout.shape[0], width), BF16),
            jax.ShapeDtypeStruct((dp,) + table.shape, BF16),
            jax.ShapeDtypeStruct((1, width), F32),
            jax.ShapeDtypeStruct((1, width), BF16),
            jax.ShapeDtypeStruct((experts_n, width), BF16),
            jax.ShapeDtypeStruct(expert_pair.shape[1:], BF16),
            jax.ShapeDtypeStruct((dp, seqs, cap, width), BF16),
            jax.ShapeDtypeStruct((dp - 1, FIRST, cap, width), BF16),
        ],
        scratch_shapes=[
            pltpu.VMEM((4, seqs, stretch, width), BF16),
            pltpu.VMEM((4, seqs, stretch, width), BF16),
            pltpu.VMEM((dp, 1, rows), BF16),
            pltpu.VMEM((dp, 1, rows), BF16),
            pltpu.VMEM((dp, rows, experts_n), BF16),
            dma((6, 3)), dma((6, 3)), dma((2, 3)), dma((2, 3)), dma((1 + seqs,)), dma((1 + seqs,)),
            dma((seqs,)), dma((seqs,)), dma((7,)), dma((2,)), dma((2, FIRST, 3)),
            pltpu.VMEM((dp,) + wout.shape, BF16),
        ],
        compiler_params=pltpu.CompilerParams(vmem_limit_bytes=VMEM_BYTES, collective_id=0, has_side_effects=True),
        cost_estimate=cost(40 * 10**9, 10**7),
    )(tokens, wqkv, wout, table, gain_attn, gain_moe, router, expert_pair, near, cot)


def block_mask(keys, queries):
    ones = jnp.ones(queries.shape, BF16)
    spread = lax.dot_general(keys, ones, (((0,), (0,)), ((), ())), preferred_element_type=F32)
    return jnp.where(spread <= queries, 0.0, MASKED)


def back_kernel(seqs, groups, cap, *refs):
    seq_refs, refs = refs[:4], refs[4:]
    din_ref, part_ref, q_ref, k_ref, v_ref, bias_ref, cot_ref, wout_ref = refs[:8]
    h_ref, place_ref, near_ref, idq_ref, idk_ref, router_ref, gain_ref = refs[8:15]
    out_ref, gmid_ref, low_ref, proj_ref, gain_grad_ref, router_grad_ref, rel_ref = refs[15:22]
    (
        mid_v, moe_v, gate_v, lse_v, din_v, part_v, q_v, k_v, v_v, bias_v, cot_v, wout_v,
        din_own, din_other, h_own, h_other, out_own, out_other, datt_v, mask_v, keep_v, give_v, core_v, y_v, far_v,
        load_sems, seq_sems, part_sems, x_sems, c_sems, y_sems,
    ) = refs[22:]
    dp = lax.axis_index("dp")
    ctx = lax.axis_index("ctx")
    tp = lax.axis_index("tp")
    greet([{"dp": dp ^ b} for b in range(1, groups)] + [{"ctx": ctx ^ 1}, {"ctx": ctx ^ 2}, {"tp": tp ^ 1}])
    rows = groups * cap
    stretch, width = mid_v.shape[1:]
    local = q_v.shape[2]
    pairs = local // (2 * HD)

    def part_copy(s, b):
        return remote(part_ref.at[b, s], part_v.at[b, s], part_sems.at[0, s, b], part_sems.at[1, s, b], dp=dp ^ b)

    for s in range(seqs):
        for b in range(groups - 1, 0, -1):
            part_copy(s, b).start()
    din_load = pltpu.make_async_copy(din_ref, din_v, load_sems.at[0])
    loads = [
        pltpu.make_async_copy(src, dst, load_sems.at[i + 1])
        for i, (src, dst) in enumerate(
            ((wout_ref, wout_v), (cot_ref, cot_v), (q_ref, q_v), (k_ref, k_v), (v_ref, v_v), (bias_ref, bias_v),
             (part_ref.at[0], part_v.at[0]))
        )
    ]
    for i, (src, dst) in enumerate(zip(seq_refs, (mid_v, moe_v, gate_v, lse_v))):
        loads.append(pltpu.make_async_copy(src, dst, seq_sems.at[i]))
    din_load.start()
    for copy in loads:
        copy.start()
    gain_grad_ref[...] = jnp.zeros_like(gain_grad_ref)
    router_grad_ref[...] = jnp.zeros_like(router_grad_ref)
    rel_ref[...] = jnp.zeros_like(rel_ref)

    def din_copy(s):
        return remote(din_own.at[s], din_other.at[s], x_sems.at[0, 0, s], x_sems.at[1, 0, s], tp=tp ^ 1)

    def h_copy(s):
        return remote(h_own.at[s], h_other.at[s], x_sems.at[0, 1, s], x_sems.at[1, 1, s], tp=tp ^ 1)

    def out_copy(s):
        return remote(out_own.at[s], out_other.at[s], x_sems.at[0, 2, s], x_sems.at[1, 2, s], tp=tp ^ 1)

    def core_copy(s):
        return remote(give_v.at[s], core_v.at[s], c_sems.at[0, s], c_sems.at[1, s], ctx=ctx ^ 1)

    def y_copy(s):
        return remote(y_v.at[s], far_v.at[s], y_sems.at[0, s], y_sems.at[1, s], ctx=ctx ^ 2)

    def chosen(place):
        picks = one_hot(place, cap)
        return picks, jnp.concatenate([jnp.where(p, 1.0, 0.0).astype(BF16) for p in picks], axis=0)

    din_load.wait()

    def gather_back(s, carry):
        picks, pick = chosen(place_ref[s])
        din_own[s] = dot_tn(pick, din_v[s].reshape(rows, width)).astype(BF16)
        eye = diagonal(cap)
        for group in range(groups):
            column = jnp.sum(jnp.where(eye, h_ref[s, group], 0.0), axis=1, keepdims=True)
            h_own[s, group : group + 1, :] = jnp.sum(jnp.where(picks[group], column, 0.0), axis=0, keepdims=True)
        h_copy(s).start()
        din_copy(s).start()
        return carry

    lax.fori_loop(0, seqs, gather_back, 0)
    for copy in loads:
        copy.wait()

    def middle_back(s):
        h = jnp.concatenate([h_own[s], h_other[s]], axis=0)
        dlogits = h - gate_v[s] * jnp.sum(h, axis=0, keepdims=True)
        dmoe = din_own[s].astype(F32) + din_other[s].astype(F32)
        dmoe = dmoe + lax.dot_general(
            dlogits, router_ref[...].astype(F32), (((0,), (0,)), ((), ())),
            precision=FULL_PRECISION, preferred_element_type=F32,
        )
        router_grad_ref[...] += lax.dot_general(
            dlogits, moe_v[s].astype(F32), (((1,), (0,)), ((), ())),
            precision=FULL_PRECISION, preferred_element_type=F32,
        )
        mid = mid_v[s]
        factor = norm_factor(mid)
        normed = mid * factor
        gain_grad_ref[...] += jnp.sum(dmoe * normed, axis=0, keepdims=True)
        scaled = dmoe * gain_ref[...].astype(F32)
        dmid = factor * (scaled - normed * jnp.mean(scaled * normed, axis=-1, keepdims=True))
        gmid = cot_v[s].astype(F32) + dmid
        gmid_ref[s] = gmid
        dattn = gmid.astype(BF16)
        low_ref[s] = dattn
        datt_v[...] = dot_nt(dattn, wout_v[...]).astype(BF16)

    def core_sum(s):
        core_copy(s).wait_recv()
        for kind in range(2):
            keep_v[s, kind, 0] += core_v[s, kind, 0].astype(F32)
            y_v[s, kind] = (keep_v[s, kind, 1] + core_v[s, kind, 1].astype(F32)).astype(BF16)
        y_copy(s).start()

    def out_sum(s):
        for b in range(1, groups):
            part_copy(s, b).wait_recv()
        pick = chosen(near_ref[s])[1]
        out_own[s] = dot_tn(pick, part_v[:, s].reshape(rows, width)).astype(BF16)
        out_copy(s).start()

    def attention_back(s):
        mask_v[...] = block_mask(idk_ref[s], idq_ref[s])

        def pair(p, carry):
            lanes = pl.ds(pl.multiple_of(p * 2 * HD, 2 * HD), 2 * HD)
            queries = q_v[s, :, lanes]
            keys = k_v[s, :, lanes]
            values = v_v[s, :, lanes]
            grad_out = datt_v[:, lanes]
            keys_t = keys.T
            low_half = lax.broadcasted_iota(jnp.int32, queries.shape, 1) < HD
            zero = jnp.zeros_like(queries)
            dk = None
            dv = None
            dq_parts = []
            for head in range(2):
                own = (lambda a: jnp.where(low_half, a, zero)) if head == 0 else (
                    lambda a: jnp.where(low_half, zero, a)
                )
                q_own = own(queries)
                do_own = own(grad_out)
                scores = dot_nt(keys, q_own) + bias_v[2 * p + head].astype(F32) + mask_v[...]
                probs = jnp.exp(scores - lse_v[s, p, head : head + 1, :])
                dprobs = dot_nt(values, do_own)
                delta = jnp.sum(probs * dprobs, axis=0, keepdims=True)
                dscores = probs * (dprobs - delta)
                low = dscores.astype(BF16)
                dv_head = dot(probs.astype(BF16), do_own)
                dk_head = dot(low, q_own)
                dv = dv_head if dv is None else dv + dv_head
                dk = dk_head if dk is None else dk + dk_head
                dq_parts.append(dot(keys_t[head * HD : (head + 1) * HD], low))
                for block in range(4):
                    tile = dscores[block * 256 : (block + 1) * 256]
                    wide = jnp.concatenate([tile, jnp.zeros_like(tile)], axis=1)
                    total = None
                    for group in range(32):
                        moved = pltpu.roll(wide[group * 8 : group * 8 + 8], 248 - 8 * group, 1)
                        total = moved if total is None else total + moved
                    row = lax.broadcasted_iota(jnp.int32, total.shape, 0)
                    amount = 7 - row
                    for bit in (1, 2, 4):
                        total = jnp.where((amount & bit) != 0, pltpu.roll(total, bit, 1), total)
                    rel_ref[p, head, block : block + 1, :] += jnp.sum(total, axis=0, keepdims=True)
            proj_ref[0, s, :, lanes] = (jnp.concatenate(dq_parts, axis=0).T * (HD ** (-0.5))).astype(BF16)
            for kind, value in enumerate((dk, dv)):
                for index in range(2):
                    at = 2 * index * stretch
                    keep_v[s, kind, index, :, lanes] = value[at : at + stretch]
                    give_v[s, kind, index, :, lanes] = value[at + stretch : at + 2 * stretch].astype(BF16)
            return carry

        lax.fori_loop(0, pairs, pair, 0)
        core_copy(s).start()

    def main(s, carry):
        h_copy(s).wait_recv()
        din_copy(s).wait_recv()
        middle_back(s)
        attention_back(s)

        @pl.when(s > 0)
        def _():
            core_sum(s - 1)
            out_sum(s - 1)

        return carry

    lax.fori_loop(0, seqs, main, 0)
    core_sum(seqs - 1)
    out_sum(seqs - 1)

    def finish_keys(s, carry):
        y_copy(s).wait_recv()
        for kind in range(2):
            proj_ref[1 + kind, s] = (keep_v[s, kind, 0] + far_v[s, kind].astype(F32)).astype(BF16)
        return carry

    def finish_out(s, carry):
        out_copy(s).wait_recv()
        out_ref[s] = (mid_v[s] + (out_own[s].astype(F32) + out_other[s].astype(F32))).astype(BF16)
        return carry

    lax.fori_loop(0, seqs, finish_keys, 0)
    lax.fori_loop(0, seqs, finish_out, 0)
    for s in range(seqs):
        for b in range(1, groups):
            part_copy(s, b).wait_send()
        for copy in (h_copy(s), din_copy(s), out_copy(s), core_copy(s), y_copy(s)):
            copy.wait_send()


def back_stage(mids, moes, gates, lse, din, parts, q, k, v, bias, cot, wout, h, places, near, ids_query, ids_key, router, gain):
    groups, _, cap, width = parts.shape
    seqs, stretch = mids.shape[:2]
    local = wout.shape[0]
    length = k.shape[1]
    pairs = local // (2 * HD)
    experts_n = router.shape[0]
    any_spec = pl.BlockSpec(memory_space=pl.ANY)
    vmem = pl.BlockSpec(memory_space=pltpu.VMEM)
    dma = pltpu.SemaphoreType.DMA
    return pl.pallas_call(
        functools.partial(back_kernel, seqs, groups, cap),
        name="back_stage",
        in_specs=[any_spec] * 12 + [vmem] * 7,
        out_specs=[vmem] * 7,
        out_shape=[
            jax.ShapeDtypeStruct((seqs, stretch, width), BF16),
            jax.ShapeDtypeStruct((seqs, stretch, width), F32),
            jax.ShapeDtypeStruct((seqs, stretch, width), BF16),
            jax.ShapeDtypeStruct((3, seqs, stretch, local), BF16),
            jax.ShapeDtypeStruct((1, width), F32),
            jax.ShapeDtypeStruct((experts_n, width), F32),
            jax.ShapeDtypeStruct((pairs, 2, 4, 2 * stretch), F32),
        ],
        scratch_shapes=[
            pltpu.VMEM((seqs, stretch, width), F32),
            pltpu.VMEM((seqs, stretch, width), BF16),
            pltpu.VMEM((seqs, experts_n, stretch), F32),
            pltpu.VMEM((seqs, pairs, 2, stretch), F32),
            pltpu.VMEM((seqs, groups, cap, width), BF16),
            pltpu.VMEM((groups, seqs, cap, width), BF16),
            pltpu.VMEM((seqs, stretch, local), BF16),
            pltpu.VMEM((seqs, length, local), BF16),
            pltpu.VMEM((seqs, length, local), BF16),
            pltpu.VMEM((2 * pairs, length, stretch), BF16),
            pltpu.VMEM((seqs, stretch, width), BF16),
            pltpu.VMEM((local, width), BF16),
            pltpu.VMEM((seqs, stretch, width), BF16),
            pltpu.VMEM((seqs, stretch, width), BF16),
            pltpu.VMEM((seqs, groups, stretch), F32),
            pltpu.VMEM((seqs, groups, stretch), F32),
            pltpu.VMEM((seqs, stretch, width), BF16),
            pltpu.VMEM((seqs, stretch, width), BF16),
            pltpu.VMEM((stretch, local), BF16),
            pltpu.VMEM((length, stretch), F32),
            pltpu.VMEM((seqs, 2, 2, stretch, local), F32),
            pltpu.VMEM((seqs, 2, 2, stretch, local), BF16),
            pltpu.VMEM((seqs, 2, 2, stretch, local), BF16),
            pltpu.VMEM((seqs, 2, stretch, local), BF16),
            pltpu.VMEM((seqs, 2, stretch, local), BF16),
            dma((8,)), dma((4,)), dma((2, seqs, groups)), dma((2, 3, seqs)), dma((2, seqs)), dma((2, seqs)),
        ],
        compiler_params=pltpu.CompilerParams(
            vmem_limit_bytes=63 * 1024 * 1024, collective_id=3, has_side_effects=True
        ),
        cost_estimate=cost(6 * 10**10, 10**7),
    )(mids, moes, gates, lse, din, parts, q, k, v, bias, cot, wout, h, places, near, ids_query, ids_key, router, gain)


def last_kernel(
    normed_ref, proj_ref, datt_ref, att_ref, small_ref, wqkv_ref, gmid_ref, x_ref, gain_ref,
    out_ref, router_out, gm_out, ga_out, table_out, gx_ref,
    dn_own, dn_other, ga_own, dn_sems, grads, core_send, core_got, y_out, y_got, z_out, z_got, wide, s_own, s_core, s_y, s_x, s_z,
    c_sems, y_sems, z_sems, w_sems, s_sems,
):
    dp = lax.axis_index("dp")
    ctx = lax.axis_index("ctx")
    tp = lax.axis_index("tp")
    core = ctx % 2
    far = ctx // 2
    greet([{"dp": dp ^ b} for b in (1, 2, 3)] + [{"ctx": ctx ^ b} for b in (1, 2, 3)] + [{"tp": tp ^ 1}])
    count = z_got.shape[0] + 1
    width = normed_ref.shape[1]
    piece = width // count

    seqs, stretch = x_ref.shape[:2]

    def unit_of(s):
        value = x_ref[s].astype(F32)
        factor = norm_factor(value)
        return factor, value * factor

    def rows_of(s):
        return pl.ds(pl.multiple_of(s * stretch, stretch), stretch)

    def input_grad(s, total):
        part = dot_nt(proj_ref[0, rows_of(s)], wqkv_ref[0])
        part = part + dot_nt(proj_ref[1, rows_of(s)], wqkv_ref[1])
        part = part + dot_nt(proj_ref[2, rows_of(s)], wqkv_ref[2])
        dn_own[s] = part.astype(BF16)
        return total + jnp.sum(part * unit_of(s)[1], axis=0, keepdims=True)

    own_gain = lax.fori_loop(0, seqs, input_grad, jnp.zeros((1, width), F32))
    lines = lax.broadcasted_iota(jnp.int32, small_ref.shape, 0)
    ga_own[...] = small_ref[...] + jnp.where(lines == 9, own_gain, 0.0)
    x_copy = remote(ga_own, s_x, s_sems.at[0, 0], s_sems.at[1, 0], tp=tp ^ 1)
    x_copy.start()
    dn_copies = [
        remote(dn_own.at[s], dn_other.at[s], dn_sems.at[0, s], dn_sems.at[1, s], tp=tp ^ 1) for s in range(seqs)
    ]
    for copy in dn_copies:
        copy.start()
    normed_t = normed_ref[...].T
    for j in range(3):
        grads[j] = dot(normed_t, proj_ref[j])
    grads[3] = dot_tn(datt_ref[...], att_ref[...])
    give = 1 - core
    core_send[0] = grads[2 * give].astype(BF16)
    core_send[1] = grads[2 * give + 1].astype(BF16)
    c_copy = remote(core_send, core_got, c_sems.at[0], c_sems.at[1], ctx=ctx ^ 1)
    c_copy.start()
    x_copy.wait_recv()
    s_own[...] = ga_own[...] + jnp.where(lines == 9, s_x[...], 0.0)
    sc_copy = remote(s_own, s_core, s_sems.at[0, 1], s_sems.at[1, 1], ctx=ctx ^ 1)
    sc_copy.start()
    c_copy.wait_recv()
    grads[2 * core] += core_got[0].astype(F32)
    grads[2 * core + 1] += core_got[1].astype(F32)
    y_out[...] = grads[2 * core + 1 - far].astype(BF16)
    order = (3, 2, 1, 0)
    y_copies = []
    for b in order:
        at = pl.ds(pl.multiple_of((dp ^ b) * piece, 16), piece)
        copy = remote(y_out.at[at], y_got.at[b], y_sems.at[0, b], y_sems.at[1, b], ctx=ctx ^ 2)
        copy.start()
        y_copies.append(copy)
    sc_copy.wait_recv()
    y_small = s_own[...] + s_core[...]
    s_y[0] = y_small
    sy_copy = remote(s_y.at[0], s_y.at[1], s_sems.at[0, 2], s_sems.at[1, 2], ctx=ctx ^ 2)
    sy_copy.start()
    mine = 2 * core + far
    z_copies = []
    total = None
    for copy, b in zip(y_copies, order):
        copy.wait_recv()
        at = pl.ds(pl.multiple_of((dp ^ b) * piece, 16), piece)
        value = grads[mine, at] + y_got[b].astype(F32)
        if b:
            z_out[b - 1] = value.astype(BF16)
            z_copy = remote(z_out.at[b - 1], z_got.at[b - 1], z_sems.at[0, b - 1], z_sems.at[1, b - 1], dp=dp ^ b)
            z_copy.start()
            z_copies.append((b, z_copy))
        else:
            total = value
    sy_copy.wait_recv()
    s_z[dp] = s_y[0] + s_y[1]
    sz_copies = []
    for b in (3, 2, 1):
        copy = remote(s_z.at[dp], s_z.at[dp], s_sems.at[0, 2 + b], s_sems.at[1, 2 + b], dp=dp ^ b)
        copy.start()
        sz_copies.append(copy)
    for b, copy in z_copies:
        copy.wait_recv()
        total = total + z_got[b - 1].astype(F32)
    wide[mine] = total.astype(BF16)
    w_copies = []
    for b in (3, 2, 1):
        copy = remote(wide.at[mine], wide.at[mine], w_sems.at[0, b - 1], w_sems.at[1, b - 1], ctx=ctx ^ b)
        copy.start()
        w_copies.append(copy)
    for copy in dn_copies:
        copy.wait_recv()

    def input_norm(s, carry):
        factor, unit = unit_of(s)
        scaled = (dn_own[s].astype(F32) + dn_other[s].astype(F32)) * gain_ref[...]
        dres = factor * (scaled - unit * jnp.mean(scaled * unit, axis=-1, keepdims=True))
        gx_ref[s] = gmid_ref[s] + dres
        return carry

    lax.fori_loop(0, seqs, input_norm, 0)
    for copy in sz_copies:
        copy.wait_recv()
    small = s_z[0]
    for d in range(1, count):
        small = small + s_z[d]

    def exact(a, b, dims):
        return lax.dot_general(a, b, (dims, ((), ())), precision=FULL_PRECISION, preferred_element_type=F32)

    row = lax.broadcasted_iota(jnp.int32, (piece, width), 0)
    col = lax.broadcasted_iota(jnp.int32, (piece, width), 1)
    select = jnp.where(col == row + dp * piece, 1.0, 0.0)
    experts_n = router_out.shape[1]
    e_row = lax.broadcasted_iota(jnp.int32, (experts_n, experts_n), 0)
    e_col = lax.broadcasted_iota(jnp.int32, (experts_n, experts_n), 1)
    slot = ((e_row % 2) ^ tp) * count + e_row // 2
    arranged = exact(jnp.where(e_col == slot, 1.0, 0.0), small[:experts_n], ((1,), (0,)))
    router_out[...] = exact(select, arranged, ((1,), (1,)))
    gains = exact(small[8:16], select, ((1,), (1,)))
    gm_out[...] = gains[0:1]
    ga_out[...] = gains[1:2]
    t_rows, heads = table_out.shape
    t_row = lax.broadcasted_iota(jnp.int32, (t_rows, width), 0)
    t_col = lax.broadcasted_iota(jnp.int32, (t_rows, width), 1)
    table_out[...] = exact(jnp.where(t_col == t_row + dp * t_rows, 1.0, 0.0), small[16:24], ((1,), (1,)))[:, :heads]
    for copy in w_copies:
        copy.wait_recv()
    out_ref[...] = wide[...].astype(F32)
    for copy in [x_copy, c_copy, sc_copy, sy_copy] + dn_copies + y_copies + [c for _, c in z_copies] + sz_copies + w_copies:
        copy.wait_send()


def last_stage(normed, proj, datt, att, small, wqkv, gmid, x, gain, dp, table_rows, heads, experts_n):
    rows, width = normed.shape
    local = att.shape[1]
    piece = width // dp
    vmem = pl.BlockSpec(memory_space=pltpu.VMEM)
    dma = pltpu.SemaphoreType.DMA
    return pl.pallas_call(
        last_kernel,
        name="last_stage",
        in_specs=[vmem] * 9,
        out_specs=[vmem] * 6,
        out_shape=[
            jax.ShapeDtypeStruct((4, piece, local), F32),
            jax.ShapeDtypeStruct((piece, experts_n), F32),
            jax.ShapeDtypeStruct((1, piece), F32),
            jax.ShapeDtypeStruct((1, piece), F32),
            jax.ShapeDtypeStruct((table_rows, heads), F32),
            jax.ShapeDtypeStruct(x.shape, F32),
        ],
        scratch_shapes=[
            pltpu.VMEM(x.shape, BF16),
            pltpu.VMEM(x.shape, BF16),
            pltpu.VMEM(small.shape, F32),
            dma((2, x.shape[0])),
            pltpu.VMEM((4, width, local), F32),
            pltpu.VMEM((2, width, local), BF16),
            pltpu.VMEM((2, width, local), BF16),
            pltpu.VMEM((width, local), BF16),
            pltpu.VMEM((4, piece, local), BF16),
            pltpu.VMEM((3, piece, local), BF16),
            pltpu.VMEM((3, piece, local), BF16),
            pltpu.VMEM((4, piece, local), BF16),
            pltpu.VMEM(small.shape, F32),
            pltpu.VMEM(small.shape, F32),
            pltpu.VMEM((2,) + small.shape, F32),
            pltpu.VMEM(small.shape, F32),
            pltpu.VMEM((dp,) + small.shape, F32),
            dma((2,)), dma((2, 4)), dma((2, 3)), dma((2, 3)), dma((2, 6)),
        ],
        compiler_params=pltpu.CompilerParams(vmem_limit_bytes=VMEM_BYTES, collective_id=1, has_side_effects=True),
        cost_estimate=cost(8 * rows * width * local, 8 * rows * width),
    )(normed, proj, datt, att, small, wqkv, gmid, x, gain)


def front_kernel(
    seqs, groups, cap,
    pair_ref, got_ref, cot_ref, q_ref, k_ref, v_ref, win_ref, idq_ref, idk_ref, x_ref, wout_ref, gain_ref, router_ref,
    hits_ref, place_ref,
    near_out, far_out, cot_out, row_out, gate_out, bias_ref, att_ref, lse_ref, mid_ref, moe_ref, gates_ref, send_ref, slot_ref,
    wout_other, att_other, mask_ref, w_sems, x_sems, z_sems, r_sems, g_sems, own_sems,
):
    dp = lax.axis_index("dp")
    ctx = lax.axis_index("ctx")
    tp = lax.axis_index("tp")
    greet([{"dp": dp ^ b} for b in range(1, groups)] + [{"ctx": ctx ^ 2}, {"tp": tp ^ 1}])
    width = x_ref.shape[2]
    local = q_ref.shape[2]
    pairs = local // (2 * HD)
    far_copies = [
        remote(pair_ref.at[tp], near_out, w_sems.at[0, 2], w_sems.at[1, 2], ctx=ctx ^ 2),
        remote(got_ref, far_out, w_sems.at[0, 0], w_sems.at[1, 0], ctx=ctx ^ 2),
    ]
    wout_copy = remote(wout_ref, wout_other, w_sems.at[0, 1], w_sems.at[1, 1], tp=tp ^ 1)
    order = tuple(range(groups - 1, 0, -1))
    cot_copies = [
        remote(
            cot_ref.at[b, s], cot_out.at[b - 1, s - FIRST],
            z_sems.at[0, s - FIRST, b - 1], z_sems.at[1, s - FIRST, b - 1], dp=dp ^ b,
        )
        for s in range(FIRST, seqs)
        for b in order
    ]
    for copy in [wout_copy] + far_copies + cot_copies:
        copy.start()

    def expand(head, carry):
        for block in range(4):
            row = win_ref[head, block : block + 1, :]
            wide = jnp.broadcast_to(row, (256, 512))
            rolled = pltpu.roll(wide, 257, 1, stride=1, stride_axis=0)
            bias_ref[head, block * 256 : (block + 1) * 256, :] = rolled[:, :256].astype(BF16)
        return carry

    lax.fori_loop(0, 2 * pairs, expand, 0)

    def att_copy(s):
        return remote(att_ref.at[s], att_other.at[s], x_sems.at[0, s], x_sems.at[1, s], tp=tp ^ 1)

    def row_copy(b):
        return remote(send_ref.at[0, dp ^ b], row_out.at[dp], r_sems.at[0, b - 1], r_sems.at[1, b - 1], dp=dp ^ b)

    def gate_copy(b):
        return remote(slot_ref.at[0, dp ^ b], gate_out.at[dp], g_sems.at[0, b - 1], g_sems.at[1, b - 1], dp=dp ^ b)

    def own_row():
        return pltpu.make_async_copy(send_ref.at[0, dp], row_out.at[dp], own_sems.at[0])

    def own_gate():
        return pltpu.make_async_copy(slot_ref.at[0, dp], gate_out.at[dp], own_sems.at[1])

    def attention(s):
        mask_ref[...] = block_mask(idk_ref[s], idq_ref[s])

        def pair(p, carry):
            lanes = pl.ds(pl.multiple_of(p * 2 * HD, 2 * HD), 2 * HD)
            queries = q_ref[s, :, lanes]
            keys = k_ref[s, :, lanes]
            values_t = v_ref[s, :, lanes].T
            low_half = lax.broadcasted_iota(jnp.int32, queries.shape, 1) < HD
            zero = jnp.zeros_like(queries)
            parts = []
            for head in range(2):
                own = jnp.where(low_half, queries, zero) if head == 0 else jnp.where(low_half, zero, queries)
                scores = dot_nt(keys, own) + bias_ref[2 * p + head].astype(F32) + mask_ref[...]
                top = jnp.max(scores, axis=0, keepdims=True)
                weights = jnp.exp(scores - top)
                total = jnp.sum(weights, axis=0, keepdims=True)
                part = dot(values_t[head * HD : (head + 1) * HD], weights.astype(BF16)) * (1.0 / total)
                parts.append(part)
                lse_ref[s, p, head : head + 1, :] = top + jnp.log(total)
            att_ref[s, :, lanes] = jnp.concatenate(parts, axis=0).T.astype(BF16)
            return carry

        lax.fori_loop(0, pairs, pair, 0)
        att_copy(s).start()

    def middle(s):
        att_copy(s).wait_recv()
        mid = x_ref[s].astype(F32) + (dot(att_ref[s], wout_ref[...]) + dot(att_other[s], wout_other[...]))
        mid_ref[s] = mid
        moe_in = (mid * norm_factor(mid) * gain_ref[...].astype(F32)).astype(BF16)
        moe_ref[s] = moe_in
        logits = dot_nt(router_ref[...], moe_in)
        hit = hits_ref[s] > 0.5
        top = jnp.max(jnp.where(hit, logits, MASKED), axis=0, keepdims=True)
        raw = jnp.where(hit, jnp.exp(jnp.where(hit, logits, top) - top), 0.0)
        gates = raw / jnp.sum(raw, axis=0, keepdims=True)
        gates_ref[s] = gates
        picks = one_hot(place_ref[s], cap)
        pick = jnp.concatenate([jnp.where(p, 1.0, 0.0).astype(BF16) for p in picks], axis=0)
        send_ref[s] = dot(pick, moe_in).astype(BF16).reshape(groups, cap, width)
        eye = diagonal(cap)
        for group in range(groups):
            column = jnp.sum(jnp.where(picks[group], gates[group : group + 1, :], 0.0), axis=1, keepdims=True)
            slot_ref[s, group] = jnp.sum(jnp.where(eye, column, 0.0), axis=0, keepdims=True)

    def main(s, carry):
        attention(s)

        @pl.when(s == 1)
        def _():
            wout_copy.wait_recv()

        @pl.when(s > 0)
        def _():
            middle(s - 1)

        @pl.when(s == 1)
        def _():
            for b in order:
                gate_copy(b).start()
                row_copy(b).start()
            own_row().start()
            own_gate().start()

        return carry

    lax.fori_loop(0, seqs, main, 0)
    middle(seqs - 1)
    for b in order:
        gate_copy(b).wait()
        row_copy(b).wait()
    own_row().wait()
    own_gate().wait()
    for copy in far_copies + cot_copies:
        copy.wait()
    wout_copy.wait_send()
    for s in range(seqs):
        att_copy(s).wait_send()


def front_stage(pair, got, cot, q, k, v, windows, ids_query, ids_key, x, wout, gain, router, hits, places, cap):
    seqs, stretch, width = x.shape
    groups = places.shape[1]
    local = q.shape[2]
    length = k.shape[1]
    pairs = local // (2 * HD)
    experts_n = router.shape[0]
    any_spec = pl.BlockSpec(memory_space=pl.ANY)
    vmem = pl.BlockSpec(memory_space=pltpu.VMEM)
    dma = pltpu.SemaphoreType.DMA
    return pl.pallas_call(
        functools.partial(front_kernel, seqs, groups, cap),
        name="front_stage",
        in_specs=[any_spec] * 3 + [vmem] * 12,
        out_specs=[any_spec] * 4 + [vmem] * 9,
        out_shape=[
            jax.ShapeDtypeStruct(got.shape, BF16),
            jax.ShapeDtypeStruct(got.shape, BF16),
            jax.ShapeDtypeStruct((groups - 1, seqs - FIRST, cap, width), BF16),
            jax.ShapeDtypeStruct((groups, cap, width), BF16),
            jax.ShapeDtypeStruct((groups, 1, cap), F32),
            jax.ShapeDtypeStruct((2 * pairs, length, stretch), BF16),
            jax.ShapeDtypeStruct((seqs, stretch, local), BF16),
            jax.ShapeDtypeStruct((seqs, pairs, 2, stretch), F32),
            jax.ShapeDtypeStruct((seqs, stretch, width), F32),
            jax.ShapeDtypeStruct((seqs, stretch, width), BF16),
            jax.ShapeDtypeStruct((seqs, experts_n, stretch), F32),
            jax.ShapeDtypeStruct((seqs, groups, cap, width), BF16),
            jax.ShapeDtypeStruct((seqs, groups, 1, cap), F32),
        ],
        scratch_shapes=[
            pltpu.VMEM((local, width), BF16),
            pltpu.VMEM((seqs, stretch, local), BF16),
            pltpu.VMEM((length, stretch), F32),
            dma((2, 3)), dma((2, seqs)), dma((2, seqs - FIRST, groups - 1)), dma((2, groups - 1)), dma((2, groups - 1)),
            dma((2,)),
        ],
        compiler_params=pltpu.CompilerParams(vmem_limit_bytes=VMEM_BYTES, collective_id=4, has_side_effects=True),
        cost_estimate=cost(4 * 10**10, 10**7),
    )(pair, got, cot, q, k, v, windows, ids_query, ids_key, x, wout, gain, router, hits, places)


def moe_kernel(
    seqs, groups, cap, tile, *refs,
):
    send_ref, slot_ref, row_ref, gate_ref, slots_ref, cot_ref, last_ref = refs[:7]
    refs = refs[7:]
    w_own, w_far, part_out, din_back, h_back, keep_out, give_out = (refs[:2], refs[2:4]) + refs[4:9]
    (
        w_all, x_all, gate_all, g_all, xt_all, dyt_all, dy_ref, hid_all, dpre_all, part_acc, din_acc,
        part_all, din_all, h_all, tile_ref,
        x_sems, gate_sems, din_sems, h_sems, w_sems, own_sems, cot_sems, part_sems, out_sems, core_sems,
    ) = refs[9:]
    dp = lax.axis_index("dp")
    ctx = lax.axis_index("ctx")
    greet([{"dp": dp ^ b} for b in range(1, groups)] + [{"ctx": ctx ^ 1}])
    width = x_all.shape[-1]
    rows = groups * cap
    slices = w_all.shape[2]
    piece = width // slices
    half_len = w_all.shape[4]
    per_half = half_len // tile
    tiles = w_all.shape[1] * per_half
    order = tuple(range(groups - 1, 0, -1))

    sent = []
    for s in range(1, seqs):
        for b in order:
            sent.append(
                remote(send_ref.at[s, dp ^ b], x_all.at[s, dp], x_sems.at[0, s, b - 1], x_sems.at[1, s, b - 1], dp=dp ^ b)
            )
            sent.append(
                remote(
                    slot_ref.at[s, dp ^ b], gate_all.at[s, dp],
                    gate_sems.at[0, s, b - 1], gate_sems.at[1, s, b - 1], dp=dp ^ b,
                )
            )
    w_copies = []
    local = []
    arrivals = []
    for half in range(2):
        for index, (ref, place) in enumerate(((w_own[half], ctx), (w_far[half], ctx ^ 2))):
            sems = (w_sems.at[0, half, index], w_sems.at[1, half, index])
            w_copies.append(remote(ref, w_all.at[:, half, place], *sems, ctx=ctx ^ 1))
            there = w_all.at[:, half, place ^ 1]
            arrivals.append(remote(there, there, *sems, ctx=ctx ^ 1))
            local.append(pltpu.make_async_copy(ref, w_all.at[:, half, place], w_sems.at[2, half, index]))
    for copy in w_copies + sent:
        copy.start()
    local.append(pltpu.make_async_copy(row_ref, x_all.at[0], own_sems.at[0]))
    local.append(pltpu.make_async_copy(gate_ref, gate_all.at[0], own_sems.at[1]))
    for s in range(1, seqs):
        local.append(pltpu.make_async_copy(send_ref.at[s, dp], x_all.at[s, dp], own_sems.at[2 * s]))
        local.append(pltpu.make_async_copy(slot_ref.at[s, dp], gate_all.at[s, dp], own_sems.at[1 + 2 * s]))
    local.append(pltpu.make_async_copy(slots_ref.at[0], g_all.at[dp], cot_sems.at[0, 0]))
    for b in range(1, groups):
        local.append(
            pltpu.make_async_copy(cot_ref.at[b - 1], g_all.at[dp ^ b, pl.ds(0, FIRST)], cot_sems.at[0, b])
        )
        local.append(
            pltpu.make_async_copy(last_ref.at[b - 1], g_all.at[dp ^ b, pl.ds(FIRST, seqs - FIRST)], cot_sems.at[1, b])
        )
    for copy in local:
        copy.start()
    for copy in local:
        copy.wait()
    for copy in arrivals:
        copy.wait_recv()
    eye = diagonal(cap)

    def weights(io, f):
        lanes = pl.ds(pl.multiple_of((f % per_half) * tile, tile), tile)
        return w_all[io, f // per_half, :, :, lanes].reshape(width, tile)

    def gate_column(s, group):
        return jnp.sum(jnp.where(eye, gate_all[s, group], 0.0), axis=1, keepdims=True)

    def din_copy(s, b):
        return remote(
            din_all.at[s, dp ^ b], din_back.at[s, dp], din_sems.at[0, s, b - 1], din_sems.at[1, s, b - 1], dp=dp ^ b
        )

    def h_copy(s, b):
        return remote(h_all.at[s, dp ^ b], h_back.at[s, dp], h_sems.at[0, s, b - 1], h_sems.at[1, s, b - 1], dp=dp ^ b)

    def part_copy(s, b):
        return pltpu.make_async_copy(part_all.at[s, dp ^ b], part_out.at[b, s], part_sems.at[s, b])

    def own_copies(s):
        return [
            pltpu.make_async_copy(din_all.at[s, dp], din_back.at[s, dp], part_sems.at[s, groups]),
            pltpu.make_async_copy(h_all.at[s, dp], h_back.at[s, dp], part_sems.at[s, groups + 1]),
        ]

    def chunk(s, carry):
        @pl.when(s > 0)
        def _():
            for b in order:
                there = x_all.at[s, dp ^ b]
                remote(there, there, x_sems.at[0, s, b - 1], x_sems.at[1, s, b - 1], dp=dp ^ b).wait_recv()
                there = gate_all.at[s, dp ^ b]
                remote(there, there, gate_sems.at[0, s, b - 1], gate_sems.at[1, s, b - 1], dp=dp ^ b).wait_recv()

        x = x_all[s].reshape(rows, width)
        xt_all[s] = x.T
        for group in range(groups):
            dy_ref[group * cap : (group + 1) * cap] = (g_all[group, s].astype(F32) * gate_column(s, group)).astype(BF16)
        dyt_all[s] = dy_ref[...].T
        part_acc[...] = jnp.zeros_like(part_acc)
        din_acc[...] = jnp.zeros_like(din_acc)

        def step(f, carry):
            x = x_all[s].reshape(rows, width)
            w_in = weights(0, f)
            w_out_t = weights(1, f)
            pre = dot(x, w_in)
            dhid = dot(dy_ref[...], w_out_t)
            square = pre * pre
            inner = jnp.tanh(GELU_C * pre * (1.0 + GELU_A * square))
            half = 0.5 * (1.0 + inner)
            hidden = (pre * half).astype(BF16)
            slope = half + (0.5 * GELU_C) * pre * (1.0 - inner * inner) * (1.0 + (3.0 * GELU_A) * square)
            dpre = (dhid * slope).astype(BF16)
            hid_all[f, s] = hidden
            dpre_all[f, s] = dpre
            part_acc[...] += dot_nt(hidden, w_out_t)
            din_acc[...] += dot_nt(dpre, w_in)
            return carry

        lax.fori_loop(0, tiles, step, 0)
        for group in range(groups):
            at = slice(group * cap, (group + 1) * cap)
            din_all[s, group] = din_acc[at].astype(BF16)
            gated = part_acc[at] * gate_column(s, group)
            part_all[s, group] = gated.astype(BF16)
            h = jnp.sum(gated * g_all[group, s].astype(F32), axis=1, keepdims=True)
            h_all[s, group] = jnp.sum(jnp.where(eye, h, 0.0), axis=0, keepdims=True)
        for b in order:
            din_copy(s, b).start()
            h_copy(s, b).start()
        for copy in own_copies(s):
            copy.start()
        for b in range(groups):
            part_copy(s, b).start()
        return carry

    lax.fori_loop(0, seqs, chunk, 0)

    def tile_of(ref, f):
        lanes = pl.ds(pl.multiple_of((f % per_half) * tile, tile), tile)
        return ref.at[f // per_half, :, :, :, lanes]

    def keep_copy(f, slot):
        return pltpu.make_async_copy(tile_ref.at[slot, 0], tile_of(keep_out, f), out_sems.at[slot, 0])

    def give_copy(f, slot):
        return remote(
            tile_ref.at[slot, 1], tile_of(give_out, f), out_sems.at[slot, 1], core_sems.at[f], ctx=ctx ^ 1
        )

    def weight_grads(f, carry):
        slot = f % 2

        @pl.when(f >= 2)
        def _():
            keep_copy(f - 2, slot).wait()
            give_copy(f - 2, slot).wait_send()

        for io, (left, right) in enumerate(((xt_all, dpre_all), (dyt_all, hid_all))):
            total = dot(left[0], right[f, 0])
            for s in range(1, seqs):
                total = total + dot(left[s], right[f, s])
            for index in range(slices):
                place = index ^ ctx
                tile_ref[slot, place % 2, place // 2, io] = total[index * piece : (index + 1) * piece].astype(BF16)
        keep_copy(f, slot).start()
        give_copy(f, slot).start()
        return carry

    lax.fori_loop(0, tiles, weight_grads, 0)
    for f in (tiles - 2, tiles - 1):
        keep_copy(f, f % 2).wait()
        give_copy(f, f % 2).wait_send()
    for f in range(tiles):
        give_copy(f, f % 2).wait_recv()
    for s in range(seqs):
        for b in order:
            there = din_back.at[s, dp ^ b]
            remote(there, there, din_sems.at[0, s, b - 1], din_sems.at[1, s, b - 1], dp=dp ^ b).wait_recv()
            there = h_back.at[s, dp ^ b]
            remote(there, there, h_sems.at[0, s, b - 1], h_sems.at[1, s, b - 1], dp=dp ^ b).wait_recv()
            din_copy(s, b).wait_send()
            h_copy(s, b).wait_send()
        for copy in own_copies(s):
            copy.wait()
        for b in range(groups):
            part_copy(s, b).wait()
    for copy in w_copies + sent:
        copy.wait_send()


def moe_stage(send, slot_gate, row, row_gate, slots, cot, last, keep, got, far_keep, far_got, tile=512):
    seqs, groups, cap, width = send.shape
    _, piece, half_len = keep.shape
    halves = 2
    slices = width // piece
    tiles = halves * half_len // tile
    rows = groups * cap
    any_spec = pl.BlockSpec(memory_space=pl.ANY)
    vmem = pl.BlockSpec(memory_space=pltpu.VMEM)
    dma = pltpu.SemaphoreType.DMA
    return pl.pallas_call(
        functools.partial(moe_kernel, seqs, groups, cap, tile),
        name="moe_stage",
        in_specs=[any_spec] * 11,
        out_specs=[any_spec, any_spec, vmem, any_spec, any_spec],
        out_shape=[
            jax.ShapeDtypeStruct((groups, seqs, cap, width), BF16),
            jax.ShapeDtypeStruct((seqs, groups, cap, width), BF16),
            jax.ShapeDtypeStruct((seqs, groups, 1, cap), F32),
            jax.ShapeDtypeStruct((halves, slices // 2, 2, piece, half_len), BF16),
            jax.ShapeDtypeStruct((halves, slices // 2, 2, piece, half_len), BF16),
        ],
        scratch_shapes=[
            pltpu.VMEM((2, halves, slices, piece, half_len), BF16),
            pltpu.VMEM((seqs, groups, cap, width), BF16),
            pltpu.VMEM((seqs, groups, 1, cap), F32),
            pltpu.VMEM((groups, seqs, cap, width), BF16),
            pltpu.VMEM((seqs, width, rows), BF16),
            pltpu.VMEM((seqs, width, rows), BF16),
            pltpu.VMEM((rows, width), BF16),
            pltpu.VMEM((tiles, seqs, rows, tile), BF16),
            pltpu.VMEM((tiles, seqs, rows, tile), BF16),
            pltpu.VMEM((rows, width), F32),
            pltpu.VMEM((rows, width), F32),
            pltpu.VMEM((seqs, groups, cap, width), BF16),
            pltpu.VMEM((seqs, groups, cap, width), BF16),
            pltpu.VMEM((seqs, groups, 1, cap), F32),
            pltpu.VMEM((2, 2, slices // 2, 2, piece, tile), BF16),
            dma((2, seqs, groups - 1)), dma((2, seqs, groups - 1)), dma((2, seqs, groups - 1)),
            dma((2, seqs, groups - 1)), dma((3, 2, 2)), dma((2 * seqs,)), dma((2, groups)), dma((seqs, groups + 2)),
            dma((2, 2)), dma((tiles,)),
        ],
        compiler_params=pltpu.CompilerParams(
            vmem_limit_bytes=63 * 1024 * 1024, collective_id=2, has_side_effects=True
        ),
        cost_estimate=cost(20 * seqs * rows * width * halves * half_len, 40 * width * halves * half_len),
    )(send, slot_gate, row, row_gate, slots, cot, last, keep, got, far_keep, far_got)


def flip(value, axis, bit):
    count = lax.axis_size(axis)
    return lax.ppermute(value, axis, [(i, i ^ bit) for i in range(count)])


def all_to_all_dp(value):
    return lax.all_to_all(value, "dp", split_axis=0, concat_axis=0, tiled=True)


def gathered(tokens, wqkv, wout, table, gain_attn, gain_moe, router):
    seqs, stretch, width = tokens.shape
    local = wqkv.shape[2]
    dp = lax.axis_size("dp")
    tp = lax.axis_index("tp")
    experts_n = router.shape[1]
    wqkv = lax.all_gather(wqkv, "dp", axis=1, tiled=True)
    wout = lax.all_gather(wout, "dp", axis=1, tiled=True)
    table = lax.all_gather(table, "dp", axis=0, tiled=True)
    gains = lax.all_gather(jnp.concatenate([gain_attn, gain_moe], axis=0), "dp", axis=1, tiled=True)
    gain_attn, gain_moe = gains[0:1].astype(F32), gains[1:2]
    router = lax.all_gather(router, "dp", axis=0, tiled=True).T.reshape(dp, 2, width).transpose(1, 0, 2)
    router = jnp.where(tp == 0, router, router[::-1]).reshape(experts_n, width)
    across = flip(tokens, "ctx", 2)
    beside, beyond = flip(jnp.stack([tokens, across]), "ctx", 1)
    x32 = jnp.stack([tokens, beside, across, beyond], axis=1).astype(F32)
    normed = (x32 * norm_factor(x32) * gain_attn[None, None]).astype(BF16)
    own = normed[:, 0].reshape(seqs * stretch, width)
    queries = jnp.dot(own, wqkv[0], preferred_element_type=F32).astype(BF16) * jnp.asarray(HD ** (-0.5), BF16)
    flat = normed.reshape(seqs * 4 * stretch, width)
    keys = jnp.dot(flat, wqkv[1], preferred_element_type=F32).astype(BF16).reshape(seqs, 4 * stretch, local)
    values = jnp.dot(flat, wqkv[2], preferred_element_type=F32).astype(BF16).reshape(seqs, 4 * stretch, local)
    return queries.reshape(seqs, stretch, local), keys, values, own, wqkv, wout, table, gain_attn, gain_moe, router


def on_device(
    tokens_in, block_ids, rel_buckets, routes, attn_gain, w_qkv, w_attn_out, bias_table, moe_gain, w_router,
    w_expert_in, w_expert_out, cotangent,
):
    seqs, stretch, width = tokens_in.shape
    dp = lax.axis_size("dp")
    ctx_count = lax.axis_size("ctx")
    tp_count = lax.axis_size("tp")
    expert_count = w_router.shape[2]
    assert w_expert_in.shape[1] == tp_count == 2 and ctx_count == 4
    cap = max(2, 2 * stretch * routes.shape[2] // expert_count)
    ctx = lax.axis_index("ctx")
    tp = lax.axis_index("tp")
    local = w_qkv.shape[3]
    heads = local // HD

    fits = dp == 4
    e_order = jnp.arange(expert_count, dtype=jnp.int32).reshape(dp, 2).T
    e_order = jnp.where(tp == 0, e_order, e_order[::-1]).reshape(1, expert_count, 1)
    hits = ((routes[:, None, :, 0] == e_order) | (routes[:, None, :, 1] == e_order)).astype(F32)
    before = (
        lax.broadcasted_iota(jnp.int32, (stretch, stretch), 0) < lax.broadcasted_iota(jnp.int32, (stretch, stretch), 1)
    ).astype(BF16)
    ranks = jnp.einsum("set,tu->seu", hits.astype(BF16), before, preferred_element_type=F32)
    places = jnp.where(hits > 0.5, ranks, -1.0)[:, :dp]

    pair = jnp.stack([w_expert_in[0], w_expert_out[0].transpose(0, 2, 1)], axis=1)

    if fits:
        me = lax.axis_index("dp")
        near_places = jnp.stack([lax.dynamic_index_in_dim(places, me ^ b, 1, keepdims=False) for b in range(dp)], axis=1)
        (
            queries, keys, values, own_normed, wqkv, wout_own, table, gain_attn, gain_moe, router, got,
            cot_slots, cot_in,
        ) = first_stage(
            tokens_in, w_qkv[0], w_attn_out[0], bias_table[0], attn_gain, moe_gain, w_router[0], pair,
            near_places, cotangent, cap,
        )
        keep = lax.dynamic_index_in_dim(pair, tp, 0, keepdims=False)
        table = table.reshape(NB, heads)
        keys = keys.reshape(seqs, 4 * stretch, local)
        values = values.reshape(seqs, 4 * stretch, local)
        own_normed = own_normed.reshape(seqs * stretch, width)
    else:
        queries, keys, values, own_normed, wqkv, wout_own, table, gain_attn, gain_moe, router = gathered(
            tokens_in, w_qkv[0], w_attn_out[0], bias_table[0], attn_gain, moe_gain, w_router[0]
        )
        keep = lax.dynamic_index_in_dim(pair, tp, 0, keepdims=False)
        got = flip(lax.dynamic_index_in_dim(pair, 1 - tp, 0, keepdims=False), "tp", 1)
        weights = lax.all_gather(jnp.stack([keep, got], axis=1), "ctx", axis=0, tiled=False)
        cot_slots = all_to_all_dp(dispatch(places, cotangent, cap))

    one_hot_bucket = (rel_buckets[:, None] == jnp.arange(NB, dtype=jnp.int32)[None, :]).astype(F32)
    one_hot_bucket = jnp.pad(one_hot_bucket, ((0, 1), (0, 0)))
    starts = [(ctx - (ctx ^ b)) * stretch + 3 * stretch for b in range(4)]
    hot_windows = jnp.stack([lax.dynamic_slice_in_dim(one_hot_bucket, s, 2 * stretch, 0) for s in starts])
    windows = jnp.einsum("bmn,nh->hbm", hot_windows, table.astype(F32), precision=FULL_PRECISION)

    ids = block_ids.reshape(seqs, 4, stretch)
    ids_pieces = [lax.dynamic_index_in_dim(ids, ctx ^ b, 1, keepdims=False) for b in range(4)]
    ids_query = ids_pieces[0].reshape(seqs, 1, stretch)
    ids_key = jnp.stack(ids_pieces, axis=1)
    if fits:
        ids_query = ids_query.astype(F32)
        ids_key = ids_key.astype(BF16).reshape(seqs, 1, 4 * stretch)
    else:
        ids_key = ids_key.reshape(seqs, 4 * stretch, 1)

    if fits:
        (
            far_keep, far_got, cot_last, row, row_gate, bias, attended, lse, mids, moes, gates, send, slot_gate,
        ) = front_stage(
            pair, got, cot_slots, queries, keys, values, windows, ids_query, ids_key, tokens_in, wout_own, gain_moe, router,
            hits, places, cap,
        )
        parts, returned_din, returned_h, kept, given = moe_stage(
            send, slot_gate, row, row_gate, cot_slots, cot_in, cot_last, keep, got, far_keep, far_got
        )
    else:
        bias = expand_bias(windows)
        wout_pair = jnp.stack([wout_own, flip(wout_own, "tp", 1)])
        attended, lse, mids, moes, gates, sends, slot_gates = [], [], [], [], [], [], []
        for s in range(seqs):
            att, stat = attend(queries[s], keys[s], values[s], bias, ids_query[s], ids_key[s])
            attended.append(att)
            lse.append(stat)
            mid, moe_in, gate, send, slot_gate = middle_stage(
                att, flip(att, "tp", 1), tokens_in[s], wout_pair, gain_moe, router, hits[s], places[s], cap
            )
            mids.append(mid)
            moes.append(moe_in)
            gates.append(gate)
            sends.append(send)
            slot_gates.append(slot_gate)
        attended = jnp.stack(attended)
        partials, returned_din, returned_h = [], [], []
        acc = None
        for s in range(seqs):
            received = all_to_all_dp(sends[s])
            received_gate = all_to_all_dp(slot_gates[s])
            part, din, h, acc = experts(received, cot_slots, s, received_gate, weights, acc, s == seqs - 1)
            returned_din.append(all_to_all_dp(din))
            returned_h.append(all_to_all_dp(h))
            partials.append(all_to_all_dp(part))
        kept, given = acc[:, 0::2], flip(acc[:, 1::2], "ctx", 1)

    far_other = flip((kept[1, 1].astype(F32) + given[1, 1].astype(F32)).astype(BF16), "ctx", 2)
    far_send = (kept[0, 1].astype(F32) + given[0, 1].astype(F32)).astype(BF16)

    def summed(half, far):
        return (kept[half, 0].astype(F32) + given[half, 0].astype(F32)) + far.astype(F32)

    hits_of = (heads, 4, 2 * stretch)
    if fits:
        tokens_out, gmid, dattn, grad_proj, gain_moe_grad, router_grad, rel_grad = back_stage(
            mids, moes, gates, lse, returned_din, parts, queries, keys, values, bias, cotangent, wout_own,
            returned_h, places, near_places, ids_query, ids_key, router, gain_moe,
        )
        far_other, far_send, grad_proj = lax.optimization_barrier((far_other, far_send, grad_proj))
        far_mine = flip(far_send, "ctx", 2)
        other = flip(summed(1, far_other).astype(BF16), "tp", 1)
        grad_proj = grad_proj.reshape(3, seqs * stretch, local)
        dattn = dattn.reshape(seqs * stretch, width)
        grad_table = jnp.einsum("bmn,hbm->nh", hot_windows, rel_grad.reshape(hits_of), precision=FULL_PRECISION)
        small = jnp.concatenate(
            [
                router_grad,
                jnp.pad(gain_moe_grad, ((0, 7), (0, 0))),
                jnp.pad(grad_table.T, ((0, 8 - heads), (0, width - NB))),
            ],
            axis=0,
        )
        wide, g_router, g_moe, g_attn, g_table, grad_tokens = last_stage(
            own_normed, grad_proj, dattn, attended.reshape(seqs * stretch, local), small, wqkv, gmid, tokens_in, gain_attn,
            dp, NB // dp, heads, expert_count,
        )
        other, far_mine, wide = lax.optimization_barrier((other, far_mine, wide))
        g_qkv = wide[:3]
        g_wout = wide[3].T
    else:
        far_mine = flip(far_send, "ctx", 2)
        other = flip(summed(1, far_other).astype(BF16), "tp", 1)
        tokens_out, gmids = [], []
        projections = []
        rel_grad = 0.0
        gain_moe_grad = 0.0
        router_grad = 0.0
        datts = []
        for s in range(seqs):
            out_own = combine_out(places[s], partials[s], cap)
            out_other = flip(out_own, "tp", 1)
            tokens_out.append((mids[s] + (out_own.astype(F32) + out_other.astype(F32))).astype(BF16))
            din_own, h_own = combine(places[s], returned_din[s], returned_h[s], cap)
            din_other = flip(din_own, "tp", 1)
            h_all = jnp.concatenate([h_own, flip(h_own, "tp", 1)], axis=0)
            gmid, datt, d_gain, d_router, dattn = middle_back(
                din_own, din_other, h_all, gates[s], router, moes[s], mids[s], gain_moe, cotangent[s], wout_own
            )
            datts.append(dattn)
            gmids.append(gmid)
            gain_moe_grad += d_gain
            router_grad += d_router
            dq, dk, dv, rel = attend_back(
                queries[s], keys[s], values[s], datt, bias, lse[s], ids_query[s], ids_key[s]
            )
            rel_grad += rel
            dkv = jnp.stack([dk, dv]).reshape(2, 4, stretch, local)
            near = dkv[:, 0::2].astype(F32) + flip(dkv[:, 1::2], "ctx", 1).astype(F32)
            full = near[:, 0] + flip(near[:, 1].astype(BF16), "ctx", 2).astype(F32)
            projections.append(jnp.concatenate([dq[None], full.astype(BF16)], axis=0))
        grad_proj = jnp.concatenate(projections, axis=1)
        dattn = jnp.concatenate(datts, axis=0)
        attended = attended.reshape(seqs * stretch, local)
        dnormed_part = jnp.einsum("jre,jde->rd", grad_proj, wqkv, preferred_element_type=F32)
        dnormed_own = dnormed_part.astype(BF16)
        dnormed = dnormed_own.astype(F32) + flip(dnormed_own, "tp", 1).astype(F32)
        own_x = tokens_in.reshape(seqs * stretch, width).astype(F32)
        factor = norm_factor(own_x)
        unit = own_x * factor
        scaled = dnormed * gain_attn
        dres = factor * (scaled - unit * jnp.mean(scaled * unit, axis=-1, keepdims=True))
        grad_tokens = jnp.concatenate(gmids, axis=0) + dres
        grad_table = jnp.einsum("bmn,hbm->nh", hot_windows, rel_grad.reshape(hits_of), precision=FULL_PRECISION)
        router_grad = router_grad.reshape(2, dp, width)
        router_grad = jnp.where(tp == 0, router_grad, router_grad[::-1])
        router_grad = router_grad.transpose(1, 0, 2).reshape(expert_count, width).T

        def reduced(value, dim):
            return lax.psum(lax.psum_scatter(value, "dp", scatter_dimension=dim, tiled=True), "ctx")

        g_attn = reduced(jnp.sum(dnormed * unit, axis=0)[None], 1)
        g_qkv = reduced(jnp.einsum("rd,jre->jde", own_normed, grad_proj, preferred_element_type=F32), 1)
        g_wout = reduced(jnp.einsum("re,rd->ed", attended, dattn, preferred_element_type=F32), 1)
        g_table = reduced(grad_table, 0)
        g_moe = reduced(gain_moe_grad, 1)
        g_router = reduced(router_grad, 0)
        tokens_out = jnp.stack(tokens_out)
    mine = summed(0, far_mine)
    other = other.astype(F32)

    def by_expert(index):
        return jnp.where(
            tp == 0, jnp.stack([mine[index], other[index]]), jnp.stack([other[index], mine[index]])
        )

    grad_expert_in = by_expert(0)
    grad_expert_out = by_expert(1).transpose(0, 2, 1)
    return (
        tokens_out,
        grad_tokens.reshape(seqs, stretch, width),
        g_attn,
        g_qkv[None],
        g_wout[None],
        g_table[None],
        g_moe,
        g_router[None],
        grad_expert_in[None],
        grad_expert_out[None],
    )


def solution(mesh):
    return jax.shard_map(
        on_device,
        mesh=mesh,
        in_specs=(
            P("dp", "ctx", None),
            P("dp", None),
            P(),
            P("dp", "ctx", None),
            P(None, "dp"),
            P(None, None, "dp", "tp"),
            P(None, "tp", "dp"),
            P(None, "dp", "tp"),
            P(None, "dp"),
            P(None, "dp", None),
            P(None, "dp", "ctx", "tp"),
            P(None, "dp", "tp", "ctx"),
            P("dp", "ctx", None),
        ),
        out_specs=(
            P("dp", "ctx", None),
            P("dp", "ctx", None),
            P(None, "dp"),
            P(None, None, "dp", "tp"),
            P(None, "tp", "dp"),
            P(None, "dp", "tp"),
            P(None, "dp"),
            P(None, "dp", None),
            P(None, "dp", "ctx", "tp"),
            P(None, "dp", "tp", "ctx"),
        ),
        check_vma=False,
    )
```

```python
import functools

import jax
import jax.numpy as jnp
from jax import lax
from jax.experimental import pallas as pl
from jax.experimental.pallas import tpu as pltpu
from jax.sharding import PartitionSpec as P

HD = 64
NB = 32
EPSILON = 1e-06
FULL_PRECISION = lax.Precision.HIGHEST
MASKED = -1e30
BF16 = jnp.bfloat16
F32 = jnp.float32
EARLY = 50
FIRST = 1
VMEM_BYTES = 60 * 1024 * 1024
GELU_C = 0.7978845608028654
GELU_A = 0.044715


def params():
    return pltpu.CompilerParams(vmem_limit_bytes=VMEM_BYTES)


def cost(flops, nbytes, trans=0, scale=1):
    return pl.CostEstimate(
        flops=int(flops) // scale, bytes_accessed=int(nbytes) // scale, transcendentals=int(trans) // scale
    )


def dot(a, b):
    return lax.dot_general(a, b, (((1,), (0,)), ((), ())), preferred_element_type=F32)


def dot_nt(a, b):
    return lax.dot_general(a, b, (((1,), (1,)), ((), ())), preferred_element_type=F32)


def dot_tn(a, b):
    return lax.dot_general(a, b, (((0,), (0,)), ((), ())), preferred_element_type=F32)


def bias_kernel(win_ref, out_ref):
    for block in range(4):
        row = win_ref[0, block : block + 1, :]
        wide = jnp.broadcast_to(row, (256, 512))
        rolled = pltpu.roll(wide, 257, 1, stride=1, stride_axis=0)
        out_ref[0, block * 256 : (block + 1) * 256, :] = rolled[:, :256].astype(BF16)


def expand_bias(windows):
    heads = windows.shape[0]
    return pl.pallas_call(
        bias_kernel,
        name="expand_bias",
        grid=(heads,),
        in_specs=[pl.BlockSpec((1, 4, 512), lambda h: (h, 0, 0))],
        out_specs=pl.BlockSpec((1, 1024, 256), lambda h: (h, 0, 0)),
        out_shape=jax.ShapeDtypeStruct((heads, 1024, 256), BF16),
        compiler_params=params(),
        cost_estimate=cost(heads * 2 * 1024 * 512, heads * 1024 * 256 * 2, scale=EARLY),
    )(windows)


def attend_kernel(q_ref, k_ref, v_ref, bias_ref, idq_ref, idk_ref, out_ref, lse_ref, mask_ref):
    @pl.when(pl.program_id(0) == 0)
    def _():
        mask_ref[...] = jnp.where(idk_ref[...] <= idq_ref[...], 0.0, MASKED)

    queries = q_ref[...]
    keys = k_ref[...]
    values_t = v_ref[...].T
    low_half = lax.broadcasted_iota(jnp.int32, queries.shape, 1) < HD
    zero = jnp.zeros_like(queries)
    parts = []
    for head in range(2):
        own = jnp.where(low_half, queries, zero) if head == 0 else jnp.where(low_half, zero, queries)
        scores = dot_nt(keys, own) + bias_ref[head].astype(F32) + mask_ref[...]
        top = jnp.max(scores, axis=0, keepdims=True)
        weights = jnp.exp(scores - top)
        total = jnp.sum(weights, axis=0, keepdims=True)
        part = dot(values_t[head * HD : (head + 1) * HD], weights.astype(BF16)) * (1.0 / total)
        parts.append(part)
        lse_ref[0, head : head + 1, :] = top + jnp.log(total)
    out_ref[...] = jnp.concatenate(parts, axis=0).T.astype(BF16)


def attend(queries, keys, values, bias, ids_query, ids_key):
    rows, width = queries.shape
    length = keys.shape[0]
    pairs = width // (2 * HD)
    return pl.pallas_call(
        attend_kernel,
        name="attend",
        grid=(pairs,),
        in_specs=[
            pl.BlockSpec((rows, 128), lambda p: (0, p)),
            pl.BlockSpec((length, 128), lambda p: (0, p)),
            pl.BlockSpec((length, 128), lambda p: (0, p)),
            pl.BlockSpec((2, length, rows), lambda p: (p, 0, 0)),
            pl.BlockSpec((1, rows), lambda p: (0, 0)),
            pl.BlockSpec((length, 1), lambda p: (0, 0)),
        ],
        out_specs=[
            pl.BlockSpec((rows, 128), lambda p: (0, p)),
            pl.BlockSpec((1, 2, rows), lambda p: (p, 0, 0)),
        ],
        out_shape=[
            jax.ShapeDtypeStruct((rows, width), BF16),
            jax.ShapeDtypeStruct((pairs, 2, rows), F32),
        ],
        scratch_shapes=[pltpu.VMEM((length, rows), F32)],
        compiler_params=params(),
        cost_estimate=cost(pairs * 2 * 4 * rows * length * 128, 6 * rows * length * 2, pairs * 2 * rows * length, scale=EARLY),
    )(queries, keys, values, bias, ids_query, ids_key)


def attend_back_kernel(
    q_ref, k_ref, v_ref, do_ref, bias_ref, lse_ref, idq_ref, idk_ref, dq_ref, dk_ref, dv_ref, rel_ref, mask_ref
):
    @pl.when(pl.program_id(0) == 0)
    def _():
        mask_ref[...] = jnp.where(idk_ref[...] <= idq_ref[...], 0.0, MASKED)

    queries = q_ref[...]
    keys = k_ref[...]
    values = v_ref[...]
    grad_out = do_ref[...]
    keys_t = keys.T
    low_half = lax.broadcasted_iota(jnp.int32, queries.shape, 1) < HD
    zero = jnp.zeros_like(queries)
    dk = None
    dv = None
    dq_parts = []
    for head in range(2):
        own = (lambda a: jnp.where(low_half, a, zero)) if head == 0 else (lambda a: jnp.where(low_half, zero, a))
        q_own = own(queries)
        do_own = own(grad_out)
        scores = dot_nt(keys, q_own) + bias_ref[head].astype(F32) + mask_ref[...]
        probs = jnp.exp(scores - lse_ref[0, head : head + 1, :])
        dprobs = dot_nt(values, do_own)
        delta = jnp.sum(probs * dprobs, axis=0, keepdims=True)
        dscores = probs * (dprobs - delta)
        low = dscores.astype(BF16)
        dv_head = dot(probs.astype(BF16), do_own)
        dk_head = dot(low, q_own)
        dv = dv_head if dv is None else dv + dv_head
        dk = dk_head if dk is None else dk + dk_head
        dq_parts.append(dot(keys_t[head * HD : (head + 1) * HD], low))
        for block in range(4):
            tile = dscores[block * 256 : (block + 1) * 256]
            wide = jnp.concatenate([tile, jnp.zeros_like(tile)], axis=1)
            total = None
            for group in range(32):
                moved = pltpu.roll(wide[group * 8 : group * 8 + 8], 248 - 8 * group, 1)
                total = moved if total is None else total + moved
            row = lax.broadcasted_iota(jnp.int32, total.shape, 0)
            amount = 7 - row
            for bit in (1, 2, 4):
                total = jnp.where((amount & bit) != 0, pltpu.roll(total, bit, 1), total)
            rel_ref[0, head, block : block + 1, :] = jnp.sum(total, axis=0, keepdims=True)
    dq_ref[...] = (jnp.concatenate(dq_parts, axis=0).T * (HD ** (-0.5))).astype(BF16)
    dk_ref[...] = dk.astype(BF16)
    dv_ref[...] = dv.astype(BF16)


def attend_back(queries, keys, values, grad_out, bias, lse, ids_query, ids_key):
    rows, width = queries.shape
    length = keys.shape[0]
    pairs = width // (2 * HD)
    return pl.pallas_call(
        attend_back_kernel,
        name="attend_back",
        grid=(pairs,),
        in_specs=[
            pl.BlockSpec((rows, 128), lambda p: (0, p)),
            pl.BlockSpec((length, 128), lambda p: (0, p)),
            pl.BlockSpec((length, 128), lambda p: (0, p)),
            pl.BlockSpec((rows, 128), lambda p: (0, p)),
            pl.BlockSpec((2, length, rows), lambda p: (p, 0, 0)),
            pl.BlockSpec((1, 2, rows), lambda p: (p, 0, 0)),
            pl.BlockSpec((1, rows), lambda p: (0, 0)),
            pl.BlockSpec((length, 1), lambda p: (0, 0)),
        ],
        out_specs=[
            pl.BlockSpec((rows, 128), lambda p: (0, p)),
            pl.BlockSpec((length, 128), lambda p: (0, p)),
            pl.BlockSpec((length, 128), lambda p: (0, p)),
            pl.BlockSpec((1, 2, 4, 512), lambda p: (p, 0, 0, 0)),
        ],
        out_shape=[
            jax.ShapeDtypeStruct((rows, width), BF16),
            jax.ShapeDtypeStruct((length, width), BF16),
            jax.ShapeDtypeStruct((length, width), BF16),
            jax.ShapeDtypeStruct((pairs, 2, 4, 512), F32),
        ],
        scratch_shapes=[pltpu.VMEM((length, rows), F32)],
        compiler_params=params(),
        cost_estimate=cost(pairs * 2 * 10 * rows * length * 128, 8 * rows * length * 2, pairs * 2 * rows * length),
    )(queries, keys, values, grad_out, bias, lse, ids_query, ids_key)


def one_hot(place, cap):
    groups, rows = place.shape
    slots = lax.broadcasted_iota(jnp.int32, (cap, rows), 0).astype(F32)
    return [slots == place[group : group + 1, :] for group in range(groups)]


def diagonal(cap):
    return lax.broadcasted_iota(jnp.int32, (cap, cap), 0) == lax.broadcasted_iota(jnp.int32, (cap, cap), 1)


def dispatch_kernel(groups, cap, place_ref, rows_ref, out_ref):
    rows = rows_ref[0]
    picks = one_hot(place_ref[0], cap)
    pick = jnp.concatenate([jnp.where(p, 1.0, 0.0).astype(BF16) for p in picks], axis=0)
    out_ref[:, 0] = dot(pick, rows).astype(BF16).reshape(groups, cap, rows.shape[1])


def dispatch(place, rows, cap):
    seqs, groups, stretch = place.shape
    width = rows.shape[2]
    return pl.pallas_call(
        functools.partial(dispatch_kernel, groups, cap),
        name="dispatch_rows",
        grid=(seqs,),
        in_specs=[
            pl.BlockSpec((1, groups, stretch), lambda s: (s, 0, 0)),
            pl.BlockSpec((1, stretch, width), lambda s: (s, 0, 0)),
        ],
        out_specs=pl.BlockSpec((groups, 1, cap, width), lambda s: (0, s, 0, 0)),
        out_shape=jax.ShapeDtypeStruct((groups, seqs, cap, width), BF16),
        compiler_params=params(),
        cost_estimate=cost(seqs * 2 * groups * cap * stretch * width, seqs * 2 * (stretch + groups * cap) * width),
    )(place, rows)


def norm_factor(value):
    return lax.rsqrt(jnp.mean(value * value, axis=-1, keepdims=True) + EPSILON)


def middle_kernel(
    groups, cap, own_ref, other_ref, x_ref, wout_ref, gain_ref, router_ref, hits_ref, place_ref,
    middle_ref, moe_ref, gates_ref, send_ref, slot_gate_ref,
):
    mid = x_ref[...].astype(F32) + (dot(own_ref[...], wout_ref[0]) + dot(other_ref[...], wout_ref[1]))
    middle_ref[...] = mid
    moe_in = (mid * norm_factor(mid) * gain_ref[...].astype(F32)).astype(BF16)
    moe_ref[...] = moe_in
    logits = dot_nt(router_ref[...], moe_in)
    hit = hits_ref[...] > 0.5
    top = jnp.max(jnp.where(hit, logits, MASKED), axis=0, keepdims=True)
    raw = jnp.where(hit, jnp.exp(jnp.where(hit, logits, top) - top), 0.0)
    gates = raw / jnp.sum(raw, axis=0, keepdims=True)
    gates_ref[...] = gates
    picks = one_hot(place_ref[...], cap)
    pick = jnp.concatenate([jnp.where(p, 1.0, 0.0).astype(BF16) for p in picks], axis=0)
    send_ref[...] = dot(pick, moe_in).astype(BF16).reshape(groups, cap, moe_in.shape[1])
    eye = diagonal(cap)
    for group in range(groups):
        column = jnp.sum(jnp.where(picks[group], gates[group : group + 1, :], 0.0), axis=1, keepdims=True)
        slot_gate_ref[group] = jnp.sum(jnp.where(eye, column, 0.0), axis=0, keepdims=True)


def middle_stage(own, other, x, wout, gain, router, hits, place, cap):
    rows, width = x.shape
    experts = router.shape[0]
    groups = place.shape[0]
    return pl.pallas_call(
        functools.partial(middle_kernel, groups, cap),
        name="middle_stage",
        out_shape=[
            jax.ShapeDtypeStruct((rows, width), F32),
            jax.ShapeDtypeStruct((rows, width), BF16),
            jax.ShapeDtypeStruct((experts, rows), F32),
            jax.ShapeDtypeStruct((groups, cap, width), BF16),
            jax.ShapeDtypeStruct((groups, 1, cap), F32),
        ],
        compiler_params=params(),
        cost_estimate=cost(2 * rows * width * width + 2 * groups * cap * rows * width, rows * width * 16, scale=EARLY),
    )(own, other, x, wout, gain, router, hits, place)


def expert_kernel(
    first, final, tiles, groups, cap, x_ref, g_ref, gate_ref, w_ref, *refs
):
    if first:
        acc_in = None
    else:
        acc_in, refs = refs[0], refs[1:]
    part_out, din_out, h_out, acc_out, xt_ref, dy_ref, dyt_ref, part_ref, din_ref = refs
    step = pl.program_id(0)
    rows = groups * cap
    width = x_ref.shape[-1]
    slices = w_ref.shape[0]
    piece = width // slices

    @pl.when(step == 0)
    def _():
        eye = diagonal(cap)
        xt_ref[...] = x_ref[...].reshape(rows, width).T
        for group in range(groups):
            gate = jnp.sum(jnp.where(eye, gate_ref[group], 0.0), axis=1, keepdims=True)
            dy_ref[group * cap : (group + 1) * cap] = (g_ref[group, 0].astype(F32) * gate).astype(BF16)
        dyt_ref[...] = dy_ref[...].T

    x = x_ref[...].reshape(rows, width)
    w_in = w_ref[:, 0, 0].reshape(width, -1)
    w_out_t = w_ref[:, 1, 0].reshape(width, -1)
    dy = dy_ref[...]
    pre = dot(x, w_in)
    square = pre * pre
    inner = jnp.tanh(GELU_C * pre * (1.0 + GELU_A * square))
    half = 0.5 * (1.0 + inner)
    hidden = (pre * half).astype(BF16)
    slope = half + (0.5 * GELU_C) * pre * (1.0 - inner * inner) * (1.0 + (3.0 * GELU_A) * square)
    dhid = dot(dy, w_out_t)
    dpre = (dhid * slope).astype(BF16)
    part = dot_nt(hidden, w_out_t)
    din = dot_nt(dpre, w_in)
    dw_in = dot(xt_ref[...], dpre)
    dw_out_t = dot(dyt_ref[...], hidden)

    @pl.when(step == 0)
    def _():
        part_ref[...] = part
        din_ref[...] = din

    @pl.when(step > 0)
    def _():
        part_ref[...] += part
        din_ref[...] += din

    me = lax.axis_index("ctx")
    for index in range(slices):
        place = index ^ me
        grad_in = dw_in[index * piece : (index + 1) * piece]
        grad_out = dw_out_t[index * piece : (index + 1) * piece]
        if not first:
            grad_in += acc_in[0, place, 0]
            grad_out += acc_in[0, place, 1]
        acc_out[0, place, 0] = grad_in.astype(acc_out.dtype)
        acc_out[0, place, 1] = grad_out.astype(acc_out.dtype)

    @pl.when(step == tiles - 1)
    def _():
        eye = diagonal(cap)
        for group in range(groups):
            gate = jnp.sum(jnp.where(eye, gate_ref[group], 0.0), axis=1, keepdims=True)
            gated = part_ref[group * cap : (group + 1) * cap] * gate
            part_out[group] = gated.astype(BF16)
            din_out[group] = din_ref[group * cap : (group + 1) * cap].astype(BF16)
            h = jnp.sum(gated * g_ref[group, 0].astype(F32), axis=1, keepdims=True)
            h_out[group] = jnp.sum(jnp.where(eye, h, 0.0), axis=0, keepdims=True)


def experts(x, cot_slots, seq_index, gate, weights, acc, final, tile=512):
    groups, cap, width = x.shape
    slices, _, halves, piece, half_len = weights.shape
    per_half = half_len // tile
    tiles = halves * per_half
    rows = groups * cap
    first = acc is None
    acc_spec = pl.BlockSpec((1, slices, 2, piece, tile), lambda f: (f // per_half, 0, 0, 0, f % per_half))
    in_specs = [
        pl.BlockSpec((groups, cap, width), lambda f: (0, 0, 0)),
        pl.BlockSpec((groups, 1, cap, width), lambda f: (0, seq_index, 0, 0)),
        pl.BlockSpec((groups, 1, cap), lambda f: (0, 0, 0)),
        pl.BlockSpec((slices, 2, 1, piece, tile), lambda f: (0, 0, f // per_half, 0, f % per_half)),
    ]
    args = [x, cot_slots, gate, weights]
    aliases = {}
    if not first:
        in_specs.append(acc_spec)
        args.append(acc)
        if not final:
            aliases = {4: 3}
    acc_shape = (halves, slices, 2, piece, half_len)
    return pl.pallas_call(
        functools.partial(expert_kernel, first, final, tiles, groups, cap),
        name="experts",
        grid=(tiles,),
        in_specs=in_specs,
        out_specs=[
            pl.BlockSpec((groups, cap, width), lambda f: (0, 0, 0)),
            pl.BlockSpec((groups, cap, width), lambda f: (0, 0, 0)),
            pl.BlockSpec((groups, 1, cap), lambda f: (0, 0, 0)),
            acc_spec,
        ],
        out_shape=[
            jax.ShapeDtypeStruct((groups, cap, width), BF16),
            jax.ShapeDtypeStruct((groups, cap, width), BF16),
            jax.ShapeDtypeStruct((groups, 1, cap), F32),
            jax.ShapeDtypeStruct(acc_shape, BF16 if final else F32),
        ],
        scratch_shapes=[
            pltpu.VMEM((width, rows), BF16),
            pltpu.VMEM((rows, width), BF16),
            pltpu.VMEM((width, rows), BF16),
            pltpu.VMEM((rows, width), F32),
            pltpu.VMEM((rows, width), F32),
        ],
        input_output_aliases=aliases,
        compiler_params=params(),
        cost_estimate=cost(12 * rows * width * halves * half_len, 2 * width * halves * half_len * 10, rows * halves * half_len),
    )(*args)


def combine_kernel(groups, cap, place_ref, din_ref, h_ref, din_out, h_out):
    picks = one_hot(place_ref[...], cap)
    pick = jnp.concatenate([jnp.where(p, 1.0, 0.0).astype(BF16) for p in picks], axis=0)
    rows = groups * cap
    din_out[...] = dot_tn(pick, din_ref[...].reshape(rows, din_ref.shape[-1])).astype(BF16)
    eye = diagonal(cap)
    for group in range(groups):
        column = jnp.sum(jnp.where(eye, h_ref[group], 0.0), axis=1, keepdims=True)
        h_out[group : group + 1, :] = jnp.sum(jnp.where(picks[group], column, 0.0), axis=0, keepdims=True)


def combine(place, din, h, cap):
    groups, stretch = place.shape
    width = din.shape[-1]
    return pl.pallas_call(
        functools.partial(combine_kernel, groups, cap),
        name="combine_back",
        out_shape=[
            jax.ShapeDtypeStruct((stretch, width), BF16),
            jax.ShapeDtypeStruct((groups, stretch), F32),
        ],
        compiler_params=params(),
        cost_estimate=cost(2 * groups * cap * stretch * width, 4 * stretch * width * 2),
    )(place, din, h)


def combine_out_kernel(groups, cap, place_ref, part_ref, out_ref):
    picks = one_hot(place_ref[...], cap)
    pick = jnp.concatenate([jnp.where(p, 1.0, 0.0).astype(BF16) for p in picks], axis=0)
    out_ref[...] = dot_tn(pick, part_ref[...].reshape(groups * cap, part_ref.shape[-1])).astype(BF16)


def combine_out(place, part, cap):
    groups, stretch = place.shape
    width = part.shape[-1]
    return pl.pallas_call(
        functools.partial(combine_out_kernel, groups, cap),
        name="combine_out",
        out_shape=jax.ShapeDtypeStruct((stretch, width), BF16),
        compiler_params=params(),
        cost_estimate=cost(2 * groups * cap * stretch * width, 4 * stretch * width * 2),
    )(place, part)


def middle_back_kernel(
    own_ref, other_ref, h_ref, gates_ref, router_ref, moe_ref, mid_ref, gain_ref, cot_ref, wout_ref,
    gmid_ref, datt_ref, gain_grad_ref, router_grad_ref, low_ref,
):
    h = h_ref[...]
    dlogits = h - gates_ref[...] * jnp.sum(h, axis=0, keepdims=True)
    router = router_ref[...]
    dmoe = own_ref[...].astype(F32) + other_ref[...].astype(F32)
    dmoe = dmoe + lax.dot_general(
        dlogits, router.astype(F32), (((0,), (0,)), ((), ())), precision=FULL_PRECISION, preferred_element_type=F32
    )
    router_grad_ref[...] = lax.dot_general(
        dlogits, moe_ref[...].astype(F32), (((1,), (0,)), ((), ())), precision=FULL_PRECISION, preferred_element_type=F32
    )
    mid = mid_ref[...]
    gain = gain_ref[...].astype(F32)
    factor = norm_factor(mid)
    normed = mid * factor
    gain_grad_ref[...] = jnp.sum(dmoe * normed, axis=0, keepdims=True)
    scaled = dmoe * gain
    dmid = factor * (scaled - normed * jnp.mean(scaled * normed, axis=-1, keepdims=True))
    gmid = cot_ref[...].astype(F32) + dmid
    gmid_ref[...] = gmid
    dattn = gmid.astype(BF16)
    datt_ref[...] = dot_nt(dattn, wout_ref[...]).astype(BF16)
    low_ref[...] = dattn


def middle_back(own, other, h, gates, router, moe_in, mid, gain, cot, wout):
    rows, width = mid.shape
    local = wout.shape[0]
    return pl.pallas_call(
        middle_back_kernel,
        name="middle_back",
        out_shape=[
            jax.ShapeDtypeStruct((rows, width), F32),
            jax.ShapeDtypeStruct((rows, local), BF16),
            jax.ShapeDtypeStruct((1, width), F32),
            jax.ShapeDtypeStruct(router.shape, F32),
            jax.ShapeDtypeStruct((rows, width), BF16),
        ],
        compiler_params=params(),
        cost_estimate=cost(2 * rows * width * local, 30 * rows * width),
    )(own, other, h, gates, router, moe_in, mid, gain, cot, wout)


MESH_ID = pl.DeviceIdType.MESH


def remote(src, dst, send_sem, recv_sem, **where):
    return pltpu.make_async_remote_copy(
        src_ref=src, dst_ref=dst, send_sem=send_sem, recv_sem=recv_sem, device_id=where, device_id_type=MESH_ID
    )


def greet(peers):
    barrier = pltpu.get_barrier_semaphore()
    for where in peers:
        pl.semaphore_signal(barrier, inc=1, device_id=where, device_id_type=MESH_ID)
    pl.semaphore_wait(barrier, len(peers))


def first_kernel(
    seqs, cap, tok_ref, wqkv_ref, wout_ref, table_ref, ga_ref, gm_ref, router_ref, win_ref, wot_ref, near_ref, cot_ref,
    q_ref, k_ref, v_ref, normed_ref, wqkv_out, wout_out, table_out, gain_ref, gm_out, router_out, got_out,
    slots_ref, cot_out,
    tok_all, n_all, ga_all, gm_all, router_all,
    z_send, z_recv, f_send, f_recv, t_send, t_recv, y_send, y_recv, l_sem, e_sems, c_sems,
):
    dp = lax.axis_index("dp")
    ctx = lax.axis_index("ctx")
    tp = lax.axis_index("tp")
    core = ctx % 2
    rows = wqkv_ref.shape[1]
    half = rows // 2
    greet([{"dp": dp ^ b} for b in (1, 2, 3)] + [{"ctx": ctx ^ 1}, {"ctx": ctx ^ 2}, {"tp": tp ^ 1}])

    def w_rows(owner, side):
        return pl.ds(pl.multiple_of(owner * rows + side * half, 16), half)

    def z_copies(b):
        to = {"dp": dp ^ b}
        return [
            remote(ga_ref, ga_all.at[dp], z_send.at[0, b - 1], z_recv.at[0, b - 1], **to),
            remote(gm_ref, gm_all.at[dp], z_send.at[1, b - 1], z_recv.at[1, b - 1], **to),
            remote(table_ref, table_out.at[dp], z_send.at[2, b - 1], z_recv.at[2, b - 1], **to),
            remote(router_ref, router_all.at[dp], z_send.at[3, b - 1], z_recv.at[3, b - 1], **to),
            remote(
                wqkv_ref.at[:, pl.ds(pl.multiple_of(core * half, 16), half)], wqkv_out.at[:, w_rows(dp, core)],
                z_send.at[4, b - 1], z_recv.at[4, b - 1], **to,
            ),
            remote(
                wout_ref.at[pl.ds(pl.multiple_of(core * half, 16), half)], wout_out.at[w_rows(dp, core)],
                z_send.at[5, b - 1], z_recv.at[5, b - 1], **to,
            ),
        ]

    small = [z_copies(b) for b in (1, 2, 3)]
    for kind in range(6):
        for b in (3, 2, 1):
            small[b - 1][kind].start()
    beside = remote(tok_ref, tok_all.at[1], t_send.at[0], t_recv.at[0], ctx=ctx ^ 1)
    beside.start()
    across = [remote(tok_ref.at[s], tok_all.at[2, s], y_send.at[s], y_recv.at[s], ctx=ctx ^ 2) for s in range(seqs)]
    expert_copies = [
        remote(win_ref.at[1 - tp], got_out.at[0], e_sems.at[0, 0], e_sems.at[1, 0], tp=tp ^ 1),
        remote(wot_ref.at[1 - tp], got_out.at[1], e_sems.at[0, 1], e_sems.at[1, 1], tp=tp ^ 1),
    ]
    for copy in across + expert_copies:
        copy.start()
    own = [
        pltpu.make_async_copy(tok_ref, tok_all.at[0], l_sem.at[0]),
        pltpu.make_async_copy(ga_ref, ga_all.at[dp], l_sem.at[1]),
        pltpu.make_async_copy(gm_ref, gm_all.at[dp], l_sem.at[2]),
        pltpu.make_async_copy(table_ref, table_out.at[dp], l_sem.at[3]),
        pltpu.make_async_copy(router_ref, router_all.at[dp], l_sem.at[4]),
        pltpu.make_async_copy(wqkv_ref, wqkv_out.at[:, pl.ds(pl.multiple_of(dp * rows, 16), rows)], l_sem.at[5]),
        pltpu.make_async_copy(wout_ref, wout_out.at[pl.ds(pl.multiple_of(dp * rows, 16), rows)], l_sem.at[6]),
    ]
    for copy in own:
        copy.start()

    groups = slots_ref.shape[0]

    def cot_copy(s, b):
        return remote(
            slots_ref.at[b, s], cot_out.at[b - 1, s], c_sems.at[0, s, b - 1], c_sems.at[1, s, b - 1], dp=dp ^ b
        )

    def dispatch_cot(s, carry):
        picks = one_hot(near_ref[s], cap)
        pick = jnp.concatenate([jnp.where(p, 1.0, 0.0).astype(BF16) for p in picks], axis=0)
        slots_ref[:, s] = dot(pick, cot_ref[s]).astype(BF16).reshape(groups, cap, cot_ref.shape[2])

        @pl.when(s < FIRST)
        def _():
            for b in (3, 2, 1):
                cot_copy(s, b).start()

        return carry

    lax.fori_loop(0, seqs, dispatch_cot, 0)
    for copy in own:
        copy.wait()

    for kind in range(4):
        for b in (3, 2, 1):
            small[b - 1][kind].wait_recv()
    count = ga_all.shape[0]
    piece = ga_all.shape[2]
    width = count * piece
    row = lax.broadcasted_iota(jnp.int32, (piece, width), 0)
    col = lax.broadcasted_iota(jnp.int32, (piece, width), 1)
    gain = 0.0
    gain_m = 0.0
    for d in range(count):
        spread = jnp.where(col == row + d * piece, 1.0, 0.0).astype(BF16)
        gain = gain + dot(ga_all[d], spread)
        gain_m = gain_m + dot(gm_all[d], spread)
    gain_ref[...] = gain
    gm_out[...] = gain_m.astype(BF16)
    experts_n = router_ref.shape[0]
    slot_row = lax.broadcasted_iota(jnp.int32, (experts_n, experts_n), 0)
    slot_col = lax.broadcasted_iota(jnp.int32, (experts_n, experts_n), 1)
    side = slot_row // count
    expert = (slot_row % count) * 2 + (side ^ tp)
    order = jnp.where(slot_col == expert, 1.0, 0.0).astype(BF16)
    router_out[...] = dot(order, jnp.concatenate([router_all[d] for d in range(count)], axis=1)).astype(BF16)

    def norm_piece(b):
        def body(s, carry):
            value = tok_all[b, s].astype(F32)
            out = (value * norm_factor(value) * gain_ref[...]).astype(BF16)
            n_all[b, s] = out
            return carry

        lax.fori_loop(0, seqs, body, 0)

    def project(b, s):
        x = n_all[b, s]
        k_ref[s, b] = dot(x, wqkv_out[1]).astype(BF16)
        v_ref[s, b] = dot(x, wqkv_out[2]).astype(BF16)

    norm_piece(0)
    normed_ref[...] = n_all[0]
    beside.wait_recv()
    norm_piece(1)

    forwards = []

    def forward(kind, ref, b):
        small[b - 1][kind + 4].wait_recv()
        copy = remote(ref, ref, f_send.at[kind, b - 1], f_recv.at[kind, b - 1], ctx=ctx ^ 1)
        copy.start()
        forwards.append(copy)

    for b in (1, 2, 3):
        forward(0, wqkv_out.at[:, w_rows(dp ^ b, core)], b)
    for copy in forwards:
        copy.wait_recv()

    def own_q(s, carry):
        q_ref[s] = (dot(n_all[0, s], wqkv_out[0]).astype(BF16) * (HD ** (-0.5))).astype(BF16)
        project(0, s)
        project(1, s)
        return carry

    lax.fori_loop(0, seqs, own_q, 0)
    for b in (1, 2, 3):
        forward(1, wout_out.at[w_rows(dp ^ b, core)], b)
    later = []
    for s in range(seqs):
        across[s].wait_recv()
        copy = remote(tok_all.at[2, s], tok_all.at[3, s], t_send.at[1 + s], t_recv.at[1 + s], ctx=ctx ^ 1)
        copy.start()
        later.append(copy)
    norm_piece(2)
    for copy in later:
        copy.wait_recv()
    norm_piece(3)

    def others(s, carry):
        project(2, s)
        project(3, s)
        return carry

    lax.fori_loop(0, seqs, others, 0)
    for copy in forwards[3:]:
        copy.wait_recv()
    for copy in expert_copies:
        copy.wait()
    for s in range(FIRST):
        for b in (3, 2, 1):
            cot_copy(s, b).wait()
    for group in small:
        for copy in group:
            copy.wait_send()
    for copy in forwards + later + across + [beside]:
        copy.wait_send()


def first_stage(tokens, wqkv, wout, table, gain_attn, gain_moe, router, w_in, w_out, near, cot, cap):
    seqs, stretch, width = tokens.shape
    count, rows, local = wqkv.shape
    dp = width // rows
    experts_n = router.shape[0]
    any_spec = pl.BlockSpec(memory_space=pl.ANY)
    vmem = pl.BlockSpec(memory_space=pltpu.VMEM)
    dma = pltpu.SemaphoreType.DMA
    return pl.pallas_call(
        functools.partial(first_kernel, seqs, cap),
        name="first_stage",
        in_specs=[any_spec] * 9 + [vmem] * 2,
        out_specs=[vmem] * 10 + [any_spec, vmem, any_spec],
        out_shape=[
            jax.ShapeDtypeStruct((seqs, stretch, local), BF16),
            jax.ShapeDtypeStruct((seqs, 4, stretch, local), BF16),
            jax.ShapeDtypeStruct((seqs, 4, stretch, local), BF16),
            jax.ShapeDtypeStruct((seqs, stretch, width), BF16),
            jax.ShapeDtypeStruct((3, width, local), BF16),
            jax.ShapeDtypeStruct((width, local), BF16),
            jax.ShapeDtypeStruct((dp,) + table.shape, BF16),
            jax.ShapeDtypeStruct((1, width), F32),
            jax.ShapeDtypeStruct((1, width), BF16),
            jax.ShapeDtypeStruct((experts_n, width), BF16),
            jax.ShapeDtypeStruct(w_in.shape, BF16),
            jax.ShapeDtypeStruct((dp, seqs, cap, width), BF16),
            jax.ShapeDtypeStruct((dp - 1, FIRST, cap, width), BF16),
        ],
        scratch_shapes=[
            pltpu.VMEM((4, seqs, stretch, width), BF16),
            pltpu.VMEM((4, seqs, stretch, width), BF16),
            pltpu.VMEM((dp, 1, rows), BF16),
            pltpu.VMEM((dp, 1, rows), BF16),
            pltpu.VMEM((dp, experts_n, rows), BF16),
            dma((6, 3)), dma((6, 3)), dma((2, 3)), dma((2, 3)), dma((1 + seqs,)), dma((1 + seqs,)),
            dma((seqs,)), dma((seqs,)), dma((7,)), dma((2, 2)), dma((2, FIRST, 3)),
        ],
        compiler_params=pltpu.CompilerParams(vmem_limit_bytes=VMEM_BYTES, collective_id=0, has_side_effects=True),
        cost_estimate=cost(40 * 10**9, 10**7),
    )(tokens, wqkv, wout, table, gain_attn, gain_moe, router, w_in, w_out, near, cot)


def block_mask(keys, queries):
    ones = jnp.ones(queries.shape, BF16)
    spread = lax.dot_general(keys, ones, (((0,), (0,)), ((), ())), preferred_element_type=F32)
    return jnp.where(spread <= queries, 0.0, MASKED)


def back_kernel(seqs, groups, cap, *refs):
    seq_refs, refs = refs[:4], refs[4:]
    din_ref, part_ref, q_ref, k_ref, v_ref, bias_ref, cot_ref, wout_ref = refs[:8]
    h_ref, place_ref, near_ref, idq_ref, idk_ref, router_ref, gain_ref = refs[8:15]
    out_ref, gmid_ref, low_ref, proj_ref, gain_grad_ref, router_grad_ref, rel_ref = refs[15:22]
    (
        mid_v, moe_v, gate_v, lse_v, din_v, part_v, q_v, k_v, v_v, bias_v, cot_v, wout_v,
        din_own, din_other, h_own, h_other, out_own, out_other, datt_v, mask_v, keep_v, give_v, core_v, y_v, far_v,
        load_sems, seq_sems, part_sems, x_sems, c_sems, y_sems,
    ) = refs[22:]
    dp = lax.axis_index("dp")
    ctx = lax.axis_index("ctx")
    tp = lax.axis_index("tp")
    greet([{"dp": dp ^ b} for b in range(1, groups)] + [{"ctx": ctx ^ 1}, {"ctx": ctx ^ 2}, {"tp": tp ^ 1}])
    rows = groups * cap
    stretch, width = mid_v.shape[1:]
    local = q_v.shape[2]
    pairs = local // (2 * HD)

    def part_copy(s, b):
        return remote(part_ref.at[b, s], part_v.at[b, s], part_sems.at[0, s, b], part_sems.at[1, s, b], dp=dp ^ b)

    for s in range(seqs):
        for b in range(groups - 1, 0, -1):
            part_copy(s, b).start()
    din_load = pltpu.make_async_copy(din_ref, din_v, load_sems.at[0])
    loads = [
        pltpu.make_async_copy(src, dst, load_sems.at[i + 1])
        for i, (src, dst) in enumerate(
            ((wout_ref, wout_v), (cot_ref, cot_v), (q_ref, q_v), (k_ref, k_v), (v_ref, v_v), (bias_ref, bias_v),
             (part_ref.at[0], part_v.at[0]))
        )
    ]
    for i, (src, dst) in enumerate(zip(seq_refs, (mid_v, moe_v, gate_v, lse_v))):
        loads.append(pltpu.make_async_copy(src, dst, seq_sems.at[i]))
    din_load.start()
    for copy in loads:
        copy.start()
    gain_grad_ref[...] = jnp.zeros_like(gain_grad_ref)
    router_grad_ref[...] = jnp.zeros_like(router_grad_ref)
    rel_ref[...] = jnp.zeros_like(rel_ref)

    def din_copy(s):
        return remote(din_own.at[s], din_other.at[s], x_sems.at[0, 0, s], x_sems.at[1, 0, s], tp=tp ^ 1)

    def h_copy(s):
        return remote(h_own.at[s], h_other.at[s], x_sems.at[0, 1, s], x_sems.at[1, 1, s], tp=tp ^ 1)

    def out_copy(s):
        return remote(out_own.at[s], out_other.at[s], x_sems.at[0, 2, s], x_sems.at[1, 2, s], tp=tp ^ 1)

    def core_copy(s):
        return remote(give_v.at[s], core_v.at[s], c_sems.at[0, s], c_sems.at[1, s], ctx=ctx ^ 1)

    def y_copy(s):
        return remote(y_v.at[s], far_v.at[s], y_sems.at[0, s], y_sems.at[1, s], ctx=ctx ^ 2)

    def chosen(place):
        picks = one_hot(place, cap)
        return picks, jnp.concatenate([jnp.where(p, 1.0, 0.0).astype(BF16) for p in picks], axis=0)

    din_load.wait()

    def gather_back(s, carry):
        picks, pick = chosen(place_ref[s])
        din_own[s] = dot_tn(pick, din_v[s].reshape(rows, width)).astype(BF16)
        eye = diagonal(cap)
        for group in range(groups):
            column = jnp.sum(jnp.where(eye, h_ref[s, group], 0.0), axis=1, keepdims=True)
            h_own[s, group : group + 1, :] = jnp.sum(jnp.where(picks[group], column, 0.0), axis=0, keepdims=True)
        h_copy(s).start()
        din_copy(s).start()
        return carry

    lax.fori_loop(0, seqs, gather_back, 0)
    for copy in loads:
        copy.wait()

    def middle_back(s):
        h = jnp.concatenate([h_own[s], h_other[s]], axis=0)
        dlogits = h - gate_v[s] * jnp.sum(h, axis=0, keepdims=True)
        dmoe = din_own[s].astype(F32) + din_other[s].astype(F32)
        dmoe = dmoe + lax.dot_general(
            dlogits, router_ref[...].astype(F32), (((0,), (0,)), ((), ())),
            precision=FULL_PRECISION, preferred_element_type=F32,
        )
        router_grad_ref[...] += lax.dot_general(
            dlogits, moe_v[s].astype(F32), (((1,), (0,)), ((), ())),
            precision=FULL_PRECISION, preferred_element_type=F32,
        )
        mid = mid_v[s]
        factor = norm_factor(mid)
        normed = mid * factor
        gain_grad_ref[...] += jnp.sum(dmoe * normed, axis=0, keepdims=True)
        scaled = dmoe * gain_ref[...].astype(F32)
        dmid = factor * (scaled - normed * jnp.mean(scaled * normed, axis=-1, keepdims=True))
        gmid = cot_v[s].astype(F32) + dmid
        gmid_ref[s] = gmid
        dattn = gmid.astype(BF16)
        low_ref[s] = dattn
        datt_v[...] = dot(dattn, wout_v[...]).astype(BF16)

    def core_sum(s):
        core_copy(s).wait_recv()
        for kind in range(2):
            keep_v[s, kind, 0] += core_v[s, kind, 0].astype(F32)
            y_v[s, kind] = (keep_v[s, kind, 1] + core_v[s, kind, 1].astype(F32)).astype(BF16)
        y_copy(s).start()

    def out_sum(s):
        for b in range(1, groups):
            part_copy(s, b).wait_recv()
        pick = chosen(near_ref[s])[1]
        out_own[s] = dot_tn(pick, part_v[:, s].reshape(rows, width)).astype(BF16)
        out_copy(s).start()

    def attention_back(s):
        mask_v[...] = block_mask(idk_ref[s], idq_ref[s])

        def pair(p, carry):
            lanes = pl.ds(pl.multiple_of(p * 2 * HD, 2 * HD), 2 * HD)
            queries = q_v[s, :, lanes]
            keys = k_v[s, :, lanes]
            values = v_v[s, :, lanes]
            grad_out = datt_v[:, lanes]
            keys_t = keys.T
            low_half = lax.broadcasted_iota(jnp.int32, queries.shape, 1) < HD
            zero = jnp.zeros_like(queries)
            dk = None
            dv = None
            dq_parts = []
            for head in range(2):
                own = (lambda a: jnp.where(low_half, a, zero)) if head == 0 else (
                    lambda a: jnp.where(low_half, zero, a)
                )
                q_own = own(queries)
                do_own = own(grad_out)
                scores = dot_nt(keys, q_own) + bias_v[2 * p + head].astype(F32) + mask_v[...]
                probs = jnp.exp(scores - lse_v[s, p, head : head + 1, :])
                dprobs = dot_nt(values, do_own)
                delta = jnp.sum(probs * dprobs, axis=0, keepdims=True)
                dscores = probs * (dprobs - delta)
                low = dscores.astype(BF16)
                dv_head = dot(probs.astype(BF16), do_own)
                dk_head = dot(low, q_own)
                dv = dv_head if dv is None else dv + dv_head
                dk = dk_head if dk is None else dk + dk_head
                dq_parts.append(dot(keys_t[head * HD : (head + 1) * HD], low))
                for block in range(4):
                    tile = dscores[block * 256 : (block + 1) * 256]
                    wide = jnp.concatenate([tile, jnp.zeros_like(tile)], axis=1)
                    total = None
                    for group in range(32):
                        moved = pltpu.roll(wide[group * 8 : group * 8 + 8], 248 - 8 * group, 1)
                        total = moved if total is None else total + moved
                    row = lax.broadcasted_iota(jnp.int32, total.shape, 0)
                    amount = 7 - row
                    for bit in (1, 2, 4):
                        total = jnp.where((amount & bit) != 0, pltpu.roll(total, bit, 1), total)
                    rel_ref[p, head, block : block + 1, :] += jnp.sum(total, axis=0, keepdims=True)
            proj_ref[0, s, :, lanes] = (jnp.concatenate(dq_parts, axis=0).T * (HD ** (-0.5))).astype(BF16)
            for kind, value in enumerate((dk, dv)):
                for index in range(2):
                    at = 2 * index * stretch
                    keep_v[s, kind, index, :, lanes] = value[at : at + stretch]
                    give_v[s, kind, index, :, lanes] = value[at + stretch : at + 2 * stretch].astype(BF16)
            return carry

        lax.fori_loop(0, pairs, pair, 0)
        core_copy(s).start()

    def main(s, carry):
        h_copy(s).wait_recv()
        din_copy(s).wait_recv()
        middle_back(s)
        attention_back(s)

        @pl.when(s > 0)
        def _():
            core_sum(s - 1)
            out_sum(s - 1)

        return carry

    lax.fori_loop(0, seqs, main, 0)
    core_sum(seqs - 1)
    out_sum(seqs - 1)

    def finish_keys(s, carry):
        y_copy(s).wait_recv()
        for kind in range(2):
            proj_ref[1 + kind, s] = (keep_v[s, kind, 0] + far_v[s, kind].astype(F32)).astype(BF16)
        return carry

    def finish_out(s, carry):
        out_copy(s).wait_recv()
        out_ref[s] = (mid_v[s] + (out_own[s].astype(F32) + out_other[s].astype(F32))).astype(BF16)
        return carry

    lax.fori_loop(0, seqs, finish_keys, 0)
    lax.fori_loop(0, seqs, finish_out, 0)
    for s in range(seqs):
        for b in range(1, groups):
            part_copy(s, b).wait_send()
        for copy in (h_copy(s), din_copy(s), out_copy(s), core_copy(s), y_copy(s)):
            copy.wait_send()


def back_stage(mids, moes, gates, lse, din, parts, q, k, v, bias, cot, wout, h, places, near, ids_query, ids_key, router, gain):
    groups, _, cap, width = parts.shape
    seqs, stretch = mids.shape[:2]
    local = wout.shape[1]
    length = k.shape[1]
    pairs = local // (2 * HD)
    experts_n = router.shape[0]
    any_spec = pl.BlockSpec(memory_space=pl.ANY)
    vmem = pl.BlockSpec(memory_space=pltpu.VMEM)
    dma = pltpu.SemaphoreType.DMA
    return pl.pallas_call(
        functools.partial(back_kernel, seqs, groups, cap),
        name="back_stage",
        in_specs=[any_spec] * 12 + [vmem] * 7,
        out_specs=[vmem] * 7,
        out_shape=[
            jax.ShapeDtypeStruct((seqs, stretch, width), BF16),
            jax.ShapeDtypeStruct((seqs, stretch, width), F32),
            jax.ShapeDtypeStruct((seqs, stretch, width), BF16),
            jax.ShapeDtypeStruct((3, seqs, stretch, local), BF16),
            jax.ShapeDtypeStruct((1, width), F32),
            jax.ShapeDtypeStruct((experts_n, width), F32),
            jax.ShapeDtypeStruct((pairs, 2, 4, 2 * stretch), F32),
        ],
        scratch_shapes=[
            pltpu.VMEM((seqs, stretch, width), F32),
            pltpu.VMEM((seqs, stretch, width), BF16),
            pltpu.VMEM((seqs, experts_n, stretch), F32),
            pltpu.VMEM((seqs, pairs, 2, stretch), F32),
            pltpu.VMEM((seqs, groups, cap, width), BF16),
            pltpu.VMEM((groups, seqs, cap, width), BF16),
            pltpu.VMEM((seqs, stretch, local), BF16),
            pltpu.VMEM((seqs, length, local), BF16),
            pltpu.VMEM((seqs, length, local), BF16),
            pltpu.VMEM((2 * pairs, length, stretch), BF16),
            pltpu.VMEM((seqs, stretch, width), BF16),
            pltpu.VMEM((width, local), BF16),
            pltpu.VMEM((seqs, stretch, width), BF16),
            pltpu.VMEM((seqs, stretch, width), BF16),
            pltpu.VMEM((seqs, groups, stretch), F32),
            pltpu.VMEM((seqs, groups, stretch), F32),
            pltpu.VMEM((seqs, stretch, width), BF16),
            pltpu.VMEM((seqs, stretch, width), BF16),
            pltpu.VMEM((stretch, local), BF16),
            pltpu.VMEM((length, stretch), F32),
            pltpu.VMEM((seqs, 2, 2, stretch, local), F32),
            pltpu.VMEM((seqs, 2, 2, stretch, local), BF16),
            pltpu.VMEM((seqs, 2, 2, stretch, local), BF16),
            pltpu.VMEM((seqs, 2, stretch, local), BF16),
            pltpu.VMEM((seqs, 2, stretch, local), BF16),
            dma((8,)), dma((4,)), dma((2, seqs, groups)), dma((2, 3, seqs)), dma((2, seqs)), dma((2, seqs)),
        ],
        compiler_params=pltpu.CompilerParams(
            vmem_limit_bytes=63 * 1024 * 1024, collective_id=3, has_side_effects=True
        ),
        cost_estimate=cost(6 * 10**10, 10**7),
    )(mids, moes, gates, lse, din, parts, q, k, v, bias, cot, wout, h, places, near, ids_query, ids_key, router, gain)


def last_kernel(
    normed_ref, proj_ref, datt_ref, att_ref, small_ref, wqkv_ref, gmid_ref, x_ref, gain_ref,
    out_ref, router_out, gm_out, ga_out, table_out, gx_ref,
    dn_own, dn_other, ga_own, dn_sems, grads, core_send, core_got, y_out, y_got, z_out, z_got, wide, s_own, s_core, s_y, s_x, s_z,
    c_sems, y_sems, z_sems, w_sems, s_sems,
):
    dp = lax.axis_index("dp")
    ctx = lax.axis_index("ctx")
    tp = lax.axis_index("tp")
    core = ctx % 2
    far = ctx // 2
    greet([{"dp": dp ^ b} for b in (1, 2, 3)] + [{"ctx": ctx ^ b} for b in (1, 2, 3)] + [{"tp": tp ^ 1}])
    count = z_got.shape[0] + 1
    width = normed_ref.shape[1]
    piece = width // count

    seqs, stretch = x_ref.shape[:2]

    def unit_of(s):
        value = x_ref[s].astype(F32)
        factor = norm_factor(value)
        return factor, value * factor

    def rows_of(s):
        return pl.ds(pl.multiple_of(s * stretch, stretch), stretch)

    def input_grad(s, total):
        part = dot_nt(proj_ref[0, rows_of(s)], wqkv_ref[0])
        part = part + dot_nt(proj_ref[1, rows_of(s)], wqkv_ref[1])
        part = part + dot_nt(proj_ref[2, rows_of(s)], wqkv_ref[2])
        dn_own[s] = part.astype(BF16)
        return total + jnp.sum(part * unit_of(s)[1], axis=0, keepdims=True)

    own_gain = lax.fori_loop(0, seqs, input_grad, jnp.zeros((1, width), F32))
    lines = lax.broadcasted_iota(jnp.int32, small_ref.shape, 0)
    ga_own[...] = small_ref[...] + jnp.where(lines == 9, own_gain, 0.0)
    x_copy = remote(ga_own, s_x, s_sems.at[0, 0], s_sems.at[1, 0], tp=tp ^ 1)
    x_copy.start()
    dn_copies = [
        remote(dn_own.at[s], dn_other.at[s], dn_sems.at[0, s], dn_sems.at[1, s], tp=tp ^ 1) for s in range(seqs)
    ]
    for copy in dn_copies:
        copy.start()
    normed_t = normed_ref[...].T
    for j in range(3):
        grads[j] = dot(normed_t, proj_ref[j])
    grads[3] = dot_tn(datt_ref[...], att_ref[...])
    give = 1 - core
    core_send[0] = grads[2 * give].astype(BF16)
    core_send[1] = grads[2 * give + 1].astype(BF16)
    c_copy = remote(core_send, core_got, c_sems.at[0], c_sems.at[1], ctx=ctx ^ 1)
    c_copy.start()
    x_copy.wait_recv()
    s_own[...] = ga_own[...] + jnp.where(lines == 9, s_x[...], 0.0)
    sc_copy = remote(s_own, s_core, s_sems.at[0, 1], s_sems.at[1, 1], ctx=ctx ^ 1)
    sc_copy.start()
    c_copy.wait_recv()
    grads[2 * core] += core_got[0].astype(F32)
    grads[2 * core + 1] += core_got[1].astype(F32)
    y_out[...] = grads[2 * core + 1 - far].astype(BF16)
    order = (3, 2, 1, 0)
    y_copies = []
    for b in order:
        at = pl.ds(pl.multiple_of((dp ^ b) * piece, 16), piece)
        copy = remote(y_out.at[at], y_got.at[b], y_sems.at[0, b], y_sems.at[1, b], ctx=ctx ^ 2)
        copy.start()
        y_copies.append(copy)
    sc_copy.wait_recv()
    y_small = s_own[...] + s_core[...]
    s_y[0] = y_small
    sy_copy = remote(s_y.at[0], s_y.at[1], s_sems.at[0, 2], s_sems.at[1, 2], ctx=ctx ^ 2)
    sy_copy.start()
    mine = 2 * core + far
    z_copies = []
    total = None
    for copy, b in zip(y_copies, order):
        copy.wait_recv()
        at = pl.ds(pl.multiple_of((dp ^ b) * piece, 16), piece)
        value = grads[mine, at] + y_got[b].astype(F32)
        if b:
            z_out[b - 1] = value.astype(BF16)
            z_copy = remote(z_out.at[b - 1], z_got.at[b - 1], z_sems.at[0, b - 1], z_sems.at[1, b - 1], dp=dp ^ b)
            z_copy.start()
            z_copies.append((b, z_copy))
        else:
            total = value
    sy_copy.wait_recv()
    s_z[dp] = s_y[0] + s_y[1]
    sz_copies = []
    for b in (3, 2, 1):
        copy = remote(s_z.at[dp], s_z.at[dp], s_sems.at[0, 2 + b], s_sems.at[1, 2 + b], dp=dp ^ b)
        copy.start()
        sz_copies.append(copy)
    for b, copy in z_copies:
        copy.wait_recv()
        total = total + z_got[b - 1].astype(F32)
    wide[mine] = total.astype(BF16)
    w_copies = []
    for b in (3, 2, 1):
        copy = remote(wide.at[mine], wide.at[mine], w_sems.at[0, b - 1], w_sems.at[1, b - 1], ctx=ctx ^ b)
        copy.start()
        w_copies.append(copy)
    for copy in dn_copies:
        copy.wait_recv()

    def input_norm(s, carry):
        factor, unit = unit_of(s)
        scaled = (dn_own[s].astype(F32) + dn_other[s].astype(F32)) * gain_ref[...]
        dres = factor * (scaled - unit * jnp.mean(scaled * unit, axis=-1, keepdims=True))
        gx_ref[s] = gmid_ref[s] + dres
        return carry

    lax.fori_loop(0, seqs, input_norm, 0)
    for copy in sz_copies:
        copy.wait_recv()
    small = s_z[0]
    for d in range(1, count):
        small = small + s_z[d]

    def exact(a, b, dims):
        return lax.dot_general(a, b, (dims, ((), ())), precision=FULL_PRECISION, preferred_element_type=F32)

    row = lax.broadcasted_iota(jnp.int32, (piece, width), 0)
    col = lax.broadcasted_iota(jnp.int32, (piece, width), 1)
    select = jnp.where(col == row + dp * piece, 1.0, 0.0)
    experts_n = router_out.shape[0]
    e_row = lax.broadcasted_iota(jnp.int32, (experts_n, experts_n), 0)
    e_col = lax.broadcasted_iota(jnp.int32, (experts_n, experts_n), 1)
    slot = ((e_row % 2) ^ tp) * count + e_row // 2
    arranged = exact(jnp.where(e_col == slot, 1.0, 0.0), small[:experts_n], ((1,), (0,)))
    router_out[...] = exact(arranged, select, ((1,), (1,)))
    gains = exact(small[8:16], select, ((1,), (1,)))
    gm_out[...] = gains[0:1]
    ga_out[...] = gains[1:2]
    heads, t_rows = table_out.shape
    t_row = lax.broadcasted_iota(jnp.int32, (t_rows, width), 0)
    t_col = lax.broadcasted_iota(jnp.int32, (t_rows, width), 1)
    table_out[...] = exact(small[16:24], jnp.where(t_col == t_row + dp * t_rows, 1.0, 0.0), ((1,), (1,)))[:heads]
    for copy in w_copies:
        copy.wait_recv()
    out_ref[...] = wide[...].astype(F32)
    for copy in [x_copy, c_copy, sc_copy, sy_copy] + dn_copies + y_copies + [c for _, c in z_copies] + sz_copies + w_copies:
        copy.wait_send()


def last_stage(normed, proj, datt, att, small, wqkv, gmid, x, gain, dp, table_rows, heads, experts_n):
    rows, width = normed.shape
    local = att.shape[1]
    piece = width // dp
    vmem = pl.BlockSpec(memory_space=pltpu.VMEM)
    dma = pltpu.SemaphoreType.DMA
    return pl.pallas_call(
        last_kernel,
        name="last_stage",
        in_specs=[vmem] * 9,
        out_specs=[vmem] * 6,
        out_shape=[
            jax.ShapeDtypeStruct((4, piece, local), F32),
            jax.ShapeDtypeStruct((experts_n, piece), F32),
            jax.ShapeDtypeStruct((1, piece), F32),
            jax.ShapeDtypeStruct((1, piece), F32),
            jax.ShapeDtypeStruct((heads, table_rows), F32),
            jax.ShapeDtypeStruct(x.shape, F32),
        ],
        scratch_shapes=[
            pltpu.VMEM(x.shape, BF16),
            pltpu.VMEM(x.shape, BF16),
            pltpu.VMEM(small.shape, F32),
            dma((2, x.shape[0])),
            pltpu.VMEM((4, width, local), F32),
            pltpu.VMEM((2, width, local), BF16),
            pltpu.VMEM((2, width, local), BF16),
            pltpu.VMEM((width, local), BF16),
            pltpu.VMEM((4, piece, local), BF16),
            pltpu.VMEM((3, piece, local), BF16),
            pltpu.VMEM((3, piece, local), BF16),
            pltpu.VMEM((4, piece, local), BF16),
            pltpu.VMEM(small.shape, F32),
            pltpu.VMEM(small.shape, F32),
            pltpu.VMEM((2,) + small.shape, F32),
            pltpu.VMEM(small.shape, F32),
            pltpu.VMEM((dp,) + small.shape, F32),
            dma((2,)), dma((2, 4)), dma((2, 3)), dma((2, 3)), dma((2, 6)),
        ],
        compiler_params=pltpu.CompilerParams(vmem_limit_bytes=VMEM_BYTES, collective_id=1, has_side_effects=True),
        cost_estimate=cost(8 * rows * width * local, 8 * rows * width),
    )(normed, proj, datt, att, small, wqkv, gmid, x, gain)


def front_kernel(
    seqs, groups, cap,
    ein_ref, eot_ref, got_ref, cot_ref, q_ref, k_ref, v_ref, win_ref, idq_ref, idk_ref, x_ref, wout_ref, gain_ref, router_ref,
    hits_ref, place_ref,
    near_out, far_out, cot_out, row_out, gate_out, bias_ref, att_ref, lse_ref, mid_ref, moe_ref, gates_ref, send_ref, slot_ref,
    wout_other, att_other, mask_ref, w_sems, x_sems, z_sems, r_sems, g_sems, own_sems,
):
    dp = lax.axis_index("dp")
    ctx = lax.axis_index("ctx")
    tp = lax.axis_index("tp")
    greet([{"dp": dp ^ b} for b in range(1, groups)] + [{"ctx": ctx ^ 2}, {"tp": tp ^ 1}])
    width = x_ref.shape[2]
    local = q_ref.shape[2]
    pairs = local // (2 * HD)
    far_copies = [
        remote(ein_ref.at[tp], near_out.at[0], w_sems.at[0, 2], w_sems.at[1, 2], ctx=ctx ^ 2),
        remote(eot_ref.at[tp], near_out.at[1], w_sems.at[0, 3], w_sems.at[1, 3], ctx=ctx ^ 2),
        remote(got_ref, far_out, w_sems.at[0, 0], w_sems.at[1, 0], ctx=ctx ^ 2),
    ]
    wout_copy = remote(wout_ref, wout_other, w_sems.at[0, 1], w_sems.at[1, 1], tp=tp ^ 1)
    order = tuple(range(groups - 1, 0, -1))
    cot_copies = [
        remote(
            cot_ref.at[b, s], cot_out.at[b - 1, s - FIRST],
            z_sems.at[0, s - FIRST, b - 1], z_sems.at[1, s - FIRST, b - 1], dp=dp ^ b,
        )
        for s in range(FIRST, seqs)
        for b in order
    ]
    for copy in [wout_copy] + far_copies + cot_copies:
        copy.start()

    def expand(head, carry):
        for block in range(4):
            row = win_ref[head, block : block + 1, :]
            wide = jnp.broadcast_to(row, (256, 512))
            rolled = pltpu.roll(wide, 257, 1, stride=1, stride_axis=0)
            bias_ref[head, block * 256 : (block + 1) * 256, :] = rolled[:, :256].astype(BF16)
        return carry

    lax.fori_loop(0, 2 * pairs, expand, 0)

    def att_copy(s):
        return remote(att_ref.at[s], att_other.at[s], x_sems.at[0, s], x_sems.at[1, s], tp=tp ^ 1)

    def row_copy(b):
        return remote(send_ref.at[0, dp ^ b], row_out.at[dp], r_sems.at[0, b - 1], r_sems.at[1, b - 1], dp=dp ^ b)

    def gate_copy(b):
        return remote(slot_ref.at[0, dp ^ b], gate_out.at[dp], g_sems.at[0, b - 1], g_sems.at[1, b - 1], dp=dp ^ b)

    def own_row():
        return pltpu.make_async_copy(send_ref.at[0, dp], row_out.at[dp], own_sems.at[0])

    def own_gate():
        return pltpu.make_async_copy(slot_ref.at[0, dp], gate_out.at[dp], own_sems.at[1])

    def attention(s):
        mask_ref[...] = block_mask(idk_ref[s], idq_ref[s])

        def pair(p, carry):
            lanes = pl.ds(pl.multiple_of(p * 2 * HD, 2 * HD), 2 * HD)
            queries = q_ref[s, :, lanes]
            keys = k_ref[s, :, lanes]
            values_t = v_ref[s, :, lanes].T
            low_half = lax.broadcasted_iota(jnp.int32, queries.shape, 1) < HD
            zero = jnp.zeros_like(queries)
            parts = []
            for head in range(2):
                own = jnp.where(low_half, queries, zero) if head == 0 else jnp.where(low_half, zero, queries)
                scores = dot_nt(keys, own) + bias_ref[2 * p + head].astype(F32) + mask_ref[...]
                top = jnp.max(scores, axis=0, keepdims=True)
                weights = jnp.exp(scores - top)
                total = jnp.sum(weights, axis=0, keepdims=True)
                part = dot(values_t[head * HD : (head + 1) * HD], weights.astype(BF16)) * (1.0 / total)
                parts.append(part)
                lse_ref[s, p, head : head + 1, :] = top + jnp.log(total)
            att_ref[s, :, lanes] = jnp.concatenate(parts, axis=0).T.astype(BF16)
            return carry

        lax.fori_loop(0, pairs, pair, 0)
        att_copy(s).start()

    def middle(s):
        att_copy(s).wait_recv()
        mid = x_ref[s].astype(F32) + (dot_nt(att_ref[s], wout_ref[...]) + dot_nt(att_other[s], wout_other[...]))
        mid_ref[s] = mid
        moe_in = (mid * norm_factor(mid) * gain_ref[...].astype(F32)).astype(BF16)
        moe_ref[s] = moe_in
        logits = dot_nt(router_ref[...], moe_in)
        hit = hits_ref[s] > 0.5
        top = jnp.max(jnp.where(hit, logits, MASKED), axis=0, keepdims=True)
        raw = jnp.where(hit, jnp.exp(jnp.where(hit, logits, top) - top), 0.0)
        gates = raw / jnp.sum(raw, axis=0, keepdims=True)
        gates_ref[s] = gates
        picks = one_hot(place_ref[s], cap)
        pick = jnp.concatenate([jnp.where(p, 1.0, 0.0).astype(BF16) for p in picks], axis=0)
        send_ref[s] = dot(pick, moe_in).astype(BF16).reshape(groups, cap, width)
        eye = diagonal(cap)
        for group in range(groups):
            column = jnp.sum(jnp.where(picks[group], gates[group : group + 1, :], 0.0), axis=1, keepdims=True)
            slot_ref[s, group] = jnp.sum(jnp.where(eye, column, 0.0), axis=0, keepdims=True)

    def main(s, carry):
        attention(s)

        @pl.when(s == 1)
        def _():
            wout_copy.wait_recv()

        @pl.when(s > 0)
        def _():
            middle(s - 1)

        @pl.when(s == 1)
        def _():
            for b in order:
                gate_copy(b).start()
                row_copy(b).start()
            own_row().start()
            own_gate().start()

        return carry

    lax.fori_loop(0, seqs, main, 0)
    middle(seqs - 1)
    for b in order:
        gate_copy(b).wait()
        row_copy(b).wait()
    own_row().wait()
    own_gate().wait()
    for copy in far_copies + cot_copies:
        copy.wait()
    wout_copy.wait_send()
    for s in range(seqs):
        att_copy(s).wait_send()


def front_stage(w_in, w_out, got, cot, q, k, v, windows, ids_query, ids_key, x, wout, gain, router, hits, places, cap):
    seqs, stretch, width = x.shape
    groups = places.shape[1]
    local = q.shape[2]
    length = k.shape[1]
    pairs = local // (2 * HD)
    experts_n = router.shape[0]
    any_spec = pl.BlockSpec(memory_space=pl.ANY)
    vmem = pl.BlockSpec(memory_space=pltpu.VMEM)
    dma = pltpu.SemaphoreType.DMA
    return pl.pallas_call(
        functools.partial(front_kernel, seqs, groups, cap),
        name="front_stage",
        in_specs=[any_spec] * 4 + [vmem] * 12,
        out_specs=[any_spec] * 4 + [vmem] * 9,
        out_shape=[
            jax.ShapeDtypeStruct(got.shape, BF16),
            jax.ShapeDtypeStruct(got.shape, BF16),
            jax.ShapeDtypeStruct((groups - 1, seqs - FIRST, cap, width), BF16),
            jax.ShapeDtypeStruct((groups, cap, width), BF16),
            jax.ShapeDtypeStruct((groups, 1, cap), F32),
            jax.ShapeDtypeStruct((2 * pairs, length, stretch), BF16),
            jax.ShapeDtypeStruct((seqs, stretch, local), BF16),
            jax.ShapeDtypeStruct((seqs, pairs, 2, stretch), F32),
            jax.ShapeDtypeStruct((seqs, stretch, width), F32),
            jax.ShapeDtypeStruct((seqs, stretch, width), BF16),
            jax.ShapeDtypeStruct((seqs, experts_n, stretch), F32),
            jax.ShapeDtypeStruct((seqs, groups, cap, width), BF16),
            jax.ShapeDtypeStruct((seqs, groups, 1, cap), F32),
        ],
        scratch_shapes=[
            pltpu.VMEM((width, local), BF16),
            pltpu.VMEM((seqs, stretch, local), BF16),
            pltpu.VMEM((length, stretch), F32),
            dma((2, 4)), dma((2, seqs)), dma((2, seqs - FIRST, groups - 1)), dma((2, groups - 1)), dma((2, groups - 1)),
            dma((2,)),
        ],
        compiler_params=pltpu.CompilerParams(vmem_limit_bytes=VMEM_BYTES, collective_id=4, has_side_effects=True),
        cost_estimate=cost(4 * 10**10, 10**7),
    )(w_in, w_out, got, cot, q, k, v, windows, ids_query, ids_key, x, wout, gain, router, hits, places)


def moe_kernel(
    seqs, groups, cap, tile, *refs,
):
    send_ref, slot_ref, row_ref, gate_ref, slots_ref, cot_ref, last_ref = refs[:7]
    refs = refs[7:]
    ein_ref, eot_ref, got_ref, near_ref, far_ref, part_out, din_back, h_back, keep_out, give_out = refs[:10]
    (
        w_all, x_all, gate_all, g_all, xt_all, dyt_all, dy_ref, hid_all, dpre_all, part_acc, din_acc,
        part_all, din_all, h_all, tile_ref,
        x_sems, gate_sems, din_sems, h_sems, w_sems, own_sems, cot_sems, part_sems, out_sems, core_sems,
    ) = refs[10:]
    dp = lax.axis_index("dp")
    ctx = lax.axis_index("ctx")
    tp = lax.axis_index("tp")
    greet([{"dp": dp ^ b} for b in range(1, groups)] + [{"ctx": ctx ^ 1}])
    width = x_all.shape[-1]
    rows = groups * cap
    slices = w_all.shape[2]
    piece = width // slices
    half_len = w_all.shape[4]
    per_half = half_len // tile
    tiles = w_all.shape[1] * per_half
    order = tuple(range(groups - 1, 0, -1))

    sent = []
    for s in range(1, seqs):
        for b in order:
            sent.append(
                remote(send_ref.at[s, dp ^ b], x_all.at[s, dp], x_sems.at[0, s, b - 1], x_sems.at[1, s, b - 1], dp=dp ^ b)
            )
            sent.append(
                remote(
                    slot_ref.at[s, dp ^ b], gate_all.at[s, dp],
                    gate_sems.at[0, s, b - 1], gate_sems.at[1, s, b - 1], dp=dp ^ b,
                )
            )
    w_copies = []
    local = []
    arrivals = []
    both = slice(None)
    sources = (
        (ein_ref.at[tp], 0, 0, ctx), (eot_ref.at[tp], 1, 0, ctx), (near_ref, both, 0, ctx ^ 2),
        (got_ref, both, 1, ctx), (far_ref, both, 1, ctx ^ 2),
    )
    for index, (ref, io, half, place) in enumerate(sources):
        here = w_all.at[io, half, place]
        there = w_all.at[io, half, place ^ 1]
        w_copies.append(remote(ref, here, w_sems.at[0, index], w_sems.at[1, index], ctx=ctx ^ 1))
        arrivals.append(remote(there, there, w_sems.at[0, index], w_sems.at[1, index], ctx=ctx ^ 1))
        local.append(pltpu.make_async_copy(ref, here, w_sems.at[2, index]))
    for copy in w_copies + sent:
        copy.start()
    local.append(pltpu.make_async_copy(row_ref, x_all.at[0], own_sems.at[0]))
    local.append(pltpu.make_async_copy(gate_ref, gate_all.at[0], own_sems.at[1]))
    for s in range(1, seqs):
        local.append(pltpu.make_async_copy(send_ref.at[s, dp], x_all.at[s, dp], own_sems.at[2 * s]))
        local.append(pltpu.make_async_copy(slot_ref.at[s, dp], gate_all.at[s, dp], own_sems.at[1 + 2 * s]))
    local.append(pltpu.make_async_copy(slots_ref.at[0], g_all.at[dp], cot_sems.at[0, 0]))
    for b in range(1, groups):
        local.append(
            pltpu.make_async_copy(cot_ref.at[b - 1], g_all.at[dp ^ b, pl.ds(0, FIRST)], cot_sems.at[0, b])
        )
        local.append(
            pltpu.make_async_copy(last_ref.at[b - 1], g_all.at[dp ^ b, pl.ds(FIRST, seqs - FIRST)], cot_sems.at[1, b])
        )
    for copy in local:
        copy.start()
    for copy in local:
        copy.wait()
    for copy in arrivals:
        copy.wait_recv()
    eye = diagonal(cap)

    def weights(io, f):
        lanes = pl.ds(pl.multiple_of((f % per_half) * tile, tile), tile)
        return w_all[io, f // per_half, :, :, lanes].reshape(width, tile)

    def gate_column(s, group):
        return jnp.sum(jnp.where(eye, gate_all[s, group], 0.0), axis=1, keepdims=True)

    def din_copy(s, b):
        return remote(
            din_all.at[s, dp ^ b], din_back.at[s, dp], din_sems.at[0, s, b - 1], din_sems.at[1, s, b - 1], dp=dp ^ b
        )

    def h_copy(s, b):
        return remote(h_all.at[s, dp ^ b], h_back.at[s, dp], h_sems.at[0, s, b - 1], h_sems.at[1, s, b - 1], dp=dp ^ b)

    def part_copy(s, b):
        return pltpu.make_async_copy(part_all.at[s, dp ^ b], part_out.at[b, s], part_sems.at[s, b])

    def own_copies(s):
        return [
            pltpu.make_async_copy(din_all.at[s, dp], din_back.at[s, dp], part_sems.at[s, groups]),
            pltpu.make_async_copy(h_all.at[s, dp], h_back.at[s, dp], part_sems.at[s, groups + 1]),
        ]

    def chunk(s, carry):
        @pl.when(s > 0)
        def _():
            for b in order:
                there = x_all.at[s, dp ^ b]
                remote(there, there, x_sems.at[0, s, b - 1], x_sems.at[1, s, b - 1], dp=dp ^ b).wait_recv()
                there = gate_all.at[s, dp ^ b]
                remote(there, there, gate_sems.at[0, s, b - 1], gate_sems.at[1, s, b - 1], dp=dp ^ b).wait_recv()

        x = x_all[s].reshape(rows, width)
        xt_all[s] = x.T
        for group in range(groups):
            dy_ref[group * cap : (group + 1) * cap] = (g_all[group, s].astype(F32) * gate_column(s, group)).astype(BF16)
        dyt_all[s] = dy_ref[...].T
        part_acc[...] = jnp.zeros_like(part_acc)
        din_acc[...] = jnp.zeros_like(din_acc)

        def step(f, carry):
            x = x_all[s].reshape(rows, width)
            w_in = weights(0, f)
            w_out_t = weights(1, f)
            pre = dot(x, w_in)
            dhid = dot(dy_ref[...], w_out_t)
            square = pre * pre
            inner = jnp.tanh(GELU_C * pre * (1.0 + GELU_A * square))
            half = 0.5 * (1.0 + inner)
            hidden = (pre * half).astype(BF16)
            slope = half + (0.5 * GELU_C) * pre * (1.0 - inner * inner) * (1.0 + (3.0 * GELU_A) * square)
            dpre = (dhid * slope).astype(BF16)
            hid_all[f, s] = hidden
            dpre_all[f, s] = dpre
            part_acc[...] += dot_nt(hidden, w_out_t)
            din_acc[...] += dot_nt(dpre, w_in)
            return carry

        lax.fori_loop(0, tiles, step, 0)
        for group in range(groups):
            at = slice(group * cap, (group + 1) * cap)
            din_all[s, group] = din_acc[at].astype(BF16)
            gated = part_acc[at] * gate_column(s, group)
            part_all[s, group] = gated.astype(BF16)
            h = jnp.sum(gated * g_all[group, s].astype(F32), axis=1, keepdims=True)
            h_all[s, group] = jnp.sum(jnp.where(eye, h, 0.0), axis=0, keepdims=True)
        for b in order:
            din_copy(s, b).start()
            h_copy(s, b).start()
        for copy in own_copies(s):
            copy.start()
        for b in range(groups):
            part_copy(s, b).start()
        return carry

    lax.fori_loop(0, seqs, chunk, 0)

    def tile_of(ref, f):
        lanes = pl.ds(pl.multiple_of((f % per_half) * tile, tile), tile)
        return ref.at[f // per_half, :, :, :, lanes]

    def keep_copy(f, slot):
        return pltpu.make_async_copy(tile_ref.at[slot, 0], tile_of(keep_out, f), out_sems.at[slot, 0])

    def give_copy(f, slot):
        return remote(
            tile_ref.at[slot, 1], tile_of(give_out, f), out_sems.at[slot, 1], core_sems.at[f], ctx=ctx ^ 1
        )

    def weight_grads(f, carry):
        slot = f % 2

        @pl.when(f >= 2)
        def _():
            keep_copy(f - 2, slot).wait()
            give_copy(f - 2, slot).wait_send()

        for io, (left, right) in enumerate(((xt_all, dpre_all), (dyt_all, hid_all))):
            total = dot(left[0], right[f, 0])
            for s in range(1, seqs):
                total = total + dot(left[s], right[f, s])
            for index in range(slices):
                place = index ^ ctx
                tile_ref[slot, place % 2, place // 2, io] = total[index * piece : (index + 1) * piece].astype(BF16)
        keep_copy(f, slot).start()
        give_copy(f, slot).start()
        return carry

    lax.fori_loop(0, tiles, weight_grads, 0)
    for f in (tiles - 2, tiles - 1):
        keep_copy(f, f % 2).wait()
        give_copy(f, f % 2).wait_send()
    for f in range(tiles):
        give_copy(f, f % 2).wait_recv()
    for s in range(seqs):
        for b in order:
            there = din_back.at[s, dp ^ b]
            remote(there, there, din_sems.at[0, s, b - 1], din_sems.at[1, s, b - 1], dp=dp ^ b).wait_recv()
            there = h_back.at[s, dp ^ b]
            remote(there, there, h_sems.at[0, s, b - 1], h_sems.at[1, s, b - 1], dp=dp ^ b).wait_recv()
            din_copy(s, b).wait_send()
            h_copy(s, b).wait_send()
        for copy in own_copies(s):
            copy.wait()
        for b in range(groups):
            part_copy(s, b).wait()
    for copy in w_copies + sent:
        copy.wait_send()


def moe_stage(send, slot_gate, row, row_gate, slots, cot, last, w_in, w_out, got, far_keep, far_got, tile=512):
    seqs, groups, cap, width = send.shape
    _, piece, half_len = got.shape
    halves = 2
    slices = width // piece
    tiles = halves * half_len // tile
    rows = groups * cap
    any_spec = pl.BlockSpec(memory_space=pl.ANY)
    vmem = pl.BlockSpec(memory_space=pltpu.VMEM)
    dma = pltpu.SemaphoreType.DMA
    return pl.pallas_call(
        functools.partial(moe_kernel, seqs, groups, cap, tile),
        name="moe_stage",
        in_specs=[any_spec] * 12,
        out_specs=[any_spec, any_spec, vmem, any_spec, any_spec],
        out_shape=[
            jax.ShapeDtypeStruct((groups, seqs, cap, width), BF16),
            jax.ShapeDtypeStruct((seqs, groups, cap, width), BF16),
            jax.ShapeDtypeStruct((seqs, groups, 1, cap), F32),
            jax.ShapeDtypeStruct((halves, slices // 2, 2, piece, half_len), BF16),
            jax.ShapeDtypeStruct((halves, slices // 2, 2, piece, half_len), BF16),
        ],
        scratch_shapes=[
            pltpu.VMEM((2, halves, slices, piece, half_len), BF16),
            pltpu.VMEM((seqs, groups, cap, width), BF16),
            pltpu.VMEM((seqs, groups, 1, cap), F32),
            pltpu.VMEM((groups, seqs, cap, width), BF16),
            pltpu.VMEM((seqs, width, rows), BF16),
            pltpu.VMEM((seqs, width, rows), BF16),
            pltpu.VMEM((rows, width), BF16),
            pltpu.VMEM((tiles, seqs, rows, tile), BF16),
            pltpu.VMEM((tiles, seqs, rows, tile), BF16),
            pltpu.VMEM((rows, width), F32),
            pltpu.VMEM((rows, width), F32),
            pltpu.VMEM((seqs, groups, cap, width), BF16),
            pltpu.VMEM((seqs, groups, cap, width), BF16),
            pltpu.VMEM((seqs, groups, 1, cap), F32),
            pltpu.VMEM((2, 2, slices // 2, 2, piece, tile), BF16),
            dma((2, seqs, groups - 1)), dma((2, seqs, groups - 1)), dma((2, seqs, groups - 1)),
            dma((2, seqs, groups - 1)), dma((3, 5)), dma((2 * seqs,)), dma((2, groups)), dma((seqs, groups + 2)),
            dma((2, 2)), dma((tiles,)),
        ],
        compiler_params=pltpu.CompilerParams(
            vmem_limit_bytes=63 * 1024 * 1024, collective_id=2, has_side_effects=True
        ),
        cost_estimate=cost(20 * seqs * rows * width * halves * half_len, 40 * width * halves * half_len),
    )(send, slot_gate, row, row_gate, slots, cot, last, w_in, w_out, got, far_keep, far_got)


def flip(value, axis, bit):
    count = lax.axis_size(axis)
    return lax.ppermute(value, axis, [(i, i ^ bit) for i in range(count)])


def all_to_all_dp(value):
    return lax.all_to_all(value, "dp", split_axis=0, concat_axis=0, tiled=True)


def gathered(tokens, wqkv, wout, table, gain_attn, gain_moe, router):
    seqs, stretch, width = tokens.shape
    local = wqkv.shape[2]
    dp = lax.axis_size("dp")
    tp = lax.axis_index("tp")
    experts_n = router.shape[1]
    wqkv = lax.all_gather(wqkv, "dp", axis=1, tiled=True)
    wout = lax.all_gather(wout, "dp", axis=1, tiled=True)
    table = lax.all_gather(table, "dp", axis=0, tiled=True)
    gains = lax.all_gather(jnp.concatenate([gain_attn, gain_moe], axis=0), "dp", axis=1, tiled=True)
    gain_attn, gain_moe = gains[0:1].astype(F32), gains[1:2]
    router = lax.all_gather(router, "dp", axis=0, tiled=True).T.reshape(dp, 2, width).transpose(1, 0, 2)
    router = jnp.where(tp == 0, router, router[::-1]).reshape(experts_n, width)
    across = flip(tokens, "ctx", 2)
    beside, beyond = flip(jnp.stack([tokens, across]), "ctx", 1)
    x32 = jnp.stack([tokens, beside, across, beyond], axis=1).astype(F32)
    normed = (x32 * norm_factor(x32) * gain_attn[None, None]).astype(BF16)
    own = normed[:, 0].reshape(seqs * stretch, width)
    queries = jnp.dot(own, wqkv[0], preferred_element_type=F32).astype(BF16) * jnp.asarray(HD ** (-0.5), BF16)
    flat = normed.reshape(seqs * 4 * stretch, width)
    keys = jnp.dot(flat, wqkv[1], preferred_element_type=F32).astype(BF16).reshape(seqs, 4 * stretch, local)
    values = jnp.dot(flat, wqkv[2], preferred_element_type=F32).astype(BF16).reshape(seqs, 4 * stretch, local)
    return queries.reshape(seqs, stretch, local), keys, values, own, wqkv, wout, table, gain_attn, gain_moe, router


def on_device(
    tokens_in, block_ids, rel_buckets, routes, attn_gain, w_qkv, w_attn_out, bias_table, moe_gain, w_router,
    w_expert_in, w_expert_out, cotangent,
):
    seqs, stretch, width = tokens_in.shape
    dp = lax.axis_size("dp")
    ctx_count = lax.axis_size("ctx")
    tp_count = lax.axis_size("tp")
    expert_count = w_router.shape[2]
    assert w_expert_in.shape[1] == tp_count == 2 and ctx_count == 4
    cap = max(2, 2 * stretch * routes.shape[2] // expert_count)
    ctx = lax.axis_index("ctx")
    tp = lax.axis_index("tp")
    local = w_qkv.shape[3]
    heads = local // HD

    fits = dp == 4
    e_order = jnp.arange(expert_count, dtype=jnp.int32).reshape(dp, 2).T
    e_order = jnp.where(tp == 0, e_order, e_order[::-1]).reshape(1, expert_count, 1)
    hits = ((routes[:, None, :, 0] == e_order) | (routes[:, None, :, 1] == e_order)).astype(F32)
    before = (
        lax.broadcasted_iota(jnp.int32, (stretch, stretch), 0) < lax.broadcasted_iota(jnp.int32, (stretch, stretch), 1)
    ).astype(BF16)
    ranks = jnp.einsum("set,tu->seu", hits.astype(BF16), before, preferred_element_type=F32)
    places = jnp.where(hits > 0.5, ranks, -1.0)[:, :dp]

    w_in, w_out = w_expert_in[0], w_expert_out[0].transpose(0, 2, 1)

    if fits:
        me = lax.axis_index("dp")
        near_places = jnp.stack([lax.dynamic_index_in_dim(places, me ^ b, 1, keepdims=False) for b in range(dp)], axis=1)
        (
            queries, keys, values, own_normed, wqkv, wout_own, table, gain_attn, gain_moe, router, got,
            cot_slots, cot_in,
        ) = first_stage(
            tokens_in, w_qkv[0], w_attn_out[0].T, bias_table[0], attn_gain, moe_gain, w_router[0].T, w_in, w_out,
            near_places, cotangent, cap,
        )
        table = table.reshape(NB, heads)
        keys = keys.reshape(seqs, 4 * stretch, local)
        values = values.reshape(seqs, 4 * stretch, local)
        own_normed = own_normed.reshape(seqs * stretch, width)
    else:
        queries, keys, values, own_normed, wqkv, wout_own, table, gain_attn, gain_moe, router = gathered(
            tokens_in, w_qkv[0], w_attn_out[0], bias_table[0], attn_gain, moe_gain, w_router[0]
        )
        pair = jnp.stack([w_in, w_out], axis=1)
        keep = lax.dynamic_index_in_dim(pair, tp, 0, keepdims=False)
        got = flip(lax.dynamic_index_in_dim(pair, 1 - tp, 0, keepdims=False), "tp", 1)
        weights = lax.all_gather(jnp.stack([keep, got], axis=1), "ctx", axis=0, tiled=False)
        cot_slots = all_to_all_dp(dispatch(places, cotangent, cap))

    one_hot_bucket = (rel_buckets[:, None] == jnp.arange(NB, dtype=jnp.int32)[None, :]).astype(F32)
    one_hot_bucket = jnp.pad(one_hot_bucket, ((0, 1), (0, 0)))
    starts = [(ctx - (ctx ^ b)) * stretch + 3 * stretch for b in range(4)]
    hot_windows = jnp.stack([lax.dynamic_slice_in_dim(one_hot_bucket, s, 2 * stretch, 0) for s in starts])
    windows = jnp.einsum("bmn,nh->hbm", hot_windows, table.astype(F32), precision=FULL_PRECISION)

    ids = block_ids.reshape(seqs, 4, stretch)
    ids_pieces = [lax.dynamic_index_in_dim(ids, ctx ^ b, 1, keepdims=False) for b in range(4)]
    ids_query = ids_pieces[0].reshape(seqs, 1, stretch)
    ids_key = jnp.stack(ids_pieces, axis=1)
    if fits:
        ids_query = ids_query.astype(F32)
        ids_key = ids_key.astype(BF16).reshape(seqs, 1, 4 * stretch)
    else:
        ids_key = ids_key.reshape(seqs, 4 * stretch, 1)

    if fits:
        (
            far_keep, far_got, cot_last, row, row_gate, bias, attended, lse, mids, moes, gates, send, slot_gate,
        ) = front_stage(
            w_in, w_out, got, cot_slots, queries, keys, values, windows, ids_query, ids_key, tokens_in, wout_own, gain_moe, router,
            hits, places, cap,
        )
        parts, returned_din, returned_h, kept, given = moe_stage(
            send, slot_gate, row, row_gate, cot_slots, cot_in, cot_last, w_in, w_out, got, far_keep, far_got
        )
    else:
        bias = expand_bias(windows)
        wout_pair = jnp.stack([wout_own, flip(wout_own, "tp", 1)])
        attended, lse, mids, moes, gates, sends, slot_gates = [], [], [], [], [], [], []
        for s in range(seqs):
            att, stat = attend(queries[s], keys[s], values[s], bias, ids_query[s], ids_key[s])
            attended.append(att)
            lse.append(stat)
            mid, moe_in, gate, send, slot_gate = middle_stage(
                att, flip(att, "tp", 1), tokens_in[s], wout_pair, gain_moe, router, hits[s], places[s], cap
            )
            mids.append(mid)
            moes.append(moe_in)
            gates.append(gate)
            sends.append(send)
            slot_gates.append(slot_gate)
        attended = jnp.stack(attended)
        partials, returned_din, returned_h = [], [], []
        acc = None
        for s in range(seqs):
            received = all_to_all_dp(sends[s])
            received_gate = all_to_all_dp(slot_gates[s])
            part, din, h, acc = experts(received, cot_slots, s, received_gate, weights, acc, s == seqs - 1)
            returned_din.append(all_to_all_dp(din))
            returned_h.append(all_to_all_dp(h))
            partials.append(all_to_all_dp(part))
        kept, given = acc[:, 0::2], flip(acc[:, 1::2], "ctx", 1)

    far_other = flip((kept[1, 1].astype(F32) + given[1, 1].astype(F32)).astype(BF16), "ctx", 2)
    far_send = (kept[0, 1].astype(F32) + given[0, 1].astype(F32)).astype(BF16)

    def summed(half, far):
        return (kept[half, 0].astype(F32) + given[half, 0].astype(F32)) + far.astype(F32)

    hits_of = (heads, 4, 2 * stretch)
    if fits:
        tokens_out, gmid, dattn, grad_proj, gain_moe_grad, router_grad, rel_grad = back_stage(
            mids, moes, gates, lse, returned_din, parts, queries, keys, values, bias, cotangent, wout_own,
            returned_h, places, near_places, ids_query, ids_key, router, gain_moe,
        )
        far_other, far_send, grad_proj = lax.optimization_barrier((far_other, far_send, grad_proj))
        far_mine = flip(far_send, "ctx", 2)
        other = flip(summed(1, far_other).astype(BF16), "tp", 1)
        grad_proj = grad_proj.reshape(3, seqs * stretch, local)
        dattn = dattn.reshape(seqs * stretch, width)
        grad_table = jnp.einsum("bmn,hbm->nh", hot_windows, rel_grad.reshape(hits_of), precision=FULL_PRECISION)
        small = jnp.concatenate(
            [
                router_grad,
                jnp.pad(gain_moe_grad, ((0, 7), (0, 0))),
                jnp.pad(grad_table.T, ((0, 8 - heads), (0, width - NB))),
            ],
            axis=0,
        )
        wide, g_router, g_moe, g_attn, g_table, grad_tokens = last_stage(
            own_normed, grad_proj, dattn, attended.reshape(seqs * stretch, local), small, wqkv, gmid, tokens_in, gain_attn,
            dp, NB // dp, heads, expert_count,
        )
        other, far_mine, wide = lax.optimization_barrier((other, far_mine, wide))
        g_qkv = wide[:3]
        g_wout = wide[3].T
        g_router, g_table = g_router.T, g_table.T
    else:
        far_mine = flip(far_send, "ctx", 2)
        other = flip(summed(1, far_other).astype(BF16), "tp", 1)
        tokens_out, gmids = [], []
        projections = []
        rel_grad = 0.0
        gain_moe_grad = 0.0
        router_grad = 0.0
        datts = []
        for s in range(seqs):
            out_own = combine_out(places[s], partials[s], cap)
            out_other = flip(out_own, "tp", 1)
            tokens_out.append((mids[s] + (out_own.astype(F32) + out_other.astype(F32))).astype(BF16))
            din_own, h_own = combine(places[s], returned_din[s], returned_h[s], cap)
            din_other = flip(din_own, "tp", 1)
            h_all = jnp.concatenate([h_own, flip(h_own, "tp", 1)], axis=0)
            gmid, datt, d_gain, d_router, dattn = middle_back(
                din_own, din_other, h_all, gates[s], router, moes[s], mids[s], gain_moe, cotangent[s], wout_own
            )
            datts.append(dattn)
            gmids.append(gmid)
            gain_moe_grad += d_gain
            router_grad += d_router
            dq, dk, dv, rel = attend_back(
                queries[s], keys[s], values[s], datt, bias, lse[s], ids_query[s], ids_key[s]
            )
            rel_grad += rel
            dkv = jnp.stack([dk, dv]).reshape(2, 4, stretch, local)
            near = dkv[:, 0::2].astype(F32) + flip(dkv[:, 1::2], "ctx", 1).astype(F32)
            full = near[:, 0] + flip(near[:, 1].astype(BF16), "ctx", 2).astype(F32)
            projections.append(jnp.concatenate([dq[None], full.astype(BF16)], axis=0))
        grad_proj = jnp.concatenate(projections, axis=1)
        dattn = jnp.concatenate(datts, axis=0)
        attended = attended.reshape(seqs * stretch, local)
        dnormed_part = jnp.einsum("jre,jde->rd", grad_proj, wqkv, preferred_element_type=F32)
        dnormed_own = dnormed_part.astype(BF16)
        dnormed = dnormed_own.astype(F32) + flip(dnormed_own, "tp", 1).astype(F32)
        own_x = tokens_in.reshape(seqs * stretch, width).astype(F32)
        factor = norm_factor(own_x)
        unit = own_x * factor
        scaled = dnormed * gain_attn
        dres = factor * (scaled - unit * jnp.mean(scaled * unit, axis=-1, keepdims=True))
        grad_tokens = jnp.concatenate(gmids, axis=0) + dres
        grad_table = jnp.einsum("bmn,hbm->nh", hot_windows, rel_grad.reshape(hits_of), precision=FULL_PRECISION)
        router_grad = router_grad.reshape(2, dp, width)
        router_grad = jnp.where(tp == 0, router_grad, router_grad[::-1])
        router_grad = router_grad.transpose(1, 0, 2).reshape(expert_count, width).T

        def reduced(value, dim):
            return lax.psum(lax.psum_scatter(value, "dp", scatter_dimension=dim, tiled=True), "ctx")

        g_attn = reduced(jnp.sum(dnormed * unit, axis=0)[None], 1)
        g_qkv = reduced(jnp.einsum("rd,jre->jde", own_normed, grad_proj, preferred_element_type=F32), 1)
        g_wout = reduced(jnp.einsum("re,rd->ed", attended, dattn, preferred_element_type=F32), 1)
        g_table = reduced(grad_table, 0)
        g_moe = reduced(gain_moe_grad, 1)
        g_router = reduced(router_grad, 0)
        tokens_out = jnp.stack(tokens_out)
    mine = summed(0, far_mine)
    other = other.astype(F32)

    def by_expert(index):
        return jnp.where(
            tp == 0, jnp.stack([mine[index], other[index]]), jnp.stack([other[index], mine[index]])
        )

    grad_expert_in = by_expert(0)
    grad_expert_out = by_expert(1).transpose(0, 2, 1)
    return (
        tokens_out,
        grad_tokens.reshape(seqs, stretch, width),
        g_attn,
        g_qkv[None],
        g_wout[None],
        g_table[None],
        g_moe,
        g_router[None],
        grad_expert_in[None],
        grad_expert_out[None],
    )


def solution(mesh):
    return jax.shard_map(
        on_device,
        mesh=mesh,
        in_specs=(
            P("dp", "ctx", None),
            P("dp", None),
            P(),
            P("dp", "ctx", None),
            P(None, "dp"),
            P(None, None, "dp", "tp"),
            P(None, "tp", "dp"),
            P(None, "dp", "tp"),
            P(None, "dp"),
            P(None, "dp", None),
            P(None, "dp", "ctx", "tp"),
            P(None, "dp", "tp", "ctx"),
            P("dp", "ctx", None),
        ),
        out_specs=(
            P("dp", "ctx", None),
            P("dp", "ctx", None),
            P(None, "dp"),
            P(None, None, "dp", "tp"),
            P(None, "tp", "dp"),
            P(None, "dp", "tp"),
            P(None, "dp"),
            P(None, "dp", None),
            P(None, "dp", "ctx", "tp"),
            P(None, "dp", "tp", "ctx"),
        ),
        check_vma=False,
    )
```
